32 devices in a mesh: dp: 4 (over y, x), seq: 8 (over z, core).
Axes of the slice: x: 2, y: 2, z: 4, core: 2. Of those that a mesh axis runs over, the one named last changes fastest.
Arguments:
- tokens: bfloat16 [4, 1024, 2048], P('dp', 'seq'), may hold values from -6 to 6
- doc_ids: int32 [4, 1024], P('dp', 'seq'), may hold values from 0 to 3, never falling along the last dimension, each value on 1 to 512 neighbouring positions
- cotangent: bfloat16 [4, 1024, 2048], P('dp', 'seq'), may hold values from -6 to 6
- w_query: bfloat16 [2048, 2048], P('dp'), may hold values from -0.125 to 0.125
- w_key: bfloat16 [2048, 2048], P('dp'), may hold values from -0.125 to 0.125
- w_value: bfloat16 [2048, 2048], P('dp'), may hold values from -0.125 to 0.125
- w_out: bfloat16 [2048, 2048], P('dp'), may hold values from -0.125 to 0.125
- w_gate: bfloat16 [2048, 8192], P('dp'), may hold values from -0.125 to 0.125
- w_up: bfloat16 [2048, 8192], P('dp'), may hold values from -0.125 to 0.125
- w_down: bfloat16 [8192, 2048], P('dp'), may hold values from -0.0625 to 0.0625
- g_query: bfloat16 [2048], replicated, may hold values from 0.5 to 1.5
- g_key: bfloat16 [2048], replicated, may hold values from 0.5 to 1.5
- g_attn: bfloat16 [2048], replicated, may hold values from 0.5 to 1.5
- g_ffn: bfloat16 [2048], replicated, may hold values from 0.5 to 1.5
Outputs:
- layer_out: bfloat16 [4, 1024, 2048], P('dp', 'seq')
- tokens_grad: float32 [4, 1024, 2048], P('dp', 'seq')
- w_query_grad: float32 [2048, 2048], P(('dp', 'seq'))
- w_key_grad: float32 [2048, 2048], P(('dp', 'seq'))
- w_value_grad: float32 [2048, 2048], P(('dp', 'seq'))
- w_out_grad: float32 [2048, 2048], P(('dp', 'seq'))
- w_gate_grad: float32 [2048, 8192], P(('dp', 'seq'))
- w_up_grad: float32 [2048, 8192], P(('dp', 'seq'))
- w_down_grad: float32 [8192, 2048], P(('dp', 'seq'))
- g_query_grad: float32 [2048], P(('dp', 'seq'))
- g_key_grad: float32 [2048], P(('dp', 'seq'))
- g_attn_grad: float32 [2048], P(('dp', 'seq'))
- g_ffn_grad: float32 [2048], P(('dp', 'seq'))
The draws below stay inside these ranges and needn't reach their ends.
Inputs may be any that keep to these rules, and one draw needn't show every extreme that they name: `doc_ids`: along a row the numbers never fall; each document holds 1 to 512 tokens and one holds exactly 512.
All inputs are finite; a program needn't handle non-finite values.
Results may differ from the reference program's by a relative error of at most 0.018.
Values may be sent and summed in bfloat16 or wider, within the bound.
No kernel may reach another device: no remote copies, remote signals or barrier semaphores. Data moves between devices by JAX's collectives and lax.ppermute only.
A program may use at most 768 MiB of HBM per device.

```python
import math
import jax
import jax.numpy as jnp
import numpy as np
from jax import lax

D = 2048
HEAD = 128
F = 2048
FF = 8192
DOCS = 4
ROWS = 4
LEN = 1024


def strengthened(values, stream_key, source, target, parts, factor):
    owner, partner = [(jnp.arange(values.shape[dim]) // (values.shape[dim] // parts)).reshape([-1 if axis == dim else 1 for axis in range(values.ndim)]) for dim in (source, target)]
    chosen = jax.random.permutation(stream_key, parts)[partner]
    strong = (owner == chosen) | (owner == (partner + parts // 2) % parts)
    return jnp.where(strong, factor * values, values)


def steps_of(stream_key, dims, pieces, least, largest):
    def one(position, parts):
        steps = jax.random.uniform(jax.random.fold_in(jax.random.fold_in(stream_key, 6), position), (parts,), jnp.float32, least / len(pieces), largest / len(pieces))
        return jnp.repeat(jnp.exp(steps), dims[position] // parts).reshape((-1,) + (1,) * (len(dims) - position - 1))

    factor_of = one(*pieces[0])
    for cut in pieces[1:]:
        factor_of = factor_of * one(*cut)
    return factor_of


def length_profile(amount, total, reach, slope):
    portions = [(1 << 20) // math.isqrt(rank ** slope) + 1 for rank in range(2, amount + 1)]
    spare, holding = total - reach - (amount - 1), [1] * (amount - 1)
    while spare > 0:
        movable = [i for i in range(amount - 1) if holding[i] < reach]
        pool, budget = sum([portions[i] for i in movable]), spare
        for i in movable:
            more = min(reach - holding[i], max(1, budget * portions[i] // pool), spare)
            holding[i] = holding[i] + more
            spare = spare - more
    return np.array([reach] + holding)


def uneven(rng, count, total, reach, slope):
    if count == 2:
        one = jax.random.randint(rng, (), max(1, total - reach), min(reach, total - 1) + 1)
        return jnp.stack([one, total - one])
    lengths = jnp.asarray(length_profile(count, total, reach, slope), jnp.int32)
    pairs = (count - 1) // 2
    source_of, receiver = lengths[1:1 + 2 * pairs:2], lengths[2:2 + 2 * pairs:2]
    room = jnp.minimum(source_of - 1, reach - receiver)
    shifted = jax.random.randint(jax.random.fold_in(rng, 1), (pairs,), 0, 1 << 20) % (room + 1)
    lengths = lengths.at[1:1 + 2 * pairs:2].set(source_of - shifted).at[2:2 + 2 * pairs:2].set(receiver + shifted)
    return lengths[jax.random.permutation(jax.random.fold_in(rng, 2), count)]


def noise(key, extent, spread, reach, shards=(), kind=jnp.bfloat16):
    level = steps_of(key, extent, shards, -0.22, 0.18) if shards else 1.0
    entries = jax.random.normal(key, extent, jnp.float32) * spread * level
    return jnp.minimum(jnp.maximum(entries, -reach), reach).astype(kind)


def noise_with(key, dims, scale, bound, cuts, heavy, kind=jnp.bfloat16):
    drawn = scale * jax.random.normal(key, dims, jnp.float32)
    if cuts:
        drawn = drawn * steps_of(key, dims, cuts, -0.22, 0.18)
    return jnp.clip(strengthened(drawn, jax.random.fold_in(key, 3), *heavy), -bound, bound).astype(kind)


def setup_inputs(seed: int = 0) -> dict:
    key_of = jax.random.split(jax.random.key(seed), 15)
    return {
        "tokens": noise_with(key_of[0], (ROWS, LEN, D), 1.0, 6.0, ((0, 4), (1, 8)), (1, 2, 8, 2.0)),
        "doc_ids": jax.vmap(lambda own: jnp.searchsorted(jnp.cumsum(uneven(own, DOCS, LEN, LEN // 2, 2)), jnp.arange(LEN), side="right"))(jax.random.split(key_of[1], ROWS)).reshape((ROWS, LEN)).astype(jnp.int32),
        "cotangent": noise(key_of[2], (ROWS, LEN, D), 1.0, 6.0, ((0, 4), (1, 8))),
        "w_query": noise(key_of[3], (D, F), D ** -0.5, 0.125, ((0, 4),)),
        "w_key": noise(key_of[4], (D, F), D ** -0.5, 0.125, ((0, 4),)),
        "w_value": noise(key_of[5], (D, F), D ** -0.5, 0.125, ((0, 4),)),
        "w_out": noise(key_of[6], (F, D), F ** -0.5, 0.125, ((0, 4),)),
        "w_gate": noise(key_of[7], (D, FF), D ** -0.5, 0.125, ((0, 4),)),
        "w_up": noise(key_of[8], (D, FF), D ** -0.5, 0.125, ((0, 4),)),
        "w_down": noise(key_of[9], (FF, D), FF ** -0.5, 0.0625, ((0, 4),)),
        "g_query": jnp.clip(jax.random.uniform(key_of[10], (F,), jnp.float32, 0.5, 1.5), 0.5, 1.5).astype(jnp.bfloat16),
        "g_key": jnp.clip(jax.random.uniform(key_of[11], (F,), jnp.float32, 0.5, 1.5), 0.5, 1.5).astype(jnp.bfloat16),
        "g_attn": jnp.clip(jax.random.uniform(key_of[12], (D,), jnp.float32, 0.5, 1.5), 0.5, 1.5).astype(jnp.bfloat16),
        "g_ffn": jnp.clip(jax.random.uniform(key_of[13], (D,), jnp.float32, 0.5, 1.5), 0.5, 1.5).astype(jnp.bfloat16),
    }


eps = 1e-06
theta = 500000.0
highest = lax.Precision.HIGHEST

@jax.custom_vjp
def low(v):
    return lax.optimization_barrier(v.astype(jnp.bfloat16)).astype(jnp.float32)

@jax.custom_vjp
def low_back(v):
    return v

def low_keep(v):
    return (low(v), None)

def low_pass(kept, grad):
    return (grad,)

def back_keep(v):
    return (v, None)

def back_low(kept, grad):
    return (low(grad),)
low.defvjp(low_keep, low_pass)
low_back.defvjp(back_keep, back_low)

def rotation(positions, head_size):
    half_size = head_size // 2
    frequency = theta ** (-(2.0 * jnp.arange(half_size, dtype=jnp.float32)) / head_size)
    angles = positions.astype(jnp.float32)[:, None] * frequency[None, :]
    return (jnp.cos(angles), jnp.sin(angles))

def rotate(tensor, cosine, sine_part):
    half_size = tensor.shape[-1] // 2
    first_half = tensor[..., :half_size]
    second_half = tensor[..., half_size:]
    cos_wide = cosine[:, None, :]
    sin_wide = sine_part[:, None, :]
    return jnp.concatenate([first_half * cos_wide - second_half * sin_wide, second_half * cos_wide + first_half * sin_wide], -1)

def normed(tensor, gain_vec):
    inverse = lax.rsqrt(lax.optimization_barrier(jnp.mean(tensor * tensor, -1, keepdims=True)) + eps)
    return tensor * inverse * gain_vec

def attend_block(query_block, first_row, key_rows, value_rows, ids_row, scale):
    block_len = query_block.shape[0]
    row_length = key_rows.shape[0]
    scores = low_back(scale * jnp.einsum('bhe,lhe->hbl', query_block, key_rows, precision=highest))
    query_at = first_row + jnp.arange(block_len, dtype=jnp.int32)
    key_at = jnp.arange(row_length, dtype=jnp.int32)
    query_ids = lax.dynamic_slice_in_dim(ids_row, first_row.astype(jnp.int32), block_len)
    allowed = (key_at[None, :] <= query_at[:, None]) & (query_ids[:, None] == ids_row[None, :])
    masked = jnp.where(allowed[None], scores, -1e+30)
    row_max = lax.optimization_barrier(jnp.max(masked, -1, keepdims=True))
    log_total = jnp.log(lax.optimization_barrier(jnp.sum(jnp.exp(masked - row_max), -1, keepdims=True))) + row_max
    weights_low = low(jnp.exp(masked - log_total))
    return jnp.einsum('hbl,lhe->bhe', weights_low, value_rows, precision=highest)

def layer_row(row_tokens, ids_row, w_query, w_key, w_value, w_out, w_gate, w_up, w_down, g_query, g_key, g_attn, g_ffn):
    row_length = row_tokens.shape[0]
    head_size = HEAD
    head_count = w_query.shape[1] // head_size
    positions = jnp.arange(row_length, dtype=jnp.int32)
    cosine, sine_part = rotation(positions, head_size)
    query_pre = low_back(jnp.dot(row_tokens, w_query, precision=highest))
    key_pre = low_back(jnp.dot(row_tokens, w_key, precision=highest))
    query_rot = rotate(normed(query_pre, g_query).reshape(row_length, head_count, head_size), cosine, sine_part)
    key_rot = rotate(normed(key_pre, g_key).reshape(row_length, head_count, head_size), cosine, sine_part)
    queries = low(low_back(query_rot))
    key_rows = low(low_back(key_rot))
    value_rows = low(low_back(jnp.dot(row_tokens, w_value, precision=highest))).reshape(row_length, head_count, head_size)
    block_len = min(512, row_length)
    scale = head_size ** (-0.5)
    starts = jnp.arange(row_length // block_len, dtype=jnp.int32) * block_len
    query_blocks = queries.reshape(row_length // block_len, block_len, head_count, head_size)

    def one_block(block_args):
        return attend_block(block_args[0], block_args[1], key_rows, value_rows, ids_row, scale)
    mixed = lax.map(jax.checkpoint(one_block), (query_blocks, starts)).reshape(row_length, head_count * head_size)
    mixed = low(low_back(mixed))
    attn_out = low_back(jnp.dot(mixed, w_out, precision=highest))
    hidden_state = row_tokens + normed(attn_out, g_attn)
    lowered = low(hidden_state)
    gate = low_back(jnp.dot(lowered, w_gate, precision=highest))
    up_proj = low_back(jnp.dot(lowered, w_up, precision=highest))
    inner = low(gate * jax.nn.sigmoid(gate) * up_proj)
    branch = low_back(jnp.dot(inner, w_down, precision=highest))
    return hidden_state + normed(branch, g_ffn)

def reference(tokens, doc_ids, cotangent, w_query, w_key, w_value, w_out, w_gate, w_up, w_down, g_query, g_key, g_attn, g_ffn):
    float_args = tuple((a.astype(jnp.float32) for a in (w_query, w_key, w_value, w_out, w_gate, w_up, w_down, g_query, g_key, g_attn, g_ffn)))

    def forward(all_tokens, *weight_list):

        def one_row(row_args):
            return layer_row(row_args[0], row_args[1], *weight_list)
        return lax.map(jax.checkpoint(one_row), (all_tokens, doc_ids))
    result, pullback = jax.vjp(forward, tokens.astype(jnp.float32), *float_args)
    gradients = pullback(cotangent.astype(jnp.float32))
    return (result.astype(jnp.bfloat16), gradients[0], gradients[1], gradients[2], gradients[3], gradients[4], gradients[5], gradients[6], gradients[7], gradients[8], gradients[9], gradients[10], gradients[11])
```

```python
import jax
import jax.numpy as jnp
from jax import lax
from jax.sharding import PartitionSpec as P

HEAD = 128
SLABS = 4


eps = 1e-06
theta = 500000.0


def rotation(positions, head_size):
    half_size = head_size // 2
    frequency = theta ** (-(2.0 * jnp.arange(half_size, dtype=jnp.float32)) / head_size)
    angles = positions.astype(jnp.float32)[:, None] * frequency[None, :]
    return (jnp.cos(angles), jnp.sin(angles))


def rotate(tensor, cosine, sine_part):
    half_size = tensor.shape[-1] // 2
    first_half = tensor[..., :half_size]
    second_half = tensor[..., half_size:]
    cos_wide = cosine[:, None, :]
    sin_wide = sine_part[:, None, :]
    return jnp.concatenate(
        [
            first_half * cos_wide - second_half * sin_wide,
            second_half * cos_wide + first_half * sin_wide,
        ],
        -1,
    )


def unrotate(tensor, cosine, sine_part):
    half_size = tensor.shape[-1] // 2
    first_half = tensor[..., :half_size]
    second_half = tensor[..., half_size:]
    cos_wide = cosine[:, None, :]
    sin_wide = sine_part[:, None, :]
    return jnp.concatenate(
        [
            first_half * cos_wide + second_half * sin_wide,
            second_half * cos_wide - first_half * sin_wide,
        ],
        -1,
    )


def inverse_rms(tensor):
    return lax.rsqrt(jnp.mean(tensor * tensor, -1, keepdims=True) + eps)


def norm_back(grad_unit, unit_vec, inverse):
    return inverse * (grad_unit - unit_vec * jnp.mean(grad_unit * unit_vec, -1, keepdims=True))


def visible(own_ids, key_ids, query_at, key_at):
    causal = key_at[None, :] <= query_at[:, None]
    same_doc = own_ids[:, :, None] == key_ids[:, None, :]
    return (causal[None] & same_doc)[:, None]


def masked_scores(query_low, pair_all, allowed, head_count, head_size):
    row_count = pair_all.shape[0]
    row_length = pair_all.shape[1]
    feature_count = head_count * head_size
    key_rows = pair_all[..., :feature_count].reshape(row_count, row_length, head_count, head_size)
    value_rows = pair_all[..., feature_count:].reshape(row_count, row_length, head_count, head_size)
    scores = jnp.einsum(
        "rche,rlhe->rhcl", query_low, key_rows, preferred_element_type=jnp.float32
    ) * head_size ** (-0.5)
    return (jnp.where(allowed, scores, -1e30), key_rows, value_rows)


def columns_of(matrix, parts, slab_count, index):
    lead = matrix.shape[0]
    width = matrix.shape[1] // (parts * slab_count)
    return matrix.reshape(lead, parts, slab_count, width)[:, :, index].reshape(lead, parts * width)


def entries_of(vector, parts, slab_count, index):
    width = vector.shape[0] // (parts * slab_count)
    return vector.reshape(parts, slab_count, width)[:, index].reshape(parts * width)


def shards_by_slab(
    tokens,
    doc_ids,
    cotangent,
    w_query,
    w_key,
    w_value,
    w_out,
    w_gate,
    w_up,
    w_down,
    g_query,
    g_key,
    g_attn,
    g_ffn,
):
    row_count, piece_len, model_width = tokens.shape
    head_size = HEAD
    feature_count = w_query.shape[1]
    head_count = feature_count // head_size
    tok_count = row_count * piece_len
    scale = head_size ** (-0.5)
    seq_count = lax.axis_size("seq")
    parts = lax.axis_size("dp") * seq_count
    slab_count = SLABS
    gather_all = (
        lax.all_gather(w_query, "dp", axis=0, tiled=True),
        lax.all_gather(w_key, "dp", axis=0, tiled=True),
        lax.all_gather(w_value, "dp", axis=0, tiled=True),
        lax.all_gather(w_out, "dp", axis=0, tiled=True),
        lax.all_gather(w_gate, "dp", axis=0, tiled=True),
        lax.all_gather(w_up, "dp", axis=0, tiled=True),
        lax.all_gather(w_down, "dp", axis=0, tiled=True),
    )
    wq_full, wk_full, wv_full, wo_full, wg_full, wu_full, wd_full = gather_all
    gain_query = g_query.astype(jnp.float32)
    gain_key = g_key.astype(jnp.float32)
    gain_attn = g_attn.astype(jnp.float32)
    gain_ffn = g_ffn.astype(jnp.float32)
    flat_tokens = tokens.reshape(tok_count, model_width)
    query_pre = jnp.dot(flat_tokens, wq_full, preferred_element_type=jnp.float32)
    key_pre = jnp.dot(flat_tokens, wk_full, preferred_element_type=jnp.float32)
    value_pre = jnp.dot(flat_tokens, wv_full, preferred_element_type=jnp.float32)
    query_inv = inverse_rms(query_pre)
    query_unit = query_pre * query_inv
    key_inv = inverse_rms(key_pre)
    key_unit = key_pre * key_inv
    first_row = lax.axis_index("seq") * piece_len
    positions = first_row + jnp.tile(jnp.arange(piece_len, dtype=jnp.int32), row_count)
    cosine, sine_part = rotation(positions, head_size)
    query_rot = rotate(
        (query_unit * gain_query).reshape(tok_count, head_count, head_size), cosine, sine_part
    )
    key_rot = rotate(
        (key_unit * gain_key).reshape(tok_count, head_count, head_size), cosine, sine_part
    )
    query_low = query_rot.astype(jnp.bfloat16).reshape(row_count, piece_len, head_count, head_size)
    key_low = key_rot.astype(jnp.bfloat16).reshape(row_count, piece_len, feature_count)
    value_low = value_pre.astype(jnp.bfloat16).reshape(row_count, piece_len, feature_count)
    pair_low = jnp.concatenate([key_low, value_low], -1)
    ids_low = doc_ids.astype(jnp.bfloat16)
    pair_all, ids_all = (
        lax.all_gather(pair_low, "seq", axis=1, tiled=True),
        lax.all_gather(ids_low, "seq", axis=1, tiled=True),
    )
    query_at = first_row + jnp.arange(piece_len, dtype=jnp.int32)
    allowed = visible(ids_low, ids_all, query_at, jnp.arange(pair_all.shape[1], dtype=jnp.int32))
    masked, key_rows, value_rows = masked_scores(
        query_low, pair_all, allowed, head_count, head_size
    )
    row_max = jnp.max(masked, -1, keepdims=True)
    log_total = jnp.log(jnp.sum(jnp.exp(masked - row_max), -1, keepdims=True)) + row_max
    probs_low = jnp.exp(masked - log_total).astype(jnp.bfloat16)
    mixed = jnp.einsum("rhcl,rlhe->rche", probs_low, value_rows, preferred_element_type=jnp.float32)
    mixed_low = mixed.reshape(tok_count, feature_count).astype(jnp.bfloat16)
    attn_out = jnp.dot(mixed_low, wo_full, preferred_element_type=jnp.float32)
    attn_inv = inverse_rms(attn_out)
    attn_unit = attn_out * attn_inv
    hidden_state = flat_tokens.astype(jnp.float32) + attn_unit * gain_attn
    hidden_low = hidden_state.astype(jnp.bfloat16)
    gate = jnp.dot(hidden_low, wg_full, preferred_element_type=jnp.float32)
    up_proj = jnp.dot(hidden_low, wu_full, preferred_element_type=jnp.float32)
    sigma = jax.nn.sigmoid(gate)
    active = gate * sigma
    inner_low = (active * up_proj).astype(jnp.bfloat16)
    branch = jnp.dot(inner_low, wd_full, preferred_element_type=jnp.float32)
    branch_inv = inverse_rms(branch)
    branch_unit = branch * branch_inv
    result = (
        (hidden_state + branch_unit * gain_ffn)
        .astype(jnp.bfloat16)
        .reshape(row_count, piece_len, model_width)
    )
    wq_back, wk_back, wv_back, wo_back, wg_back, wu_back, wd_back = gather_all
    pair_back, ids_back = (pair_all, ids_all)
    grad_out = cotangent.reshape(tok_count, model_width).astype(jnp.float32)
    ffn_gain_term = jnp.sum(grad_out * branch_unit, 0)
    d_branch = norm_back(grad_out * gain_ffn, branch_unit, branch_inv).astype(jnp.bfloat16)
    d_inner = jnp.einsum("nd,fd->nf", d_branch, wd_back, preferred_element_type=jnp.float32)
    d_gate = (d_inner * up_proj * sigma * (1.0 + gate * (1.0 - sigma))).astype(jnp.bfloat16)
    d_up = (d_inner * active).astype(jnp.bfloat16)
    d_hidden = grad_out + jnp.einsum(
        "nf,df->nd", d_gate, wg_back, preferred_element_type=jnp.float32
    )
    d_hidden = d_hidden + jnp.einsum("nf,df->nd", d_up, wu_back, preferred_element_type=jnp.float32)
    mlp_shares = []
    for index in range(slab_count):
        hidden_part = columns_of(hidden_low, parts, slab_count, index)
        inner_part = columns_of(inner_low, parts, slab_count, index)
        gate_term = jnp.einsum("nd,nf->df", hidden_part, d_gate, preferred_element_type=jnp.float32)
        up_term = jnp.einsum("nd,nf->df", hidden_part, d_up, preferred_element_type=jnp.float32)
        down_term = jnp.einsum(
            "nf,nd->fd", inner_part, d_branch, preferred_element_type=jnp.float32
        )
        ffn_term = entries_of(ffn_gain_term, parts, slab_count, index)
        shares = (
            lax.psum_scatter(down_term, ("dp", "seq"), scatter_dimension=0, tiled=True),
            lax.psum_scatter(gate_term, ("dp", "seq"), scatter_dimension=0, tiled=True),
            lax.psum_scatter(up_term, ("dp", "seq"), scatter_dimension=0, tiled=True),
            lax.psum_scatter(ffn_term, ("dp", "seq"), scatter_dimension=0, tiled=True),
        )
        mlp_shares.append(shares)
    down_grad = jnp.concatenate([s[0] for s in mlp_shares], 0)
    gate_grad = jnp.concatenate([s[1] for s in mlp_shares], 0)
    up_grad = jnp.concatenate([s[2] for s in mlp_shares], 0)
    ffn_grad = jnp.concatenate([s[3] for s in mlp_shares], 0)
    attn_gain_term = jnp.sum(d_hidden * attn_unit, 0)
    d_attn = norm_back(d_hidden * gain_attn, attn_unit, attn_inv).astype(jnp.bfloat16)
    d_mixed = jnp.einsum("nd,fd->nf", d_attn, wo_back, preferred_element_type=jnp.float32).astype(
        jnp.bfloat16
    )
    d_mixed = d_mixed.reshape(row_count, piece_len, head_count, head_size)
    sub_len = piece_len // slab_count
    pair_width = pair_back.shape[-1]
    pair_view = pair_back.reshape(row_count, seq_count, slab_count, sub_len, pair_width)
    ids_view = ids_back.reshape(row_count, seq_count, slab_count, sub_len)

    def slab_scores(index):
        pair_part = pair_view[:, :, index].reshape(row_count, seq_count * sub_len, pair_width)
        ids_part = ids_view[:, :, index].reshape(row_count, seq_count * sub_len)
        key_at = (
            jnp.arange(seq_count, dtype=jnp.int32)[:, None] * piece_len
            + index * sub_len
            + jnp.arange(sub_len, dtype=jnp.int32)[None, :]
        ).reshape(seq_count * sub_len)
        allowed_part = visible(ids_low, ids_part, query_at, key_at)
        masked_part, key_part, value_part = masked_scores(
            query_low, pair_part, allowed_part, head_count, head_size
        )
        probs_part = jnp.exp(masked_part - log_total)
        d_probs_part = jnp.einsum(
            "rche,rlhe->rhcl", d_mixed, value_part, preferred_element_type=jnp.float32
        )
        return (probs_part, d_probs_part, key_part)

    row_dot = jnp.zeros((row_count, head_count, piece_len, 1), jnp.float32)
    for index in range(slab_count):
        probs_part, d_probs_part, key_part = slab_scores(index)
        row_dot = row_dot + jnp.sum(probs_part * d_probs_part, -1, keepdims=True)
    query_acc = jnp.zeros((row_count, piece_len, head_count, head_size), jnp.float32)
    pair_shares = []
    for index in range(slab_count):
        probs_part, d_probs_part, key_part = slab_scores(index)
        d_scores = (probs_part * (d_probs_part - row_dot)).astype(jnp.bfloat16)
        query_acc = query_acc + jnp.einsum(
            "rhcl,rlhe->rche", d_scores, key_part, preferred_element_type=jnp.float32
        )
        key_term = (
            jnp.einsum("rhcl,rche->rlhe", d_scores, query_low, preferred_element_type=jnp.float32)
            * scale
        )
        value_term = jnp.einsum(
            "rhcl,rche->rlhe",
            probs_part.astype(jnp.bfloat16),
            d_mixed,
            preferred_element_type=jnp.float32,
        )
        key_count = seq_count * sub_len
        pair_term = jnp.concatenate(
            [
                key_term.reshape(row_count, key_count, feature_count),
                value_term.reshape(row_count, key_count, feature_count),
            ],
            -1,
        )
        pair_shares.append(
            lax.psum_scatter(
                pair_term.astype(jnp.bfloat16), "seq", scatter_dimension=1, tiled=True
            ).astype(jnp.float32)
        )
    pair_grad = jnp.concatenate(pair_shares, 1)
    d_query = (query_acc * scale).astype(jnp.bfloat16)
    d_key = (
        pair_grad[..., :feature_count]
        .astype(jnp.bfloat16)
        .reshape(tok_count, head_count, head_size)
    )
    d_value = pair_grad[..., feature_count:].astype(jnp.bfloat16).reshape(tok_count, feature_count)
    dq_norm = unrotate(
        d_query.reshape(tok_count, head_count, head_size).astype(jnp.float32), cosine, sine_part
    ).reshape(tok_count, feature_count)
    dk_norm = unrotate(d_key.astype(jnp.float32), cosine, sine_part).reshape(
        tok_count, feature_count
    )
    query_gain_term = jnp.sum(dq_norm * query_unit, 0)
    key_gain_term = jnp.sum(dk_norm * key_unit, 0)
    dq_pre = norm_back(dq_norm * gain_query, query_unit, query_inv).astype(jnp.bfloat16)
    dk_pre = norm_back(dk_norm * gain_key, key_unit, key_inv).astype(jnp.bfloat16)
    d_tokens = d_hidden + jnp.einsum(
        "nf,df->nd", dq_pre, wq_back, preferred_element_type=jnp.float32
    )
    d_tokens = d_tokens + jnp.einsum(
        "nf,df->nd", dk_pre, wk_back, preferred_element_type=jnp.float32
    )
    d_tokens = d_tokens + jnp.einsum(
        "nf,df->nd", d_value, wv_back, preferred_element_type=jnp.float32
    )
    attn_shares = []
    for index in range(slab_count):
        token_part = columns_of(flat_tokens, parts, slab_count, index)
        mixed_part = columns_of(mixed_low, parts, slab_count, index)
        query_term = jnp.einsum("nd,nf->df", token_part, dq_pre, preferred_element_type=jnp.float32)
        key_wterm = jnp.einsum("nd,nf->df", token_part, dk_pre, preferred_element_type=jnp.float32)
        value_wterm = jnp.einsum(
            "nd,nf->df", token_part, d_value, preferred_element_type=jnp.float32
        )
        out_term = jnp.einsum("nf,nd->fd", mixed_part, d_attn, preferred_element_type=jnp.float32)
        gq_term = entries_of(query_gain_term, parts, slab_count, index)
        gk_term = entries_of(key_gain_term, parts, slab_count, index)
        ga_term = entries_of(attn_gain_term, parts, slab_count, index)
        shares = (
            lax.psum_scatter(query_term, ("dp", "seq"), scatter_dimension=0, tiled=True),
            lax.psum_scatter(key_wterm, ("dp", "seq"), scatter_dimension=0, tiled=True),
            lax.psum_scatter(value_wterm, ("dp", "seq"), scatter_dimension=0, tiled=True),
            lax.psum_scatter(out_term, ("dp", "seq"), scatter_dimension=0, tiled=True),
            lax.psum_scatter(gq_term, ("dp", "seq"), scatter_dimension=0, tiled=True),
            lax.psum_scatter(gk_term, ("dp", "seq"), scatter_dimension=0, tiled=True),
            lax.psum_scatter(ga_term, ("dp", "seq"), scatter_dimension=0, tiled=True),
        )
        attn_shares.append(shares)
    query_grad = jnp.concatenate([s[0] for s in attn_shares], 0)
    key_grad = jnp.concatenate([s[1] for s in attn_shares], 0)
    value_grad = jnp.concatenate([s[2] for s in attn_shares], 0)
    out_grad = jnp.concatenate([s[3] for s in attn_shares], 0)
    gq_grad = jnp.concatenate([s[4] for s in attn_shares], 0)
    gk_grad = jnp.concatenate([s[5] for s in attn_shares], 0)
    ga_grad = jnp.concatenate([s[6] for s in attn_shares], 0)
    tokens_grad = d_tokens.reshape(row_count, piece_len, model_width)
    return (
        result,
        tokens_grad,
        query_grad,
        key_grad,
        value_grad,
        out_grad,
        gate_grad,
        up_grad,
        down_grad,
        gq_grad,
        gk_grad,
        ga_grad,
        ffn_grad,
    )


def own_columns(matrix, groups, parts, index):
    lead = matrix.shape[0]
    width = matrix.shape[1] // (groups * parts)
    view = matrix.reshape(lead, groups, parts, width)
    return lax.dynamic_index_in_dim(view, index, 2, False).reshape(lead, groups * width)


def gather_seq(piece):
    return lax.all_gather(piece, "seq", axis=1, tiled=True)


def scatter_seq(partial):
    return lax.psum_scatter(partial, "seq", scatter_dimension=1, tiled=True)


def rows_home(partial, seq_count):
    summed = lax.psum_scatter(partial, "dp", scatter_dimension=0, tiled=True)
    lead, width = summed.shape
    return lax.all_to_all(
        summed.reshape(seq_count, lead // seq_count, width), "seq", split_axis=0, concat_axis=0
    )


def shards_by_feature(
    tokens,
    doc_ids,
    cotangent,
    w_query,
    w_key,
    w_value,
    w_out,
    w_gate,
    w_up,
    w_down,
    g_query,
    g_key,
    g_attn,
    g_ffn,
):
    row_count, piece_len, model_width = tokens.shape
    head_size = HEAD
    feature_count = w_query.shape[1]
    scale = head_size ** (-0.5)
    seq_count = lax.axis_size("seq")
    dp_count = lax.axis_size("dp")
    seq_at = lax.axis_index("seq")
    row_len = piece_len * seq_count
    all_count = row_count * row_len
    tok_count = row_count * piece_len
    own_features = feature_count // seq_count
    own_heads = own_features // head_size
    own_hidden = w_gate.shape[1] // seq_count
    low = jnp.bfloat16

    def gather_dp(piece):
        return lax.all_gather(piece, "dp", axis=0, tiled=True)

    def own_piece(tensor):
        view = tensor.reshape(row_count, row_len, -1)
        return lax.dynamic_slice_in_dim(view, seq_at * piece_len, piece_len, 1).reshape(tok_count, -1)

    w_qkv = gather_dp(
        jnp.concatenate([own_columns(w, 1, seq_count, seq_at) for w in (w_query, w_key, w_value)], 1)
    )
    tokens_all = gather_seq(tokens).reshape(all_count, model_width)
    ids_all = gather_seq(doc_ids)
    wo_full = gather_dp(w_out)
    w_hidden = gather_dp(
        jnp.concatenate([own_columns(w, dp_count, seq_count, seq_at) for w in (w_gate, w_up)], 1)
    )
    w_back = gather_dp(
        lax.dynamic_slice_in_dim(
            w_down, seq_at * (own_hidden // dp_count), own_hidden // dp_count, 0
        )
    )
    gain_query = lax.dynamic_slice_in_dim(g_query, seq_at * own_features, own_features).astype(jnp.float32)
    gain_key = lax.dynamic_slice_in_dim(g_key, seq_at * own_features, own_features).astype(jnp.float32)
    gain_attn = g_attn.astype(jnp.float32)
    gain_ffn = g_ffn.astype(jnp.float32)

    qkv = jnp.dot(tokens_all, w_qkv, preferred_element_type=jnp.float32)
    query_pre = qkv[:, :own_features]
    key_pre = qkv[:, own_features : 2 * own_features]
    value_low = qkv[:, 2 * own_features :].astype(low).reshape(row_count, row_len, own_heads, head_size)
    squares = jnp.stack([jnp.sum(query_pre * query_pre, -1), jnp.sum(key_pre * key_pre, -1)])
    inverse = lax.rsqrt(lax.psum(squares, "seq") / feature_count + eps)
    query_inv, key_inv = inverse[0][:, None], inverse[1][:, None]
    query_unit = query_pre * query_inv
    key_unit = key_pre * key_inv
    positions = jnp.tile(jnp.arange(row_len, dtype=jnp.int32), row_count)
    cosine, sine_part = rotation(positions, head_size)
    heads = (all_count, own_heads, head_size)
    split = (row_count, row_len, own_heads, head_size)
    query_low = rotate((query_unit * gain_query).reshape(heads), cosine, sine_part).astype(low).reshape(split)
    key_low = rotate((key_unit * gain_key).reshape(heads), cosine, sine_part).astype(low).reshape(split)
    at = jnp.arange(row_len, dtype=jnp.int32)
    allowed = visible(ids_all, ids_all, at, at)
    scores = jnp.einsum("rche,rlhe->rhcl", query_low, key_low, preferred_element_type=jnp.float32) * scale
    masked = jnp.where(allowed, scores, -1e30)
    row_max = jnp.max(masked, -1, keepdims=True)
    log_total = jnp.log(jnp.sum(jnp.exp(masked - row_max), -1, keepdims=True)) + row_max
    probs = jnp.exp(masked - log_total)
    probs_low = probs.astype(low)
    mixed = jnp.einsum("rhcl,rlhe->rche", probs_low, value_low, preferred_element_type=jnp.float32)
    mixed_low = mixed.astype(low).reshape(all_count, own_features)
    mixed_all = lax.all_gather(mixed_low, "seq", axis=1, tiled=True)
    attn_out = jnp.dot(mixed_all, wo_full, preferred_element_type=jnp.float32)
    attn_inv_all = inverse_rms(attn_out)
    hidden_all = tokens_all.astype(jnp.float32) + attn_out * attn_inv_all * gain_attn
    hidden_low = hidden_all.astype(low)
    attn_inv = own_piece(attn_inv_all)
    attn_unit = own_piece(attn_out) * attn_inv
    hidden_state = tokens.reshape(tok_count, model_width).astype(jnp.float32) + attn_unit * gain_attn

    gate_up = jnp.dot(hidden_low, w_hidden, preferred_element_type=jnp.float32)
    gate, up_proj = gate_up[:, :own_hidden], gate_up[:, own_hidden:]
    sigma = jax.nn.sigmoid(gate)
    active = gate * sigma
    inner_low = (active * up_proj).astype(low)
    branch_part = jnp.dot(inner_low, w_back, preferred_element_type=jnp.float32).astype(low)
    branch = (
        scatter_seq(branch_part.reshape(row_count, row_len, model_width))
        .astype(jnp.float32)
        .reshape(tok_count, model_width)
    )
    branch_inv = inverse_rms(branch)
    branch_unit = branch * branch_inv
    result = (
        (hidden_state + branch_unit * gain_ffn)
        .astype(low)
        .reshape(row_count, piece_len, model_width)
    )

    grad_out = cotangent.reshape(tok_count, model_width).astype(jnp.float32)
    ffn_gain_term = jnp.sum(grad_out * branch_unit, 0)
    d_branch = norm_back(grad_out * gain_ffn, branch_unit, branch_inv).astype(low)
    d_branch_all = gather_seq(d_branch.reshape(row_count, piece_len, model_width)).reshape(all_count, model_width)
    d_inner = jnp.einsum("nd,fd->nf", d_branch_all, w_back, preferred_element_type=jnp.float32)
    d_gate = (d_inner * up_proj * sigma * (1.0 + gate * (1.0 - sigma))).astype(low)
    d_up = (d_inner * active).astype(low)
    d_gate_up = jnp.concatenate([d_gate, d_up], 1)
    d_hidden_part = jnp.einsum("nf,df->nd", d_gate_up, w_hidden, preferred_element_type=jnp.float32).astype(low)
    d_hidden = grad_out + scatter_seq(d_hidden_part.reshape(row_count, row_len, model_width)).astype(
        jnp.float32
    ).reshape(tok_count, model_width)

    attn_gain_term = jnp.sum(d_hidden * attn_unit, 0)
    d_attn = norm_back(d_hidden * gain_attn, attn_unit, attn_inv).astype(low)
    d_mixed = jnp.einsum("nd,fd->nf", d_attn, wo_full, preferred_element_type=jnp.float32).astype(low)
    both = jnp.concatenate(
        [
            d_mixed.reshape(row_count, piece_len, seq_count, own_features),
            d_attn.reshape(row_count, piece_len, seq_count, model_width // seq_count),
        ],
        -1,
    )
    both = lax.all_to_all(both, "seq", split_axis=2, concat_axis=1, tiled=True).reshape(all_count, -1)
    d_mixed = both[:, :own_features].reshape(split)
    d_attn_own = both[:, own_features:]

    down_part = jnp.einsum("nf,nd->fd", inner_low, d_branch_all, preferred_element_type=jnp.float32).astype(low)
    down_grad = lax.psum_scatter(down_part, "dp", scatter_dimension=0, tiled=True).astype(jnp.float32)
    hidden_part = jnp.einsum("nd,nf->df", hidden_low, d_gate_up, preferred_element_type=jnp.float32).astype(low)
    hidden_home = rows_home(hidden_part, seq_count).astype(jnp.float32)
    home_rows = hidden_home.shape[1]
    hidden_home = (
        hidden_home.reshape(seq_count, home_rows, 2, dp_count, own_hidden // dp_count)
        .transpose(2, 1, 3, 0, 4)
        .reshape(2, home_rows, own_hidden * seq_count)
    )
    gate_grad, up_grad = hidden_home[0], hidden_home[1]

    d_probs = jnp.einsum("rche,rlhe->rhcl", d_mixed, value_low, preferred_element_type=jnp.float32)
    row_dot = jnp.sum(probs * d_probs, -1, keepdims=True)
    d_scores = (probs * (d_probs - row_dot)).astype(low)
    d_query = (
        jnp.einsum("rhcl,rlhe->rche", d_scores, key_low, preferred_element_type=jnp.float32) * scale
    ).astype(low)
    d_key = (
        jnp.einsum("rhcl,rche->rlhe", d_scores, query_low, preferred_element_type=jnp.float32) * scale
    ).astype(low)
    d_value = (
        jnp.einsum("rhcl,rche->rlhe", probs_low, d_mixed, preferred_element_type=jnp.float32)
        .astype(low)
        .reshape(all_count, own_features)
    )
    dq_norm = unrotate(d_query.reshape(heads).astype(jnp.float32), cosine, sine_part).reshape(all_count, own_features)
    dk_norm = unrotate(d_key.reshape(heads).astype(jnp.float32), cosine, sine_part).reshape(all_count, own_features)
    query_gain_term = jnp.sum(dq_norm * query_unit, 0)
    key_gain_term = jnp.sum(dk_norm * key_unit, 0)
    dq_gained = dq_norm * gain_query
    dk_gained = dk_norm * gain_key
    dots = jnp.stack([jnp.sum(dq_gained * query_unit, -1), jnp.sum(dk_gained * key_unit, -1)])
    means = lax.psum(dots, "seq") / feature_count
    dq_pre = (query_inv * (dq_gained - query_unit * means[0][:, None])).astype(low)
    dk_pre = (key_inv * (dk_gained - key_unit * means[1][:, None])).astype(low)
    d_qkv = jnp.concatenate([dq_pre, dk_pre, d_value], 1)
    d_tokens_part = jnp.einsum("nf,df->nd", d_qkv, w_qkv, preferred_element_type=jnp.float32).astype(low)
    d_tokens = d_hidden + scatter_seq(d_tokens_part.reshape(row_count, row_len, model_width)).astype(
        jnp.float32
    ).reshape(tok_count, model_width)

    qkv_part = jnp.einsum("nd,nf->df", tokens_all, d_qkv, preferred_element_type=jnp.float32).astype(low)
    out_part = jnp.einsum("nf,nd->fd", mixed_all, d_attn_own, preferred_element_type=jnp.float32).astype(low)
    attn_home = rows_home(jnp.concatenate([qkv_part, out_part], 1), seq_count).astype(jnp.float32)
    attn_rows = attn_home.shape[1]
    attn_home = (
        attn_home.reshape(seq_count, attn_rows, 4, own_features)
        .transpose(2, 1, 0, 3)
        .reshape(4, attn_rows, feature_count)
    )
    zeros = jnp.zeros((feature_count,), jnp.float32)
    gains = jnp.stack(
        [
            lax.dynamic_update_slice_in_dim(zeros, query_gain_term, seq_at * own_features, 0),
            lax.dynamic_update_slice_in_dim(zeros, key_gain_term, seq_at * own_features, 0),
            attn_gain_term,
            ffn_gain_term,
        ]
    )
    gains = lax.psum(gains, ("dp", "seq"))
    share = feature_count // (dp_count * seq_count)
    gains = lax.dynamic_slice_in_dim(
        gains, (lax.axis_index("dp") * seq_count + seq_at) * share, share, 1
    )
    return (
        result,
        d_tokens.reshape(row_count, piece_len, model_width),
        attn_home[0],
        attn_home[1],
        attn_home[2],
        attn_home[3],
        gate_grad,
        up_grad,
        down_grad,
        gains[0],
        gains[1],
        gains[2],
        gains[3],
    )


def shards(tokens, doc_ids, cotangent, w_query, *rest):
    whole_heads = w_query.shape[1] // HEAD % lax.axis_size("seq") == 0
    body = shards_by_feature if whole_heads else shards_by_slab
    return body(tokens, doc_ids, cotangent, w_query, *rest)


def solution(mesh):
    return jax.shard_map(
        shards,
        mesh=mesh,
        in_specs=(
            P("dp", "seq", None),
            P("dp", "seq"),
            P("dp", "seq", None),
            P("dp", None),
            P("dp", None),
            P("dp", None),
            P("dp", None),
            P("dp", None),
            P("dp", None),
            P("dp", None),
            P(),
            P(),
            P(),
            P(),
        ),
        out_specs=(
            P("dp", "seq", None),
            P("dp", "seq", None),
            P(("dp", "seq"), None),
            P(("dp", "seq"), None),
            P(("dp", "seq"), None),
            P(("dp", "seq"), None),
            P(("dp", "seq"), None),
            P(("dp", "seq"), None),
            P(("dp", "seq"), None),
            P(("dp", "seq")),
            P(("dp", "seq")),
            P(("dp", "seq")),
            P(("dp", "seq")),
        ),
        check_vma=False,
    )
```

```python
import functools

import jax
import jax.numpy as jnp
from jax import lax
from jax.experimental import pallas as pl
from jax.experimental.pallas import tpu as pltpu
from jax.sharding import PartitionSpec as P


HEAD = 128
SLABS = 4


eps = 1e-06
theta = 500000.0


def rotation(positions, head_size):
    half_size = head_size // 2
    frequency = theta ** (-(2.0 * jnp.arange(half_size, dtype=jnp.float32)) / head_size)
    angles = positions.astype(jnp.float32)[:, None] * frequency[None, :]
    return (jnp.cos(angles), jnp.sin(angles))


def rotate(tensor, cosine, sine_part):
    half_size = tensor.shape[-1] // 2
    first_half = tensor[..., :half_size]
    second_half = tensor[..., half_size:]
    cos_wide = cosine[:, None, :]
    sin_wide = sine_part[:, None, :]
    return jnp.concatenate(
        [
            first_half * cos_wide - second_half * sin_wide,
            second_half * cos_wide + first_half * sin_wide,
        ],
        -1,
    )


def unrotate(tensor, cosine, sine_part):
    half_size = tensor.shape[-1] // 2
    first_half = tensor[..., :half_size]
    second_half = tensor[..., half_size:]
    cos_wide = cosine[:, None, :]
    sin_wide = sine_part[:, None, :]
    return jnp.concatenate(
        [
            first_half * cos_wide + second_half * sin_wide,
            second_half * cos_wide - first_half * sin_wide,
        ],
        -1,
    )


def inverse_rms(tensor):
    return lax.rsqrt(jnp.mean(tensor * tensor, -1, keepdims=True) + eps)


def norm_back(grad_unit, unit_vec, inverse):
    return inverse * (grad_unit - unit_vec * jnp.mean(grad_unit * unit_vec, -1, keepdims=True))


def visible(own_ids, key_ids, query_at, key_at):
    causal = key_at[None, :] <= query_at[:, None]
    same_doc = own_ids[:, :, None] == key_ids[:, None, :]
    return (causal[None] & same_doc)[:, None]


def masked_scores(query_low, pair_all, allowed, head_count, head_size):
    row_count = pair_all.shape[0]
    row_length = pair_all.shape[1]
    feature_count = head_count * head_size
    key_rows = pair_all[..., :feature_count].reshape(row_count, row_length, head_count, head_size)
    value_rows = pair_all[..., feature_count:].reshape(row_count, row_length, head_count, head_size)
    scores = jnp.einsum(
        "rche,rlhe->rhcl", query_low, key_rows, preferred_element_type=jnp.float32
    ) * head_size ** (-0.5)
    return (jnp.where(allowed, scores, -1e30), key_rows, value_rows)


def columns_of(matrix, parts, slab_count, index):
    lead = matrix.shape[0]
    width = matrix.shape[1] // (parts * slab_count)
    return matrix.reshape(lead, parts, slab_count, width)[:, :, index].reshape(lead, parts * width)


def entries_of(vector, parts, slab_count, index):
    width = vector.shape[0] // (parts * slab_count)
    return vector.reshape(parts, slab_count, width)[:, index].reshape(parts * width)


def shards_by_slab(
    tokens,
    doc_ids,
    cotangent,
    w_query,
    w_key,
    w_value,
    w_out,
    w_gate,
    w_up,
    w_down,
    g_query,
    g_key,
    g_attn,
    g_ffn,
):
    row_count, piece_len, model_width = tokens.shape
    head_size = HEAD
    feature_count = w_query.shape[1]
    head_count = feature_count // head_size
    tok_count = row_count * piece_len
    scale = head_size ** (-0.5)
    seq_count = lax.axis_size("seq")
    parts = lax.axis_size("dp") * seq_count
    slab_count = SLABS
    gather_all = (
        lax.all_gather(w_query, "dp", axis=0, tiled=True),
        lax.all_gather(w_key, "dp", axis=0, tiled=True),
        lax.all_gather(w_value, "dp", axis=0, tiled=True),
        lax.all_gather(w_out, "dp", axis=0, tiled=True),
        lax.all_gather(w_gate, "dp", axis=0, tiled=True),
        lax.all_gather(w_up, "dp", axis=0, tiled=True),
        lax.all_gather(w_down, "dp", axis=0, tiled=True),
    )
    wq_full, wk_full, wv_full, wo_full, wg_full, wu_full, wd_full = gather_all
    gain_query = g_query.astype(jnp.float32)
    gain_key = g_key.astype(jnp.float32)
    gain_attn = g_attn.astype(jnp.float32)
    gain_ffn = g_ffn.astype(jnp.float32)
    flat_tokens = tokens.reshape(tok_count, model_width)
    query_pre = jnp.dot(flat_tokens, wq_full, preferred_element_type=jnp.float32)
    key_pre = jnp.dot(flat_tokens, wk_full, preferred_element_type=jnp.float32)
    value_pre = jnp.dot(flat_tokens, wv_full, preferred_element_type=jnp.float32)
    query_inv = inverse_rms(query_pre)
    query_unit = query_pre * query_inv
    key_inv = inverse_rms(key_pre)
    key_unit = key_pre * key_inv
    first_row = lax.axis_index("seq") * piece_len
    positions = first_row + jnp.tile(jnp.arange(piece_len, dtype=jnp.int32), row_count)
    cosine, sine_part = rotation(positions, head_size)
    query_rot = rotate(
        (query_unit * gain_query).reshape(tok_count, head_count, head_size), cosine, sine_part
    )
    key_rot = rotate(
        (key_unit * gain_key).reshape(tok_count, head_count, head_size), cosine, sine_part
    )
    query_low = query_rot.astype(jnp.bfloat16).reshape(row_count, piece_len, head_count, head_size)
    key_low = key_rot.astype(jnp.bfloat16).reshape(row_count, piece_len, feature_count)
    value_low = value_pre.astype(jnp.bfloat16).reshape(row_count, piece_len, feature_count)
    pair_low = jnp.concatenate([key_low, value_low], -1)
    ids_low = doc_ids.astype(jnp.bfloat16)
    pair_all, ids_all = (
        lax.all_gather(pair_low, "seq", axis=1, tiled=True),
        lax.all_gather(ids_low, "seq", axis=1, tiled=True),
    )
    query_at = first_row + jnp.arange(piece_len, dtype=jnp.int32)
    allowed = visible(ids_low, ids_all, query_at, jnp.arange(pair_all.shape[1], dtype=jnp.int32))
    masked, _, value_rows = masked_scores(
        query_low, pair_all, allowed, head_count, head_size
    )
    row_max = jnp.max(masked, -1, keepdims=True)
    log_total = jnp.log(jnp.sum(jnp.exp(masked - row_max), -1, keepdims=True)) + row_max
    probs_low = jnp.exp(masked - log_total).astype(jnp.bfloat16)
    mixed = jnp.einsum("rhcl,rlhe->rche", probs_low, value_rows, preferred_element_type=jnp.float32)
    mixed_low = mixed.reshape(tok_count, feature_count).astype(jnp.bfloat16)
    attn_out = jnp.dot(mixed_low, wo_full, preferred_element_type=jnp.float32)
    attn_inv = inverse_rms(attn_out)
    attn_unit = attn_out * attn_inv
    hidden_state = flat_tokens.astype(jnp.float32) + attn_unit * gain_attn
    hidden_low = hidden_state.astype(jnp.bfloat16)
    gate = jnp.dot(hidden_low, wg_full, preferred_element_type=jnp.float32)
    up_proj = jnp.dot(hidden_low, wu_full, preferred_element_type=jnp.float32)
    sigma = jax.nn.sigmoid(gate)
    active = gate * sigma
    inner_low = (active * up_proj).astype(jnp.bfloat16)
    branch = jnp.dot(inner_low, wd_full, preferred_element_type=jnp.float32)
    branch_inv = inverse_rms(branch)
    branch_unit = branch * branch_inv
    result = (
        (hidden_state + branch_unit * gain_ffn)
        .astype(jnp.bfloat16)
        .reshape(row_count, piece_len, model_width)
    )
    wq_back, wk_back, wv_back, wo_back, wg_back, wu_back, wd_back = gather_all
    pair_back, ids_back = (pair_all, ids_all)
    grad_out = cotangent.reshape(tok_count, model_width).astype(jnp.float32)
    ffn_gain_term = jnp.sum(grad_out * branch_unit, 0)
    d_branch = norm_back(grad_out * gain_ffn, branch_unit, branch_inv).astype(jnp.bfloat16)
    d_inner = jnp.einsum("nd,fd->nf", d_branch, wd_back, preferred_element_type=jnp.float32)
    d_gate = (d_inner * up_proj * sigma * (1.0 + gate * (1.0 - sigma))).astype(jnp.bfloat16)
    d_up = (d_inner * active).astype(jnp.bfloat16)
    d_hidden = grad_out + jnp.einsum(
        "nf,df->nd", d_gate, wg_back, preferred_element_type=jnp.float32
    )
    d_hidden = d_hidden + jnp.einsum("nf,df->nd", d_up, wu_back, preferred_element_type=jnp.float32)
    mlp_shares = []
    for index in range(slab_count):
        hidden_part = columns_of(hidden_low, parts, slab_count, index)
        inner_part = columns_of(inner_low, parts, slab_count, index)
        gate_term = jnp.einsum("nd,nf->df", hidden_part, d_gate, preferred_element_type=jnp.float32)
        up_term = jnp.einsum("nd,nf->df", hidden_part, d_up, preferred_element_type=jnp.float32)
        down_term = jnp.einsum(
            "nf,nd->fd", inner_part, d_branch, preferred_element_type=jnp.float32
        )
        ffn_term = entries_of(ffn_gain_term, parts, slab_count, index)
        shares = (
            lax.psum_scatter(down_term, ("dp", "seq"), scatter_dimension=0, tiled=True),
            lax.psum_scatter(gate_term, ("dp", "seq"), scatter_dimension=0, tiled=True),
            lax.psum_scatter(up_term, ("dp", "seq"), scatter_dimension=0, tiled=True),
            lax.psum_scatter(ffn_term, ("dp", "seq"), scatter_dimension=0, tiled=True),
        )
        mlp_shares.append(shares)
    down_grad = jnp.concatenate([s[0] for s in mlp_shares], 0)
    gate_grad = jnp.concatenate([s[1] for s in mlp_shares], 0)
    up_grad = jnp.concatenate([s[2] for s in mlp_shares], 0)
    ffn_grad = jnp.concatenate([s[3] for s in mlp_shares], 0)
    attn_gain_term = jnp.sum(d_hidden * attn_unit, 0)
    d_attn = norm_back(d_hidden * gain_attn, attn_unit, attn_inv).astype(jnp.bfloat16)
    d_mixed = jnp.einsum("nd,fd->nf", d_attn, wo_back, preferred_element_type=jnp.float32).astype(
        jnp.bfloat16
    )
    d_mixed = d_mixed.reshape(row_count, piece_len, head_count, head_size)
    sub_len = piece_len // slab_count
    pair_width = pair_back.shape[-1]
    pair_view = pair_back.reshape(row_count, seq_count, slab_count, sub_len, pair_width)
    ids_view = ids_back.reshape(row_count, seq_count, slab_count, sub_len)

    def slab_scores(index):
        pair_part = pair_view[:, :, index].reshape(row_count, seq_count * sub_len, pair_width)
        ids_part = ids_view[:, :, index].reshape(row_count, seq_count * sub_len)
        key_at = (
            jnp.arange(seq_count, dtype=jnp.int32)[:, None] * piece_len
            + index * sub_len
            + jnp.arange(sub_len, dtype=jnp.int32)[None, :]
        ).reshape(seq_count * sub_len)
        allowed_part = visible(ids_low, ids_part, query_at, key_at)
        masked_part, key_part, value_part = masked_scores(
            query_low, pair_part, allowed_part, head_count, head_size
        )
        probs_part = jnp.exp(masked_part - log_total)
        d_probs_part = jnp.einsum(
            "rche,rlhe->rhcl", d_mixed, value_part, preferred_element_type=jnp.float32
        )
        return (probs_part, d_probs_part, key_part)

    row_dot = jnp.zeros((row_count, head_count, piece_len, 1), jnp.float32)
    for index in range(slab_count):
        probs_part, d_probs_part, key_part = slab_scores(index)
        row_dot = row_dot + jnp.sum(probs_part * d_probs_part, -1, keepdims=True)
    query_acc = jnp.zeros((row_count, piece_len, head_count, head_size), jnp.float32)
    pair_shares = []
    for index in range(slab_count):
        probs_part, d_probs_part, key_part = slab_scores(index)
        d_scores = (probs_part * (d_probs_part - row_dot)).astype(jnp.bfloat16)
        query_acc = query_acc + jnp.einsum(
            "rhcl,rlhe->rche", d_scores, key_part, preferred_element_type=jnp.float32
        )
        key_term = (
            jnp.einsum("rhcl,rche->rlhe", d_scores, query_low, preferred_element_type=jnp.float32)
            * scale
        )
        value_term = jnp.einsum(
            "rhcl,rche->rlhe",
            probs_part.astype(jnp.bfloat16),
            d_mixed,
            preferred_element_type=jnp.float32,
        )
        key_count = seq_count * sub_len
        pair_term = jnp.concatenate(
            [
                key_term.reshape(row_count, key_count, feature_count),
                value_term.reshape(row_count, key_count, feature_count),
            ],
            -1,
        )
        pair_shares.append(
            lax.psum_scatter(
                pair_term.astype(jnp.bfloat16), "seq", scatter_dimension=1, tiled=True
            ).astype(jnp.float32)
        )
    pair_grad = jnp.concatenate(pair_shares, 1)
    d_query = (query_acc * scale).astype(jnp.bfloat16)
    d_key = (
        pair_grad[..., :feature_count]
        .astype(jnp.bfloat16)
        .reshape(tok_count, head_count, head_size)
    )
    d_value = pair_grad[..., feature_count:].astype(jnp.bfloat16).reshape(tok_count, feature_count)
    dq_norm = unrotate(
        d_query.reshape(tok_count, head_count, head_size).astype(jnp.float32), cosine, sine_part
    ).reshape(tok_count, feature_count)
    dk_norm = unrotate(d_key.astype(jnp.float32), cosine, sine_part).reshape(
        tok_count, feature_count
    )
    query_gain_term = jnp.sum(dq_norm * query_unit, 0)
    key_gain_term = jnp.sum(dk_norm * key_unit, 0)
    dq_pre = norm_back(dq_norm * gain_query, query_unit, query_inv).astype(jnp.bfloat16)
    dk_pre = norm_back(dk_norm * gain_key, key_unit, key_inv).astype(jnp.bfloat16)
    d_tokens = d_hidden + jnp.einsum(
        "nf,df->nd", dq_pre, wq_back, preferred_element_type=jnp.float32
    )
    d_tokens = d_tokens + jnp.einsum(
        "nf,df->nd", dk_pre, wk_back, preferred_element_type=jnp.float32
    )
    d_tokens = d_tokens + jnp.einsum(
        "nf,df->nd", d_value, wv_back, preferred_element_type=jnp.float32
    )
    attn_shares = []
    for index in range(slab_count):
        token_part = columns_of(flat_tokens, parts, slab_count, index)
        mixed_part = columns_of(mixed_low, parts, slab_count, index)
        query_term = jnp.einsum("nd,nf->df", token_part, dq_pre, preferred_element_type=jnp.float32)
        key_wterm = jnp.einsum("nd,nf->df", token_part, dk_pre, preferred_element_type=jnp.float32)
        value_wterm = jnp.einsum(
            "nd,nf->df", token_part, d_value, preferred_element_type=jnp.float32
        )
        out_term = jnp.einsum("nf,nd->fd", mixed_part, d_attn, preferred_element_type=jnp.float32)
        gq_term = entries_of(query_gain_term, parts, slab_count, index)
        gk_term = entries_of(key_gain_term, parts, slab_count, index)
        ga_term = entries_of(attn_gain_term, parts, slab_count, index)
        shares = (
            lax.psum_scatter(query_term, ("dp", "seq"), scatter_dimension=0, tiled=True),
            lax.psum_scatter(key_wterm, ("dp", "seq"), scatter_dimension=0, tiled=True),
            lax.psum_scatter(value_wterm, ("dp", "seq"), scatter_dimension=0, tiled=True),
            lax.psum_scatter(out_term, ("dp", "seq"), scatter_dimension=0, tiled=True),
            lax.psum_scatter(gq_term, ("dp", "seq"), scatter_dimension=0, tiled=True),
            lax.psum_scatter(gk_term, ("dp", "seq"), scatter_dimension=0, tiled=True),
            lax.psum_scatter(ga_term, ("dp", "seq"), scatter_dimension=0, tiled=True),
        )
        attn_shares.append(shares)
    query_grad = jnp.concatenate([s[0] for s in attn_shares], 0)
    key_grad = jnp.concatenate([s[1] for s in attn_shares], 0)
    value_grad = jnp.concatenate([s[2] for s in attn_shares], 0)
    out_grad = jnp.concatenate([s[3] for s in attn_shares], 0)
    gq_grad = jnp.concatenate([s[4] for s in attn_shares], 0)
    gk_grad = jnp.concatenate([s[5] for s in attn_shares], 0)
    ga_grad = jnp.concatenate([s[6] for s in attn_shares], 0)
    tokens_grad = d_tokens.reshape(row_count, piece_len, model_width)
    return (
        result,
        tokens_grad,
        query_grad,
        key_grad,
        value_grad,
        out_grad,
        gate_grad,
        up_grad,
        down_grad,
        gq_grad,
        gk_grad,
        ga_grad,
        ffn_grad,
    )


def own_columns(matrix, groups, parts, index):
    width = matrix.shape[1] // (groups * parts)
    pieces = [
        lax.dynamic_slice_in_dim(matrix, (group * parts + index) * width, width, 1)
        for group in range(groups)
    ]
    return jnp.concatenate(pieces, 1) if groups > 1 else pieces[0]


def gather_seq(piece):
    return lax.all_gather(piece, "seq", axis=1, tiled=True)


def scatter_seq(partial):
    return lax.psum_scatter(partial, "seq", scatter_dimension=1, tiled=True)


def swap(value, axis, flip):
    return lax.ppermute(value, axis, [(at, at ^ flip) for at in range(lax.axis_size(axis))])


def placed(pieces, index, axis, count):
    width = pieces[0].shape[axis]
    shape = list(pieces[0].shape)
    shape[axis] = width * count
    whole = jnp.zeros(shape, pieces[0].dtype)
    for flip, piece in enumerate(pieces):
        whole = lax.dynamic_update_slice_in_dim(whole, piece, (index ^ flip) * width, axis)
    return whole


def pieces_for(value, name, split_axis):
    count, index = lax.axis_size(name), lax.axis_index(name)
    width = value.shape[split_axis] // count
    return [
        lax.dynamic_slice_in_dim(value, (index ^ flip) * width, width, split_axis)
        for flip in range(count)
    ]


def swapped(pieces, name):
    return [swap(piece, name, flip) if flip else piece for flip, piece in enumerate(pieces)]


def exchanged(value, name, split_axis):
    return swapped(pieces_for(value, name, split_axis), name)


def gather_dp(piece):
    half = piece.shape[0] // 2
    first, second = swap(piece, "dp", 1), swap(piece, "dp", 2)
    top, bottom = swap(first[:half], "dp", 2), swap(second[half:], "dp", 1)
    index = lax.axis_index("dp")
    width = piece.shape[0]
    whole = placed([piece], index, 0, 4)
    for part, place in (
        (first, (index ^ 1) * width),
        (second, (index ^ 2) * width),
        (top, (index ^ 3) * width),
        (bottom, (index ^ 3) * width + half),
    ):
        whole = lax.dynamic_update_slice_in_dim(whole, part, place, 0)
    return whole


def sum_dp(sent, kept):
    got = swap(sent[0], "dp", 1), swap(sent[1], "dp", 2)
    wide = [(kept[at].astype(jnp.float32) + got[at].astype(jnp.float32)) for at in range(2)]
    onward = [side[1].astype(jnp.bfloat16) for side in wide]
    last = swap(onward[0], "dp", 2), swap(onward[1], "dp", 1)
    return jnp.concatenate(
        [wide[at][0] + last[at].astype(jnp.float32) for at in range(2)], 0
    )


def shares_for(partial):
    index = lax.axis_index("dp")
    width = partial.shape[0] // 4
    half = width // 2

    def part(flip, side):
        return lax.dynamic_slice_in_dim(partial, (index ^ flip) * width + side * half, half, 0)

    sent = [jnp.stack([part(1, 0), part(3, 0)]), jnp.stack([part(2, 1), part(3, 1)])]
    kept = [jnp.stack([part(0, 0), part(2, 0)]), jnp.stack([part(0, 1), part(1, 1)])]
    return sent, kept


def total_seq(value):
    flip = 1
    while flip < lax.axis_size("seq"):
        value = value + swap(value, "seq", flip)
        flip *= 2
    return value


def share_of_total(rows):
    for name in ("dp", "seq"):
        flip = lax.axis_size(name) // 2
        while flip:
            halves = rows.reshape(2, rows.shape[0] // 2, rows.shape[1])
            side = lax.axis_index(name) // flip % 2
            kept = lax.dynamic_index_in_dim(halves, side, 0, False)
            sent = lax.dynamic_index_in_dim(halves, 1 - side, 0, False)
            rows = kept + swap(sent, name, flip)
            flip //= 2
    return rows[0]


def rows_home(summed, seq_count):
    lead, width = summed.shape
    return lax.all_to_all(
        summed.reshape(seq_count, lead // seq_count, width), "seq", split_axis=0, concat_axis=0
    ).astype(jnp.float32)


QUERY_BLOCK = 256


def attention_masks(ids_col, ids_row, block, width, start):
    rows = start + lax.broadcasted_iota(jnp.int32, (block, width), 0)
    columns = lax.broadcasted_iota(jnp.int32, (block, width), 1)
    return (columns <= rows) & (ids_col[start : start + block] == ids_row[:, :width])


def attend_kernel(
    q_ref, k_ref, v_ref, qinv_ref, kinv_ref, cos_ref, sin_ref, gq_ref, gk_ref, col_ref, row_ref,
    qlow_ref, klow_ref, vlow_ref, mixed_ref, total_ref, *, scale
):
    low = jnp.bfloat16
    half = q_ref.shape[-1] // 2
    cosine, sine_part = cos_ref[...], sin_ref[...]

    def rotated(ref, inv_ref, gain_ref):
        value = ref[0] * inv_ref[0] * gain_ref[...]
        return (value * cosine + pltpu.roll(value, half, 1) * sine_part).astype(low)

    qlow_ref[0] = rotated(q_ref, qinv_ref, gq_ref)
    klow_ref[0] = rotated(k_ref, kinv_ref, gk_ref)
    vlow_ref[0] = v_ref[0].astype(low)
    length = q_ref.shape[1]
    block = min(QUERY_BLOCK, length)
    ids_col, ids_row = col_ref[0], row_ref[0]
    for start in range(0, length, block):
        width = start + block
        scores = lax.dot_general(
            qlow_ref[0, start:width], klow_ref[0, :width], (((1,), (1,)), ((), ())),
            preferred_element_type=jnp.float32,
        ) * scale
        allowed = attention_masks(ids_col, ids_row, block, width, start)
        masked = jnp.where(allowed, scores, -1e30)
        row_max = jnp.max(masked, -1, keepdims=True)
        log_total = jnp.log(jnp.sum(jnp.exp(masked - row_max), -1, keepdims=True)) + row_max
        total_ref[0, 0, start:width] = log_total
        probs = jnp.exp(masked - log_total).astype(low)
        mixed_ref[0, start:width] = jnp.dot(
            probs, vlow_ref[0, :width], preferred_element_type=jnp.float32
        ).astype(low)


def attend_back_kernel(
    q_ref, k_ref, qinv_ref, kinv_ref, cos_ref, sin_ref, gq_ref, gk_ref, col_ref, row_ref,
    qlow_ref, klow_ref, vlow_ref, total_ref, dmixed_ref,
    dq_ref, dk_ref, dv_ref, dots_ref, gains_ref, key_acc, value_acc, query_acc, *, scale
):
    low = jnp.bfloat16
    half = q_ref.shape[-1] // 2
    length = q_ref.shape[1]
    block = min(QUERY_BLOCK, length)
    ids_col, ids_row = col_ref[0], row_ref[0]
    turned = (((0,), (0,)), ((), ()))
    across = (((1,), (1,)), ((), ()))
    key_acc[...] = jnp.zeros_like(key_acc)
    value_acc[...] = jnp.zeros_like(value_acc)
    for start in range(0, length, block):
        width = start + block
        query = qlow_ref[0, start:width]
        d_mixed = dmixed_ref[0, start:width]
        keys = klow_ref[0, :width]
        scores = lax.dot_general(query, keys, across, preferred_element_type=jnp.float32) * scale
        allowed = attention_masks(ids_col, ids_row, block, width, start)
        probs = jnp.exp(jnp.where(allowed, scores, -1e30) - total_ref[0, 0, start:width])
        d_probs = lax.dot_general(
            d_mixed, vlow_ref[0, :width], across, preferred_element_type=jnp.float32
        )
        row_dot = jnp.sum(probs * d_probs, -1, keepdims=True)
        d_scores = (probs * (d_probs - row_dot)).astype(low)
        query_acc[start:width] = jnp.dot(d_scores, keys, preferred_element_type=jnp.float32)
        key_acc[:width] += lax.dot_general(d_scores, query, turned, preferred_element_type=jnp.float32)
        value_acc[:width] += lax.dot_general(
            probs.astype(low), d_mixed, turned, preferred_element_type=jnp.float32
        )
    dv_ref[0] = value_acc[...].astype(low)
    cosine, sine_part = cos_ref[...], sin_ref[...]

    def turned_back(acc, ref, inv_ref, gain_ref, out_ref, at):
        value = (acc[...] * scale).astype(low).astype(jnp.float32)
        value = value * cosine - pltpu.roll(value, half, 1) * sine_part
        unit = ref[0] * inv_ref[0]
        gains_ref[0, at : at + 1] = jnp.sum(value * unit, 0, keepdims=True)
        value = value * gain_ref[...]
        out_ref[0] = value
        dots_ref[0, 0, :, at : at + 1] = jnp.sum(value * unit, -1, keepdims=True)

    turned_back(query_acc, q_ref, qinv_ref, gq_ref, dq_ref, 0)
    turned_back(key_acc, k_ref, kinv_ref, gk_ref, dk_ref, 1)


def attention_specs(length, heads, head_size):
    wide = lambda at: pl.BlockSpec((1, length, head_size), lambda r, h, at=at: (r, 0, at * heads + h))
    thin = pl.BlockSpec((1, length, 1), lambda r, h: (r, 0, 0))
    table = pl.BlockSpec((length, head_size), lambda r, h: (0, 0))
    gain = pl.BlockSpec((1, head_size), lambda r, h: (0, h))
    flat = pl.BlockSpec((1, 1, length), lambda r, h: (r, 0, 0))
    total = pl.BlockSpec((1, 1, length, 1), lambda r, h: (r, h, 0, 0))
    return wide, thin, table, gain, flat, total


def attend(qkv, inverses, tables, gains, ids, head_size, scale):
    rows, length, width = qkv.shape
    heads = width // (3 * head_size)
    wide, thin, table, gain, flat, total = attention_specs(length, heads, head_size)
    narrow = jax.ShapeDtypeStruct((rows, length, heads * head_size), jnp.bfloat16)
    return pl.pallas_call(
        functools.partial(attend_kernel, scale=scale),
        grid=(rows, heads),
        in_specs=[wide(0), wide(1), wide(2), thin, thin, table, table, gain, gain, thin, flat],
        out_specs=[wide(0), wide(0), wide(0), wide(0), total],
        out_shape=[narrow] * 4 + [jax.ShapeDtypeStruct((rows, heads, length, 1), jnp.float32)],
        name="attend",
    )(qkv, qkv, qkv, *inverses, *tables, *gains, ids[:, :, None], ids[:, None, :])


def attend_back(qkv, inverses, tables, gains, ids, kept, d_mixed, head_size, scale):
    rows, length, width = qkv.shape
    heads = width // (3 * head_size)
    wide, thin, table, gain, flat, total = attention_specs(length, heads, head_size)
    shape = (rows, length, heads * head_size)
    return pl.pallas_call(
        functools.partial(attend_back_kernel, scale=scale),
        grid=(rows, heads),
        in_specs=[wide(0), wide(1), thin, thin, table, table, gain, gain, thin, flat]
        + [wide(0), wide(0), wide(0), total, wide(0)],
        out_specs=[
            wide(0),
            wide(0),
            wide(0),
            pl.BlockSpec((1, 1, length, 2), lambda r, h: (r, h, 0, 0)),
            pl.BlockSpec((1, 2, head_size), lambda r, h: (r, 0, h)),
        ],
        out_shape=[
            jax.ShapeDtypeStruct(shape, jnp.float32),
            jax.ShapeDtypeStruct(shape, jnp.float32),
            jax.ShapeDtypeStruct(shape, jnp.bfloat16),
            jax.ShapeDtypeStruct((rows, heads, length, 2), jnp.float32),
            jax.ShapeDtypeStruct((rows, 2, heads * head_size), jnp.float32),
        ],
        scratch_shapes=[pltpu.VMEM((length, head_size), jnp.float32)] * 3,
        name="attend_back",
    )(qkv, qkv, *inverses, *tables, *gains, ids[:, :, None], ids[:, None, :], *kept, d_mixed)


def shards_by_feature(
    tokens,
    doc_ids,
    cotangent,
    w_query,
    w_key,
    w_value,
    w_out,
    w_gate,
    w_up,
    w_down,
    g_query,
    g_key,
    g_attn,
    g_ffn,
):
    row_count, piece_len, model_width = tokens.shape
    head_size = HEAD
    feature_count = w_query.shape[1]
    scale = head_size ** (-0.5)
    seq_count = lax.axis_size("seq")
    dp_count = lax.axis_size("dp")
    seq_at = lax.axis_index("seq")
    row_len = piece_len * seq_count
    all_count = row_count * row_len
    tok_count = row_count * piece_len
    own_features = feature_count // seq_count
    own_hidden = w_gate.shape[1] // seq_count
    low = jnp.bfloat16

    def own_piece(tensor):
        view = tensor.reshape(row_count, row_len, -1)
        return lax.dynamic_slice_in_dim(view, seq_at * piece_len, piece_len, 1).reshape(tok_count, -1)

    w_qkv = gather_dp(jnp.concatenate([own_columns(w, 1, seq_count, seq_at) for w in (w_query, w_key, w_value)], 1))
    tokens_all = gather_seq(tokens).reshape(all_count, model_width)
    ids_all = total_seq(
        lax.dynamic_update_slice_in_dim(
            jnp.zeros((row_count, row_len), jnp.int32), doc_ids, seq_at * piece_len, 1
        )
    )
    core = seq_at % 2
    half = model_width // 2
    wo_half = gather_dp(lax.dynamic_slice_in_dim(w_out, core * half, half, 1))
    wo_full = placed([wo_half, swap(wo_half, "seq", 1)], core, 1, 2)
    w_hidden = gather_dp(jnp.concatenate([own_columns(w, dp_count, seq_count, seq_at) for w in (w_gate, w_up)], 1))
    w_back = gather_dp(
        lax.dynamic_slice_in_dim(
            w_down, seq_at * (own_hidden // dp_count), own_hidden // dp_count, 0
        ),
    )
    gain_query = lax.dynamic_slice_in_dim(g_query, seq_at * own_features, own_features).astype(jnp.float32)
    gain_key = lax.dynamic_slice_in_dim(g_key, seq_at * own_features, own_features).astype(jnp.float32)
    gain_attn = g_attn.astype(jnp.float32)
    gain_ffn = g_ffn.astype(jnp.float32)

    qkv = jnp.dot(tokens_all, w_qkv, preferred_element_type=jnp.float32)
    query_pre = qkv[:, :own_features]
    key_pre = qkv[:, own_features : 2 * own_features]
    squares = jnp.stack([jnp.sum(query_pre * query_pre, -1), jnp.sum(key_pre * key_pre, -1)])
    cosine, sine_part = rotation(jnp.arange(row_len, dtype=jnp.int32), head_size)
    tables = jnp.concatenate([cosine, cosine], 1), jnp.concatenate([-sine_part, sine_part], 1)
    inverse = lax.rsqrt(total_seq(squares) / feature_count + eps)
    inverses = [inverse[at].reshape(row_count, row_len, 1) for at in range(2)]
    norm_gains = gain_query[None, :], gain_key[None, :]
    qkv_rows = qkv.reshape(row_count, row_len, 3 * own_features)
    *kept, mixed_low, log_total = attend(
        qkv_rows, inverses, tables, norm_gains, ids_all, head_size, scale
    )
    mixed_low = mixed_low.reshape(all_count, own_features)
    mixed_all = lax.all_gather(mixed_low, "seq", axis=1, tiled=True)
    attn_out = jnp.dot(mixed_all, wo_full, preferred_element_type=jnp.float32)
    attn_inv_all = inverse_rms(attn_out)
    hidden_all = tokens_all.astype(jnp.float32) + attn_out * attn_inv_all * gain_attn
    hidden_low = hidden_all.astype(low)
    attn_inv = own_piece(attn_inv_all)
    attn_unit = own_piece(attn_out) * attn_inv
    hidden_state = tokens.reshape(tok_count, model_width).astype(jnp.float32) + attn_unit * gain_attn

    gate_up = jnp.dot(hidden_low, w_hidden, preferred_element_type=jnp.float32)
    gate, up_proj = gate_up[:, :own_hidden], gate_up[:, own_hidden:]
    sigma = jax.nn.sigmoid(gate)
    active = gate * sigma
    inner_low = (active * up_proj).astype(low)
    branch_part = jnp.dot(inner_low, w_back, preferred_element_type=jnp.float32).astype(low)
    branch = (
        scatter_seq(branch_part.reshape(row_count, row_len, model_width))
        .astype(jnp.float32)
        .reshape(tok_count, model_width)
    )
    branch_inv = inverse_rms(branch)
    branch_unit = branch * branch_inv
    result = (
        (hidden_state + branch_unit * gain_ffn)
        .astype(low)
        .reshape(row_count, piece_len, model_width)
    )

    grad_out = cotangent.reshape(tok_count, model_width).astype(jnp.float32)
    ffn_gain_term = jnp.sum(grad_out * branch_unit, 0)
    d_branch = norm_back(grad_out * gain_ffn, branch_unit, branch_inv).astype(low)
    d_branch_all = gather_seq(d_branch.reshape(row_count, piece_len, model_width)).reshape(all_count, model_width)
    d_inner = jnp.einsum("nd,fd->nf", d_branch_all, w_back, preferred_element_type=jnp.float32)
    d_gate = (d_inner * up_proj * sigma * (1.0 + gate * (1.0 - sigma))).astype(low)
    d_up = (d_inner * active).astype(low)
    d_gate_up = jnp.concatenate([d_gate, d_up], 1)
    d_hidden_part = jnp.einsum("nf,df->nd", d_gate_up, w_hidden, preferred_element_type=jnp.float32).astype(low)
    d_hidden_sum = scatter_seq(d_hidden_part.reshape(row_count, row_len, model_width))
    down_part = jnp.einsum("nf,nd->fd", inner_low, d_branch_all, preferred_element_type=jnp.float32).astype(low)
    hidden_part = jnp.einsum("nd,nf->df", hidden_low, d_gate_up, preferred_element_type=jnp.float32).astype(low)
    down_grad = sum_dp(*shares_for(down_part))
    hidden_own = sum_dp(*shares_for(hidden_part)).astype(low)
    d_hidden = grad_out + d_hidden_sum.astype(jnp.float32).reshape(tok_count, model_width)

    attn_gain_term = jnp.sum(d_hidden * attn_unit, 0)
    d_attn = norm_back(d_hidden * gain_attn, attn_unit, attn_inv).astype(low)
    d_mixed = jnp.einsum("nd,fd->nf", d_attn, wo_full, preferred_element_type=jnp.float32).astype(low)
    d_mixed = placed(
        exchanged(d_mixed.reshape(row_count, piece_len, feature_count), "seq", 2), seq_at, 1, seq_count
    )
    d_attn_own = placed(
        exchanged(d_attn.reshape(row_count, piece_len, model_width), "seq", 2), seq_at, 1, seq_count
    ).reshape(all_count, -1)

    out_part = jnp.einsum("nf,nd->fd", mixed_all, d_attn_own, preferred_element_type=jnp.float32).astype(low)
    out_own = sum_dp(*shares_for(out_part)).astype(low)
    home = rows_home(jnp.concatenate([hidden_own, out_own], 1), seq_count)
    home_rows = home.shape[1]
    out_grad = home[..., 2 * own_hidden :].transpose(1, 0, 2).reshape(home_rows, feature_count)
    hidden_home = (
        home[..., : 2 * own_hidden]
        .reshape(seq_count, home_rows, 2, dp_count, own_hidden // dp_count)
        .transpose(2, 1, 3, 0, 4)
        .reshape(2, home_rows, own_hidden * seq_count)
    )
    gate_grad, up_grad = hidden_home[0], hidden_home[1]

    dq_gained, dk_gained, d_value, dots, gain_terms = attend_back(
        qkv_rows, inverses, tables, norm_gains, ids_all, (*kept, log_total), d_mixed, head_size, scale
    )
    query_gain_term, key_gain_term = jnp.sum(gain_terms, 0)
    means = total_seq(jnp.sum(dots, 1).reshape(all_count, 2).T) / feature_count

    def norm_back_wide(gained, pre, at):
        inv = inverse[at][:, None]
        gained = gained.reshape(all_count, own_features)
        return (inv * (gained - pre * inv * means[at][:, None])).astype(low)

    dq_pre = norm_back_wide(dq_gained, query_pre, 0)
    dk_pre = norm_back_wide(dk_gained, key_pre, 1)
    d_value = d_value.reshape(all_count, own_features)
    d_qkv = jnp.concatenate([dq_pre, dk_pre, d_value], 1)
    d_tokens_part = jnp.einsum("nf,df->nd", d_qkv, w_qkv, preferred_element_type=jnp.float32).astype(low)
    d_tokens = d_hidden + scatter_seq(d_tokens_part.reshape(row_count, row_len, model_width)).astype(
        jnp.float32
    ).reshape(tok_count, model_width)

    qkv_part = jnp.einsum("nd,nf->df", tokens_all, d_qkv, preferred_element_type=jnp.float32).astype(low)
    attn_home = rows_home(sum_dp(*shares_for(qkv_part)).astype(low), seq_count)
    attn_home = (
        attn_home.reshape(seq_count, home_rows, 3, own_features)
        .transpose(2, 1, 0, 3)
        .reshape(3, home_rows, feature_count)
    )
    zeros = jnp.zeros((feature_count,), jnp.float32)
    gains = jnp.stack(
        [
            lax.dynamic_update_slice_in_dim(zeros, query_gain_term, seq_at * own_features, 0),
            lax.dynamic_update_slice_in_dim(zeros, key_gain_term, seq_at * own_features, 0),
            attn_gain_term,
            ffn_gain_term,
        ]
    )
    share = feature_count // (dp_count * seq_count)
    gains = share_of_total(
        gains.reshape(4, dp_count * seq_count, share).transpose(1, 0, 2).reshape(dp_count * seq_count, 4 * share)
    ).reshape(4, share)
    return (
        result,
        d_tokens.reshape(row_count, piece_len, model_width),
        attn_home[0],
        attn_home[1],
        attn_home[2],
        out_grad,
        gate_grad,
        up_grad,
        down_grad,
        gains[0],
        gains[1],
        gains[2],
        gains[3],
    )


def shards(tokens, doc_ids, cotangent, w_query, *rest):
    if w_query.shape[1] // HEAD % lax.axis_size("seq"):
        return shards_by_slab(tokens, doc_ids, cotangent, w_query, *rest)
    return shards_by_feature(tokens, doc_ids, cotangent, w_query, *rest)


def solution(mesh):
    return jax.shard_map(
        shards,
        mesh=mesh,
        in_specs=(
            P("dp", "seq", None),
            P("dp", "seq"),
            P("dp", "seq", None),
            P("dp", None),
            P("dp", None),
            P("dp", None),
            P("dp", None),
            P("dp", None),
            P("dp", None),
            P("dp", None),
            P(),
            P(),
            P(),
            P(),
        ),
        out_specs=(
            P("dp", "seq", None),
            P("dp", "seq", None),
            P(("dp", "seq"), None),
            P(("dp", "seq"), None),
            P(("dp", "seq"), None),
            P(("dp", "seq"), None),
            P(("dp", "seq"), None),
            P(("dp", "seq"), None),
            P(("dp", "seq"), None),
            P(("dp", "seq")),
            P(("dp", "seq")),
            P(("dp", "seq")),
            P(("dp", "seq")),
        ),
        check_vma=False,
    )
```

```python
import functools

import jax
import jax.numpy as jnp
from jax import lax
from jax.experimental import pallas as pl
from jax.experimental.pallas import tpu as pltpu
from jax.sharding import PartitionSpec as P


HEAD = 128
SLABS = 4
LANES = 128


eps = 1e-06
theta = 500000.0


def rotation(positions, head_size):
    half_size = head_size // 2
    frequency = theta ** (-(2.0 * jnp.arange(half_size, dtype=jnp.float32)) / head_size)
    angles = positions.astype(jnp.float32)[:, None] * frequency[None, :]
    return (jnp.cos(angles), jnp.sin(angles))


def rotate(tensor, cosine, sine_part):
    half_size = tensor.shape[-1] // 2
    first_half = tensor[..., :half_size]
    second_half = tensor[..., half_size:]
    cos_wide = cosine[:, None, :]
    sin_wide = sine_part[:, None, :]
    return jnp.concatenate(
        [
            first_half * cos_wide - second_half * sin_wide,
            second_half * cos_wide + first_half * sin_wide,
        ],
        -1,
    )


def unrotate(tensor, cosine, sine_part):
    half_size = tensor.shape[-1] // 2
    first_half = tensor[..., :half_size]
    second_half = tensor[..., half_size:]
    cos_wide = cosine[:, None, :]
    sin_wide = sine_part[:, None, :]
    return jnp.concatenate(
        [
            first_half * cos_wide + second_half * sin_wide,
            second_half * cos_wide - first_half * sin_wide,
        ],
        -1,
    )


def inverse_rms(tensor):
    return lax.rsqrt(jnp.mean(tensor * tensor, -1, keepdims=True) + eps)


def norm_back(grad_unit, unit_vec, inverse):
    return inverse * (grad_unit - unit_vec * jnp.mean(grad_unit * unit_vec, -1, keepdims=True))


def visible(own_ids, key_ids, query_at, key_at):
    causal = key_at[None, :] <= query_at[:, None]
    same_doc = own_ids[:, :, None] == key_ids[:, None, :]
    return (causal[None] & same_doc)[:, None]


def masked_scores(query_low, pair_all, allowed, head_count, head_size):
    row_count = pair_all.shape[0]
    row_length = pair_all.shape[1]
    feature_count = head_count * head_size
    key_rows = pair_all[..., :feature_count].reshape(row_count, row_length, head_count, head_size)
    value_rows = pair_all[..., feature_count:].reshape(row_count, row_length, head_count, head_size)
    scores = jnp.einsum(
        "rche,rlhe->rhcl", query_low, key_rows, preferred_element_type=jnp.float32
    ) * head_size ** (-0.5)
    return (jnp.where(allowed, scores, -1e30), key_rows, value_rows)


def columns_of(matrix, parts, slab_count, index):
    lead = matrix.shape[0]
    width = matrix.shape[1] // (parts * slab_count)
    return matrix.reshape(lead, parts, slab_count, width)[:, :, index].reshape(lead, parts * width)


def entries_of(vector, parts, slab_count, index):
    width = vector.shape[0] // (parts * slab_count)
    return vector.reshape(parts, slab_count, width)[:, index].reshape(parts * width)


def shards_by_slab(
    tokens,
    doc_ids,
    cotangent,
    w_query,
    w_key,
    w_value,
    w_out,
    w_gate,
    w_up,
    w_down,
    g_query,
    g_key,
    g_attn,
    g_ffn,
):
    row_count, piece_len, model_width = tokens.shape
    head_size = HEAD
    feature_count = w_query.shape[1]
    head_count = feature_count // head_size
    tok_count = row_count * piece_len
    scale = head_size ** (-0.5)
    seq_count = lax.axis_size("seq")
    parts = lax.axis_size("dp") * seq_count
    slab_count = SLABS
    gather_all = (
        lax.all_gather(w_query, "dp", axis=0, tiled=True),
        lax.all_gather(w_key, "dp", axis=0, tiled=True),
        lax.all_gather(w_value, "dp", axis=0, tiled=True),
        lax.all_gather(w_out, "dp", axis=0, tiled=True),
        lax.all_gather(w_gate, "dp", axis=0, tiled=True),
        lax.all_gather(w_up, "dp", axis=0, tiled=True),
        lax.all_gather(w_down, "dp", axis=0, tiled=True),
    )
    wq_full, wk_full, wv_full, wo_full, wg_full, wu_full, wd_full = gather_all
    gain_query = g_query.astype(jnp.float32)
    gain_key = g_key.astype(jnp.float32)
    gain_attn = g_attn.astype(jnp.float32)
    gain_ffn = g_ffn.astype(jnp.float32)
    flat_tokens = tokens.reshape(tok_count, model_width)
    query_pre = jnp.dot(flat_tokens, wq_full, preferred_element_type=jnp.float32)
    key_pre = jnp.dot(flat_tokens, wk_full, preferred_element_type=jnp.float32)
    value_pre = jnp.dot(flat_tokens, wv_full, preferred_element_type=jnp.float32)
    query_inv = inverse_rms(query_pre)
    query_unit = query_pre * query_inv
    key_inv = inverse_rms(key_pre)
    key_unit = key_pre * key_inv
    first_row = lax.axis_index("seq") * piece_len
    positions = first_row + jnp.tile(jnp.arange(piece_len, dtype=jnp.int32), row_count)
    cosine, sine_part = rotation(positions, head_size)
    query_rot = rotate(
        (query_unit * gain_query).reshape(tok_count, head_count, head_size), cosine, sine_part
    )
    key_rot = rotate(
        (key_unit * gain_key).reshape(tok_count, head_count, head_size), cosine, sine_part
    )
    query_low = query_rot.astype(jnp.bfloat16).reshape(row_count, piece_len, head_count, head_size)
    key_low = key_rot.astype(jnp.bfloat16).reshape(row_count, piece_len, feature_count)
    value_low = value_pre.astype(jnp.bfloat16).reshape(row_count, piece_len, feature_count)
    pair_low = jnp.concatenate([key_low, value_low], -1)
    ids_low = doc_ids.astype(jnp.bfloat16)
    pair_all, ids_all = (
        lax.all_gather(pair_low, "seq", axis=1, tiled=True),
        lax.all_gather(ids_low, "seq", axis=1, tiled=True),
    )
    query_at = first_row + jnp.arange(piece_len, dtype=jnp.int32)
    allowed = visible(ids_low, ids_all, query_at, jnp.arange(pair_all.shape[1], dtype=jnp.int32))
    masked, _, value_rows = masked_scores(
        query_low, pair_all, allowed, head_count, head_size
    )
    row_max = jnp.max(masked, -1, keepdims=True)
    log_total = jnp.log(jnp.sum(jnp.exp(masked - row_max), -1, keepdims=True)) + row_max
    probs_low = jnp.exp(masked - log_total).astype(jnp.bfloat16)
    mixed = jnp.einsum("rhcl,rlhe->rche", probs_low, value_rows, preferred_element_type=jnp.float32)
    mixed_low = mixed.reshape(tok_count, feature_count).astype(jnp.bfloat16)
    attn_out = jnp.dot(mixed_low, wo_full, preferred_element_type=jnp.float32)
    attn_inv = inverse_rms(attn_out)
    attn_unit = attn_out * attn_inv
    hidden_state = flat_tokens.astype(jnp.float32) + attn_unit * gain_attn
    hidden_low = hidden_state.astype(jnp.bfloat16)
    gate = jnp.dot(hidden_low, wg_full, preferred_element_type=jnp.float32)
    up_proj = jnp.dot(hidden_low, wu_full, preferred_element_type=jnp.float32)
    sigma = jax.nn.sigmoid(gate)
    active = gate * sigma
    inner_low = (active * up_proj).astype(jnp.bfloat16)
    branch = jnp.dot(inner_low, wd_full, preferred_element_type=jnp.float32)
    branch_inv = inverse_rms(branch)
    branch_unit = branch * branch_inv
    result = (
        (hidden_state + branch_unit * gain_ffn)
        .astype(jnp.bfloat16)
        .reshape(row_count, piece_len, model_width)
    )
    wq_back, wk_back, wv_back, wo_back, wg_back, wu_back, wd_back = gather_all
    pair_back, ids_back = (pair_all, ids_all)
    grad_out = cotangent.reshape(tok_count, model_width).astype(jnp.float32)
    ffn_gain_term = jnp.sum(grad_out * branch_unit, 0)
    d_branch = norm_back(grad_out * gain_ffn, branch_unit, branch_inv).astype(jnp.bfloat16)
    d_inner = jnp.einsum("nd,fd->nf", d_branch, wd_back, preferred_element_type=jnp.float32)
    d_gate = (d_inner * up_proj * sigma * (1.0 + gate * (1.0 - sigma))).astype(jnp.bfloat16)
    d_up = (d_inner * active).astype(jnp.bfloat16)
    d_hidden = grad_out + jnp.einsum(
        "nf,df->nd", d_gate, wg_back, preferred_element_type=jnp.float32
    )
    d_hidden = d_hidden + jnp.einsum("nf,df->nd", d_up, wu_back, preferred_element_type=jnp.float32)
    mlp_shares = []
    for index in range(slab_count):
        hidden_part = columns_of(hidden_low, parts, slab_count, index)
        inner_part = columns_of(inner_low, parts, slab_count, index)
        gate_term = jnp.einsum("nd,nf->df", hidden_part, d_gate, preferred_element_type=jnp.float32)
        up_term = jnp.einsum("nd,nf->df", hidden_part, d_up, preferred_element_type=jnp.float32)
        down_term = jnp.einsum(
            "nf,nd->fd", inner_part, d_branch, preferred_element_type=jnp.float32
        )
        ffn_term = entries_of(ffn_gain_term, parts, slab_count, index)
        shares = (
            lax.psum_scatter(down_term, ("dp", "seq"), scatter_dimension=0, tiled=True),
            lax.psum_scatter(gate_term, ("dp", "seq"), scatter_dimension=0, tiled=True),
            lax.psum_scatter(up_term, ("dp", "seq"), scatter_dimension=0, tiled=True),
            lax.psum_scatter(ffn_term, ("dp", "seq"), scatter_dimension=0, tiled=True),
        )
        mlp_shares.append(shares)
    down_grad = jnp.concatenate([s[0] for s in mlp_shares], 0)
    gate_grad = jnp.concatenate([s[1] for s in mlp_shares], 0)
    up_grad = jnp.concatenate([s[2] for s in mlp_shares], 0)
    ffn_grad = jnp.concatenate([s[3] for s in mlp_shares], 0)
    attn_gain_term = jnp.sum(d_hidden * attn_unit, 0)
    d_attn = norm_back(d_hidden * gain_attn, attn_unit, attn_inv).astype(jnp.bfloat16)
    d_mixed = jnp.einsum("nd,fd->nf", d_attn, wo_back, preferred_element_type=jnp.float32).astype(
        jnp.bfloat16
    )
    d_mixed = d_mixed.reshape(row_count, piece_len, head_count, head_size)
    sub_len = piece_len // slab_count
    pair_width = pair_back.shape[-1]
    pair_view = pair_back.reshape(row_count, seq_count, slab_count, sub_len, pair_width)
    ids_view = ids_back.reshape(row_count, seq_count, slab_count, sub_len)

    def slab_scores(index):
        pair_part = pair_view[:, :, index].reshape(row_count, seq_count * sub_len, pair_width)
        ids_part = ids_view[:, :, index].reshape(row_count, seq_count * sub_len)
        key_at = (
            jnp.arange(seq_count, dtype=jnp.int32)[:, None] * piece_len
            + index * sub_len
            + jnp.arange(sub_len, dtype=jnp.int32)[None, :]
        ).reshape(seq_count * sub_len)
        allowed_part = visible(ids_low, ids_part, query_at, key_at)
        masked_part, key_part, value_part = masked_scores(
            query_low, pair_part, allowed_part, head_count, head_size
        )
        probs_part = jnp.exp(masked_part - log_total)
        d_probs_part = jnp.einsum(
            "rche,rlhe->rhcl", d_mixed, value_part, preferred_element_type=jnp.float32
        )
        return (probs_part, d_probs_part, key_part)

    row_dot = jnp.zeros((row_count, head_count, piece_len, 1), jnp.float32)
    for index in range(slab_count):
        probs_part, d_probs_part, key_part = slab_scores(index)
        row_dot = row_dot + jnp.sum(probs_part * d_probs_part, -1, keepdims=True)
    query_acc = jnp.zeros((row_count, piece_len, head_count, head_size), jnp.float32)
    pair_shares = []
    for index in range(slab_count):
        probs_part, d_probs_part, key_part = slab_scores(index)
        d_scores = (probs_part * (d_probs_part - row_dot)).astype(jnp.bfloat16)
        query_acc = query_acc + jnp.einsum(
            "rhcl,rlhe->rche", d_scores, key_part, preferred_element_type=jnp.float32
        )
        key_term = (
            jnp.einsum("rhcl,rche->rlhe", d_scores, query_low, preferred_element_type=jnp.float32)
            * scale
        )
        value_term = jnp.einsum(
            "rhcl,rche->rlhe",
            probs_part.astype(jnp.bfloat16),
            d_mixed,
            preferred_element_type=jnp.float32,
        )
        key_count = seq_count * sub_len
        pair_term = jnp.concatenate(
            [
                key_term.reshape(row_count, key_count, feature_count),
                value_term.reshape(row_count, key_count, feature_count),
            ],
            -1,
        )
        pair_shares.append(
            lax.psum_scatter(
                pair_term.astype(jnp.bfloat16), "seq", scatter_dimension=1, tiled=True
            ).astype(jnp.float32)
        )
    pair_grad = jnp.concatenate(pair_shares, 1)
    d_query = (query_acc * scale).astype(jnp.bfloat16)
    d_key = (
        pair_grad[..., :feature_count]
        .astype(jnp.bfloat16)
        .reshape(tok_count, head_count, head_size)
    )
    d_value = pair_grad[..., feature_count:].astype(jnp.bfloat16).reshape(tok_count, feature_count)
    dq_norm = unrotate(
        d_query.reshape(tok_count, head_count, head_size).astype(jnp.float32), cosine, sine_part
    ).reshape(tok_count, feature_count)
    dk_norm = unrotate(d_key.astype(jnp.float32), cosine, sine_part).reshape(
        tok_count, feature_count
    )
    query_gain_term = jnp.sum(dq_norm * query_unit, 0)
    key_gain_term = jnp.sum(dk_norm * key_unit, 0)
    dq_pre = norm_back(dq_norm * gain_query, query_unit, query_inv).astype(jnp.bfloat16)
    dk_pre = norm_back(dk_norm * gain_key, key_unit, key_inv).astype(jnp.bfloat16)
    d_tokens = d_hidden + jnp.einsum(
        "nf,df->nd", dq_pre, wq_back, preferred_element_type=jnp.float32
    )
    d_tokens = d_tokens + jnp.einsum(
        "nf,df->nd", dk_pre, wk_back, preferred_element_type=jnp.float32
    )
    d_tokens = d_tokens + jnp.einsum(
        "nf,df->nd", d_value, wv_back, preferred_element_type=jnp.float32
    )
    attn_shares = []
    for index in range(slab_count):
        token_part = columns_of(flat_tokens, parts, slab_count, index)
        mixed_part = columns_of(mixed_low, parts, slab_count, index)
        query_term = jnp.einsum("nd,nf->df", token_part, dq_pre, preferred_element_type=jnp.float32)
        key_wterm = jnp.einsum("nd,nf->df", token_part, dk_pre, preferred_element_type=jnp.float32)
        value_wterm = jnp.einsum(
            "nd,nf->df", token_part, d_value, preferred_element_type=jnp.float32
        )
        out_term = jnp.einsum("nf,nd->fd", mixed_part, d_attn, preferred_element_type=jnp.float32)
        gq_term = entries_of(query_gain_term, parts, slab_count, index)
        gk_term = entries_of(key_gain_term, parts, slab_count, index)
        ga_term = entries_of(attn_gain_term, parts, slab_count, index)
        shares = (
            lax.psum_scatter(query_term, ("dp", "seq"), scatter_dimension=0, tiled=True),
            lax.psum_scatter(key_wterm, ("dp", "seq"), scatter_dimension=0, tiled=True),
            lax.psum_scatter(value_wterm, ("dp", "seq"), scatter_dimension=0, tiled=True),
            lax.psum_scatter(out_term, ("dp", "seq"), scatter_dimension=0, tiled=True),
            lax.psum_scatter(gq_term, ("dp", "seq"), scatter_dimension=0, tiled=True),
            lax.psum_scatter(gk_term, ("dp", "seq"), scatter_dimension=0, tiled=True),
            lax.psum_scatter(ga_term, ("dp", "seq"), scatter_dimension=0, tiled=True),
        )
        attn_shares.append(shares)
    query_grad = jnp.concatenate([s[0] for s in attn_shares], 0)
    key_grad = jnp.concatenate([s[1] for s in attn_shares], 0)
    value_grad = jnp.concatenate([s[2] for s in attn_shares], 0)
    out_grad = jnp.concatenate([s[3] for s in attn_shares], 0)
    gq_grad = jnp.concatenate([s[4] for s in attn_shares], 0)
    gk_grad = jnp.concatenate([s[5] for s in attn_shares], 0)
    ga_grad = jnp.concatenate([s[6] for s in attn_shares], 0)
    tokens_grad = d_tokens.reshape(row_count, piece_len, model_width)
    return (
        result,
        tokens_grad,
        query_grad,
        key_grad,
        value_grad,
        out_grad,
        gate_grad,
        up_grad,
        down_grad,
        gq_grad,
        gk_grad,
        ga_grad,
        ffn_grad,
    )


def own_columns(matrix, groups, parts, index):
    width = matrix.shape[1] // (groups * parts)
    pieces = [
        lax.dynamic_slice_in_dim(matrix, (group * parts + index) * width, width, 1)
        for group in range(groups)
    ]
    return jnp.concatenate(pieces, 1) if groups > 1 else pieces[0]


def gather_seq(piece):
    return lax.all_gather(piece, "seq", axis=1, tiled=True)


def scatter_seq(partial):
    return lax.psum_scatter(partial, "seq", scatter_dimension=1, tiled=True)


def swap(value, axis, flip):
    return lax.ppermute(value, axis, [(at, at ^ flip) for at in range(lax.axis_size(axis))])


def placed(pieces, index, axis, count):
    width = pieces[0].shape[axis]
    shape = list(pieces[0].shape)
    shape[axis] = width * count
    whole = jnp.zeros(shape, pieces[0].dtype)
    for flip, piece in enumerate(pieces):
        whole = lax.dynamic_update_slice_in_dim(whole, piece, (index ^ flip) * width, axis)
    return whole


def pieces_for(value, name, split_axis):
    count, index = lax.axis_size(name), lax.axis_index(name)
    width = value.shape[split_axis] // count
    return [
        lax.dynamic_slice_in_dim(value, (index ^ flip) * width, width, split_axis)
        for flip in range(count)
    ]


def swapped(pieces, name):
    return [swap(piece, name, flip) if flip else piece for flip, piece in enumerate(pieces)]


def exchanged(value, name, split_axis):
    return swapped(pieces_for(value, name, split_axis), name)


def gather_dp(piece):
    half = piece.shape[0] // 2
    first, second = swap(piece, "dp", 1), swap(piece, "dp", 2)
    top, bottom = swap(first[:half], "dp", 2), swap(second[half:], "dp", 1)
    index = lax.axis_index("dp")
    width = piece.shape[0]
    whole = placed([piece], index, 0, 4)
    for part, place in (
        (first, (index ^ 1) * width),
        (second, (index ^ 2) * width),
        (top, (index ^ 3) * width),
        (bottom, (index ^ 3) * width + half),
    ):
        whole = lax.dynamic_update_slice_in_dim(whole, part, place, 0)
    return whole


def sum_dp(sent, kept):
    got = swap(sent[0], "dp", 1), swap(sent[1], "dp", 2)
    wide = [(kept[at].astype(jnp.float32) + got[at].astype(jnp.float32)) for at in range(2)]
    onward = [side[1].astype(jnp.bfloat16) for side in wide]
    last = swap(onward[0], "dp", 2), swap(onward[1], "dp", 1)
    return jnp.concatenate(
        [wide[at][0] + last[at].astype(jnp.float32) for at in range(2)], 0
    )


def shares_for(partial):
    index = lax.axis_index("dp")
    width = partial.shape[0] // 4
    half = width // 2

    def part(flip, side):
        return lax.dynamic_slice_in_dim(partial, (index ^ flip) * width + side * half, half, 0)

    sent = [jnp.stack([part(1, 0), part(3, 0)]), jnp.stack([part(2, 1), part(3, 1)])]
    kept = [jnp.stack([part(0, 0), part(2, 0)]), jnp.stack([part(0, 1), part(1, 1)])]
    return sent, kept


def total_seq(value):
    shape = value.shape
    value = value.reshape(-1, LANES)
    flip = 1
    while flip < lax.axis_size("seq"):
        value = value + swap(value, "seq", flip)
        flip *= 2
    return value.reshape(shape)


def share_of_total(rows):
    for name in ("dp", "seq"):
        flip = lax.axis_size(name) // 2
        while flip:
            halves = rows.reshape(2, rows.shape[0] // 2, rows.shape[1])
            side = lax.axis_index(name) // flip % 2
            kept = lax.dynamic_index_in_dim(halves, side, 0, False)
            sent = lax.dynamic_index_in_dim(halves, 1 - side, 0, False)
            rows = kept + swap(sent, name, flip)
            flip //= 2
    return rows[0]


def settle_kernel(index_ref, *refs, groups, width, count):
    in_refs, out_refs = refs[:count], refs[count:]
    for flip, in_ref in enumerate(in_refs):
        source = index_ref[0] ^ flip
        for at, out_ref in enumerate(out_refs):
            for group in range(groups):
                column = (at * groups + group) * width
                place = pl.multiple_of((group * count + source) * width, width)
                out_ref[:, pl.ds(place, width)] = in_ref[:, column : column + width].astype(jnp.float32)


def rows_home(summed, groups, width):
    pieces = exchanged(summed, "seq", 0)
    count = len(pieces)
    rows, total = pieces[0].shape
    outs = total // (groups * width)
    step = min(16, rows)
    wide = count * groups * width
    return pl.pallas_call(
        functools.partial(settle_kernel, groups=groups, width=width, count=count),
        grid_spec=pltpu.PrefetchScalarGridSpec(
            num_scalar_prefetch=1,
            grid=(rows // step,),
            in_specs=[pl.BlockSpec((step, total), lambda r, index: (r, 0))] * count,
            out_specs=[pl.BlockSpec((step, wide), lambda r, index: (r, 0))] * outs,
        ),
        out_shape=[jax.ShapeDtypeStruct((rows, wide), jnp.float32)] * outs,
        name="settle",
    )(lax.axis_index("seq").reshape(1), *pieces)


QUERY_BLOCK = 256


def attention_masks(ids_col, ids_row, block, width, start):
    rows = start + lax.broadcasted_iota(jnp.int32, (block, width), 0)
    columns = lax.broadcasted_iota(jnp.int32, (block, width), 1)
    return (columns <= rows) & (ids_col[start : start + block] == ids_row[:, :width])


def attend_kernel(
    q_ref, k_ref, v_ref, qinv_ref, kinv_ref, cos_ref, sin_ref, gq_ref, gk_ref, col_ref, row_ref,
    qlow_ref, klow_ref, vlow_ref, mixed_ref, total_ref, *, scale
):
    low = jnp.bfloat16
    half = q_ref.shape[-1] // 2
    cosine, sine_part = cos_ref[...], sin_ref[...]

    def rotated(ref, inv_ref, gain_ref):
        value = ref[0] * inv_ref[0] * gain_ref[...]
        return (value * cosine + pltpu.roll(value, half, 1) * sine_part).astype(low)

    qlow_ref[0] = rotated(q_ref, qinv_ref, gq_ref)
    klow_ref[0] = rotated(k_ref, kinv_ref, gk_ref)
    vlow_ref[0] = v_ref[0].astype(low)
    length = q_ref.shape[1]
    block = min(QUERY_BLOCK, length)
    ids_col, ids_row = col_ref[0], row_ref[0]
    for start in range(0, length, block):
        width = start + block
        scores = lax.dot_general(
            qlow_ref[0, start:width], klow_ref[0, :width], (((1,), (1,)), ((), ())),
            preferred_element_type=jnp.float32,
        ) * scale
        allowed = attention_masks(ids_col, ids_row, block, width, start)
        masked = jnp.where(allowed, scores, -1e30)
        row_max = jnp.max(masked, -1, keepdims=True)
        log_total = jnp.log(jnp.sum(jnp.exp(masked - row_max), -1, keepdims=True)) + row_max
        total_ref[0, 0, start:width] = log_total
        probs = jnp.exp(masked - log_total).astype(low)
        mixed_ref[0, start:width] = jnp.dot(
            probs, vlow_ref[0, :width], preferred_element_type=jnp.float32
        ).astype(low)


def attend_back_kernel(
    q_ref, k_ref, qinv_ref, kinv_ref, cos_ref, sin_ref, gq_ref, gk_ref, col_ref, row_ref,
    qlow_ref, klow_ref, vlow_ref, total_ref, dmixed_ref,
    dq_ref, dk_ref, dv_ref, dots_ref, gains_ref, key_acc, value_acc, query_acc, *, scale
):
    low = jnp.bfloat16
    half = q_ref.shape[-1] // 2
    length = q_ref.shape[1]
    block = min(QUERY_BLOCK, length)
    ids_col, ids_row = col_ref[0], row_ref[0]
    turned = (((0,), (0,)), ((), ()))
    across = (((1,), (1,)), ((), ()))
    key_acc[...] = jnp.zeros_like(key_acc)
    value_acc[...] = jnp.zeros_like(value_acc)
    for start in range(0, length, block):
        width = start + block
        query = qlow_ref[0, start:width]
        d_mixed = dmixed_ref[0, start:width]
        keys = klow_ref[0, :width]
        scores = lax.dot_general(query, keys, across, preferred_element_type=jnp.float32) * scale
        allowed = attention_masks(ids_col, ids_row, block, width, start)
        probs = jnp.exp(jnp.where(allowed, scores, -1e30) - total_ref[0, 0, start:width])
        d_probs = lax.dot_general(
            d_mixed, vlow_ref[0, :width], across, preferred_element_type=jnp.float32
        )
        row_dot = jnp.sum(probs * d_probs, -1, keepdims=True)
        d_scores = (probs * (d_probs - row_dot)).astype(low)
        query_acc[start:width] = jnp.dot(d_scores, keys, preferred_element_type=jnp.float32)
        key_acc[:width] += lax.dot_general(d_scores, query, turned, preferred_element_type=jnp.float32)
        value_acc[:width] += lax.dot_general(
            probs.astype(low), d_mixed, turned, preferred_element_type=jnp.float32
        )
    dv_ref[0] = value_acc[...].astype(low)
    cosine, sine_part = cos_ref[...], sin_ref[...]

    def turned_back(acc, ref, inv_ref, gain_ref, out_ref, at):
        value = (acc[...] * scale).astype(low).astype(jnp.float32)
        value = value * cosine - pltpu.roll(value, half, 1) * sine_part
        unit = ref[0] * inv_ref[0]
        gains_ref[0, at : at + 1] = jnp.sum(value * unit, 0, keepdims=True)
        value = value * gain_ref[...]
        out_ref[0] = value
        dots_ref[0, 0, :, at : at + 1] = jnp.sum(value * unit, -1, keepdims=True)

    turned_back(query_acc, q_ref, qinv_ref, gq_ref, dq_ref, 0)
    turned_back(key_acc, k_ref, kinv_ref, gk_ref, dk_ref, 1)


def attention_specs(length, heads, head_size):
    wide = lambda at: pl.BlockSpec((1, length, head_size), lambda r, h, at=at: (r, 0, at * heads + h))
    thin = pl.BlockSpec((1, length, 1), lambda r, h: (r, 0, 0))
    table = pl.BlockSpec((length, head_size), lambda r, h: (0, 0))
    gain = pl.BlockSpec((1, head_size), lambda r, h: (0, h))
    flat = pl.BlockSpec((1, 1, length), lambda r, h: (r, 0, 0))
    total = pl.BlockSpec((1, 1, length, 1), lambda r, h: (r, h, 0, 0))
    return wide, thin, table, gain, flat, total


def attend(qkv, inverses, tables, gains, ids, head_size, scale):
    rows, length, width = qkv.shape
    heads = width // (3 * head_size)
    wide, thin, table, gain, flat, total = attention_specs(length, heads, head_size)
    narrow = jax.ShapeDtypeStruct((rows, length, heads * head_size), jnp.bfloat16)
    return pl.pallas_call(
        functools.partial(attend_kernel, scale=scale),
        grid=(rows, heads),
        in_specs=[wide(0), wide(1), wide(2), thin, thin, table, table, gain, gain, thin, flat],
        out_specs=[wide(0), wide(0), wide(0), wide(0), total],
        out_shape=[narrow] * 4 + [jax.ShapeDtypeStruct((rows, heads, length, 1), jnp.float32)],
        name="attend",
    )(qkv, qkv, qkv, *inverses, *tables, *gains, ids[:, :, None], ids[:, None, :])


def attend_back(qkv, inverses, tables, gains, ids, kept, d_mixed, head_size, scale):
    rows, length, width = qkv.shape
    heads = width // (3 * head_size)
    wide, thin, table, gain, flat, total = attention_specs(length, heads, head_size)
    shape = (rows, length, heads * head_size)
    return pl.pallas_call(
        functools.partial(attend_back_kernel, scale=scale),
        grid=(rows, heads),
        in_specs=[wide(0), wide(1), thin, thin, table, table, gain, gain, thin, flat]
        + [wide(0), wide(0), wide(0), total, wide(0)],
        out_specs=[
            wide(0),
            wide(0),
            wide(0),
            pl.BlockSpec((1, 1, length, 2), lambda r, h: (r, h, 0, 0)),
            pl.BlockSpec((1, 2, head_size), lambda r, h: (r, 0, h)),
        ],
        out_shape=[
            jax.ShapeDtypeStruct(shape, jnp.float32),
            jax.ShapeDtypeStruct(shape, jnp.float32),
            jax.ShapeDtypeStruct(shape, jnp.bfloat16),
            jax.ShapeDtypeStruct((rows, heads, length, 2), jnp.float32),
            jax.ShapeDtypeStruct((rows, 2, heads * head_size), jnp.float32),
        ],
        scratch_shapes=[pltpu.VMEM((length, head_size), jnp.float32)] * 3,
        name="attend_back",
    )(qkv, qkv, *inverses, *tables, *gains, ids[:, :, None], ids[:, None, :], *kept, d_mixed)


def shards_by_feature(
    tokens,
    doc_ids,
    cotangent,
    w_query,
    w_key,
    w_value,
    w_out,
    w_gate,
    w_up,
    w_down,
    g_query,
    g_key,
    g_attn,
    g_ffn,
):
    row_count, piece_len, model_width = tokens.shape
    head_size = HEAD
    feature_count = w_query.shape[1]
    scale = head_size ** (-0.5)
    seq_count = lax.axis_size("seq")
    dp_count = lax.axis_size("dp")
    seq_at = lax.axis_index("seq")
    row_len = piece_len * seq_count
    all_count = row_count * row_len
    tok_count = row_count * piece_len
    own_features = feature_count // seq_count
    own_hidden = w_gate.shape[1] // seq_count
    low = jnp.bfloat16

    def own_piece(tensor):
        view = tensor.reshape(row_count, row_len, -1)
        return lax.dynamic_slice_in_dim(view, seq_at * piece_len, piece_len, 1).reshape(tok_count, -1)

    w_qkv = gather_dp(jnp.concatenate([own_columns(w, 1, seq_count, seq_at) for w in (w_query, w_key, w_value)], 1))
    tokens_all = gather_seq(tokens).reshape(all_count, model_width)
    ids_all = total_seq(
        lax.dynamic_update_slice_in_dim(
            jnp.zeros((row_count, row_len), jnp.int32), doc_ids, seq_at * piece_len, 1
        )
    )
    core = seq_at % 2
    half = model_width // 2
    wo_half = gather_dp(lax.dynamic_slice_in_dim(w_out, core * half, half, 1))
    wo_full = placed([wo_half, swap(wo_half, "seq", 1)], core, 1, 2)
    w_hidden = gather_dp(jnp.concatenate([own_columns(w, dp_count, seq_count, seq_at) for w in (w_gate, w_up)], 1))
    w_back = gather_dp(
        lax.dynamic_slice_in_dim(
            w_down, seq_at * (own_hidden // dp_count), own_hidden // dp_count, 0
        ),
    )
    gain_query = lax.dynamic_slice_in_dim(g_query, seq_at * own_features, own_features).astype(jnp.float32)
    gain_key = lax.dynamic_slice_in_dim(g_key, seq_at * own_features, own_features).astype(jnp.float32)
    gain_attn = g_attn.astype(jnp.float32)
    gain_ffn = g_ffn.astype(jnp.float32)

    qkv = jnp.dot(tokens_all, w_qkv, preferred_element_type=jnp.float32)
    query_pre = qkv[:, :own_features]
    key_pre = qkv[:, own_features : 2 * own_features]
    squares = jnp.stack([jnp.sum(query_pre * query_pre, -1), jnp.sum(key_pre * key_pre, -1)])
    cosine, sine_part = rotation(jnp.arange(row_len, dtype=jnp.int32), head_size)
    tables = jnp.concatenate([cosine, cosine], 1), jnp.concatenate([-sine_part, sine_part], 1)
    inverse = lax.rsqrt(total_seq(squares) / feature_count + eps)
    inverses = [inverse[at].reshape(row_count, row_len, 1) for at in range(2)]
    norm_gains = gain_query[None, :], gain_key[None, :]
    qkv_rows = qkv.reshape(row_count, row_len, 3 * own_features)
    *kept, mixed_low, log_total = attend(
        qkv_rows, inverses, tables, norm_gains, ids_all, head_size, scale
    )
    mixed_low = mixed_low.reshape(all_count, own_features)
    mixed_all = lax.all_gather(mixed_low, "seq", axis=1, tiled=True)
    attn_out = jnp.dot(mixed_all, wo_full, preferred_element_type=jnp.float32)
    attn_inv_all = inverse_rms(attn_out)
    hidden_all = tokens_all.astype(jnp.float32) + attn_out * attn_inv_all * gain_attn
    hidden_low = hidden_all.astype(low)
    attn_inv = own_piece(attn_inv_all)
    attn_unit = own_piece(attn_out) * attn_inv
    hidden_state = tokens.reshape(tok_count, model_width).astype(jnp.float32) + attn_unit * gain_attn

    gate_up = jnp.dot(hidden_low, w_hidden, preferred_element_type=jnp.float32)
    gate, up_proj = gate_up[:, :own_hidden], gate_up[:, own_hidden:]
    sigma = jax.nn.sigmoid(gate)
    active = gate * sigma
    inner_low = (active * up_proj).astype(low)
    branch_part = jnp.dot(inner_low, w_back, preferred_element_type=jnp.float32).astype(low)
    branch = (
        scatter_seq(branch_part.reshape(row_count, row_len, model_width))
        .astype(jnp.float32)
        .reshape(tok_count, model_width)
    )
    branch_inv = inverse_rms(branch)
    branch_unit = branch * branch_inv
    result = (
        (hidden_state + branch_unit * gain_ffn)
        .astype(low)
        .reshape(row_count, piece_len, model_width)
    )

    grad_out = cotangent.reshape(tok_count, model_width).astype(jnp.float32)
    ffn_gain_term = jnp.sum(grad_out * branch_unit, 0)
    d_branch = norm_back(grad_out * gain_ffn, branch_unit, branch_inv).astype(low)
    d_branch_all = gather_seq(d_branch.reshape(row_count, piece_len, model_width)).reshape(all_count, model_width)
    d_inner = jnp.einsum("nd,fd->nf", d_branch_all, w_back, preferred_element_type=jnp.float32)
    d_gate = (d_inner * up_proj * sigma * (1.0 + gate * (1.0 - sigma))).astype(low)
    d_up = (d_inner * active).astype(low)
    d_gate_up = jnp.concatenate([d_gate, d_up], 1)
    d_hidden_part = jnp.einsum("nf,df->nd", d_gate_up, w_hidden, preferred_element_type=jnp.float32).astype(low)
    d_hidden_sum = scatter_seq(d_hidden_part.reshape(row_count, row_len, model_width))
    hidden_part = jnp.einsum("nd,nf->df", hidden_low, d_gate_up, preferred_element_type=jnp.float32).astype(low)
    down_part = jnp.einsum("nf,nd->fd", inner_low, d_branch_all, preferred_element_type=jnp.float32).astype(low)
    down_grad = sum_dp(*shares_for(down_part))
    hidden_own = sum_dp(*shares_for(hidden_part)).astype(low)
    d_hidden = grad_out + d_hidden_sum.astype(jnp.float32).reshape(tok_count, model_width)

    attn_gain_term = jnp.sum(d_hidden * attn_unit, 0)
    d_attn = norm_back(d_hidden * gain_attn, attn_unit, attn_inv).astype(low)
    d_mixed = jnp.einsum("nd,fd->nf", d_attn, wo_full, preferred_element_type=jnp.float32).astype(low)
    mixed_pieces = exchanged(d_mixed.reshape(row_count, piece_len, feature_count), "seq", 2)
    d_mixed = placed(mixed_pieces, seq_at, 1, seq_count)
    attn_pieces = exchanged(d_attn.reshape(row_count, piece_len, model_width), "seq", 2)
    d_attn_own = placed(attn_pieces, seq_at, 1, seq_count).reshape(all_count, -1)

    out_part = jnp.einsum("nf,nd->fd", mixed_all, d_attn_own, preferred_element_type=jnp.float32).astype(low)
    out_own = sum_dp(*shares_for(out_part)).astype(low)
    gate_grad, up_grad = rows_home(hidden_own, dp_count, own_hidden // dp_count)

    dq_gained, dk_gained, d_value, dots, gain_terms = attend_back(
        qkv_rows, inverses, tables, norm_gains, ids_all, (*kept, log_total), d_mixed, head_size, scale
    )
    query_gain_term, key_gain_term = jnp.sum(gain_terms, 0)
    means = total_seq(jnp.sum(dots, 1).reshape(all_count, 2).T) / feature_count

    def norm_back_wide(gained, pre, at):
        inv = inverse[at][:, None]
        gained = gained.reshape(all_count, own_features)
        return (inv * (gained - pre * inv * means[at][:, None])).astype(low)

    dq_pre = norm_back_wide(dq_gained, query_pre, 0)
    dk_pre = norm_back_wide(dk_gained, key_pre, 1)
    d_value = d_value.reshape(all_count, own_features)
    d_qkv = jnp.concatenate([dq_pre, dk_pre, d_value], 1)
    d_tokens_part = jnp.einsum("nf,df->nd", d_qkv, w_qkv, preferred_element_type=jnp.float32).astype(low)
    d_qkv, d_tokens_part = lax.optimization_barrier((d_qkv, d_tokens_part))
    d_tokens_sum = scatter_seq(d_tokens_part.reshape(row_count, row_len, model_width))
    d_tokens = d_hidden + d_tokens_sum.astype(jnp.float32).reshape(tok_count, model_width)
    qkv_part = jnp.einsum("nd,nf->df", tokens_all, d_qkv, preferred_element_type=jnp.float32).astype(low)
    qkv_own = sum_dp(*shares_for(qkv_part)).astype(low)
    attn_home = rows_home(jnp.concatenate([qkv_own, out_own], 1), 1, own_features)
    zeros = jnp.zeros((feature_count,), jnp.float32)
    gains = jnp.stack(
        [
            lax.dynamic_update_slice_in_dim(zeros, query_gain_term, seq_at * own_features, 0),
            lax.dynamic_update_slice_in_dim(zeros, key_gain_term, seq_at * own_features, 0),
            attn_gain_term,
            ffn_gain_term,
        ]
    )
    share = feature_count // (dp_count * seq_count)
    gains = share_of_total(
        gains.reshape(4, dp_count * seq_count, share).transpose(1, 0, 2).reshape(dp_count * seq_count, 4 * share)
    ).reshape(4, share)
    return (
        result,
        d_tokens.reshape(row_count, piece_len, model_width),
        attn_home[0],
        attn_home[1],
        attn_home[2],
        attn_home[3],
        gate_grad,
        up_grad,
        down_grad,
        gains[0],
        gains[1],
        gains[2],
        gains[3],
    )


def shards(tokens, doc_ids, cotangent, w_query, *rest):
    if w_query.shape[1] // HEAD % lax.axis_size("seq"):
        return shards_by_slab(tokens, doc_ids, cotangent, w_query, *rest)
    return shards_by_feature(tokens, doc_ids, cotangent, w_query, *rest)


def solution(mesh):
    return jax.shard_map(
        shards,
        mesh=mesh,
        in_specs=(
            P("dp", "seq", None),
            P("dp", "seq"),
            P("dp", "seq", None),
            P("dp", None),
            P("dp", None),
            P("dp", None),
            P("dp", None),
            P("dp", None),
            P("dp", None),
            P("dp", None),
            P(),
            P(),
            P(),
            P(),
        ),
        out_specs=(
            P("dp", "seq", None),
            P("dp", "seq", None),
            P(("dp", "seq"), None),
            P(("dp", "seq"), None),
            P(("dp", "seq"), None),
            P(("dp", "seq"), None),
            P(("dp", "seq"), None),
            P(("dp", "seq"), None),
            P(("dp", "seq"), None),
            P(("dp", "seq")),
            P(("dp", "seq")),
            P(("dp", "seq")),
            P(("dp", "seq")),
        ),
        check_vma=False,
    )
```

```python
import functools

import jax
import jax.numpy as jnp
from jax import lax
from jax.experimental import pallas as pl
from jax.experimental.pallas import tpu as pltpu
from jax.sharding import PartitionSpec as P


HEAD = 128
SLABS = 4
LANES = 128


eps = 1e-06
theta = 500000.0


def rotation(positions, head_size):
    half_size = head_size // 2
    frequency = theta ** (-(2.0 * jnp.arange(half_size, dtype=jnp.float32)) / head_size)
    angles = positions.astype(jnp.float32)[:, None] * frequency[None, :]
    return (jnp.cos(angles), jnp.sin(angles))


def rotate(tensor, cosine, sine_part):
    half_size = tensor.shape[-1] // 2
    first_half = tensor[..., :half_size]
    second_half = tensor[..., half_size:]
    cos_wide = cosine[:, None, :]
    sin_wide = sine_part[:, None, :]
    return jnp.concatenate(
        [
            first_half * cos_wide - second_half * sin_wide,
            second_half * cos_wide + first_half * sin_wide,
        ],
        -1,
    )


def unrotate(tensor, cosine, sine_part):
    half_size = tensor.shape[-1] // 2
    first_half = tensor[..., :half_size]
    second_half = tensor[..., half_size:]
    cos_wide = cosine[:, None, :]
    sin_wide = sine_part[:, None, :]
    return jnp.concatenate(
        [
            first_half * cos_wide + second_half * sin_wide,
            second_half * cos_wide - first_half * sin_wide,
        ],
        -1,
    )


def inverse_rms(tensor):
    return lax.rsqrt(jnp.mean(tensor * tensor, -1, keepdims=True) + eps)


def norm_back(grad_unit, unit_vec, inverse):
    return inverse * (grad_unit - unit_vec * jnp.mean(grad_unit * unit_vec, -1, keepdims=True))


def visible(own_ids, key_ids, query_at, key_at):
    causal = key_at[None, :] <= query_at[:, None]
    same_doc = own_ids[:, :, None] == key_ids[:, None, :]
    return (causal[None] & same_doc)[:, None]


def masked_scores(query_low, pair_all, allowed, head_count, head_size):
    row_count = pair_all.shape[0]
    row_length = pair_all.shape[1]
    feature_count = head_count * head_size
    key_rows = pair_all[..., :feature_count].reshape(row_count, row_length, head_count, head_size)
    value_rows = pair_all[..., feature_count:].reshape(row_count, row_length, head_count, head_size)
    scores = jnp.einsum(
        "rche,rlhe->rhcl", query_low, key_rows, preferred_element_type=jnp.float32
    ) * head_size ** (-0.5)
    return (jnp.where(allowed, scores, -1e30), key_rows, value_rows)


def columns_of(matrix, parts, slab_count, index):
    lead = matrix.shape[0]
    width = matrix.shape[1] // (parts * slab_count)
    return matrix.reshape(lead, parts, slab_count, width)[:, :, index].reshape(lead, parts * width)


def entries_of(vector, parts, slab_count, index):
    width = vector.shape[0] // (parts * slab_count)
    return vector.reshape(parts, slab_count, width)[:, index].reshape(parts * width)


def shards_by_slab(
    tokens,
    doc_ids,
    cotangent,
    w_query,
    w_key,
    w_value,
    w_out,
    w_gate,
    w_up,
    w_down,
    g_query,
    g_key,
    g_attn,
    g_ffn,
):
    row_count, piece_len, model_width = tokens.shape
    head_size = HEAD
    feature_count = w_query.shape[1]
    head_count = feature_count // head_size
    tok_count = row_count * piece_len
    scale = head_size ** (-0.5)
    seq_count = lax.axis_size("seq")
    parts = lax.axis_size("dp") * seq_count
    slab_count = SLABS
    gather_all = (
        lax.all_gather(w_query, "dp", axis=0, tiled=True),
        lax.all_gather(w_key, "dp", axis=0, tiled=True),
        lax.all_gather(w_value, "dp", axis=0, tiled=True),
        lax.all_gather(w_out, "dp", axis=0, tiled=True),
        lax.all_gather(w_gate, "dp", axis=0, tiled=True),
        lax.all_gather(w_up, "dp", axis=0, tiled=True),
        lax.all_gather(w_down, "dp", axis=0, tiled=True),
    )
    wq_full, wk_full, wv_full, wo_full, wg_full, wu_full, wd_full = gather_all
    gain_query = g_query.astype(jnp.float32)
    gain_key = g_key.astype(jnp.float32)
    gain_attn = g_attn.astype(jnp.float32)
    gain_ffn = g_ffn.astype(jnp.float32)
    flat_tokens = tokens.reshape(tok_count, model_width)
    query_pre = jnp.dot(flat_tokens, wq_full, preferred_element_type=jnp.float32)
    key_pre = jnp.dot(flat_tokens, wk_full, preferred_element_type=jnp.float32)
    value_pre = jnp.dot(flat_tokens, wv_full, preferred_element_type=jnp.float32)
    query_inv = inverse_rms(query_pre)
    query_unit = query_pre * query_inv
    key_inv = inverse_rms(key_pre)
    key_unit = key_pre * key_inv
    first_row = lax.axis_index("seq") * piece_len
    positions = first_row + jnp.tile(jnp.arange(piece_len, dtype=jnp.int32), row_count)
    cosine, sine_part = rotation(positions, head_size)
    query_rot = rotate(
        (query_unit * gain_query).reshape(tok_count, head_count, head_size), cosine, sine_part
    )
    key_rot = rotate(
        (key_unit * gain_key).reshape(tok_count, head_count, head_size), cosine, sine_part
    )
    query_low = query_rot.astype(jnp.bfloat16).reshape(row_count, piece_len, head_count, head_size)
    key_low = key_rot.astype(jnp.bfloat16).reshape(row_count, piece_len, feature_count)
    value_low = value_pre.astype(jnp.bfloat16).reshape(row_count, piece_len, feature_count)
    pair_low = jnp.concatenate([key_low, value_low], -1)
    ids_low = doc_ids.astype(jnp.bfloat16)
    pair_all, ids_all = (
        lax.all_gather(pair_low, "seq", axis=1, tiled=True),
        lax.all_gather(ids_low, "seq", axis=1, tiled=True),
    )
    query_at = first_row + jnp.arange(piece_len, dtype=jnp.int32)
    allowed = visible(ids_low, ids_all, query_at, jnp.arange(pair_all.shape[1], dtype=jnp.int32))
    masked, _, value_rows = masked_scores(
        query_low, pair_all, allowed, head_count, head_size
    )
    row_max = jnp.max(masked, -1, keepdims=True)
    log_total = jnp.log(jnp.sum(jnp.exp(masked - row_max), -1, keepdims=True)) + row_max
    probs_low = jnp.exp(masked - log_total).astype(jnp.bfloat16)
    mixed = jnp.einsum("rhcl,rlhe->rche", probs_low, value_rows, preferred_element_type=jnp.float32)
    mixed_low = mixed.reshape(tok_count, feature_count).astype(jnp.bfloat16)
    attn_out = jnp.dot(mixed_low, wo_full, preferred_element_type=jnp.float32)
    attn_inv = inverse_rms(attn_out)
    attn_unit = attn_out * attn_inv
    hidden_state = flat_tokens.astype(jnp.float32) + attn_unit * gain_attn
    hidden_low = hidden_state.astype(jnp.bfloat16)
    gate = jnp.dot(hidden_low, wg_full, preferred_element_type=jnp.float32)
    up_proj = jnp.dot(hidden_low, wu_full, preferred_element_type=jnp.float32)
    sigma = jax.nn.sigmoid(gate)
    active = gate * sigma
    inner_low = (active * up_proj).astype(jnp.bfloat16)
    branch = jnp.dot(inner_low, wd_full, preferred_element_type=jnp.float32)
    branch_inv = inverse_rms(branch)
    branch_unit = branch * branch_inv
    result = (
        (hidden_state + branch_unit * gain_ffn)
        .astype(jnp.bfloat16)
        .reshape(row_count, piece_len, model_width)
    )
    wq_back, wk_back, wv_back, wo_back, wg_back, wu_back, wd_back = gather_all
    pair_back, ids_back = (pair_all, ids_all)
    grad_out = cotangent.reshape(tok_count, model_width).astype(jnp.float32)
    ffn_gain_term = jnp.sum(grad_out * branch_unit, 0)
    d_branch = norm_back(grad_out * gain_ffn, branch_unit, branch_inv).astype(jnp.bfloat16)
    d_inner = jnp.einsum("nd,fd->nf", d_branch, wd_back, preferred_element_type=jnp.float32)
    d_gate = (d_inner * up_proj * sigma * (1.0 + gate * (1.0 - sigma))).astype(jnp.bfloat16)
    d_up = (d_inner * active).astype(jnp.bfloat16)
    d_hidden = grad_out + jnp.einsum(
        "nf,df->nd", d_gate, wg_back, preferred_element_type=jnp.float32
    )
    d_hidden = d_hidden + jnp.einsum("nf,df->nd", d_up, wu_back, preferred_element_type=jnp.float32)
    mlp_shares = []
    for index in range(slab_count):
        hidden_part = columns_of(hidden_low, parts, slab_count, index)
        inner_part = columns_of(inner_low, parts, slab_count, index)
        gate_term = jnp.einsum("nd,nf->df", hidden_part, d_gate, preferred_element_type=jnp.float32)
        up_term = jnp.einsum("nd,nf->df", hidden_part, d_up, preferred_element_type=jnp.float32)
        down_term = jnp.einsum(
            "nf,nd->fd", inner_part, d_branch, preferred_element_type=jnp.float32
        )
        ffn_term = entries_of(ffn_gain_term, parts, slab_count, index)
        shares = (
            lax.psum_scatter(down_term, ("dp", "seq"), scatter_dimension=0, tiled=True),
            lax.psum_scatter(gate_term, ("dp", "seq"), scatter_dimension=0, tiled=True),
            lax.psum_scatter(up_term, ("dp", "seq"), scatter_dimension=0, tiled=True),
            lax.psum_scatter(ffn_term, ("dp", "seq"), scatter_dimension=0, tiled=True),
        )
        mlp_shares.append(shares)
    down_grad = jnp.concatenate([s[0] for s in mlp_shares], 0)
    gate_grad = jnp.concatenate([s[1] for s in mlp_shares], 0)
    up_grad = jnp.concatenate([s[2] for s in mlp_shares], 0)
    ffn_grad = jnp.concatenate([s[3] for s in mlp_shares], 0)
    attn_gain_term = jnp.sum(d_hidden * attn_unit, 0)
    d_attn = norm_back(d_hidden * gain_attn, attn_unit, attn_inv).astype(jnp.bfloat16)
    d_mixed = jnp.einsum("nd,fd->nf", d_attn, wo_back, preferred_element_type=jnp.float32).astype(
        jnp.bfloat16
    )
    d_mixed = d_mixed.reshape(row_count, piece_len, head_count, head_size)
    sub_len = piece_len // slab_count
    pair_width = pair_back.shape[-1]
    pair_view = pair_back.reshape(row_count, seq_count, slab_count, sub_len, pair_width)
    ids_view = ids_back.reshape(row_count, seq_count, slab_count, sub_len)

    def slab_scores(index):
        pair_part = pair_view[:, :, index].reshape(row_count, seq_count * sub_len, pair_width)
        ids_part = ids_view[:, :, index].reshape(row_count, seq_count * sub_len)
        key_at = (
            jnp.arange(seq_count, dtype=jnp.int32)[:, None] * piece_len
            + index * sub_len
            + jnp.arange(sub_len, dtype=jnp.int32)[None, :]
        ).reshape(seq_count * sub_len)
        allowed_part = visible(ids_low, ids_part, query_at, key_at)
        masked_part, key_part, value_part = masked_scores(
            query_low, pair_part, allowed_part, head_count, head_size
        )
        probs_part = jnp.exp(masked_part - log_total)
        d_probs_part = jnp.einsum(
            "rche,rlhe->rhcl", d_mixed, value_part, preferred_element_type=jnp.float32
        )
        return (probs_part, d_probs_part, key_part)

    row_dot = jnp.zeros((row_count, head_count, piece_len, 1), jnp.float32)
    for index in range(slab_count):
        probs_part, d_probs_part, key_part = slab_scores(index)
        row_dot = row_dot + jnp.sum(probs_part * d_probs_part, -1, keepdims=True)
    query_acc = jnp.zeros((row_count, piece_len, head_count, head_size), jnp.float32)
    pair_shares = []
    for index in range(slab_count):
        probs_part, d_probs_part, key_part = slab_scores(index)
        d_scores = (probs_part * (d_probs_part - row_dot)).astype(jnp.bfloat16)
        query_acc = query_acc + jnp.einsum(
            "rhcl,rlhe->rche", d_scores, key_part, preferred_element_type=jnp.float32
        )
        key_term = (
            jnp.einsum("rhcl,rche->rlhe", d_scores, query_low, preferred_element_type=jnp.float32)
            * scale
        )
        value_term = jnp.einsum(
            "rhcl,rche->rlhe",
            probs_part.astype(jnp.bfloat16),
            d_mixed,
            preferred_element_type=jnp.float32,
        )
        key_count = seq_count * sub_len
        pair_term = jnp.concatenate(
            [
                key_term.reshape(row_count, key_count, feature_count),
                value_term.reshape(row_count, key_count, feature_count),
            ],
            -1,
        )
        pair_shares.append(
            lax.psum_scatter(
                pair_term.astype(jnp.bfloat16), "seq", scatter_dimension=1, tiled=True
            ).astype(jnp.float32)
        )
    pair_grad = jnp.concatenate(pair_shares, 1)
    d_query = (query_acc * scale).astype(jnp.bfloat16)
    d_key = (
        pair_grad[..., :feature_count]
        .astype(jnp.bfloat16)
        .reshape(tok_count, head_count, head_size)
    )
    d_value = pair_grad[..., feature_count:].astype(jnp.bfloat16).reshape(tok_count, feature_count)
    dq_norm = unrotate(
        d_query.reshape(tok_count, head_count, head_size).astype(jnp.float32), cosine, sine_part
    ).reshape(tok_count, feature_count)
    dk_norm = unrotate(d_key.astype(jnp.float32), cosine, sine_part).reshape(
        tok_count, feature_count
    )
    query_gain_term = jnp.sum(dq_norm * query_unit, 0)
    key_gain_term = jnp.sum(dk_norm * key_unit, 0)
    dq_pre = norm_back(dq_norm * gain_query, query_unit, query_inv).astype(jnp.bfloat16)
    dk_pre = norm_back(dk_norm * gain_key, key_unit, key_inv).astype(jnp.bfloat16)
    d_tokens = d_hidden + jnp.einsum(
        "nf,df->nd", dq_pre, wq_back, preferred_element_type=jnp.float32
    )
    d_tokens = d_tokens + jnp.einsum(
        "nf,df->nd", dk_pre, wk_back, preferred_element_type=jnp.float32
    )
    d_tokens = d_tokens + jnp.einsum(
        "nf,df->nd", d_value, wv_back, preferred_element_type=jnp.float32
    )
    attn_shares = []
    for index in range(slab_count):
        token_part = columns_of(flat_tokens, parts, slab_count, index)
        mixed_part = columns_of(mixed_low, parts, slab_count, index)
        query_term = jnp.einsum("nd,nf->df", token_part, dq_pre, preferred_element_type=jnp.float32)
        key_wterm = jnp.einsum("nd,nf->df", token_part, dk_pre, preferred_element_type=jnp.float32)
        value_wterm = jnp.einsum(
            "nd,nf->df", token_part, d_value, preferred_element_type=jnp.float32
        )
        out_term = jnp.einsum("nf,nd->fd", mixed_part, d_attn, preferred_element_type=jnp.float32)
        gq_term = entries_of(query_gain_term, parts, slab_count, index)
        gk_term = entries_of(key_gain_term, parts, slab_count, index)
        ga_term = entries_of(attn_gain_term, parts, slab_count, index)
        shares = (
            lax.psum_scatter(query_term, ("dp", "seq"), scatter_dimension=0, tiled=True),
            lax.psum_scatter(key_wterm, ("dp", "seq"), scatter_dimension=0, tiled=True),
            lax.psum_scatter(value_wterm, ("dp", "seq"), scatter_dimension=0, tiled=True),
            lax.psum_scatter(out_term, ("dp", "seq"), scatter_dimension=0, tiled=True),
            lax.psum_scatter(gq_term, ("dp", "seq"), scatter_dimension=0, tiled=True),
            lax.psum_scatter(gk_term, ("dp", "seq"), scatter_dimension=0, tiled=True),
            lax.psum_scatter(ga_term, ("dp", "seq"), scatter_dimension=0, tiled=True),
        )
        attn_shares.append(shares)
    query_grad = jnp.concatenate([s[0] for s in attn_shares], 0)
    key_grad = jnp.concatenate([s[1] for s in attn_shares], 0)
    value_grad = jnp.concatenate([s[2] for s in attn_shares], 0)
    out_grad = jnp.concatenate([s[3] for s in attn_shares], 0)
    gq_grad = jnp.concatenate([s[4] for s in attn_shares], 0)
    gk_grad = jnp.concatenate([s[5] for s in attn_shares], 0)
    ga_grad = jnp.concatenate([s[6] for s in attn_shares], 0)
    tokens_grad = d_tokens.reshape(row_count, piece_len, model_width)
    return (
        result,
        tokens_grad,
        query_grad,
        key_grad,
        value_grad,
        out_grad,
        gate_grad,
        up_grad,
        down_grad,
        gq_grad,
        gk_grad,
        ga_grad,
        ffn_grad,
    )


def own_columns(matrix, groups, parts, index):
    width = matrix.shape[1] // (groups * parts)
    pieces = [
        lax.dynamic_slice_in_dim(matrix, (group * parts + index) * width, width, 1)
        for group in range(groups)
    ]
    return jnp.concatenate(pieces, 1) if groups > 1 else pieces[0]


def gather_seq(piece):
    return lax.all_gather(piece, "seq", axis=1, tiled=True)


def scatter_seq(partial):
    return lax.psum_scatter(partial, "seq", scatter_dimension=1, tiled=True)


def swap(value, axis, flip):
    return lax.ppermute(value, axis, [(at, at ^ flip) for at in range(lax.axis_size(axis))])


def place_kernel(spots_ref, *refs):
    *in_refs, out_ref, sems = refs
    copies = []
    for at, in_ref in enumerate(in_refs):
        rows, width = in_ref.shape
        row = pl.multiple_of(spots_ref[2 * at], LANES)
        column = pl.multiple_of(spots_ref[2 * at + 1], LANES)
        copies.append(
            pltpu.make_async_copy(
                in_ref, out_ref.at[pl.ds(row, rows), pl.ds(column, width)], sems.at[at]
            )
        )
    for copy in copies:
        copy.start()
    for copy in copies:
        copy.wait()


def placed(pieces, shape):
    spots = jnp.stack([jnp.int32(at) for _, row, column in pieces for at in (row, column)])
    anywhere = pl.BlockSpec(memory_space=pl.ANY)
    return pl.pallas_call(
        place_kernel,
        grid_spec=pltpu.PrefetchScalarGridSpec(
            num_scalar_prefetch=1,
            grid=(1,),
            in_specs=[anywhere] * len(pieces),
            out_specs=anywhere,
            scratch_shapes=[pltpu.SemaphoreType.DMA((len(pieces),))],
        ),
        out_shape=jax.ShapeDtypeStruct(shape, pieces[0][0].dtype),
        name="place",
    )(spots, *[piece for piece, _, _ in pieces])


def pieces_for(value, name, split_axis):
    count, index = lax.axis_size(name), lax.axis_index(name)
    width = value.shape[split_axis] // count
    return [
        lax.dynamic_slice_in_dim(value, (index ^ flip) * width, width, split_axis)
        for flip in range(count)
    ]


def swapped(pieces, name):
    return [swap(piece, name, flip) if flip else piece for flip, piece in enumerate(pieces)]


def exchanged(value, name, split_axis):
    return swapped(pieces_for(value, name, split_axis), name)


def pieces_dp(piece):
    half = piece.shape[0] // 2
    first, second = swap(piece, "dp", 1), swap(piece, "dp", 2)
    top, bottom = swap(first[:half], "dp", 2), swap(second[half:], "dp", 1)
    index = lax.axis_index("dp")
    width = piece.shape[0]
    far = (index ^ 3) * width
    return [
        (first, (index ^ 1) * width),
        (second, (index ^ 2) * width),
        (top, far),
        (bottom, far + half),
    ]


def gather_dp(piece):
    rows, width = piece.shape
    pieces = [(piece, lax.axis_index("dp") * rows), *pieces_dp(piece)]
    return placed([(part, row, 0) for part, row in pieces], (4 * rows, width))


def sum_dp(sent, kept):
    got = swap(sent[0], "dp", 1), swap(sent[1], "dp", 2)
    wide = [(kept[at].astype(jnp.float32) + got[at].astype(jnp.float32)) for at in range(2)]
    onward = [side[1].astype(jnp.bfloat16) for side in wide]
    last = swap(onward[0], "dp", 2), swap(onward[1], "dp", 1)
    return jnp.concatenate(
        [wide[at][0] + last[at].astype(jnp.float32) for at in range(2)], 0
    )


def shares_for(partial):
    index = lax.axis_index("dp")
    width = partial.shape[0] // 4
    half = width // 2

    def part(flip, side):
        return lax.dynamic_slice_in_dim(partial, (index ^ flip) * width + side * half, half, 0)

    sent = [jnp.stack([part(1, 0), part(3, 0)]), jnp.stack([part(2, 1), part(3, 1)])]
    kept = [jnp.stack([part(0, 0), part(2, 0)]), jnp.stack([part(0, 1), part(1, 1)])]
    return sent, kept


def total_seq(value):
    shape = value.shape
    value = value.reshape(-1, LANES)
    flip = 1
    while flip < lax.axis_size("seq"):
        value = value + swap(value, "seq", flip)
        flip *= 2
    return value.reshape(shape)


def share_dp(rows):
    flip = lax.axis_size("dp") // 2
    while flip:
        halves = rows.reshape(2, rows.shape[0] // 2, rows.shape[1])
        side = lax.axis_index("dp") // flip % 2
        kept = lax.dynamic_index_in_dim(halves, side, 0, False)
        sent = lax.dynamic_index_in_dim(halves, 1 - side, 0, False)
        rows = kept + swap(sent, "dp", flip)
        flip //= 2
    return rows[0]


def settle_kernel(index_ref, *refs, groups, width, count):
    in_refs, out_refs = refs[:count], refs[count:]
    for flip, in_ref in enumerate(in_refs):
        source = index_ref[0] ^ flip
        for at, out_ref in enumerate(out_refs):
            for group in range(groups):
                column = (at * groups + group) * width
                place = pl.multiple_of((group * count + source) * width, width)
                out_ref[:, pl.ds(place, width)] = in_ref[:, column : column + width].astype(jnp.float32)


def rows_home(summed, groups, width):
    pieces = exchanged(summed, "seq", 0)
    count = len(pieces)
    rows, total = pieces[0].shape
    outs = total // (groups * width)
    step = min(16, rows)
    wide = count * groups * width
    return pl.pallas_call(
        functools.partial(settle_kernel, groups=groups, width=width, count=count),
        grid_spec=pltpu.PrefetchScalarGridSpec(
            num_scalar_prefetch=1,
            grid=(rows // step,),
            in_specs=[pl.BlockSpec((step, total), lambda r, index: (r, 0))] * count,
            out_specs=[pl.BlockSpec((step, wide), lambda r, index: (r, 0))] * outs,
        ),
        out_shape=[jax.ShapeDtypeStruct((rows, wide), jnp.float32)] * outs,
        name="settle",
    )(lax.axis_index("seq").reshape(1), *pieces)


QUERY_BLOCK = 256


def attention_masks(ids_col, ids_row, block, width, start):
    rows = start + lax.broadcasted_iota(jnp.int32, (block, width), 0)
    columns = lax.broadcasted_iota(jnp.int32, (block, width), 1)
    return (columns <= rows) & (ids_col[start : start + block] == ids_row[:, :width])


def attend_kernel(
    q_ref, k_ref, v_ref, qinv_ref, kinv_ref, cos_ref, sin_ref, gq_ref, gk_ref, col_ref, row_ref,
    qlow_ref, klow_ref, vlow_ref, mixed_ref, total_ref, *, scale
):
    low = jnp.bfloat16
    half = q_ref.shape[-1] // 2
    cosine, sine_part = cos_ref[...], sin_ref[...]

    def rotated(ref, inv_ref, gain_ref):
        value = ref[0] * inv_ref[0] * gain_ref[...]
        return (value * cosine + pltpu.roll(value, half, 1) * sine_part).astype(low)

    qlow_ref[0] = rotated(q_ref, qinv_ref, gq_ref)
    klow_ref[0] = rotated(k_ref, kinv_ref, gk_ref)
    vlow_ref[0] = v_ref[0].astype(low)
    length = q_ref.shape[1]
    block = min(QUERY_BLOCK, length)
    ids_col, ids_row = col_ref[0], row_ref[0]
    for start in range(0, length, block):
        width = start + block
        scores = lax.dot_general(
            qlow_ref[0, start:width], klow_ref[0, :width], (((1,), (1,)), ((), ())),
            preferred_element_type=jnp.float32,
        ) * scale
        allowed = attention_masks(ids_col, ids_row, block, width, start)
        masked = jnp.where(allowed, scores, -1e30)
        row_max = jnp.max(masked, -1, keepdims=True)
        log_total = jnp.log(jnp.sum(jnp.exp(masked - row_max), -1, keepdims=True)) + row_max
        total_ref[0, 0, start:width] = log_total
        probs = jnp.exp(masked - log_total).astype(low)
        mixed_ref[0, start:width] = jnp.dot(
            probs, vlow_ref[0, :width], preferred_element_type=jnp.float32
        ).astype(low)


def attend_back_kernel(
    q_ref, k_ref, qinv_ref, kinv_ref, cos_ref, sin_ref, gq_ref, gk_ref, col_ref, row_ref,
    qlow_ref, klow_ref, vlow_ref, total_ref, dmixed_ref,
    dq_ref, dk_ref, dv_ref, dots_ref, gains_ref, key_acc, value_acc, query_acc, *, scale
):
    low = jnp.bfloat16
    half = q_ref.shape[-1] // 2
    length = q_ref.shape[1]
    block = min(QUERY_BLOCK, length)
    ids_col, ids_row = col_ref[0], row_ref[0]
    turned = (((0,), (0,)), ((), ()))
    across = (((1,), (1,)), ((), ()))
    key_acc[...] = jnp.zeros_like(key_acc)
    value_acc[...] = jnp.zeros_like(value_acc)
    for start in range(0, length, block):
        width = start + block
        query = qlow_ref[0, start:width]
        d_mixed = dmixed_ref[0, start:width]
        keys = klow_ref[0, :width]
        scores = lax.dot_general(query, keys, across, preferred_element_type=jnp.float32) * scale
        allowed = attention_masks(ids_col, ids_row, block, width, start)
        probs = jnp.exp(jnp.where(allowed, scores, -1e30) - total_ref[0, 0, start:width])
        d_probs = lax.dot_general(
            d_mixed, vlow_ref[0, :width], across, preferred_element_type=jnp.float32
        )
        row_dot = jnp.sum(probs * d_probs, -1, keepdims=True)
        d_scores = (probs * (d_probs - row_dot)).astype(low)
        query_acc[start:width] = jnp.dot(d_scores, keys, preferred_element_type=jnp.float32)
        key_acc[:width] += lax.dot_general(d_scores, query, turned, preferred_element_type=jnp.float32)
        value_acc[:width] += lax.dot_general(
            probs.astype(low), d_mixed, turned, preferred_element_type=jnp.float32
        )
    dv_ref[0] = value_acc[...].astype(low)
    cosine, sine_part = cos_ref[...], sin_ref[...]

    def turned_back(acc, ref, inv_ref, gain_ref, out_ref, at):
        value = (acc[...] * scale).astype(low).astype(jnp.float32)
        value = value * cosine - pltpu.roll(value, half, 1) * sine_part
        unit = ref[0] * inv_ref[0]
        gains_ref[0, at : at + 1] = jnp.sum(value * unit, 0, keepdims=True)
        value = value * gain_ref[...]
        out_ref[0] = value
        return jnp.sum(value * unit, -1, keepdims=True)

    query_dot = turned_back(query_acc, q_ref, qinv_ref, gq_ref, dq_ref, 0)
    key_dot = turned_back(key_acc, k_ref, kinv_ref, gk_ref, dk_ref, 1)
    lane = lax.broadcasted_iota(jnp.int32, (length, LANES), 1)
    dots = jnp.where(lane == 0, query_dot, jnp.where(lane == 1, key_dot, 0.0)).T[:8]

    @pl.when(pl.program_id(1) == 0)
    def _():
        dots_ref[0] = dots

    @pl.when(pl.program_id(1) != 0)
    def _():
        dots_ref[0] += dots


def attention_specs(length, heads, head_size):
    wide = lambda at: pl.BlockSpec((1, length, head_size), lambda r, h, at=at: (r, 0, at * heads + h))
    thin = pl.BlockSpec((1, length, 1), lambda r, h: (r, 0, 0))
    table = pl.BlockSpec((length, head_size), lambda r, h: (0, 0))
    gain = pl.BlockSpec((1, head_size), lambda r, h: (0, h))
    flat = pl.BlockSpec((1, 1, length), lambda r, h: (r, 0, 0))
    total = pl.BlockSpec((1, 1, length, 1), lambda r, h: (r, h, 0, 0))
    return wide, thin, table, gain, flat, total


def attend(qkv, inverses, tables, gains, ids, head_size, scale):
    rows, length, width = qkv.shape
    heads = width // (3 * head_size)
    wide, thin, table, gain, flat, total = attention_specs(length, heads, head_size)
    narrow = jax.ShapeDtypeStruct((rows, length, heads * head_size), jnp.bfloat16)
    return pl.pallas_call(
        functools.partial(attend_kernel, scale=scale),
        grid=(rows, heads),
        in_specs=[wide(0), wide(1), wide(2), thin, thin, table, table, gain, gain, thin, flat],
        out_specs=[wide(0), wide(0), wide(0), wide(0), total],
        out_shape=[narrow] * 4 + [jax.ShapeDtypeStruct((rows, heads, length, 1), jnp.float32)],
        name="attend",
    )(qkv, qkv, qkv, *inverses, *tables, *gains, ids[:, :, None], ids[:, None, :])


def attend_back(qkv, inverses, tables, gains, ids, kept, d_mixed, head_size, scale):
    rows, length, width = qkv.shape
    heads = width // (3 * head_size)
    wide, thin, table, gain, flat, total = attention_specs(length, heads, head_size)
    shape = (rows, length, heads * head_size)
    return pl.pallas_call(
        functools.partial(attend_back_kernel, scale=scale),
        grid=(rows, heads),
        in_specs=[wide(0), wide(1), thin, thin, table, table, gain, gain, thin, flat]
        + [wide(0), wide(0), wide(0), total, wide(0)],
        out_specs=[
            wide(0),
            wide(0),
            wide(0),
            pl.BlockSpec((1, 8, length), lambda r, h: (r, 0, 0)),
            pl.BlockSpec((1, 2, head_size), lambda r, h: (r, 0, h)),
        ],
        out_shape=[
            jax.ShapeDtypeStruct(shape, jnp.float32),
            jax.ShapeDtypeStruct(shape, jnp.float32),
            jax.ShapeDtypeStruct(shape, jnp.bfloat16),
            jax.ShapeDtypeStruct((rows, 8, length), jnp.float32),
            jax.ShapeDtypeStruct((rows, 2, heads * head_size), jnp.float32),
        ],
        scratch_shapes=[pltpu.VMEM((length, head_size), jnp.float32)] * 3,
        name="attend_back",
    )(qkv, qkv, *inverses, *tables, *gains, ids[:, :, None], ids[:, None, :], *kept, d_mixed)


def shards_by_feature(
    tokens,
    doc_ids,
    cotangent,
    w_query,
    w_key,
    w_value,
    w_out,
    w_gate,
    w_up,
    w_down,
    g_query,
    g_key,
    g_attn,
    g_ffn,
):
    row_count, piece_len, model_width = tokens.shape
    head_size = HEAD
    feature_count = w_query.shape[1]
    scale = head_size ** (-0.5)
    seq_count = lax.axis_size("seq")
    dp_count = lax.axis_size("dp")
    seq_at = lax.axis_index("seq")
    row_len = piece_len * seq_count
    all_count = row_count * row_len
    tok_count = row_count * piece_len
    own_features = feature_count // seq_count
    own_hidden = w_gate.shape[1] // seq_count
    low = jnp.bfloat16

    def own_piece(tensor):
        view = tensor.reshape(row_count, row_len, -1)
        return lax.dynamic_slice_in_dim(view, seq_at * piece_len, piece_len, 1).reshape(tok_count, -1)

    w_qkv = gather_dp(jnp.concatenate([own_columns(w, 1, seq_count, seq_at) for w in (w_query, w_key, w_value)], 1))
    tokens_all = gather_seq(tokens).reshape(all_count, model_width)
    ids_all = total_seq(
        lax.dynamic_update_slice_in_dim(
            jnp.zeros((row_count, row_len), jnp.int32), doc_ids, seq_at * piece_len, 1
        )
    )
    core = seq_at % 2
    half = model_width // 2
    out_rows = w_out.shape[0]
    out_pieces = pieces_dp(lax.dynamic_slice_in_dim(w_out, core * half, half, 1))
    other_pieces = [(swap(piece, "seq", 1), row) for piece, row in out_pieces]
    wo_full = placed(
        [(w_out, lax.axis_index("dp") * out_rows, 0)]
        + [(piece, row, core * half) for piece, row in out_pieces]
        + [(piece, row, half - core * half) for piece, row in other_pieces],
        (feature_count, model_width),
    )
    w_hidden = gather_dp(jnp.concatenate([own_columns(w, dp_count, seq_count, seq_at) for w in (w_gate, w_up)], 1))
    w_back = gather_dp(
        lax.dynamic_slice_in_dim(
            w_down, seq_at * (own_hidden // dp_count), own_hidden // dp_count, 0
        ),
    )
    gain_query = lax.dynamic_slice_in_dim(g_query, seq_at * own_features, own_features).astype(jnp.float32)
    gain_key = lax.dynamic_slice_in_dim(g_key, seq_at * own_features, own_features).astype(jnp.float32)
    gain_attn = g_attn.astype(jnp.float32)
    gain_ffn = g_ffn.astype(jnp.float32)

    tokens_all, ids_all = lax.optimization_barrier((tokens_all, ids_all))
    qkv = jnp.dot(tokens_all, w_qkv, preferred_element_type=jnp.float32)
    query_pre = qkv[:, :own_features]
    key_pre = qkv[:, own_features : 2 * own_features]
    squares = jnp.stack([jnp.sum(query_pre * query_pre, -1), jnp.sum(key_pre * key_pre, -1)])
    cosine, sine_part = rotation(jnp.arange(row_len, dtype=jnp.int32), head_size)
    tables = jnp.concatenate([cosine, cosine], 1), jnp.concatenate([-sine_part, sine_part], 1)
    inverse = lax.rsqrt(total_seq(squares) / feature_count + eps)
    inverses = [inverse[at].reshape(row_count, row_len, 1) for at in range(2)]
    norm_gains = gain_query[None, :], gain_key[None, :]
    qkv_rows = qkv.reshape(row_count, row_len, 3 * own_features)
    *kept, mixed_low, log_total = attend(
        qkv_rows, inverses, tables, norm_gains, ids_all, head_size, scale
    )
    mixed_low = mixed_low.reshape(all_count, own_features)
    mixed_all = lax.all_gather(mixed_low, "seq", axis=1, tiled=True)
    attn_out = jnp.dot(mixed_all, wo_full, preferred_element_type=jnp.float32)
    attn_inv_all = inverse_rms(attn_out)
    hidden_all = tokens_all.astype(jnp.float32) + attn_out * attn_inv_all * gain_attn
    hidden_low = hidden_all.astype(low)
    attn_inv = own_piece(attn_inv_all)
    attn_unit = own_piece(attn_out) * attn_inv
    hidden_state = tokens.reshape(tok_count, model_width).astype(jnp.float32) + attn_unit * gain_attn

    gate_up = jnp.dot(hidden_low, w_hidden, preferred_element_type=jnp.float32)
    gate, up_proj = gate_up[:, :own_hidden], gate_up[:, own_hidden:]
    sigma = jax.nn.sigmoid(gate)
    active = gate * sigma
    inner_low = (active * up_proj).astype(low)
    branch_part = jnp.dot(inner_low, w_back, preferred_element_type=jnp.float32).astype(low)
    branch = (
        scatter_seq(branch_part.reshape(row_count, row_len, model_width))
        .astype(jnp.float32)
        .reshape(tok_count, model_width)
    )
    branch_inv = inverse_rms(branch)
    branch_unit = branch * branch_inv
    result = (
        (hidden_state + branch_unit * gain_ffn)
        .astype(low)
        .reshape(row_count, piece_len, model_width)
    )

    grad_out = cotangent.reshape(tok_count, model_width).astype(jnp.float32)
    ffn_gain_term = jnp.sum(grad_out * branch_unit, 0)
    d_branch = norm_back(grad_out * gain_ffn, branch_unit, branch_inv).astype(low)
    d_branch_all = gather_seq(d_branch.reshape(row_count, piece_len, model_width)).reshape(all_count, model_width)
    d_inner = jnp.einsum("nd,fd->nf", d_branch_all, w_back, preferred_element_type=jnp.float32)
    d_gate = (d_inner * up_proj * sigma * (1.0 + gate * (1.0 - sigma))).astype(low)
    d_up = (d_inner * active).astype(low)
    d_gate_up = jnp.concatenate([d_gate, d_up], 1)
    d_hidden_part = jnp.einsum("nf,df->nd", d_gate_up, w_hidden, preferred_element_type=jnp.float32).astype(low)
    d_hidden_sum = scatter_seq(d_hidden_part.reshape(row_count, row_len, model_width))
    hidden_part = jnp.einsum("nd,nf->df", hidden_low, d_gate_up, preferred_element_type=jnp.float32).astype(low)
    down_part = jnp.einsum("nf,nd->fd", inner_low, d_branch_all, preferred_element_type=jnp.float32).astype(low)
    down_grad = sum_dp(*shares_for(down_part))
    hidden_own = sum_dp(*shares_for(hidden_part)).astype(low)
    d_hidden = grad_out + d_hidden_sum.astype(jnp.float32).reshape(tok_count, model_width)

    attn_gain_term = jnp.sum(d_hidden * attn_unit, 0)
    d_attn = norm_back(d_hidden * gain_attn, attn_unit, attn_inv).astype(low)
    d_mixed = jnp.einsum("nd,fd->nf", d_attn, wo_full, preferred_element_type=jnp.float32).astype(low)

    def own_columns_of_all(tensor):
        split = tensor.reshape(row_count, piece_len, seq_count, -1).transpose(2, 0, 1, 3)
        width = split.shape[-1]
        split = lax.all_to_all(split.reshape(seq_count, tok_count, width), "seq", split_axis=0, concat_axis=0)
        split = split.reshape(seq_count, row_count, piece_len, width).transpose(1, 0, 2, 3)
        return split.reshape(row_count, row_len, width)

    d_mixed = own_columns_of_all(d_mixed)
    d_mixed, d_attn = lax.optimization_barrier((d_mixed, d_attn))
    d_attn_own = own_columns_of_all(d_attn).reshape(all_count, -1)
    out_part = jnp.einsum("nf,nd->fd", mixed_all, d_attn_own, preferred_element_type=jnp.float32).astype(low)
    out_own = sum_dp(*shares_for(out_part)).astype(low)
    gate_grad, up_grad = rows_home(hidden_own, dp_count, own_hidden // dp_count)

    dq_gained, dk_gained, d_value, dots, gain_terms = attend_back(
        qkv_rows, inverses, tables, norm_gains, ids_all, (*kept, log_total), d_mixed, head_size, scale
    )
    norm_terms = lax.dynamic_update_slice_in_dim(
        jnp.zeros((2, feature_count), jnp.float32), jnp.sum(gain_terms, 0), seq_at * own_features, 1
    )
    dots = dots[:, :2].transpose(1, 0, 2).reshape(-1, LANES)
    stat_rows = dots.shape[0]
    sums = total_seq(
        jnp.concatenate(
            [dots]
            + [part.reshape(-1, LANES) for part in (norm_terms, attn_gain_term, ffn_gain_term)]
        )
    )
    means = sums[:stat_rows].reshape(2, all_count) / feature_count

    def norm_back_wide(gained, pre, at):
        inv = inverse[at][:, None]
        gained = gained.reshape(all_count, own_features)
        return (inv * (gained - pre * inv * means[at][:, None])).astype(low)

    dq_pre = norm_back_wide(dq_gained, query_pre, 0)
    dk_pre = norm_back_wide(dk_gained, key_pre, 1)
    d_value = d_value.reshape(all_count, own_features)
    d_qkv = jnp.concatenate([dq_pre, dk_pre, d_value], 1)
    d_tokens_part = jnp.einsum("nf,df->nd", d_qkv, w_qkv, preferred_element_type=jnp.float32).astype(low)
    d_qkv, d_tokens_part = lax.optimization_barrier((d_qkv, d_tokens_part))
    d_tokens_sum = scatter_seq(d_tokens_part.reshape(row_count, row_len, model_width))
    d_tokens = d_hidden + d_tokens_sum.astype(jnp.float32).reshape(tok_count, model_width)
    qkv_part = jnp.einsum("nd,nf->df", tokens_all, d_qkv, preferred_element_type=jnp.float32).astype(low)
    qkv_own = sum_dp(*shares_for(qkv_part)).astype(low)
    attn_home = rows_home(jnp.concatenate([qkv_own, out_own], 1), 1, own_features)
    share = feature_count // (dp_count * seq_count)
    gains = lax.dynamic_index_in_dim(
        sums[stat_rows:].reshape(4, dp_count, seq_count, share), seq_at, 2, False
    )
    gains = share_dp(gains.transpose(1, 0, 2).reshape(dp_count, 4 * share)).reshape(4, share)
    return (
        result,
        d_tokens.reshape(row_count, piece_len, model_width),
        attn_home[0],
        attn_home[1],
        attn_home[2],
        attn_home[3],
        gate_grad,
        up_grad,
        down_grad,
        gains[0],
        gains[1],
        gains[2],
        gains[3],
    )


def shards(tokens, doc_ids, cotangent, w_query, *rest):
    if w_query.shape[1] // HEAD % lax.axis_size("seq"):
        return shards_by_slab(tokens, doc_ids, cotangent, w_query, *rest)
    return shards_by_feature(tokens, doc_ids, cotangent, w_query, *rest)


def solution(mesh):
    return jax.shard_map(
        shards,
        mesh=mesh,
        in_specs=(
            P("dp", "seq", None),
            P("dp", "seq"),
            P("dp", "seq", None),
            P("dp", None),
            P("dp", None),
            P("dp", None),
            P("dp", None),
            P("dp", None),
            P("dp", None),
            P("dp", None),
            P(),
            P(),
            P(),
            P(),
        ),
        out_specs=(
            P("dp", "seq", None),
            P("dp", "seq", None),
            P(("dp", "seq"), None),
            P(("dp", "seq"), None),
            P(("dp", "seq"), None),
            P(("dp", "seq"), None),
            P(("dp", "seq"), None),
            P(("dp", "seq"), None),
            P(("dp", "seq"), None),
            P(("dp", "seq")),
            P(("dp", "seq")),
            P(("dp", "seq")),
            P(("dp", "seq")),
        ),
        check_vma=False,
    )
```

```python
import functools

import jax
import jax.numpy as jnp
from jax import lax
from jax.experimental import pallas as pl
from jax.experimental.pallas import tpu as pltpu
from jax.sharding import PartitionSpec as P


HEAD = 128
SLABS = 4
LANES = 128


eps = 1e-06
theta = 500000.0


def rotation(positions, head_size):
    half_size = head_size // 2
    frequency = theta ** (-(2.0 * jnp.arange(half_size, dtype=jnp.float32)) / head_size)
    angles = positions.astype(jnp.float32)[:, None] * frequency[None, :]
    return (jnp.cos(angles), jnp.sin(angles))


def rotate(tensor, cosine, sine_part):
    half_size = tensor.shape[-1] // 2
    first_half = tensor[..., :half_size]
    second_half = tensor[..., half_size:]
    cos_wide = cosine[:, None, :]
    sin_wide = sine_part[:, None, :]
    return jnp.concatenate(
        [
            first_half * cos_wide - second_half * sin_wide,
            second_half * cos_wide + first_half * sin_wide,
        ],
        -1,
    )


def unrotate(tensor, cosine, sine_part):
    half_size = tensor.shape[-1] // 2
    first_half = tensor[..., :half_size]
    second_half = tensor[..., half_size:]
    cos_wide = cosine[:, None, :]
    sin_wide = sine_part[:, None, :]
    return jnp.concatenate(
        [
            first_half * cos_wide + second_half * sin_wide,
            second_half * cos_wide - first_half * sin_wide,
        ],
        -1,
    )


def inverse_rms(tensor):
    return lax.rsqrt(jnp.mean(tensor * tensor, -1, keepdims=True) + eps)


def norm_back(grad_unit, unit_vec, inverse):
    return inverse * (grad_unit - unit_vec * jnp.mean(grad_unit * unit_vec, -1, keepdims=True))


def visible(own_ids, key_ids, query_at, key_at):
    causal = key_at[None, :] <= query_at[:, None]
    same_doc = own_ids[:, :, None] == key_ids[:, None, :]
    return (causal[None] & same_doc)[:, None]


def masked_scores(query_low, pair_all, allowed, head_count, head_size):
    row_count = pair_all.shape[0]
    row_length = pair_all.shape[1]
    feature_count = head_count * head_size
    key_rows = pair_all[..., :feature_count].reshape(row_count, row_length, head_count, head_size)
    value_rows = pair_all[..., feature_count:].reshape(row_count, row_length, head_count, head_size)
    scores = jnp.einsum(
        "rche,rlhe->rhcl", query_low, key_rows, preferred_element_type=jnp.float32
    ) * head_size ** (-0.5)
    return (jnp.where(allowed, scores, -1e30), key_rows, value_rows)


def columns_of(matrix, parts, slab_count, index):
    lead = matrix.shape[0]
    width = matrix.shape[1] // (parts * slab_count)
    return matrix.reshape(lead, parts, slab_count, width)[:, :, index].reshape(lead, parts * width)


def entries_of(vector, parts, slab_count, index):
    width = vector.shape[0] // (parts * slab_count)
    return vector.reshape(parts, slab_count, width)[:, index].reshape(parts * width)


def shards_by_slab(
    tokens,
    doc_ids,
    cotangent,
    w_query,
    w_key,
    w_value,
    w_out,
    w_gate,
    w_up,
    w_down,
    g_query,
    g_key,
    g_attn,
    g_ffn,
):
    row_count, piece_len, model_width = tokens.shape
    head_size = HEAD
    feature_count = w_query.shape[1]
    head_count = feature_count // head_size
    tok_count = row_count * piece_len
    scale = head_size ** (-0.5)
    seq_count = lax.axis_size("seq")
    parts = lax.axis_size("dp") * seq_count
    slab_count = SLABS
    gather_all = (
        lax.all_gather(w_query, "dp", axis=0, tiled=True),
        lax.all_gather(w_key, "dp", axis=0, tiled=True),
        lax.all_gather(w_value, "dp", axis=0, tiled=True),
        lax.all_gather(w_out, "dp", axis=0, tiled=True),
        lax.all_gather(w_gate, "dp", axis=0, tiled=True),
        lax.all_gather(w_up, "dp", axis=0, tiled=True),
        lax.all_gather(w_down, "dp", axis=0, tiled=True),
    )
    wq_full, wk_full, wv_full, wo_full, wg_full, wu_full, wd_full = gather_all
    gain_query = g_query.astype(jnp.float32)
    gain_key = g_key.astype(jnp.float32)
    gain_attn = g_attn.astype(jnp.float32)
    gain_ffn = g_ffn.astype(jnp.float32)
    flat_tokens = tokens.reshape(tok_count, model_width)
    query_pre = jnp.dot(flat_tokens, wq_full, preferred_element_type=jnp.float32)
    key_pre = jnp.dot(flat_tokens, wk_full, preferred_element_type=jnp.float32)
    value_pre = jnp.dot(flat_tokens, wv_full, preferred_element_type=jnp.float32)
    query_inv = inverse_rms(query_pre)
    query_unit = query_pre * query_inv
    key_inv = inverse_rms(key_pre)
    key_unit = key_pre * key_inv
    first_row = lax.axis_index("seq") * piece_len
    positions = first_row + jnp.tile(jnp.arange(piece_len, dtype=jnp.int32), row_count)
    cosine, sine_part = rotation(positions, head_size)
    query_rot = rotate(
        (query_unit * gain_query).reshape(tok_count, head_count, head_size), cosine, sine_part
    )
    key_rot = rotate(
        (key_unit * gain_key).reshape(tok_count, head_count, head_size), cosine, sine_part
    )
    query_low = query_rot.astype(jnp.bfloat16).reshape(row_count, piece_len, head_count, head_size)
    key_low = key_rot.astype(jnp.bfloat16).reshape(row_count, piece_len, feature_count)
    value_low = value_pre.astype(jnp.bfloat16).reshape(row_count, piece_len, feature_count)
    pair_low = jnp.concatenate([key_low, value_low], -1)
    ids_low = doc_ids.astype(jnp.bfloat16)
    pair_all, ids_all = (
        lax.all_gather(pair_low, "seq", axis=1, tiled=True),
        lax.all_gather(ids_low, "seq", axis=1, tiled=True),
    )
    query_at = first_row + jnp.arange(piece_len, dtype=jnp.int32)
    allowed = visible(ids_low, ids_all, query_at, jnp.arange(pair_all.shape[1], dtype=jnp.int32))
    masked, _, value_rows = masked_scores(
        query_low, pair_all, allowed, head_count, head_size
    )
    row_max = jnp.max(masked, -1, keepdims=True)
    log_total = jnp.log(jnp.sum(jnp.exp(masked - row_max), -1, keepdims=True)) + row_max
    probs_low = jnp.exp(masked - log_total).astype(jnp.bfloat16)
    mixed = jnp.einsum("rhcl,rlhe->rche", probs_low, value_rows, preferred_element_type=jnp.float32)
    mixed_low = mixed.reshape(tok_count, feature_count).astype(jnp.bfloat16)
    attn_out = jnp.dot(mixed_low, wo_full, preferred_element_type=jnp.float32)
    attn_inv = inverse_rms(attn_out)
    attn_unit = attn_out * attn_inv
    hidden_state = flat_tokens.astype(jnp.float32) + attn_unit * gain_attn
    hidden_low = hidden_state.astype(jnp.bfloat16)
    gate = jnp.dot(hidden_low, wg_full, preferred_element_type=jnp.float32)
    up_proj = jnp.dot(hidden_low, wu_full, preferred_element_type=jnp.float32)
    sigma = jax.nn.sigmoid(gate)
    active = gate * sigma
    inner_low = (active * up_proj).astype(jnp.bfloat16)
    branch = jnp.dot(inner_low, wd_full, preferred_element_type=jnp.float32)
    branch_inv = inverse_rms(branch)
    branch_unit = branch * branch_inv
    result = (
        (hidden_state + branch_unit * gain_ffn)
        .astype(jnp.bfloat16)
        .reshape(row_count, piece_len, model_width)
    )
    wq_back, wk_back, wv_back, wo_back, wg_back, wu_back, wd_back = gather_all
    pair_back, ids_back = (pair_all, ids_all)
    grad_out = cotangent.reshape(tok_count, model_width).astype(jnp.float32)
    ffn_gain_term = jnp.sum(grad_out * branch_unit, 0)
    d_branch = norm_back(grad_out * gain_ffn, branch_unit, branch_inv).astype(jnp.bfloat16)
    d_inner = jnp.einsum("nd,fd->nf", d_branch, wd_back, preferred_element_type=jnp.float32)
    d_gate = (d_inner * up_proj * sigma * (1.0 + gate * (1.0 - sigma))).astype(jnp.bfloat16)
    d_up = (d_inner * active).astype(jnp.bfloat16)
    d_hidden = grad_out + jnp.einsum(
        "nf,df->nd", d_gate, wg_back, preferred_element_type=jnp.float32
    )
    d_hidden = d_hidden + jnp.einsum("nf,df->nd", d_up, wu_back, preferred_element_type=jnp.float32)
    mlp_shares = []
    for index in range(slab_count):
        hidden_part = columns_of(hidden_low, parts, slab_count, index)
        inner_part = columns_of(inner_low, parts, slab_count, index)
        gate_term = jnp.einsum("nd,nf->df", hidden_part, d_gate, preferred_element_type=jnp.float32)
        up_term = jnp.einsum("nd,nf->df", hidden_part, d_up, preferred_element_type=jnp.float32)
        down_term = jnp.einsum(
            "nf,nd->fd", inner_part, d_branch, preferred_element_type=jnp.float32
        )
        ffn_term = entries_of(ffn_gain_term, parts, slab_count, index)
        shares = (
            lax.psum_scatter(down_term, ("dp", "seq"), scatter_dimension=0, tiled=True),
            lax.psum_scatter(gate_term, ("dp", "seq"), scatter_dimension=0, tiled=True),
            lax.psum_scatter(up_term, ("dp", "seq"), scatter_dimension=0, tiled=True),
            lax.psum_scatter(ffn_term, ("dp", "seq"), scatter_dimension=0, tiled=True),
        )
        mlp_shares.append(shares)
    down_grad = jnp.concatenate([s[0] for s in mlp_shares], 0)
    gate_grad = jnp.concatenate([s[1] for s in mlp_shares], 0)
    up_grad = jnp.concatenate([s[2] for s in mlp_shares], 0)
    ffn_grad = jnp.concatenate([s[3] for s in mlp_shares], 0)
    attn_gain_term = jnp.sum(d_hidden * attn_unit, 0)
    d_attn = norm_back(d_hidden * gain_attn, attn_unit, attn_inv).astype(jnp.bfloat16)
    d_mixed = jnp.einsum("nd,fd->nf", d_attn, wo_back, preferred_element_type=jnp.float32).astype(
        jnp.bfloat16
    )
    d_mixed = d_mixed.reshape(row_count, piece_len, head_count, head_size)
    sub_len = piece_len // slab_count
    pair_width = pair_back.shape[-1]
    pair_view = pair_back.reshape(row_count, seq_count, slab_count, sub_len, pair_width)
    ids_view = ids_back.reshape(row_count, seq_count, slab_count, sub_len)

    def slab_scores(index):
        pair_part = pair_view[:, :, index].reshape(row_count, seq_count * sub_len, pair_width)
        ids_part = ids_view[:, :, index].reshape(row_count, seq_count * sub_len)
        key_at = (
            jnp.arange(seq_count, dtype=jnp.int32)[:, None] * piece_len
            + index * sub_len
            + jnp.arange(sub_len, dtype=jnp.int32)[None, :]
        ).reshape(seq_count * sub_len)
        allowed_part = visible(ids_low, ids_part, query_at, key_at)
        masked_part, key_part, value_part = masked_scores(
            query_low, pair_part, allowed_part, head_count, head_size
        )
        probs_part = jnp.exp(masked_part - log_total)
        d_probs_part = jnp.einsum(
            "rche,rlhe->rhcl", d_mixed, value_part, preferred_element_type=jnp.float32
        )
        return (probs_part, d_probs_part, key_part)

    row_dot = jnp.zeros((row_count, head_count, piece_len, 1), jnp.float32)
    for index in range(slab_count):
        probs_part, d_probs_part, key_part = slab_scores(index)
        row_dot = row_dot + jnp.sum(probs_part * d_probs_part, -1, keepdims=True)
    query_acc = jnp.zeros((row_count, piece_len, head_count, head_size), jnp.float32)
    pair_shares = []
    for index in range(slab_count):
        probs_part, d_probs_part, key_part = slab_scores(index)
        d_scores = (probs_part * (d_probs_part - row_dot)).astype(jnp.bfloat16)
        query_acc = query_acc + jnp.einsum(
            "rhcl,rlhe->rche", d_scores, key_part, preferred_element_type=jnp.float32
        )
        key_term = (
            jnp.einsum("rhcl,rche->rlhe", d_scores, query_low, preferred_element_type=jnp.float32)
            * scale
        )
        value_term = jnp.einsum(
            "rhcl,rche->rlhe",
            probs_part.astype(jnp.bfloat16),
            d_mixed,
            preferred_element_type=jnp.float32,
        )
        key_count = seq_count * sub_len
        pair_term = jnp.concatenate(
            [
                key_term.reshape(row_count, key_count, feature_count),
                value_term.reshape(row_count, key_count, feature_count),
            ],
            -1,
        )
        pair_shares.append(
            lax.psum_scatter(
                pair_term.astype(jnp.bfloat16), "seq", scatter_dimension=1, tiled=True
            ).astype(jnp.float32)
        )
    pair_grad = jnp.concatenate(pair_shares, 1)
    d_query = (query_acc * scale).astype(jnp.bfloat16)
    d_key = (
        pair_grad[..., :feature_count]
        .astype(jnp.bfloat16)
        .reshape(tok_count, head_count, head_size)
    )
    d_value = pair_grad[..., feature_count:].astype(jnp.bfloat16).reshape(tok_count, feature_count)
    dq_norm = unrotate(
        d_query.reshape(tok_count, head_count, head_size).astype(jnp.float32), cosine, sine_part
    ).reshape(tok_count, feature_count)
    dk_norm = unrotate(d_key.astype(jnp.float32), cosine, sine_part).reshape(
        tok_count, feature_count
    )
    query_gain_term = jnp.sum(dq_norm * query_unit, 0)
    key_gain_term = jnp.sum(dk_norm * key_unit, 0)
    dq_pre = norm_back(dq_norm * gain_query, query_unit, query_inv).astype(jnp.bfloat16)
    dk_pre = norm_back(dk_norm * gain_key, key_unit, key_inv).astype(jnp.bfloat16)
    d_tokens = d_hidden + jnp.einsum(
        "nf,df->nd", dq_pre, wq_back, preferred_element_type=jnp.float32
    )
    d_tokens = d_tokens + jnp.einsum(
        "nf,df->nd", dk_pre, wk_back, preferred_element_type=jnp.float32
    )
    d_tokens = d_tokens + jnp.einsum(
        "nf,df->nd", d_value, wv_back, preferred_element_type=jnp.float32
    )
    attn_shares = []
    for index in range(slab_count):
        token_part = columns_of(flat_tokens, parts, slab_count, index)
        mixed_part = columns_of(mixed_low, parts, slab_count, index)
        query_term = jnp.einsum("nd,nf->df", token_part, dq_pre, preferred_element_type=jnp.float32)
        key_wterm = jnp.einsum("nd,nf->df", token_part, dk_pre, preferred_element_type=jnp.float32)
        value_wterm = jnp.einsum(
            "nd,nf->df", token_part, d_value, preferred_element_type=jnp.float32
        )
        out_term = jnp.einsum("nf,nd->fd", mixed_part, d_attn, preferred_element_type=jnp.float32)
        gq_term = entries_of(query_gain_term, parts, slab_count, index)
        gk_term = entries_of(key_gain_term, parts, slab_count, index)
        ga_term = entries_of(attn_gain_term, parts, slab_count, index)
        shares = (
            lax.psum_scatter(query_term, ("dp", "seq"), scatter_dimension=0, tiled=True),
            lax.psum_scatter(key_wterm, ("dp", "seq"), scatter_dimension=0, tiled=True),
            lax.psum_scatter(value_wterm, ("dp", "seq"), scatter_dimension=0, tiled=True),
            lax.psum_scatter(out_term, ("dp", "seq"), scatter_dimension=0, tiled=True),
            lax.psum_scatter(gq_term, ("dp", "seq"), scatter_dimension=0, tiled=True),
            lax.psum_scatter(gk_term, ("dp", "seq"), scatter_dimension=0, tiled=True),
            lax.psum_scatter(ga_term, ("dp", "seq"), scatter_dimension=0, tiled=True),
        )
        attn_shares.append(shares)
    query_grad = jnp.concatenate([s[0] for s in attn_shares], 0)
    key_grad = jnp.concatenate([s[1] for s in attn_shares], 0)
    value_grad = jnp.concatenate([s[2] for s in attn_shares], 0)
    out_grad = jnp.concatenate([s[3] for s in attn_shares], 0)
    gq_grad = jnp.concatenate([s[4] for s in attn_shares], 0)
    gk_grad = jnp.concatenate([s[5] for s in attn_shares], 0)
    ga_grad = jnp.concatenate([s[6] for s in attn_shares], 0)
    tokens_grad = d_tokens.reshape(row_count, piece_len, model_width)
    return (
        result,
        tokens_grad,
        query_grad,
        key_grad,
        value_grad,
        out_grad,
        gate_grad,
        up_grad,
        down_grad,
        gq_grad,
        gk_grad,
        ga_grad,
        ffn_grad,
    )


def own_columns(matrix, groups, parts, index):
    width = matrix.shape[1] // (groups * parts)
    pieces = [
        lax.dynamic_slice_in_dim(matrix, (group * parts + index) * width, width, 1)
        for group in range(groups)
    ]
    return jnp.concatenate(pieces, 1) if groups > 1 else pieces[0]


def gather_seq(piece):
    return lax.all_gather(piece, "seq", axis=1, tiled=True)


def scatter_seq(partial):
    return lax.psum_scatter(partial, "seq", scatter_dimension=1, tiled=True)


def swap(value, axis, flip):
    return lax.ppermute(value, axis, [(at, at ^ flip) for at in range(lax.axis_size(axis))])


def place_kernel(spots_ref, *refs):
    *in_refs, out_ref, sems = refs
    copies = []
    for at, in_ref in enumerate(in_refs):
        rows, width = in_ref.shape
        row = pl.multiple_of(spots_ref[2 * at], LANES)
        column = pl.multiple_of(spots_ref[2 * at + 1], LANES)
        copies.append(
            pltpu.make_async_copy(
                in_ref, out_ref.at[pl.ds(row, rows), pl.ds(column, width)], sems.at[at]
            )
        )
    for copy in copies:
        copy.start()
    for copy in copies:
        copy.wait()


def placed(pieces, shape):
    spots = jnp.stack([jnp.int32(at) for _, row, column in pieces for at in (row, column)])
    return pl.pallas_call(
        place_kernel,
        grid_spec=pltpu.PrefetchScalarGridSpec(
            num_scalar_prefetch=1,
            grid=(1,),
            in_specs=[
                pl.BlockSpec(piece.shape, lambda at, spots: (0, 0), pipeline_mode=pl.Buffered(1))
                for piece, _, _ in pieces
            ],
            out_specs=pl.BlockSpec(memory_space=pl.ANY),
            scratch_shapes=[pltpu.SemaphoreType.DMA((len(pieces),))],
        ),
        out_shape=jax.ShapeDtypeStruct(shape, pieces[0][0].dtype),
        name="place",
    )(spots, *[piece for piece, _, _ in pieces])


def pieces_for(value, name, split_axis):
    count, index = lax.axis_size(name), lax.axis_index(name)
    width = value.shape[split_axis] // count
    return [
        lax.dynamic_slice_in_dim(value, (index ^ flip) * width, width, split_axis)
        for flip in range(count)
    ]


def swapped(pieces, name):
    return [swap(piece, name, flip) if flip else piece for flip, piece in enumerate(pieces)]


def exchanged(value, name, split_axis):
    return swapped(pieces_for(value, name, split_axis), name)


def pieces_dp(piece):
    half = piece.shape[0] // 2
    first, second = swap(piece, "dp", 1), swap(piece, "dp", 2)
    top, bottom = swap(first[:half], "dp", 2), swap(second[half:], "dp", 1)
    index = lax.axis_index("dp")
    width = piece.shape[0]
    far = (index ^ 3) * width
    return [
        (first, (index ^ 1) * width),
        (second, (index ^ 2) * width),
        (top, far),
        (bottom, far + half),
    ]


def gather_dp(piece):
    rows, width = piece.shape
    pieces = [(piece, lax.axis_index("dp") * rows), *pieces_dp(piece)]
    return placed([(part, row, 0) for part, row in pieces], (4 * rows, width))


def sum_dp(sent, kept):
    got = swap(sent[0], "dp", 1), swap(sent[1], "dp", 2)
    wide = [(kept[at].astype(jnp.float32) + got[at].astype(jnp.float32)) for at in range(2)]
    onward = [side[1].astype(jnp.bfloat16) for side in wide]
    last = swap(onward[0], "dp", 2), swap(onward[1], "dp", 1)
    return jnp.concatenate(
        [wide[at][0] + last[at].astype(jnp.float32) for at in range(2)], 0
    )


def shares_for(partial):
    index = lax.axis_index("dp")
    width = partial.shape[0] // 4
    half = width // 2

    def part(flip, side):
        return lax.dynamic_slice_in_dim(partial, (index ^ flip) * width + side * half, half, 0)

    sent = [jnp.stack([part(1, 0), part(3, 0)]), jnp.stack([part(2, 1), part(3, 1)])]
    kept = [jnp.stack([part(0, 0), part(2, 0)]), jnp.stack([part(0, 1), part(1, 1)])]
    return sent, kept


def total_seq(value):
    shape = value.shape
    value = value.reshape(-1, LANES)
    flip = 1
    while flip < lax.axis_size("seq"):
        value = value + swap(value, "seq", flip)
        flip *= 2
    return value.reshape(shape)


def share_dp(rows):
    flip = lax.axis_size("dp") // 2
    while flip:
        halves = rows.reshape(2, rows.shape[0] // 2, rows.shape[1])
        side = lax.axis_index("dp") // flip % 2
        kept = lax.dynamic_index_in_dim(halves, side, 0, False)
        sent = lax.dynamic_index_in_dim(halves, 1 - side, 0, False)
        rows = kept + swap(sent, "dp", flip)
        flip //= 2
    return rows[0]


def settle_kernel(index_ref, *refs, groups, width, count):
    in_refs, out_refs = refs[:count], refs[count:]
    for flip, in_ref in enumerate(in_refs):
        source = index_ref[0] ^ flip
        for at, out_ref in enumerate(out_refs):
            for group in range(groups):
                column = (at * groups + group) * width
                place = pl.multiple_of((group * count + source) * width, width)
                out_ref[:, pl.ds(place, width)] = in_ref[:, column : column + width].astype(jnp.float32)


def rows_home(summed, groups, width):
    pieces = exchanged(summed, "seq", 0)
    count = len(pieces)
    rows, total = pieces[0].shape
    outs = total // (groups * width)
    step = min(16, rows)
    wide = count * groups * width
    return pl.pallas_call(
        functools.partial(settle_kernel, groups=groups, width=width, count=count),
        grid_spec=pltpu.PrefetchScalarGridSpec(
            num_scalar_prefetch=1,
            grid=(rows // step,),
            in_specs=[pl.BlockSpec((step, total), lambda r, index: (r, 0))] * count,
            out_specs=[pl.BlockSpec((step, wide), lambda r, index: (r, 0))] * outs,
        ),
        out_shape=[jax.ShapeDtypeStruct((rows, wide), jnp.float32)] * outs,
        name="settle",
    )(lax.axis_index("seq").reshape(1), *pieces)


QUERY_BLOCK = 256


def attention_masks(ids_col, ids_row, block, width, start):
    rows = start + lax.broadcasted_iota(jnp.int32, (block, width), 0)
    columns = lax.broadcasted_iota(jnp.int32, (block, width), 1)
    return (columns <= rows) & (ids_col[start : start + block] == ids_row[:, :width])


def attend_kernel(
    q_ref, k_ref, v_ref, qinv_ref, kinv_ref, cos_ref, sin_ref, gq_ref, gk_ref, col_ref, row_ref,
    qlow_ref, klow_ref, vlow_ref, mixed_ref, total_ref, *, scale
):
    low = jnp.bfloat16
    half = q_ref.shape[-1] // 2
    cosine, sine_part = cos_ref[...], sin_ref[...]

    def rotated(ref, inv_ref, gain_ref):
        value = ref[0] * inv_ref[0] * gain_ref[...]
        return (value * cosine + pltpu.roll(value, half, 1) * sine_part).astype(low)

    qlow_ref[0] = rotated(q_ref, qinv_ref, gq_ref)
    klow_ref[0] = rotated(k_ref, kinv_ref, gk_ref)
    vlow_ref[0] = v_ref[0].astype(low)
    length = q_ref.shape[1]
    block = min(QUERY_BLOCK, length)
    ids_col, ids_row = col_ref[0], row_ref[0]
    for start in range(0, length, block):
        width = start + block
        scores = lax.dot_general(
            qlow_ref[0, start:width], klow_ref[0, :width], (((1,), (1,)), ((), ())),
            preferred_element_type=jnp.float32,
        ) * scale
        allowed = attention_masks(ids_col, ids_row, block, width, start)
        masked = jnp.where(allowed, scores, -1e30)
        row_max = jnp.max(masked, -1, keepdims=True)
        log_total = jnp.log(jnp.sum(jnp.exp(masked - row_max), -1, keepdims=True)) + row_max
        total_ref[0, 0, start:width] = log_total
        probs = jnp.exp(masked - log_total).astype(low)
        mixed_ref[0, start:width] = jnp.dot(
            probs, vlow_ref[0, :width], preferred_element_type=jnp.float32
        ).astype(low)


def attend_back_kernel(
    q_ref, k_ref, qinv_ref, kinv_ref, cos_ref, sin_ref, gq_ref, gk_ref, col_ref, row_ref,
    qlow_ref, klow_ref, vlow_ref, total_ref, dmixed_ref,
    dq_ref, dk_ref, dv_ref, dots_ref, gains_ref, key_acc, value_acc, query_acc, *, scale
):
    low = jnp.bfloat16
    half = q_ref.shape[-1] // 2
    length = q_ref.shape[1]
    block = min(QUERY_BLOCK, length)
    ids_col, ids_row = col_ref[0], row_ref[0]
    turned = (((0,), (0,)), ((), ()))
    across = (((1,), (1,)), ((), ()))
    key_acc[...] = jnp.zeros_like(key_acc)
    value_acc[...] = jnp.zeros_like(value_acc)
    for start in range(0, length, block):
        width = start + block
        query = qlow_ref[0, start:width]
        d_mixed = dmixed_ref[0, start:width]
        keys = klow_ref[0, :width]
        scores = lax.dot_general(query, keys, across, preferred_element_type=jnp.float32) * scale
        allowed = attention_masks(ids_col, ids_row, block, width, start)
        probs = jnp.exp(jnp.where(allowed, scores, -1e30) - total_ref[0, 0, start:width])
        d_probs = lax.dot_general(
            d_mixed, vlow_ref[0, :width], across, preferred_element_type=jnp.float32
        )
        row_dot = jnp.sum(probs * d_probs, -1, keepdims=True)
        d_scores = (probs * (d_probs - row_dot)).astype(low)
        query_acc[start:width] = jnp.dot(d_scores, keys, preferred_element_type=jnp.float32)
        key_acc[:width] += lax.dot_general(d_scores, query, turned, preferred_element_type=jnp.float32)
        value_acc[:width] += lax.dot_general(
            probs.astype(low), d_mixed, turned, preferred_element_type=jnp.float32
        )
    dv_ref[0] = value_acc[...].astype(low)
    cosine, sine_part = cos_ref[...], sin_ref[...]

    def turned_back(acc, ref, inv_ref, gain_ref, out_ref, at):
        value = (acc[...] * scale).astype(low).astype(jnp.float32)
        value = value * cosine - pltpu.roll(value, half, 1) * sine_part
        unit = ref[0] * inv_ref[0]
        gains_ref[0, at : at + 1] = jnp.sum(value * unit, 0, keepdims=True)
        value = value * gain_ref[...]
        out_ref[0] = value
        return jnp.sum(value * unit, -1, keepdims=True)

    query_dot = turned_back(query_acc, q_ref, qinv_ref, gq_ref, dq_ref, 0)
    key_dot = turned_back(key_acc, k_ref, kinv_ref, gk_ref, dk_ref, 1)
    lane = lax.broadcasted_iota(jnp.int32, (length, LANES), 1)
    dots = jnp.where(lane == 0, query_dot, jnp.where(lane == 1, key_dot, 0.0)).T[:8]

    @pl.when(pl.program_id(1) == 0)
    def _():
        dots_ref[0] = dots

    @pl.when(pl.program_id(1) != 0)
    def _():
        dots_ref[0] += dots


def attention_specs(length, heads, head_size):
    wide = lambda at: pl.BlockSpec((1, length, head_size), lambda r, h, at=at: (r, 0, at * heads + h))
    thin = pl.BlockSpec((1, length, 1), lambda r, h: (r, 0, 0))
    table = pl.BlockSpec((length, head_size), lambda r, h: (0, 0))
    gain = pl.BlockSpec((1, head_size), lambda r, h: (0, h))
    flat = pl.BlockSpec((1, 1, length), lambda r, h: (r, 0, 0))
    total = pl.BlockSpec((1, 1, length, 1), lambda r, h: (r, h, 0, 0))
    return wide, thin, table, gain, flat, total


def attend(qkv, inverses, tables, gains, ids, head_size, scale):
    rows, length, width = qkv.shape
    heads = width // (3 * head_size)
    wide, thin, table, gain, flat, total = attention_specs(length, heads, head_size)
    narrow = jax.ShapeDtypeStruct((rows, length, heads * head_size), jnp.bfloat16)
    return pl.pallas_call(
        functools.partial(attend_kernel, scale=scale),
        grid=(rows, heads),
        in_specs=[wide(0), wide(1), wide(2), thin, thin, table, table, gain, gain, thin, flat],
        out_specs=[wide(0), wide(0), wide(0), wide(0), total],
        out_shape=[narrow] * 4 + [jax.ShapeDtypeStruct((rows, heads, length, 1), jnp.float32)],
        name="attend",
    )(qkv, qkv, qkv, *inverses, *tables, *gains, ids[:, :, None], ids[:, None, :])


def attend_back(qkv, inverses, tables, gains, ids, kept, d_mixed, head_size, scale):
    rows, length, width = qkv.shape
    heads = width // (3 * head_size)
    wide, thin, table, gain, flat, total = attention_specs(length, heads, head_size)
    shape = (rows, length, heads * head_size)
    return pl.pallas_call(
        functools.partial(attend_back_kernel, scale=scale),
        grid=(rows, heads),
        in_specs=[wide(0), wide(1), thin, thin, table, table, gain, gain, thin, flat]
        + [wide(0), wide(0), wide(0), total, wide(0)],
        out_specs=[
            wide(0),
            wide(0),
            wide(0),
            pl.BlockSpec((1, 8, length), lambda r, h: (r, 0, 0)),
            pl.BlockSpec((1, 2, head_size), lambda r, h: (r, 0, h)),
        ],
        out_shape=[
            jax.ShapeDtypeStruct(shape, jnp.float32),
            jax.ShapeDtypeStruct(shape, jnp.float32),
            jax.ShapeDtypeStruct(shape, jnp.bfloat16),
            jax.ShapeDtypeStruct((rows, 8, length), jnp.float32),
            jax.ShapeDtypeStruct((rows, 2, heads * head_size), jnp.float32),
        ],
        scratch_shapes=[pltpu.VMEM((length, head_size), jnp.float32)] * 3,
        name="attend_back",
    )(qkv, qkv, *inverses, *tables, *gains, ids[:, :, None], ids[:, None, :], *kept, d_mixed)


def shards_by_feature(
    tokens,
    doc_ids,
    cotangent,
    w_query,
    w_key,
    w_value,
    w_out,
    w_gate,
    w_up,
    w_down,
    g_query,
    g_key,
    g_attn,
    g_ffn,
):
    row_count, piece_len, model_width = tokens.shape
    head_size = HEAD
    feature_count = w_query.shape[1]
    scale = head_size ** (-0.5)
    seq_count = lax.axis_size("seq")
    dp_count = lax.axis_size("dp")
    seq_at = lax.axis_index("seq")
    row_len = piece_len * seq_count
    all_count = row_count * row_len
    tok_count = row_count * piece_len
    own_features = feature_count // seq_count
    own_hidden = w_gate.shape[1] // seq_count
    low = jnp.bfloat16

    def own_piece(tensor):
        view = tensor.reshape(row_count, row_len, -1)
        return lax.dynamic_slice_in_dim(view, seq_at * piece_len, piece_len, 1).reshape(tok_count, -1)

    w_qkv = gather_dp(jnp.concatenate([own_columns(w, 1, seq_count, seq_at) for w in (w_query, w_key, w_value)], 1))
    tokens_all = gather_seq(tokens).reshape(all_count, model_width)
    ids_all = total_seq(
        lax.dynamic_update_slice_in_dim(
            jnp.zeros((row_count, row_len), jnp.int32), doc_ids, seq_at * piece_len, 1
        )
    )
    core = seq_at % 2
    half = model_width // 2
    out_rows = w_out.shape[0]
    out_pieces = pieces_dp(lax.dynamic_slice_in_dim(w_out, core * half, half, 1))
    other_pieces = [(swap(piece, "seq", 1), row) for piece, row in out_pieces]
    wo_full = placed(
        [(w_out, lax.axis_index("dp") * out_rows, 0)]
        + [(piece, row, core * half) for piece, row in out_pieces]
        + [(piece, row, half - core * half) for piece, row in other_pieces],
        (feature_count, model_width),
    )
    w_hidden = gather_dp(jnp.concatenate([own_columns(w, dp_count, seq_count, seq_at) for w in (w_gate, w_up)], 1))
    w_back = gather_dp(
        lax.dynamic_slice_in_dim(
            w_down, seq_at * (own_hidden // dp_count), own_hidden // dp_count, 0
        ),
    )
    gain_query = lax.dynamic_slice_in_dim(g_query, seq_at * own_features, own_features).astype(jnp.float32)
    gain_key = lax.dynamic_slice_in_dim(g_key, seq_at * own_features, own_features).astype(jnp.float32)
    gain_attn = g_attn.astype(jnp.float32)
    gain_ffn = g_ffn.astype(jnp.float32)

    tokens_all, ids_all = lax.optimization_barrier((tokens_all, ids_all))
    qkv = jnp.dot(tokens_all, w_qkv, preferred_element_type=jnp.float32)
    query_pre = qkv[:, :own_features]
    key_pre = qkv[:, own_features : 2 * own_features]
    squares = jnp.stack([jnp.sum(query_pre * query_pre, -1), jnp.sum(key_pre * key_pre, -1)])
    cosine, sine_part = rotation(jnp.arange(row_len, dtype=jnp.int32), head_size)
    tables = jnp.concatenate([cosine, cosine], 1), jnp.concatenate([-sine_part, sine_part], 1)
    inverse = lax.rsqrt(total_seq(squares) / feature_count + eps)
    inverses = [inverse[at].reshape(row_count, row_len, 1) for at in range(2)]
    norm_gains = gain_query[None, :], gain_key[None, :]
    qkv_rows = qkv.reshape(row_count, row_len, 3 * own_features)
    *kept, mixed_low, log_total = attend(
        qkv_rows, inverses, tables, norm_gains, ids_all, head_size, scale
    )
    mixed_low = mixed_low.reshape(all_count, own_features)
    mixed_all = lax.all_gather(mixed_low, "seq", axis=1, tiled=True)
    attn_out = jnp.dot(mixed_all, wo_full, preferred_element_type=jnp.float32)
    attn_inv_all = inverse_rms(attn_out)
    hidden_all = tokens_all.astype(jnp.float32) + attn_out * attn_inv_all * gain_attn
    hidden_low = hidden_all.astype(low)
    attn_inv = own_piece(attn_inv_all)
    attn_unit = own_piece(attn_out) * attn_inv
    hidden_state = tokens.reshape(tok_count, model_width).astype(jnp.float32) + attn_unit * gain_attn

    gate_up = jnp.dot(hidden_low, w_hidden, preferred_element_type=jnp.float32)
    gate, up_proj = gate_up[:, :own_hidden], gate_up[:, own_hidden:]
    sigma = jax.nn.sigmoid(gate)
    active = gate * sigma
    inner_low = (active * up_proj).astype(low)
    branch_part = jnp.dot(inner_low, w_back, preferred_element_type=jnp.float32).astype(low)
    branch = (
        scatter_seq(branch_part.reshape(row_count, row_len, model_width))
        .astype(jnp.float32)
        .reshape(tok_count, model_width)
    )
    branch_inv = inverse_rms(branch)
    branch_unit = branch * branch_inv
    result = (
        (hidden_state + branch_unit * gain_ffn)
        .astype(low)
        .reshape(row_count, piece_len, model_width)
    )

    grad_out = cotangent.reshape(tok_count, model_width).astype(jnp.float32)
    ffn_gain_term = jnp.sum(grad_out * branch_unit, 0)
    d_branch = norm_back(grad_out * gain_ffn, branch_unit, branch_inv).astype(low)
    d_branch_all = gather_seq(d_branch.reshape(row_count, piece_len, model_width)).reshape(all_count, model_width)
    d_inner = jnp.einsum("nd,fd->nf", d_branch_all, w_back, preferred_element_type=jnp.float32)
    d_gate = (d_inner * up_proj * sigma * (1.0 + gate * (1.0 - sigma))).astype(low)
    d_up = (d_inner * active).astype(low)
    d_gate_up = jnp.concatenate([d_gate, d_up], 1)
    d_hidden_part = jnp.einsum("nf,df->nd", d_gate_up, w_hidden, preferred_element_type=jnp.float32).astype(low)
    d_hidden_sum = scatter_seq(d_hidden_part.reshape(row_count, row_len, model_width))
    hidden_part = jnp.einsum("nd,nf->df", hidden_low, d_gate_up, preferred_element_type=jnp.float32).astype(low)
    down_part = jnp.einsum("nf,nd->fd", inner_low, d_branch_all, preferred_element_type=jnp.float32).astype(low)
    down_grad = sum_dp(*shares_for(down_part))
    hidden_own = sum_dp(*shares_for(hidden_part)).astype(low)
    d_hidden = grad_out + d_hidden_sum.astype(jnp.float32).reshape(tok_count, model_width)

    attn_gain_term = jnp.sum(d_hidden * attn_unit, 0)
    d_attn = norm_back(d_hidden * gain_attn, attn_unit, attn_inv).astype(low)
    d_mixed = jnp.einsum("nd,fd->nf", d_attn, wo_full, preferred_element_type=jnp.float32).astype(low)

    def own_columns_of_all(tensor):
        split = tensor.reshape(row_count, piece_len, seq_count, -1).transpose(2, 0, 1, 3)
        width = split.shape[-1]
        split = lax.all_to_all(split.reshape(seq_count, tok_count, width), "seq", split_axis=0, concat_axis=0)
        split = split.reshape(seq_count, row_count, piece_len, width).transpose(1, 0, 2, 3)
        return split.reshape(row_count, row_len, width)

    d_mixed = own_columns_of_all(d_mixed)
    d_mixed, d_attn = lax.optimization_barrier((d_mixed, d_attn))
    d_attn_own = own_columns_of_all(d_attn).reshape(all_count, -1)
    out_part = jnp.einsum("nf,nd->fd", mixed_all, d_attn_own, preferred_element_type=jnp.float32).astype(low)
    out_own = sum_dp(*shares_for(out_part)).astype(low)
    gate_grad, up_grad = rows_home(hidden_own, dp_count, own_hidden // dp_count)

    dq_gained, dk_gained, d_value, dots, gain_terms = attend_back(
        qkv_rows, inverses, tables, norm_gains, ids_all, (*kept, log_total), d_mixed, head_size, scale
    )
    norm_terms = lax.dynamic_update_slice_in_dim(
        jnp.zeros((2, feature_count), jnp.float32), jnp.sum(gain_terms, 0), seq_at * own_features, 1
    )
    dots = dots[:, :2].transpose(1, 0, 2).reshape(-1, LANES)
    stat_rows = dots.shape[0]
    sums = total_seq(
        jnp.concatenate(
            [dots]
            + [part.reshape(-1, LANES) for part in (norm_terms, attn_gain_term, ffn_gain_term)]
        )
    )
    means = sums[:stat_rows].reshape(2, all_count) / feature_count

    def norm_back_wide(gained, pre, at):
        inv = inverse[at][:, None]
        gained = gained.reshape(all_count, own_features)
        return (inv * (gained - pre * inv * means[at][:, None])).astype(low)

    dq_pre = norm_back_wide(dq_gained, query_pre, 0)
    dk_pre = norm_back_wide(dk_gained, key_pre, 1)
    d_value = d_value.reshape(all_count, own_features)
    d_qkv = jnp.concatenate([dq_pre, dk_pre, d_value], 1)
    d_tokens_part = jnp.einsum("nf,df->nd", d_qkv, w_qkv, preferred_element_type=jnp.float32).astype(low)
    d_qkv, d_tokens_part = lax.optimization_barrier((d_qkv, d_tokens_part))
    d_tokens_sum = scatter_seq(d_tokens_part.reshape(row_count, row_len, model_width))
    d_tokens = d_hidden + d_tokens_sum.astype(jnp.float32).reshape(tok_count, model_width)
    qkv_part = jnp.einsum("nd,nf->df", tokens_all, d_qkv, preferred_element_type=jnp.float32).astype(low)
    qkv_own = sum_dp(*shares_for(qkv_part)).astype(low)
    attn_home = rows_home(jnp.concatenate([qkv_own, out_own], 1), 1, own_features)
    share = feature_count // (dp_count * seq_count)
    gains = lax.dynamic_index_in_dim(
        sums[stat_rows:].reshape(4, dp_count, seq_count, share), seq_at, 2, False
    )
    gains = share_dp(gains.transpose(1, 0, 2).reshape(dp_count, 4 * share)).reshape(4, share)
    return (
        result,
        d_tokens.reshape(row_count, piece_len, model_width),
        attn_home[0],
        attn_home[1],
        attn_home[2],
        attn_home[3],
        gate_grad,
        up_grad,
        down_grad,
        gains[0],
        gains[1],
        gains[2],
        gains[3],
    )


def shards(tokens, doc_ids, cotangent, w_query, *rest):
    if w_query.shape[1] // HEAD % lax.axis_size("seq"):
        return shards_by_slab(tokens, doc_ids, cotangent, w_query, *rest)
    return shards_by_feature(tokens, doc_ids, cotangent, w_query, *rest)


def solution(mesh):
    return jax.shard_map(
        shards,
        mesh=mesh,
        in_specs=(
            P("dp", "seq", None),
            P("dp", "seq"),
            P("dp", "seq", None),
            P("dp", None),
            P("dp", None),
            P("dp", None),
            P("dp", None),
            P("dp", None),
            P("dp", None),
            P("dp", None),
            P(),
            P(),
            P(),
            P(),
        ),
        out_specs=(
            P("dp", "seq", None),
            P("dp", "seq", None),
            P(("dp", "seq"), None),
            P(("dp", "seq"), None),
            P(("dp", "seq"), None),
            P(("dp", "seq"), None),
            P(("dp", "seq"), None),
            P(("dp", "seq"), None),
            P(("dp", "seq"), None),
            P(("dp", "seq")),
            P(("dp", "seq")),
            P(("dp", "seq")),
            P(("dp", "seq")),
        ),
        check_vma=False,
    )
```

```python
import functools

import jax
import jax.numpy as jnp
from jax import lax
from jax.experimental import pallas as pl
from jax.experimental.layout import Layout, with_layout_constraint
from jax.experimental.pallas import tpu as pltpu
from jax.sharding import PartitionSpec as P


HEAD = 128
SLABS = 4
LANES = 128


eps = 1e-06
theta = 500000.0


def rotation(positions, head_size):
    half_size = head_size // 2
    frequency = theta ** (-(2.0 * jnp.arange(half_size, dtype=jnp.float32)) / head_size)
    angles = positions.astype(jnp.float32)[:, None] * frequency[None, :]
    return (jnp.cos(angles), jnp.sin(angles))


def rotate(tensor, cosine, sine_part):
    half_size = tensor.shape[-1] // 2
    first_half = tensor[..., :half_size]
    second_half = tensor[..., half_size:]
    cos_wide = cosine[:, None, :]
    sin_wide = sine_part[:, None, :]
    return jnp.concatenate(
        [
            first_half * cos_wide - second_half * sin_wide,
            second_half * cos_wide + first_half * sin_wide,
        ],
        -1,
    )


def unrotate(tensor, cosine, sine_part):
    half_size = tensor.shape[-1] // 2
    first_half = tensor[..., :half_size]
    second_half = tensor[..., half_size:]
    cos_wide = cosine[:, None, :]
    sin_wide = sine_part[:, None, :]
    return jnp.concatenate(
        [
            first_half * cos_wide + second_half * sin_wide,
            second_half * cos_wide - first_half * sin_wide,
        ],
        -1,
    )


def inverse_rms(tensor):
    return lax.rsqrt(jnp.mean(tensor * tensor, -1, keepdims=True) + eps)


def norm_back(grad_unit, unit_vec, inverse):
    return inverse * (grad_unit - unit_vec * jnp.mean(grad_unit * unit_vec, -1, keepdims=True))


def visible(own_ids, key_ids, query_at, key_at):
    causal = key_at[None, :] <= query_at[:, None]
    same_doc = own_ids[:, :, None] == key_ids[:, None, :]
    return (causal[None] & same_doc)[:, None]


def masked_scores(query_low, pair_all, allowed, head_count, head_size):
    row_count = pair_all.shape[0]
    row_length = pair_all.shape[1]
    feature_count = head_count * head_size
    key_rows = pair_all[..., :feature_count].reshape(row_count, row_length, head_count, head_size)
    value_rows = pair_all[..., feature_count:].reshape(row_count, row_length, head_count, head_size)
    scores = jnp.einsum(
        "rche,rlhe->rhcl", query_low, key_rows, preferred_element_type=jnp.float32
    ) * head_size ** (-0.5)
    return (jnp.where(allowed, scores, -1e30), key_rows, value_rows)


def columns_of(matrix, parts, slab_count, index):
    lead = matrix.shape[0]
    width = matrix.shape[1] // (parts * slab_count)
    return matrix.reshape(lead, parts, slab_count, width)[:, :, index].reshape(lead, parts * width)


def entries_of(vector, parts, slab_count, index):
    width = vector.shape[0] // (parts * slab_count)
    return vector.reshape(parts, slab_count, width)[:, index].reshape(parts * width)


def shards_by_slab(
    tokens,
    doc_ids,
    cotangent,
    w_query,
    w_key,
    w_value,
    w_out,
    w_gate,
    w_up,
    w_down,
    g_query,
    g_key,
    g_attn,
    g_ffn,
):
    row_count, piece_len, model_width = tokens.shape
    head_size = HEAD
    feature_count = w_query.shape[1]
    head_count = feature_count // head_size
    tok_count = row_count * piece_len
    scale = head_size ** (-0.5)
    seq_count = lax.axis_size("seq")
    parts = lax.axis_size("dp") * seq_count
    slab_count = SLABS
    gather_all = (
        lax.all_gather(w_query, "dp", axis=0, tiled=True),
        lax.all_gather(w_key, "dp", axis=0, tiled=True),
        lax.all_gather(w_value, "dp", axis=0, tiled=True),
        lax.all_gather(w_out, "dp", axis=0, tiled=True),
        lax.all_gather(w_gate, "dp", axis=0, tiled=True),
        lax.all_gather(w_up, "dp", axis=0, tiled=True),
        lax.all_gather(w_down, "dp", axis=0, tiled=True),
    )
    wq_full, wk_full, wv_full, wo_full, wg_full, wu_full, wd_full = gather_all
    gain_query = g_query.astype(jnp.float32)
    gain_key = g_key.astype(jnp.float32)
    gain_attn = g_attn.astype(jnp.float32)
    gain_ffn = g_ffn.astype(jnp.float32)
    flat_tokens = tokens.reshape(tok_count, model_width)
    query_pre = jnp.dot(flat_tokens, wq_full, preferred_element_type=jnp.float32)
    key_pre = jnp.dot(flat_tokens, wk_full, preferred_element_type=jnp.float32)
    value_pre = jnp.dot(flat_tokens, wv_full, preferred_element_type=jnp.float32)
    query_inv = inverse_rms(query_pre)
    query_unit = query_pre * query_inv
    key_inv = inverse_rms(key_pre)
    key_unit = key_pre * key_inv
    first_row = lax.axis_index("seq") * piece_len
    positions = first_row + jnp.tile(jnp.arange(piece_len, dtype=jnp.int32), row_count)
    cosine, sine_part = rotation(positions, head_size)
    query_rot = rotate(
        (query_unit * gain_query).reshape(tok_count, head_count, head_size), cosine, sine_part
    )
    key_rot = rotate(
        (key_unit * gain_key).reshape(tok_count, head_count, head_size), cosine, sine_part
    )
    query_low = query_rot.astype(jnp.bfloat16).reshape(row_count, piece_len, head_count, head_size)
    key_low = key_rot.astype(jnp.bfloat16).reshape(row_count, piece_len, feature_count)
    value_low = value_pre.astype(jnp.bfloat16).reshape(row_count, piece_len, feature_count)
    pair_low = jnp.concatenate([key_low, value_low], -1)
    ids_low = doc_ids.astype(jnp.bfloat16)
    pair_all, ids_all = (
        lax.all_gather(pair_low, "seq", axis=1, tiled=True),
        lax.all_gather(ids_low, "seq", axis=1, tiled=True),
    )
    query_at = first_row + jnp.arange(piece_len, dtype=jnp.int32)
    allowed = visible(ids_low, ids_all, query_at, jnp.arange(pair_all.shape[1], dtype=jnp.int32))
    masked, _, value_rows = masked_scores(
        query_low, pair_all, allowed, head_count, head_size
    )
    row_max = jnp.max(masked, -1, keepdims=True)
    log_total = jnp.log(jnp.sum(jnp.exp(masked - row_max), -1, keepdims=True)) + row_max
    probs_low = jnp.exp(masked - log_total).astype(jnp.bfloat16)
    mixed = jnp.einsum("rhcl,rlhe->rche", probs_low, value_rows, preferred_element_type=jnp.float32)
    mixed_low = mixed.reshape(tok_count, feature_count).astype(jnp.bfloat16)
    attn_out = jnp.dot(mixed_low, wo_full, preferred_element_type=jnp.float32)
    attn_inv = inverse_rms(attn_out)
    attn_unit = attn_out * attn_inv
    hidden_state = flat_tokens.astype(jnp.float32) + attn_unit * gain_attn
    hidden_low = hidden_state.astype(jnp.bfloat16)
    gate = jnp.dot(hidden_low, wg_full, preferred_element_type=jnp.float32)
    up_proj = jnp.dot(hidden_low, wu_full, preferred_element_type=jnp.float32)
    sigma = jax.nn.sigmoid(gate)
    active = gate * sigma
    inner_low = (active * up_proj).astype(jnp.bfloat16)
    branch = jnp.dot(inner_low, wd_full, preferred_element_type=jnp.float32)
    branch_inv = inverse_rms(branch)
    branch_unit = branch * branch_inv
    result = (
        (hidden_state + branch_unit * gain_ffn)
        .astype(jnp.bfloat16)
        .reshape(row_count, piece_len, model_width)
    )
    wq_back, wk_back, wv_back, wo_back, wg_back, wu_back, wd_back = gather_all
    pair_back, ids_back = (pair_all, ids_all)
    grad_out = cotangent.reshape(tok_count, model_width).astype(jnp.float32)
    ffn_gain_term = jnp.sum(grad_out * branch_unit, 0)
    d_branch = norm_back(grad_out * gain_ffn, branch_unit, branch_inv).astype(jnp.bfloat16)
    d_inner = jnp.einsum("nd,fd->nf", d_branch, wd_back, preferred_element_type=jnp.float32)
    d_gate = (d_inner * up_proj * sigma * (1.0 + gate * (1.0 - sigma))).astype(jnp.bfloat16)
    d_up = (d_inner * active).astype(jnp.bfloat16)
    d_hidden = grad_out + jnp.einsum(
        "nf,df->nd", d_gate, wg_back, preferred_element_type=jnp.float32
    )
    d_hidden = d_hidden + jnp.einsum("nf,df->nd", d_up, wu_back, preferred_element_type=jnp.float32)
    mlp_shares = []
    for index in range(slab_count):
        hidden_part = columns_of(hidden_low, parts, slab_count, index)
        inner_part = columns_of(inner_low, parts, slab_count, index)
        gate_term = jnp.einsum("nd,nf->df", hidden_part, d_gate, preferred_element_type=jnp.float32)
        up_term = jnp.einsum("nd,nf->df", hidden_part, d_up, preferred_element_type=jnp.float32)
        down_term = jnp.einsum(
            "nf,nd->fd", inner_part, d_branch, preferred_element_type=jnp.float32
        )
        ffn_term = entries_of(ffn_gain_term, parts, slab_count, index)
        shares = (
            lax.psum_scatter(down_term, ("dp", "seq"), scatter_dimension=0, tiled=True),
            lax.psum_scatter(gate_term, ("dp", "seq"), scatter_dimension=0, tiled=True),
            lax.psum_scatter(up_term, ("dp", "seq"), scatter_dimension=0, tiled=True),
            lax.psum_scatter(ffn_term, ("dp", "seq"), scatter_dimension=0, tiled=True),
        )
        mlp_shares.append(shares)
    down_grad = jnp.concatenate([s[0] for s in mlp_shares], 0)
    gate_grad = jnp.concatenate([s[1] for s in mlp_shares], 0)
    up_grad = jnp.concatenate([s[2] for s in mlp_shares], 0)
    ffn_grad = jnp.concatenate([s[3] for s in mlp_shares], 0)
    attn_gain_term = jnp.sum(d_hidden * attn_unit, 0)
    d_attn = norm_back(d_hidden * gain_attn, attn_unit, attn_inv).astype(jnp.bfloat16)
    d_mixed = jnp.einsum("nd,fd->nf", d_attn, wo_back, preferred_element_type=jnp.float32).astype(
        jnp.bfloat16
    )
    d_mixed = d_mixed.reshape(row_count, piece_len, head_count, head_size)
    sub_len = piece_len // slab_count
    pair_width = pair_back.shape[-1]
    pair_view = pair_back.reshape(row_count, seq_count, slab_count, sub_len, pair_width)
    ids_view = ids_back.reshape(row_count, seq_count, slab_count, sub_len)

    def slab_scores(index):
        pair_part = pair_view[:, :, index].reshape(row_count, seq_count * sub_len, pair_width)
        ids_part = ids_view[:, :, index].reshape(row_count, seq_count * sub_len)
        key_at = (
            jnp.arange(seq_count, dtype=jnp.int32)[:, None] * piece_len
            + index * sub_len
            + jnp.arange(sub_len, dtype=jnp.int32)[None, :]
        ).reshape(seq_count * sub_len)
        allowed_part = visible(ids_low, ids_part, query_at, key_at)
        masked_part, key_part, value_part = masked_scores(
            query_low, pair_part, allowed_part, head_count, head_size
        )
        probs_part = jnp.exp(masked_part - log_total)
        d_probs_part = jnp.einsum(
            "rche,rlhe->rhcl", d_mixed, value_part, preferred_element_type=jnp.float32
        )
        return (probs_part, d_probs_part, key_part)

    row_dot = jnp.zeros((row_count, head_count, piece_len, 1), jnp.float32)
    for index in range(slab_count):
        probs_part, d_probs_part, key_part = slab_scores(index)
        row_dot = row_dot + jnp.sum(probs_part * d_probs_part, -1, keepdims=True)
    query_acc = jnp.zeros((row_count, piece_len, head_count, head_size), jnp.float32)
    pair_shares = []
    for index in range(slab_count):
        probs_part, d_probs_part, key_part = slab_scores(index)
        d_scores = (probs_part * (d_probs_part - row_dot)).astype(jnp.bfloat16)
        query_acc = query_acc + jnp.einsum(
            "rhcl,rlhe->rche", d_scores, key_part, preferred_element_type=jnp.float32
        )
        key_term = (
            jnp.einsum("rhcl,rche->rlhe", d_scores, query_low, preferred_element_type=jnp.float32)
            * scale
        )
        value_term = jnp.einsum(
            "rhcl,rche->rlhe",
            probs_part.astype(jnp.bfloat16),
            d_mixed,
            preferred_element_type=jnp.float32,
        )
        key_count = seq_count * sub_len
        pair_term = jnp.concatenate(
            [
                key_term.reshape(row_count, key_count, feature_count),
                value_term.reshape(row_count, key_count, feature_count),
            ],
            -1,
        )
        pair_shares.append(
            lax.psum_scatter(
                pair_term.astype(jnp.bfloat16), "seq", scatter_dimension=1, tiled=True
            ).astype(jnp.float32)
        )
    pair_grad = jnp.concatenate(pair_shares, 1)
    d_query = (query_acc * scale).astype(jnp.bfloat16)
    d_key = (
        pair_grad[..., :feature_count]
        .astype(jnp.bfloat16)
        .reshape(tok_count, head_count, head_size)
    )
    d_value = pair_grad[..., feature_count:].astype(jnp.bfloat16).reshape(tok_count, feature_count)
    dq_norm = unrotate(
        d_query.reshape(tok_count, head_count, head_size).astype(jnp.float32), cosine, sine_part
    ).reshape(tok_count, feature_count)
    dk_norm = unrotate(d_key.astype(jnp.float32), cosine, sine_part).reshape(
        tok_count, feature_count
    )
    query_gain_term = jnp.sum(dq_norm * query_unit, 0)
    key_gain_term = jnp.sum(dk_norm * key_unit, 0)
    dq_pre = norm_back(dq_norm * gain_query, query_unit, query_inv).astype(jnp.bfloat16)
    dk_pre = norm_back(dk_norm * gain_key, key_unit, key_inv).astype(jnp.bfloat16)
    d_tokens = d_hidden + jnp.einsum(
        "nf,df->nd", dq_pre, wq_back, preferred_element_type=jnp.float32
    )
    d_tokens = d_tokens + jnp.einsum(
        "nf,df->nd", dk_pre, wk_back, preferred_element_type=jnp.float32
    )
    d_tokens = d_tokens + jnp.einsum(
        "nf,df->nd", d_value, wv_back, preferred_element_type=jnp.float32
    )
    attn_shares = []
    for index in range(slab_count):
        token_part = columns_of(flat_tokens, parts, slab_count, index)
        mixed_part = columns_of(mixed_low, parts, slab_count, index)
        query_term = jnp.einsum("nd,nf->df", token_part, dq_pre, preferred_element_type=jnp.float32)
        key_wterm = jnp.einsum("nd,nf->df", token_part, dk_pre, preferred_element_type=jnp.float32)
        value_wterm = jnp.einsum(
            "nd,nf->df", token_part, d_value, preferred_element_type=jnp.float32
        )
        out_term = jnp.einsum("nf,nd->fd", mixed_part, d_attn, preferred_element_type=jnp.float32)
        gq_term = entries_of(query_gain_term, parts, slab_count, index)
        gk_term = entries_of(key_gain_term, parts, slab_count, index)
        ga_term = entries_of(attn_gain_term, parts, slab_count, index)
        shares = (
            lax.psum_scatter(query_term, ("dp", "seq"), scatter_dimension=0, tiled=True),
            lax.psum_scatter(key_wterm, ("dp", "seq"), scatter_dimension=0, tiled=True),
            lax.psum_scatter(value_wterm, ("dp", "seq"), scatter_dimension=0, tiled=True),
            lax.psum_scatter(out_term, ("dp", "seq"), scatter_dimension=0, tiled=True),
            lax.psum_scatter(gq_term, ("dp", "seq"), scatter_dimension=0, tiled=True),
            lax.psum_scatter(gk_term, ("dp", "seq"), scatter_dimension=0, tiled=True),
            lax.psum_scatter(ga_term, ("dp", "seq"), scatter_dimension=0, tiled=True),
        )
        attn_shares.append(shares)
    query_grad = jnp.concatenate([s[0] for s in attn_shares], 0)
    key_grad = jnp.concatenate([s[1] for s in attn_shares], 0)
    value_grad = jnp.concatenate([s[2] for s in attn_shares], 0)
    out_grad = jnp.concatenate([s[3] for s in attn_shares], 0)
    gq_grad = jnp.concatenate([s[4] for s in attn_shares], 0)
    gk_grad = jnp.concatenate([s[5] for s in attn_shares], 0)
    ga_grad = jnp.concatenate([s[6] for s in attn_shares], 0)
    tokens_grad = d_tokens.reshape(row_count, piece_len, model_width)
    return (
        result,
        tokens_grad,
        query_grad,
        key_grad,
        value_grad,
        out_grad,
        gate_grad,
        up_grad,
        down_grad,
        gq_grad,
        gk_grad,
        ga_grad,
        ffn_grad,
    )


def own_columns(matrix, groups, parts, index):
    width = matrix.shape[1] // (groups * parts)
    pieces = [
        lax.dynamic_slice_in_dim(matrix, (group * parts + index) * width, width, 1)
        for group in range(groups)
    ]
    return jnp.concatenate(pieces, 1) if groups > 1 else pieces[0]


def gather_seq(piece):
    return lax.all_gather(piece, "seq", axis=1, tiled=True)


def scatter_seq(partial):
    return lax.psum_scatter(partial, "seq", scatter_dimension=1, tiled=True)


def swap(value, axis, flip):
    return lax.ppermute(value, axis, [(at, at ^ flip) for at in range(lax.axis_size(axis))])


def place_kernel(spots_ref, *refs):
    *in_refs, out_ref, sems = refs
    copies = []
    for at, in_ref in enumerate(in_refs):
        rows, width = in_ref.shape
        row = pl.multiple_of(spots_ref[2 * at], LANES)
        column = pl.multiple_of(spots_ref[2 * at + 1], LANES)
        copies.append(
            pltpu.make_async_copy(
                in_ref, out_ref.at[pl.ds(row, rows), pl.ds(column, width)], sems.at[at]
            )
        )
    for copy in copies:
        copy.start()
    for copy in copies:
        copy.wait()


def placed(pieces, shape):
    spots = jnp.stack([jnp.int32(at) for _, row, column in pieces for at in (row, column)])
    return pl.pallas_call(
        place_kernel,
        grid_spec=pltpu.PrefetchScalarGridSpec(
            num_scalar_prefetch=1,
            grid=(1,),
            in_specs=[
                pl.BlockSpec(piece.shape, lambda at, spots: (0, 0), pipeline_mode=pl.Buffered(1))
                for piece, _, _ in pieces
            ],
            out_specs=pl.BlockSpec(memory_space=pl.ANY),
            scratch_shapes=[pltpu.SemaphoreType.DMA((len(pieces),))],
        ),
        out_shape=jax.ShapeDtypeStruct(shape, pieces[0][0].dtype),
        name="place",
    )(spots, *[piece for piece, _, _ in pieces])


def pieces_for(value, name, split_axis):
    count, index = lax.axis_size(name), lax.axis_index(name)
    width = value.shape[split_axis] // count
    return [
        lax.dynamic_slice_in_dim(value, (index ^ flip) * width, width, split_axis)
        for flip in range(count)
    ]


def swapped(pieces, name):
    return [swap(piece, name, flip) if flip else piece for flip, piece in enumerate(pieces)]


def exchanged(value, name, split_axis):
    return swapped(pieces_for(value, name, split_axis), name)


def pieces_dp(piece):
    half = piece.shape[0] // 2
    first, second = swap(piece, "dp", 1), swap(piece, "dp", 2)
    top, bottom = swap(first[:half], "dp", 2), swap(second[half:], "dp", 1)
    index = lax.axis_index("dp")
    width = piece.shape[0]
    far = (index ^ 3) * width
    return [
        (first, (index ^ 1) * width),
        (second, (index ^ 2) * width),
        (top, far),
        (bottom, far + half),
    ]


def gather_dp(piece):
    rows, width = piece.shape
    pieces = [(piece, lax.axis_index("dp") * rows), *pieces_dp(piece)]
    return placed([(part, row, 0) for part, row in pieces], (4 * rows, width))


def sum_dp(sent, kept):
    got = swap(sent[0], "dp", 1), swap(sent[1], "dp", 2)
    wide = [(kept[at].astype(jnp.float32) + got[at].astype(jnp.float32)) for at in range(2)]
    onward = [side[1].astype(jnp.bfloat16) for side in wide]
    last = swap(onward[0], "dp", 2), swap(onward[1], "dp", 1)
    return jnp.concatenate(
        [wide[at][0] + last[at].astype(jnp.float32) for at in range(2)], 0
    )


def shares_for(partial):
    index = lax.axis_index("dp")
    width = partial.shape[0] // 4
    half = width // 2

    def part(flip, side):
        return lax.dynamic_slice_in_dim(partial, (index ^ flip) * width + side * half, half, 0)

    sent = [jnp.stack([part(1, 0), part(3, 0)]), jnp.stack([part(2, 1), part(3, 1)])]
    kept = [jnp.stack([part(0, 0), part(2, 0)]), jnp.stack([part(0, 1), part(1, 1)])]
    return sent, kept


def stored_turned(matrix, after):
    matrix, after = lax.optimization_barrier((matrix, after))
    return with_layout_constraint(matrix.T, Layout((0, 1))), after


def total_seq(value):
    shape = value.shape
    value = value.reshape(-1, LANES)
    flip = 1
    while flip < lax.axis_size("seq"):
        value = value + swap(value, "seq", flip)
        flip *= 2
    return value.reshape(shape)


def share_dp(rows):
    flip = lax.axis_size("dp") // 2
    while flip:
        halves = rows.reshape(2, rows.shape[0] // 2, rows.shape[1])
        side = lax.axis_index("dp") // flip % 2
        kept = lax.dynamic_index_in_dim(halves, side, 0, False)
        sent = lax.dynamic_index_in_dim(halves, 1 - side, 0, False)
        rows = kept + swap(sent, "dp", flip)
        flip //= 2
    return rows[0]


def settle_kernel(index_ref, *refs, groups, width, count):
    in_refs, out_refs = refs[:count], refs[count:]
    for flip, in_ref in enumerate(in_refs):
        source = index_ref[0] ^ flip
        for at, out_ref in enumerate(out_refs):
            for group in range(groups):
                column = (at * groups + group) * width
                place = pl.multiple_of((group * count + source) * width, width)
                out_ref[:, pl.ds(place, width)] = in_ref[:, column : column + width].astype(jnp.float32)


def rows_home(summed, groups, width):
    pieces = exchanged(summed, "seq", 0)
    count = len(pieces)
    rows, total = pieces[0].shape
    outs = total // (groups * width)
    step = min(16, rows)
    wide = count * groups * width
    return pl.pallas_call(
        functools.partial(settle_kernel, groups=groups, width=width, count=count),
        grid_spec=pltpu.PrefetchScalarGridSpec(
            num_scalar_prefetch=1,
            grid=(rows // step,),
            in_specs=[pl.BlockSpec((step, total), lambda r, index: (r, 0))] * count,
            out_specs=[pl.BlockSpec((step, wide), lambda r, index: (r, 0))] * outs,
        ),
        out_shape=[jax.ShapeDtypeStruct((rows, wide), jnp.float32)] * outs,
        name="settle",
    )(lax.axis_index("seq").reshape(1), *pieces)


QUERY_BLOCK = 256


def attention_masks(ids_col, ids_row, block, width, start):
    rows = start + lax.broadcasted_iota(jnp.int32, (block, width), 0)
    columns = lax.broadcasted_iota(jnp.int32, (block, width), 1)
    return (columns <= rows) & (ids_col[start : start + block] == ids_row[:, :width])


def attend_kernel(
    q_ref, k_ref, v_ref, qinv_ref, kinv_ref, cos_ref, sin_ref, gq_ref, gk_ref, col_ref, row_ref,
    qlow_ref, klow_ref, vlow_ref, mixed_ref, total_ref, *, scale
):
    low = jnp.bfloat16
    half = q_ref.shape[-1] // 2
    cosine, sine_part = cos_ref[...], sin_ref[...]

    def rotated(ref, inv_ref, gain_ref):
        value = ref[0] * inv_ref[0] * gain_ref[...]
        return (value * cosine + pltpu.roll(value, half, 1) * sine_part).astype(low)

    qlow_ref[0] = rotated(q_ref, qinv_ref, gq_ref)
    klow_ref[0] = rotated(k_ref, kinv_ref, gk_ref)
    vlow_ref[0] = v_ref[0].astype(low)
    length = q_ref.shape[1]
    block = min(QUERY_BLOCK, length)
    ids_col, ids_row = col_ref[0], row_ref[0]
    for start in range(0, length, block):
        width = start + block
        scores = lax.dot_general(
            qlow_ref[0, start:width], klow_ref[0, :width], (((1,), (1,)), ((), ())),
            preferred_element_type=jnp.float32,
        ) * scale
        allowed = attention_masks(ids_col, ids_row, block, width, start)
        masked = jnp.where(allowed, scores, -1e30)
        row_max = jnp.max(masked, -1, keepdims=True)
        log_total = jnp.log(jnp.sum(jnp.exp(masked - row_max), -1, keepdims=True)) + row_max
        total_ref[0, 0, start:width] = log_total
        probs = jnp.exp(masked - log_total).astype(low)
        mixed_ref[0, start:width] = jnp.dot(
            probs, vlow_ref[0, :width], preferred_element_type=jnp.float32
        ).astype(low)


def attend_back_kernel(
    q_ref, k_ref, qinv_ref, kinv_ref, cos_ref, sin_ref, gq_ref, gk_ref, col_ref, row_ref,
    qlow_ref, klow_ref, vlow_ref, total_ref, dmixed_ref,
    dq_ref, dk_ref, dv_ref, dots_ref, gains_ref, key_acc, value_acc, query_acc, *, scale
):
    low = jnp.bfloat16
    half = q_ref.shape[-1] // 2
    length = q_ref.shape[1]
    block = min(QUERY_BLOCK, length)
    ids_col, ids_row = col_ref[0], row_ref[0]
    turned = (((0,), (0,)), ((), ()))
    across = (((1,), (1,)), ((), ()))
    key_acc[...] = jnp.zeros_like(key_acc)
    value_acc[...] = jnp.zeros_like(value_acc)
    for start in range(0, length, block):
        width = start + block
        query = qlow_ref[0, start:width]
        d_mixed = dmixed_ref[0, start:width]
        keys = klow_ref[0, :width]
        scores = lax.dot_general(query, keys, across, preferred_element_type=jnp.float32) * scale
        allowed = attention_masks(ids_col, ids_row, block, width, start)
        probs = jnp.exp(jnp.where(allowed, scores, -1e30) - total_ref[0, 0, start:width])
        d_probs = lax.dot_general(
            d_mixed, vlow_ref[0, :width], across, preferred_element_type=jnp.float32
        )
        row_dot = jnp.sum(probs * d_probs, -1, keepdims=True)
        d_scores = (probs * (d_probs - row_dot)).astype(low)
        query_acc[start:width] = jnp.dot(d_scores, keys, preferred_element_type=jnp.float32)
        key_acc[:width] += lax.dot_general(d_scores, query, turned, preferred_element_type=jnp.float32)
        value_acc[:width] += lax.dot_general(
            probs.astype(low), d_mixed, turned, preferred_element_type=jnp.float32
        )
    dv_ref[0] = value_acc[...].astype(low)
    cosine, sine_part = cos_ref[...], sin_ref[...]

    def turned_back(acc, ref, inv_ref, gain_ref, out_ref, at):
        value = (acc[...] * scale).astype(low).astype(jnp.float32)
        value = value * cosine - pltpu.roll(value, half, 1) * sine_part
        unit = ref[0] * inv_ref[0]
        gains_ref[0, at : at + 1] = jnp.sum(value * unit, 0, keepdims=True)
        value = value * gain_ref[...]
        out_ref[0] = value
        return jnp.sum(value * unit, -1, keepdims=True)

    query_dot = turned_back(query_acc, q_ref, qinv_ref, gq_ref, dq_ref, 0)
    key_dot = turned_back(key_acc, k_ref, kinv_ref, gk_ref, dk_ref, 1)
    lane = lax.broadcasted_iota(jnp.int32, (length, LANES), 1)
    dots = jnp.where(lane == 0, query_dot, jnp.where(lane == 1, key_dot, 0.0)).T[:8]

    @pl.when(pl.program_id(1) == 0)
    def _():
        dots_ref[0] = dots

    @pl.when(pl.program_id(1) != 0)
    def _():
        dots_ref[0] += dots


def attention_specs(length, heads, head_size):
    wide = lambda at: pl.BlockSpec((1, length, head_size), lambda r, h, at=at: (r, 0, at * heads + h))
    thin = pl.BlockSpec((1, length, 1), lambda r, h: (r, 0, 0))
    table = pl.BlockSpec((length, head_size), lambda r, h: (0, 0))
    gain = pl.BlockSpec((1, head_size), lambda r, h: (0, h))
    flat = pl.BlockSpec((1, 1, length), lambda r, h: (r, 0, 0))
    total = pl.BlockSpec((1, 1, length, 1), lambda r, h: (r, h, 0, 0))
    return wide, thin, table, gain, flat, total


def attend(qkv, inverses, tables, gains, ids, head_size, scale):
    rows, length, width = qkv.shape
    heads = width // (3 * head_size)
    wide, thin, table, gain, flat, total = attention_specs(length, heads, head_size)
    narrow = jax.ShapeDtypeStruct((rows, length, heads * head_size), jnp.bfloat16)
    return pl.pallas_call(
        functools.partial(attend_kernel, scale=scale),
        grid=(rows, heads),
        in_specs=[wide(0), wide(1), wide(2), thin, thin, table, table, gain, gain, thin, flat],
        out_specs=[wide(0), wide(0), wide(0), wide(0), total],
        out_shape=[narrow] * 4 + [jax.ShapeDtypeStruct((rows, heads, length, 1), jnp.float32)],
        name="attend",
    )(qkv, qkv, qkv, *inverses, *tables, *gains, ids[:, :, None], ids[:, None, :])


def attend_back(qkv, inverses, tables, gains, ids, kept, d_mixed, head_size, scale):
    rows, length, width = qkv.shape
    heads = width // (3 * head_size)
    wide, thin, table, gain, flat, total = attention_specs(length, heads, head_size)
    shape = (rows, length, heads * head_size)
    return pl.pallas_call(
        functools.partial(attend_back_kernel, scale=scale),
        grid=(rows, heads),
        in_specs=[wide(0), wide(1), thin, thin, table, table, gain, gain, thin, flat]
        + [wide(0), wide(0), wide(0), total, wide(0)],
        out_specs=[
            wide(0),
            wide(0),
            wide(0),
            pl.BlockSpec((1, 8, length), lambda r, h: (r, 0, 0)),
            pl.BlockSpec((1, 2, head_size), lambda r, h: (r, 0, h)),
        ],
        out_shape=[
            jax.ShapeDtypeStruct(shape, jnp.float32),
            jax.ShapeDtypeStruct(shape, jnp.float32),
            jax.ShapeDtypeStruct(shape, jnp.bfloat16),
            jax.ShapeDtypeStruct((rows, 8, length), jnp.float32),
            jax.ShapeDtypeStruct((rows, 2, heads * head_size), jnp.float32),
        ],
        scratch_shapes=[pltpu.VMEM((length, head_size), jnp.float32)] * 3,
        name="attend_back",
    )(qkv, qkv, *inverses, *tables, *gains, ids[:, :, None], ids[:, None, :], *kept, d_mixed)


def shards_by_feature(
    tokens,
    doc_ids,
    cotangent,
    w_query,
    w_key,
    w_value,
    w_out,
    w_gate,
    w_up,
    w_down,
    g_query,
    g_key,
    g_attn,
    g_ffn,
):
    row_count, piece_len, model_width = tokens.shape
    head_size = HEAD
    feature_count = w_query.shape[1]
    scale = head_size ** (-0.5)
    seq_count = lax.axis_size("seq")
    dp_count = lax.axis_size("dp")
    seq_at = lax.axis_index("seq")
    row_len = piece_len * seq_count
    all_count = row_count * row_len
    tok_count = row_count * piece_len
    own_features = feature_count // seq_count
    own_hidden = w_gate.shape[1] // seq_count
    low = jnp.bfloat16

    def own_piece(tensor):
        view = tensor.reshape(row_count, row_len, -1)
        return lax.dynamic_slice_in_dim(view, seq_at * piece_len, piece_len, 1).reshape(tok_count, -1)

    w_qkv = gather_dp(jnp.concatenate([own_columns(w, 1, seq_count, seq_at) for w in (w_query, w_key, w_value)], 1))
    tokens_all = gather_seq(tokens).reshape(all_count, model_width)
    ids_all = total_seq(
        lax.dynamic_update_slice_in_dim(
            jnp.zeros((row_count, row_len), jnp.int32), doc_ids, seq_at * piece_len, 1
        )
    )
    core = seq_at % 2
    half = model_width // 2
    out_rows = w_out.shape[0]
    out_pieces = pieces_dp(lax.dynamic_slice_in_dim(w_out, core * half, half, 1))
    other_pieces = [(swap(piece, "seq", 1), row) for piece, row in out_pieces]
    wo_full = placed(
        [(w_out, lax.axis_index("dp") * out_rows, 0)]
        + [(piece, row, core * half) for piece, row in out_pieces]
        + [(piece, row, half - core * half) for piece, row in other_pieces],
        (feature_count, model_width),
    )
    w_hidden = gather_dp(jnp.concatenate([own_columns(w, dp_count, seq_count, seq_at) for w in (w_gate, w_up)], 1))
    w_back = gather_dp(
        lax.dynamic_slice_in_dim(
            w_down, seq_at * (own_hidden // dp_count), own_hidden // dp_count, 0
        ),
    )
    gain_query = lax.dynamic_slice_in_dim(g_query, seq_at * own_features, own_features).astype(jnp.float32)
    gain_key = lax.dynamic_slice_in_dim(g_key, seq_at * own_features, own_features).astype(jnp.float32)
    gain_attn = g_attn.astype(jnp.float32)
    gain_ffn = g_ffn.astype(jnp.float32)

    tokens_all, ids_all = lax.optimization_barrier((tokens_all, ids_all))
    qkv = jnp.dot(tokens_all, w_qkv, preferred_element_type=jnp.float32)
    query_pre = qkv[:, :own_features]
    key_pre = qkv[:, own_features : 2 * own_features]
    squares = jnp.stack([jnp.sum(query_pre * query_pre, -1), jnp.sum(key_pre * key_pre, -1)])
    cosine, sine_part = rotation(jnp.arange(row_len, dtype=jnp.int32), head_size)
    tables = jnp.concatenate([cosine, cosine], 1), jnp.concatenate([-sine_part, sine_part], 1)
    inverse = lax.rsqrt(total_seq(squares) / feature_count + eps)
    inverses = [inverse[at].reshape(row_count, row_len, 1) for at in range(2)]
    norm_gains = gain_query[None, :], gain_key[None, :]
    qkv_rows = qkv.reshape(row_count, row_len, 3 * own_features)
    *kept, mixed_low, log_total = attend(
        qkv_rows, inverses, tables, norm_gains, ids_all, head_size, scale
    )
    mixed_low = mixed_low.reshape(all_count, own_features)
    mixed_all = lax.all_gather(mixed_low, "seq", axis=1, tiled=True)
    attn_out = jnp.dot(mixed_all, wo_full, preferred_element_type=jnp.float32)
    attn_inv_all = inverse_rms(attn_out)
    hidden_all = tokens_all.astype(jnp.float32) + attn_out * attn_inv_all * gain_attn
    hidden_low = hidden_all.astype(low)
    attn_inv = own_piece(attn_inv_all)
    attn_unit = own_piece(attn_out) * attn_inv
    hidden_state = tokens.reshape(tok_count, model_width).astype(jnp.float32) + attn_unit * gain_attn

    gate_up = jnp.dot(hidden_low, w_hidden, preferred_element_type=jnp.float32)
    gate, up_proj = gate_up[:, :own_hidden], gate_up[:, own_hidden:]
    sigma = jax.nn.sigmoid(gate)
    active = gate * sigma
    inner_low = (active * up_proj).astype(low)
    branch_part = jnp.dot(inner_low, w_back, preferred_element_type=jnp.float32).astype(low)
    w_hidden_turned, branch_part = stored_turned(w_hidden, branch_part)
    w_back_turned, branch_part = stored_turned(w_back, branch_part)
    branch = (
        scatter_seq(branch_part.reshape(row_count, row_len, model_width))
        .astype(jnp.float32)
        .reshape(tok_count, model_width)
    )
    branch_inv = inverse_rms(branch)
    branch_unit = branch * branch_inv
    result = (
        (hidden_state + branch_unit * gain_ffn)
        .astype(low)
        .reshape(row_count, piece_len, model_width)
    )

    grad_out = cotangent.reshape(tok_count, model_width).astype(jnp.float32)
    ffn_gain_term = jnp.sum(grad_out * branch_unit, 0)
    d_branch = norm_back(grad_out * gain_ffn, branch_unit, branch_inv).astype(low)
    d_branch_all = gather_seq(d_branch.reshape(row_count, piece_len, model_width)).reshape(all_count, model_width)
    d_inner = jnp.dot(d_branch_all, w_back_turned, preferred_element_type=jnp.float32)
    d_gate = (d_inner * up_proj * sigma * (1.0 + gate * (1.0 - sigma))).astype(low)
    d_up = (d_inner * active).astype(low)
    d_gate_up = jnp.concatenate([d_gate, d_up], 1)
    d_hidden_part = jnp.dot(d_gate_up, w_hidden_turned, preferred_element_type=jnp.float32).astype(low)
    d_hidden_sum = scatter_seq(d_hidden_part.reshape(row_count, row_len, model_width))
    hidden_part = jnp.einsum("nd,nf->df", hidden_low, d_gate_up, preferred_element_type=jnp.float32).astype(low)
    down_part = jnp.einsum("nf,nd->fd", inner_low, d_branch_all, preferred_element_type=jnp.float32).astype(low)
    down_grad = sum_dp(*shares_for(down_part))
    hidden_own = sum_dp(*shares_for(hidden_part)).astype(low)
    d_hidden = grad_out + d_hidden_sum.astype(jnp.float32).reshape(tok_count, model_width)

    attn_gain_term = jnp.sum(d_hidden * attn_unit, 0)
    d_attn = norm_back(d_hidden * gain_attn, attn_unit, attn_inv).astype(low)
    d_mixed = jnp.einsum("nd,fd->nf", d_attn, wo_full, preferred_element_type=jnp.float32).astype(low)

    def own_columns_of_all(tensor):
        split = tensor.reshape(row_count, piece_len, seq_count, -1).transpose(2, 0, 1, 3)
        width = split.shape[-1]
        split = lax.all_to_all(split.reshape(seq_count, tok_count, width), "seq", split_axis=0, concat_axis=0)
        split = split.reshape(seq_count, row_count, piece_len, width).transpose(1, 0, 2, 3)
        return split.reshape(row_count, row_len, width)

    d_mixed = own_columns_of_all(d_mixed)
    d_mixed, d_attn = lax.optimization_barrier((d_mixed, d_attn))
    d_attn_own = own_columns_of_all(d_attn).reshape(all_count, -1)
    out_part = jnp.einsum("nf,nd->fd", mixed_all, d_attn_own, preferred_element_type=jnp.float32).astype(low)
    out_own = sum_dp(*shares_for(out_part)).astype(low)
    gate_grad, up_grad = rows_home(hidden_own, dp_count, own_hidden // dp_count)

    dq_gained, dk_gained, d_value, dots, gain_terms = attend_back(
        qkv_rows, inverses, tables, norm_gains, ids_all, (*kept, log_total), d_mixed, head_size, scale
    )
    norm_terms = lax.dynamic_update_slice_in_dim(
        jnp.zeros((2, feature_count), jnp.float32), jnp.sum(gain_terms, 0), seq_at * own_features, 1
    )
    dots = dots[:, :2].transpose(1, 0, 2).reshape(-1, LANES)
    stat_rows = dots.shape[0]
    sums = total_seq(
        jnp.concatenate(
            [dots]
            + [part.reshape(-1, LANES) for part in (norm_terms, attn_gain_term, ffn_gain_term)]
        )
    )
    means = sums[:stat_rows].reshape(2, all_count) / feature_count

    def norm_back_wide(gained, pre, at):
        inv = inverse[at][:, None]
        gained = gained.reshape(all_count, own_features)
        return (inv * (gained - pre * inv * means[at][:, None])).astype(low)

    dq_pre = norm_back_wide(dq_gained, query_pre, 0)
    dk_pre = norm_back_wide(dk_gained, key_pre, 1)
    d_value = d_value.reshape(all_count, own_features)
    d_qkv = jnp.concatenate([dq_pre, dk_pre, d_value], 1)
    d_tokens_part = jnp.einsum("nf,df->nd", d_qkv, w_qkv, preferred_element_type=jnp.float32).astype(low)
    d_qkv, d_tokens_part = lax.optimization_barrier((d_qkv, d_tokens_part))
    d_tokens_sum = scatter_seq(d_tokens_part.reshape(row_count, row_len, model_width))
    d_tokens = d_hidden + d_tokens_sum.astype(jnp.float32).reshape(tok_count, model_width)
    qkv_part = jnp.einsum("nd,nf->df", tokens_all, d_qkv, preferred_element_type=jnp.float32).astype(low)
    qkv_own = sum_dp(*shares_for(qkv_part)).astype(low)
    attn_home = rows_home(jnp.concatenate([qkv_own, out_own], 1), 1, own_features)
    share = feature_count // (dp_count * seq_count)
    gains = lax.dynamic_index_in_dim(
        sums[stat_rows:].reshape(4, dp_count, seq_count, share), seq_at, 2, False
    )
    gains = share_dp(gains.transpose(1, 0, 2).reshape(dp_count, 4 * share)).reshape(4, share)
    return (
        result,
        d_tokens.reshape(row_count, piece_len, model_width),
        attn_home[0],
        attn_home[1],
        attn_home[2],
        attn_home[3],
        gate_grad,
        up_grad,
        down_grad,
        gains[0],
        gains[1],
        gains[2],
        gains[3],
    )


def shards(tokens, doc_ids, cotangent, w_query, *rest):
    if w_query.shape[1] // HEAD % lax.axis_size("seq"):
        return shards_by_slab(tokens, doc_ids, cotangent, w_query, *rest)
    return shards_by_feature(tokens, doc_ids, cotangent, w_query, *rest)


def solution(mesh):
    return jax.shard_map(
        shards,
        mesh=mesh,
        in_specs=(
            P("dp", "seq", None),
            P("dp", "seq"),
            P("dp", "seq", None),
            P("dp", None),
            P("dp", None),
            P("dp", None),
            P("dp", None),
            P("dp", None),
            P("dp", None),
            P("dp", None),
            P(),
            P(),
            P(),
            P(),
        ),
        out_specs=(
            P("dp", "seq", None),
            P("dp", "seq", None),
            P(("dp", "seq"), None),
            P(("dp", "seq"), None),
            P(("dp", "seq"), None),
            P(("dp", "seq"), None),
            P(("dp", "seq"), None),
            P(("dp", "seq"), None),
            P(("dp", "seq"), None),
            P(("dp", "seq")),
            P(("dp", "seq")),
            P(("dp", "seq")),
            P(("dp", "seq")),
        ),
        check_vma=False,
    )
```

```python
import functools

import jax
import jax.numpy as jnp
from jax import lax
from jax.experimental import pallas as pl
from jax.experimental.layout import Layout, with_layout_constraint
from jax.experimental.pallas import tpu as pltpu
from jax.sharding import PartitionSpec as P


HEAD = 128
SLABS = 4
LANES = 128


eps = 1e-06
theta = 500000.0


def rotation(positions, head_size):
    half_size = head_size // 2
    frequency = theta ** (-(2.0 * jnp.arange(half_size, dtype=jnp.float32)) / head_size)
    angles = positions.astype(jnp.float32)[:, None] * frequency[None, :]
    return (jnp.cos(angles), jnp.sin(angles))


def rotate(tensor, cosine, sine_part):
    half_size = tensor.shape[-1] // 2
    first_half = tensor[..., :half_size]
    second_half = tensor[..., half_size:]
    cos_wide = cosine[:, None, :]
    sin_wide = sine_part[:, None, :]
    return jnp.concatenate(
        [
            first_half * cos_wide - second_half * sin_wide,
            second_half * cos_wide + first_half * sin_wide,
        ],
        -1,
    )


def unrotate(tensor, cosine, sine_part):
    half_size = tensor.shape[-1] // 2
    first_half = tensor[..., :half_size]
    second_half = tensor[..., half_size:]
    cos_wide = cosine[:, None, :]
    sin_wide = sine_part[:, None, :]
    return jnp.concatenate(
        [
            first_half * cos_wide + second_half * sin_wide,
            second_half * cos_wide - first_half * sin_wide,
        ],
        -1,
    )


def inverse_rms(tensor):
    return lax.rsqrt(jnp.mean(tensor * tensor, -1, keepdims=True) + eps)


def norm_back(grad_unit, unit_vec, inverse):
    return inverse * (grad_unit - unit_vec * jnp.mean(grad_unit * unit_vec, -1, keepdims=True))


def visible(own_ids, key_ids, query_at, key_at):
    causal = key_at[None, :] <= query_at[:, None]
    same_doc = own_ids[:, :, None] == key_ids[:, None, :]
    return (causal[None] & same_doc)[:, None]


def masked_scores(query_low, pair_all, allowed, head_count, head_size):
    row_count = pair_all.shape[0]
    row_length = pair_all.shape[1]
    feature_count = head_count * head_size
    key_rows = pair_all[..., :feature_count].reshape(row_count, row_length, head_count, head_size)
    value_rows = pair_all[..., feature_count:].reshape(row_count, row_length, head_count, head_size)
    scores = jnp.einsum(
        "rche,rlhe->rhcl", query_low, key_rows, preferred_element_type=jnp.float32
    ) * head_size ** (-0.5)
    return (jnp.where(allowed, scores, -1e30), key_rows, value_rows)


def columns_of(matrix, parts, slab_count, index):
    lead = matrix.shape[0]
    width = matrix.shape[1] // (parts * slab_count)
    return matrix.reshape(lead, parts, slab_count, width)[:, :, index].reshape(lead, parts * width)


def entries_of(vector, parts, slab_count, index):
    width = vector.shape[0] // (parts * slab_count)
    return vector.reshape(parts, slab_count, width)[:, index].reshape(parts * width)


def shards_by_slab(
    tokens,
    doc_ids,
    cotangent,
    w_query,
    w_key,
    w_value,
    w_out,
    w_gate,
    w_up,
    w_down,
    g_query,
    g_key,
    g_attn,
    g_ffn,
):
    row_count, piece_len, model_width = tokens.shape
    head_size = HEAD
    feature_count = w_query.shape[1]
    head_count = feature_count // head_size
    tok_count = row_count * piece_len
    scale = head_size ** (-0.5)
    seq_count = lax.axis_size("seq")
    parts = lax.axis_size("dp") * seq_count
    slab_count = SLABS
    gather_all = (
        lax.all_gather(w_query, "dp", axis=0, tiled=True),
        lax.all_gather(w_key, "dp", axis=0, tiled=True),
        lax.all_gather(w_value, "dp", axis=0, tiled=True),
        lax.all_gather(w_out, "dp", axis=0, tiled=True),
        lax.all_gather(w_gate, "dp", axis=0, tiled=True),
        lax.all_gather(w_up, "dp", axis=0, tiled=True),
        lax.all_gather(w_down, "dp", axis=0, tiled=True),
    )
    wq_full, wk_full, wv_full, wo_full, wg_full, wu_full, wd_full = gather_all
    gain_query = g_query.astype(jnp.float32)
    gain_key = g_key.astype(jnp.float32)
    gain_attn = g_attn.astype(jnp.float32)
    gain_ffn = g_ffn.astype(jnp.float32)
    flat_tokens = tokens.reshape(tok_count, model_width)
    query_pre = jnp.dot(flat_tokens, wq_full, preferred_element_type=jnp.float32)
    key_pre = jnp.dot(flat_tokens, wk_full, preferred_element_type=jnp.float32)
    value_pre = jnp.dot(flat_tokens, wv_full, preferred_element_type=jnp.float32)
    query_inv = inverse_rms(query_pre)
    query_unit = query_pre * query_inv
    key_inv = inverse_rms(key_pre)
    key_unit = key_pre * key_inv
    first_row = lax.axis_index("seq") * piece_len
    positions = first_row + jnp.tile(jnp.arange(piece_len, dtype=jnp.int32), row_count)
    cosine, sine_part = rotation(positions, head_size)
    query_rot = rotate(
        (query_unit * gain_query).reshape(tok_count, head_count, head_size), cosine, sine_part
    )
    key_rot = rotate(
        (key_unit * gain_key).reshape(tok_count, head_count, head_size), cosine, sine_part
    )
    query_low = query_rot.astype(jnp.bfloat16).reshape(row_count, piece_len, head_count, head_size)
    key_low = key_rot.astype(jnp.bfloat16).reshape(row_count, piece_len, feature_count)
    value_low = value_pre.astype(jnp.bfloat16).reshape(row_count, piece_len, feature_count)
    pair_low = jnp.concatenate([key_low, value_low], -1)
    ids_low = doc_ids.astype(jnp.bfloat16)
    pair_all, ids_all = (
        lax.all_gather(pair_low, "seq", axis=1, tiled=True),
        lax.all_gather(ids_low, "seq", axis=1, tiled=True),
    )
    query_at = first_row + jnp.arange(piece_len, dtype=jnp.int32)
    allowed = visible(ids_low, ids_all, query_at, jnp.arange(pair_all.shape[1], dtype=jnp.int32))
    masked, _, value_rows = masked_scores(
        query_low, pair_all, allowed, head_count, head_size
    )
    row_max = jnp.max(masked, -1, keepdims=True)
    log_total = jnp.log(jnp.sum(jnp.exp(masked - row_max), -1, keepdims=True)) + row_max
    probs_low = jnp.exp(masked - log_total).astype(jnp.bfloat16)
    mixed = jnp.einsum("rhcl,rlhe->rche", probs_low, value_rows, preferred_element_type=jnp.float32)
    mixed_low = mixed.reshape(tok_count, feature_count).astype(jnp.bfloat16)
    attn_out = jnp.dot(mixed_low, wo_full, preferred_element_type=jnp.float32)
    attn_inv = inverse_rms(attn_out)
    attn_unit = attn_out * attn_inv
    hidden_state = flat_tokens.astype(jnp.float32) + attn_unit * gain_attn
    hidden_low = hidden_state.astype(jnp.bfloat16)
    gate = jnp.dot(hidden_low, wg_full, preferred_element_type=jnp.float32)
    up_proj = jnp.dot(hidden_low, wu_full, preferred_element_type=jnp.float32)
    sigma = jax.nn.sigmoid(gate)
    active = gate * sigma
    inner_low = (active * up_proj).astype(jnp.bfloat16)
    branch = jnp.dot(inner_low, wd_full, preferred_element_type=jnp.float32)
    branch_inv = inverse_rms(branch)
    branch_unit = branch * branch_inv
    result = (
        (hidden_state + branch_unit * gain_ffn)
        .astype(jnp.bfloat16)
        .reshape(row_count, piece_len, model_width)
    )
    wq_back, wk_back, wv_back, wo_back, wg_back, wu_back, wd_back = gather_all
    pair_back, ids_back = (pair_all, ids_all)
    grad_out = cotangent.reshape(tok_count, model_width).astype(jnp.float32)
    ffn_gain_term = jnp.sum(grad_out * branch_unit, 0)
    d_branch = norm_back(grad_out * gain_ffn, branch_unit, branch_inv).astype(jnp.bfloat16)
    d_inner = jnp.einsum("nd,fd->nf", d_branch, wd_back, preferred_element_type=jnp.float32)
    d_gate = (d_inner * up_proj * sigma * (1.0 + gate * (1.0 - sigma))).astype(jnp.bfloat16)
    d_up = (d_inner * active).astype(jnp.bfloat16)
    d_hidden = grad_out + jnp.einsum(
        "nf,df->nd", d_gate, wg_back, preferred_element_type=jnp.float32
    )
    d_hidden = d_hidden + jnp.einsum("nf,df->nd", d_up, wu_back, preferred_element_type=jnp.float32)
    mlp_shares = []
    for index in range(slab_count):
        hidden_part = columns_of(hidden_low, parts, slab_count, index)
        inner_part = columns_of(inner_low, parts, slab_count, index)
        gate_term = jnp.einsum("nd,nf->df", hidden_part, d_gate, preferred_element_type=jnp.float32)
        up_term = jnp.einsum("nd,nf->df", hidden_part, d_up, preferred_element_type=jnp.float32)
        down_term = jnp.einsum(
            "nf,nd->fd", inner_part, d_branch, preferred_element_type=jnp.float32
        )
        ffn_term = entries_of(ffn_gain_term, parts, slab_count, index)
        shares = (
            lax.psum_scatter(down_term, ("dp", "seq"), scatter_dimension=0, tiled=True),
            lax.psum_scatter(gate_term, ("dp", "seq"), scatter_dimension=0, tiled=True),
            lax.psum_scatter(up_term, ("dp", "seq"), scatter_dimension=0, tiled=True),
            lax.psum_scatter(ffn_term, ("dp", "seq"), scatter_dimension=0, tiled=True),
        )
        mlp_shares.append(shares)
    down_grad = jnp.concatenate([s[0] for s in mlp_shares], 0)
    gate_grad = jnp.concatenate([s[1] for s in mlp_shares], 0)
    up_grad = jnp.concatenate([s[2] for s in mlp_shares], 0)
    ffn_grad = jnp.concatenate([s[3] for s in mlp_shares], 0)
    attn_gain_term = jnp.sum(d_hidden * attn_unit, 0)
    d_attn = norm_back(d_hidden * gain_attn, attn_unit, attn_inv).astype(jnp.bfloat16)
    d_mixed = jnp.einsum("nd,fd->nf", d_attn, wo_back, preferred_element_type=jnp.float32).astype(
        jnp.bfloat16
    )
    d_mixed = d_mixed.reshape(row_count, piece_len, head_count, head_size)
    sub_len = piece_len // slab_count
    pair_width = pair_back.shape[-1]
    pair_view = pair_back.reshape(row_count, seq_count, slab_count, sub_len, pair_width)
    ids_view = ids_back.reshape(row_count, seq_count, slab_count, sub_len)

    def slab_scores(index):
        pair_part = pair_view[:, :, index].reshape(row_count, seq_count * sub_len, pair_width)
        ids_part = ids_view[:, :, index].reshape(row_count, seq_count * sub_len)
        key_at = (
            jnp.arange(seq_count, dtype=jnp.int32)[:, None] * piece_len
            + index * sub_len
            + jnp.arange(sub_len, dtype=jnp.int32)[None, :]
        ).reshape(seq_count * sub_len)
        allowed_part = visible(ids_low, ids_part, query_at, key_at)
        masked_part, key_part, value_part = masked_scores(
            query_low, pair_part, allowed_part, head_count, head_size
        )
        probs_part = jnp.exp(masked_part - log_total)
        d_probs_part = jnp.einsum(
            "rche,rlhe->rhcl", d_mixed, value_part, preferred_element_type=jnp.float32
        )
        return (probs_part, d_probs_part, key_part)

    row_dot = jnp.zeros((row_count, head_count, piece_len, 1), jnp.float32)
    for index in range(slab_count):
        probs_part, d_probs_part, key_part = slab_scores(index)
        row_dot = row_dot + jnp.sum(probs_part * d_probs_part, -1, keepdims=True)
    query_acc = jnp.zeros((row_count, piece_len, head_count, head_size), jnp.float32)
    pair_shares = []
    for index in range(slab_count):
        probs_part, d_probs_part, key_part = slab_scores(index)
        d_scores = (probs_part * (d_probs_part - row_dot)).astype(jnp.bfloat16)
        query_acc = query_acc + jnp.einsum(
            "rhcl,rlhe->rche", d_scores, key_part, preferred_element_type=jnp.float32
        )
        key_term = (
            jnp.einsum("rhcl,rche->rlhe", d_scores, query_low, preferred_element_type=jnp.float32)
            * scale
        )
        value_term = jnp.einsum(
            "rhcl,rche->rlhe",
            probs_part.astype(jnp.bfloat16),
            d_mixed,
            preferred_element_type=jnp.float32,
        )
        key_count = seq_count * sub_len
        pair_term = jnp.concatenate(
            [
                key_term.reshape(row_count, key_count, feature_count),
                value_term.reshape(row_count, key_count, feature_count),
            ],
            -1,
        )
        pair_shares.append(
            lax.psum_scatter(
                pair_term.astype(jnp.bfloat16), "seq", scatter_dimension=1, tiled=True
            ).astype(jnp.float32)
        )
    pair_grad = jnp.concatenate(pair_shares, 1)
    d_query = (query_acc * scale).astype(jnp.bfloat16)
    d_key = (
        pair_grad[..., :feature_count]
        .astype(jnp.bfloat16)
        .reshape(tok_count, head_count, head_size)
    )
    d_value = pair_grad[..., feature_count:].astype(jnp.bfloat16).reshape(tok_count, feature_count)
    dq_norm = unrotate(
        d_query.reshape(tok_count, head_count, head_size).astype(jnp.float32), cosine, sine_part
    ).reshape(tok_count, feature_count)
    dk_norm = unrotate(d_key.astype(jnp.float32), cosine, sine_part).reshape(
        tok_count, feature_count
    )
    query_gain_term = jnp.sum(dq_norm * query_unit, 0)
    key_gain_term = jnp.sum(dk_norm * key_unit, 0)
    dq_pre = norm_back(dq_norm * gain_query, query_unit, query_inv).astype(jnp.bfloat16)
    dk_pre = norm_back(dk_norm * gain_key, key_unit, key_inv).astype(jnp.bfloat16)
    d_tokens = d_hidden + jnp.einsum(
        "nf,df->nd", dq_pre, wq_back, preferred_element_type=jnp.float32
    )
    d_tokens = d_tokens + jnp.einsum(
        "nf,df->nd", dk_pre, wk_back, preferred_element_type=jnp.float32
    )
    d_tokens = d_tokens + jnp.einsum(
        "nf,df->nd", d_value, wv_back, preferred_element_type=jnp.float32
    )
    attn_shares = []
    for index in range(slab_count):
        token_part = columns_of(flat_tokens, parts, slab_count, index)
        mixed_part = columns_of(mixed_low, parts, slab_count, index)
        query_term = jnp.einsum("nd,nf->df", token_part, dq_pre, preferred_element_type=jnp.float32)
        key_wterm = jnp.einsum("nd,nf->df", token_part, dk_pre, preferred_element_type=jnp.float32)
        value_wterm = jnp.einsum(
            "nd,nf->df", token_part, d_value, preferred_element_type=jnp.float32
        )
        out_term = jnp.einsum("nf,nd->fd", mixed_part, d_attn, preferred_element_type=jnp.float32)
        gq_term = entries_of(query_gain_term, parts, slab_count, index)
        gk_term = entries_of(key_gain_term, parts, slab_count, index)
        ga_term = entries_of(attn_gain_term, parts, slab_count, index)
        shares = (
            lax.psum_scatter(query_term, ("dp", "seq"), scatter_dimension=0, tiled=True),
            lax.psum_scatter(key_wterm, ("dp", "seq"), scatter_dimension=0, tiled=True),
            lax.psum_scatter(value_wterm, ("dp", "seq"), scatter_dimension=0, tiled=True),
            lax.psum_scatter(out_term, ("dp", "seq"), scatter_dimension=0, tiled=True),
            lax.psum_scatter(gq_term, ("dp", "seq"), scatter_dimension=0, tiled=True),
            lax.psum_scatter(gk_term, ("dp", "seq"), scatter_dimension=0, tiled=True),
            lax.psum_scatter(ga_term, ("dp", "seq"), scatter_dimension=0, tiled=True),
        )
        attn_shares.append(shares)
    query_grad = jnp.concatenate([s[0] for s in attn_shares], 0)
    key_grad = jnp.concatenate([s[1] for s in attn_shares], 0)
    value_grad = jnp.concatenate([s[2] for s in attn_shares], 0)
    out_grad = jnp.concatenate([s[3] for s in attn_shares], 0)
    gq_grad = jnp.concatenate([s[4] for s in attn_shares], 0)
    gk_grad = jnp.concatenate([s[5] for s in attn_shares], 0)
    ga_grad = jnp.concatenate([s[6] for s in attn_shares], 0)
    tokens_grad = d_tokens.reshape(row_count, piece_len, model_width)
    return (
        result,
        tokens_grad,
        query_grad,
        key_grad,
        value_grad,
        out_grad,
        gate_grad,
        up_grad,
        down_grad,
        gq_grad,
        gk_grad,
        ga_grad,
        ffn_grad,
    )


def own_columns(matrix, groups, parts, index):
    width = matrix.shape[1] // (groups * parts)
    pieces = [
        lax.dynamic_slice_in_dim(matrix, (group * parts + index) * width, width, 1)
        for group in range(groups)
    ]
    return jnp.concatenate(pieces, 1) if groups > 1 else pieces[0]


def gather_seq(piece):
    return lax.all_gather(piece, "seq", axis=1, tiled=True)


def scatter_seq(partial):
    return lax.psum_scatter(partial, "seq", scatter_dimension=1, tiled=True)


def swap(value, axis, flip):
    return lax.ppermute(value, axis, [(at, at ^ flip) for at in range(lax.axis_size(axis))])


def place_kernel(spots_ref, *refs, count):
    in_refs, (out_ref, sems) = refs[:count], refs[-2:]
    copies = []
    for at, in_ref in enumerate(in_refs):
        rows, width = in_ref.shape
        row = pl.multiple_of(spots_ref[2 * at], LANES)
        column = pl.multiple_of(spots_ref[2 * at + 1], LANES)
        copies.append(
            pltpu.make_async_copy(
                in_ref, out_ref.at[pl.ds(row, rows), pl.ds(column, width)], sems.at[at]
            )
        )
    for copy in copies:
        copy.start()
    for copy in copies:
        copy.wait()


def placed(pieces, shape, whole=None):
    spots = jnp.stack([jnp.int32(at) for _, row, column in pieces for at in (row, column)])
    outside = pl.BlockSpec(memory_space=pl.ANY)
    given = [] if whole is None else [whole]
    return pl.pallas_call(
        functools.partial(place_kernel, count=len(pieces)),
        grid_spec=pltpu.PrefetchScalarGridSpec(
            num_scalar_prefetch=1,
            grid=(1,),
            in_specs=[
                pl.BlockSpec(piece.shape, lambda at, spots: (0, 0), pipeline_mode=pl.Buffered(1))
                for piece, _, _ in pieces
            ]
            + [outside] * len(given),
            out_specs=outside,
            scratch_shapes=[pltpu.SemaphoreType.DMA((len(pieces),))],
        ),
        out_shape=jax.ShapeDtypeStruct(shape, pieces[0][0].dtype),
        input_output_aliases={1 + len(pieces): 0} if given else {},
        name="place",
    )(spots, *[piece for piece, _, _ in pieces], *given)


def pieces_for(value, name, split_axis):
    count, index = lax.axis_size(name), lax.axis_index(name)
    width = value.shape[split_axis] // count
    return [
        lax.dynamic_slice_in_dim(value, (index ^ flip) * width, width, split_axis)
        for flip in range(count)
    ]


def swapped(pieces, name):
    return [swap(piece, name, flip) if flip else piece for flip, piece in enumerate(pieces)]


def exchanged(value, name, split_axis):
    return swapped(pieces_for(value, name, split_axis), name)


def pieces_dp(piece):
    half = piece.shape[0] // 2
    first, second = swap(piece, "dp", 1), swap(piece, "dp", 2)
    top, bottom = swap(first[:half], "dp", 2), swap(second[half:], "dp", 1)
    index = lax.axis_index("dp")
    width = piece.shape[0]
    far = (index ^ 3) * width
    return [
        (first, (index ^ 1) * width),
        (second, (index ^ 2) * width),
        (top, far),
        (bottom, far + half),
    ]


def gather_dp(piece):
    rows, width = piece.shape
    pieces = [(piece, lax.axis_index("dp") * rows), *pieces_dp(piece)]
    pieces = [(part, row, 0) for part, row in pieces]
    whole = placed(pieces[:3], (4 * rows, width))
    return placed(pieces[3:], (4 * rows, width), whole)


def sum_dp(sent, kept):
    got = swap(sent[0], "dp", 1), swap(sent[1], "dp", 2)
    wide = [(kept[at].astype(jnp.float32) + got[at].astype(jnp.float32)) for at in range(2)]
    onward = [side[1].astype(jnp.bfloat16) for side in wide]
    last = swap(onward[0], "dp", 2), swap(onward[1], "dp", 1)
    return jnp.concatenate(
        [wide[at][0] + last[at].astype(jnp.float32) for at in range(2)], 0
    )


def shares_for(partial):
    index = lax.axis_index("dp")
    width = partial.shape[0] // 4
    half = width // 2

    def part(flip, side):
        return lax.dynamic_slice_in_dim(partial, (index ^ flip) * width + side * half, half, 0)

    sent = [jnp.stack([part(1, 0), part(3, 0)]), jnp.stack([part(2, 1), part(3, 1)])]
    kept = [jnp.stack([part(0, 0), part(2, 0)]), jnp.stack([part(0, 1), part(1, 1)])]
    return sent, kept


def stored_turned(matrix, after):
    matrix, after = lax.optimization_barrier((matrix, after))
    return with_layout_constraint(matrix.T, Layout((0, 1))), after


def total_seq(value):
    shape = value.shape
    value = value.reshape(-1, LANES)
    flip = 1
    while flip < lax.axis_size("seq"):
        value = value + swap(value, "seq", flip)
        flip *= 2
    return value.reshape(shape)


def share_dp(rows):
    flip = lax.axis_size("dp") // 2
    while flip:
        halves = rows.reshape(2, rows.shape[0] // 2, rows.shape[1])
        side = lax.axis_index("dp") // flip % 2
        kept = lax.dynamic_index_in_dim(halves, side, 0, False)
        sent = lax.dynamic_index_in_dim(halves, 1 - side, 0, False)
        rows = kept + swap(sent, "dp", flip)
        flip //= 2
    return rows[0]


def settle_kernel(index_ref, *refs, groups, width, count):
    in_refs, out_refs = refs[:count], refs[count:]
    for flip, in_ref in enumerate(in_refs):
        source = index_ref[0] ^ flip
        for at, out_ref in enumerate(out_refs):
            for group in range(groups):
                column = (at * groups + group) * width
                place = pl.multiple_of((group * count + source) * width, width)
                out_ref[:, pl.ds(place, width)] = in_ref[:, column : column + width].astype(jnp.float32)


def rows_home(summed, groups, width):
    pieces = exchanged(summed, "seq", 0)
    count = len(pieces)
    rows, total = pieces[0].shape
    outs = total // (groups * width)
    step = min(16, rows)
    wide = count * groups * width
    return pl.pallas_call(
        functools.partial(settle_kernel, groups=groups, width=width, count=count),
        grid_spec=pltpu.PrefetchScalarGridSpec(
            num_scalar_prefetch=1,
            grid=(rows // step,),
            in_specs=[pl.BlockSpec((step, total), lambda r, index: (r, 0))] * count,
            out_specs=[pl.BlockSpec((step, wide), lambda r, index: (r, 0))] * outs,
        ),
        out_shape=[jax.ShapeDtypeStruct((rows, wide), jnp.float32)] * outs,
        name="settle",
    )(lax.axis_index("seq").reshape(1), *pieces)


QUERY_BLOCK = 256


def attention_masks(ids_col, ids_row, block, width, start):
    rows = start + lax.broadcasted_iota(jnp.int32, (block, width), 0)
    columns = lax.broadcasted_iota(jnp.int32, (block, width), 1)
    return (columns <= rows) & (ids_col[start : start + block] == ids_row[:, :width])


def attend_kernel(
    q_ref, k_ref, v_ref, qinv_ref, kinv_ref, cos_ref, sin_ref, gq_ref, gk_ref, col_ref, row_ref,
    qlow_ref, klow_ref, vlow_ref, mixed_ref, total_ref, *, scale
):
    low = jnp.bfloat16
    half = q_ref.shape[-1] // 2
    cosine, sine_part = cos_ref[...], sin_ref[...]

    def rotated(ref, inv_ref, gain_ref):
        value = ref[0] * inv_ref[0] * gain_ref[...]
        return (value * cosine + pltpu.roll(value, half, 1) * sine_part).astype(low)

    qlow_ref[0] = rotated(q_ref, qinv_ref, gq_ref)
    klow_ref[0] = rotated(k_ref, kinv_ref, gk_ref)
    vlow_ref[0] = v_ref[0].astype(low)
    length = q_ref.shape[1]
    block = min(QUERY_BLOCK, length)
    ids_col, ids_row = col_ref[0], row_ref[0]
    for start in range(0, length, block):
        width = start + block
        scores = lax.dot_general(
            qlow_ref[0, start:width], klow_ref[0, :width], (((1,), (1,)), ((), ())),
            preferred_element_type=jnp.float32,
        ) * scale
        allowed = attention_masks(ids_col, ids_row, block, width, start)
        masked = jnp.where(allowed, scores, -1e30)
        row_max = jnp.max(masked, -1, keepdims=True)
        log_total = jnp.log(jnp.sum(jnp.exp(masked - row_max), -1, keepdims=True)) + row_max
        total_ref[0, 0, start:width] = log_total
        probs = jnp.exp(masked - log_total).astype(low)
        mixed_ref[0, start:width] = jnp.dot(
            probs, vlow_ref[0, :width], preferred_element_type=jnp.float32
        ).astype(low)


def attend_back_kernel(
    q_ref, k_ref, qinv_ref, kinv_ref, cos_ref, sin_ref, gq_ref, gk_ref, col_ref, row_ref,
    qlow_ref, klow_ref, vlow_ref, total_ref, dmixed_ref,
    dq_ref, dk_ref, dv_ref, dots_ref, gains_ref, key_acc, value_acc, query_acc, *, scale
):
    low = jnp.bfloat16
    half = q_ref.shape[-1] // 2
    length = q_ref.shape[1]
    block = min(QUERY_BLOCK, length)
    ids_col, ids_row = col_ref[0], row_ref[0]
    turned = (((0,), (0,)), ((), ()))
    across = (((1,), (1,)), ((), ()))
    key_acc[...] = jnp.zeros_like(key_acc)
    value_acc[...] = jnp.zeros_like(value_acc)
    for start in range(0, length, block):
        width = start + block
        query = qlow_ref[0, start:width]
        d_mixed = dmixed_ref[0, start:width]
        keys = klow_ref[0, :width]
        scores = lax.dot_general(query, keys, across, preferred_element_type=jnp.float32) * scale
        allowed = attention_masks(ids_col, ids_row, block, width, start)
        probs = jnp.exp(jnp.where(allowed, scores, -1e30) - total_ref[0, 0, start:width])
        d_probs = lax.dot_general(
            d_mixed, vlow_ref[0, :width], across, preferred_element_type=jnp.float32
        )
        row_dot = jnp.sum(probs * d_probs, -1, keepdims=True)
        d_scores = (probs * (d_probs - row_dot)).astype(low)
        query_acc[start:width] = jnp.dot(d_scores, keys, preferred_element_type=jnp.float32)
        key_acc[:width] += lax.dot_general(d_scores, query, turned, preferred_element_type=jnp.float32)
        value_acc[:width] += lax.dot_general(
            probs.astype(low), d_mixed, turned, preferred_element_type=jnp.float32
        )
    dv_ref[0] = value_acc[...].astype(low)
    cosine, sine_part = cos_ref[...], sin_ref[...]

    def turned_back(acc, ref, inv_ref, gain_ref, out_ref, at):
        value = (acc[...] * scale).astype(low).astype(jnp.float32)
        value = value * cosine - pltpu.roll(value, half, 1) * sine_part
        unit = ref[0] * inv_ref[0]
        gains_ref[0, at : at + 1] = jnp.sum(value * unit, 0, keepdims=True)
        value = value * gain_ref[...]
        out_ref[0] = value
        return jnp.sum(value * unit, -1, keepdims=True)

    query_dot = turned_back(query_acc, q_ref, qinv_ref, gq_ref, dq_ref, 0)
    key_dot = turned_back(key_acc, k_ref, kinv_ref, gk_ref, dk_ref, 1)
    lane = lax.broadcasted_iota(jnp.int32, (length, LANES), 1)
    dots = jnp.where(lane == 0, query_dot, jnp.where(lane == 1, key_dot, 0.0)).T[:8]

    @pl.when(pl.program_id(1) == 0)
    def _():
        dots_ref[0] = dots

    @pl.when(pl.program_id(1) != 0)
    def _():
        dots_ref[0] += dots


def attention_specs(length, heads, head_size):
    wide = lambda at: pl.BlockSpec((1, length, head_size), lambda r, h, at=at: (r, 0, at * heads + h))
    thin = pl.BlockSpec((1, length, 1), lambda r, h: (r, 0, 0))
    table = pl.BlockSpec((length, head_size), lambda r, h: (0, 0))
    gain = pl.BlockSpec((1, head_size), lambda r, h: (0, h))
    flat = pl.BlockSpec((1, 1, length), lambda r, h: (r, 0, 0))
    total = pl.BlockSpec((1, 1, length, 1), lambda r, h: (r, h, 0, 0))
    return wide, thin, table, gain, flat, total


def attend(qkv, inverses, tables, gains, ids, head_size, scale):
    rows, length, width = qkv.shape
    heads = width // (3 * head_size)
    wide, thin, table, gain, flat, total = attention_specs(length, heads, head_size)
    narrow = jax.ShapeDtypeStruct((rows, length, heads * head_size), jnp.bfloat16)
    return pl.pallas_call(
        functools.partial(attend_kernel, scale=scale),
        grid=(rows, heads),
        in_specs=[wide(0), wide(1), wide(2), thin, thin, table, table, gain, gain, thin, flat],
        out_specs=[wide(0), wide(0), wide(0), wide(0), total],
        out_shape=[narrow] * 4 + [jax.ShapeDtypeStruct((rows, heads, length, 1), jnp.float32)],
        name="attend",
    )(qkv, qkv, qkv, *inverses, *tables, *gains, ids[:, :, None], ids[:, None, :])


def attend_back(qkv, inverses, tables, gains, ids, kept, d_mixed, head_size, scale):
    rows, length, width = qkv.shape
    heads = width // (3 * head_size)
    wide, thin, table, gain, flat, total = attention_specs(length, heads, head_size)
    shape = (rows, length, heads * head_size)
    return pl.pallas_call(
        functools.partial(attend_back_kernel, scale=scale),
        grid=(rows, heads),
        in_specs=[wide(0), wide(1), thin, thin, table, table, gain, gain, thin, flat]
        + [wide(0), wide(0), wide(0), total, wide(0)],
        out_specs=[
            wide(0),
            wide(0),
            wide(0),
            pl.BlockSpec((1, 8, length), lambda r, h: (r, 0, 0)),
            pl.BlockSpec((1, 2, head_size), lambda r, h: (r, 0, h)),
        ],
        out_shape=[
            jax.ShapeDtypeStruct(shape, jnp.float32),
            jax.ShapeDtypeStruct(shape, jnp.float32),
            jax.ShapeDtypeStruct(shape, jnp.bfloat16),
            jax.ShapeDtypeStruct((rows, 8, length), jnp.float32),
            jax.ShapeDtypeStruct((rows, 2, heads * head_size), jnp.float32),
        ],
        scratch_shapes=[pltpu.VMEM((length, head_size), jnp.float32)] * 3,
        name="attend_back",
    )(qkv, qkv, *inverses, *tables, *gains, ids[:, :, None], ids[:, None, :], *kept, d_mixed)


def shards_by_feature(
    tokens,
    doc_ids,
    cotangent,
    w_query,
    w_key,
    w_value,
    w_out,
    w_gate,
    w_up,
    w_down,
    g_query,
    g_key,
    g_attn,
    g_ffn,
):
    row_count, piece_len, model_width = tokens.shape
    head_size = HEAD
    feature_count = w_query.shape[1]
    scale = head_size ** (-0.5)
    seq_count = lax.axis_size("seq")
    dp_count = lax.axis_size("dp")
    seq_at = lax.axis_index("seq")
    row_len = piece_len * seq_count
    all_count = row_count * row_len
    tok_count = row_count * piece_len
    own_features = feature_count // seq_count
    own_hidden = w_gate.shape[1] // seq_count
    low = jnp.bfloat16

    def own_piece(tensor):
        view = tensor.reshape(row_count, row_len, -1)
        return lax.dynamic_slice_in_dim(view, seq_at * piece_len, piece_len, 1).reshape(tok_count, -1)

    w_qkv = gather_dp(jnp.concatenate([own_columns(w, 1, seq_count, seq_at) for w in (w_query, w_key, w_value)], 1))
    tokens_all = gather_seq(tokens).reshape(all_count, model_width)
    ids_all = total_seq(
        lax.dynamic_update_slice_in_dim(
            jnp.zeros((row_count, row_len), jnp.int32), doc_ids, seq_at * piece_len, 1
        )
    )
    core = seq_at % 2
    half = model_width // 2
    out_rows = w_out.shape[0]
    out_pieces = pieces_dp(lax.dynamic_slice_in_dim(w_out, core * half, half, 1))
    other_pieces = [(swap(piece, "seq", 1), row) for piece, row in out_pieces]
    wo_full = placed(
        [(w_out, lax.axis_index("dp") * out_rows, 0)]
        + [(piece, row, core * half) for piece, row in out_pieces]
        + [(piece, row, half - core * half) for piece, row in other_pieces],
        (feature_count, model_width),
    )
    w_hidden = gather_dp(jnp.concatenate([own_columns(w, dp_count, seq_count, seq_at) for w in (w_gate, w_up)], 1))
    w_back = gather_dp(
        lax.dynamic_slice_in_dim(
            w_down, seq_at * (own_hidden // dp_count), own_hidden // dp_count, 0
        ),
    )
    gain_query = lax.dynamic_slice_in_dim(g_query, seq_at * own_features, own_features).astype(jnp.float32)
    gain_key = lax.dynamic_slice_in_dim(g_key, seq_at * own_features, own_features).astype(jnp.float32)
    gain_attn = g_attn.astype(jnp.float32)
    gain_ffn = g_ffn.astype(jnp.float32)

    tokens_all, ids_all = lax.optimization_barrier((tokens_all, ids_all))
    qkv = jnp.dot(tokens_all, w_qkv, preferred_element_type=jnp.float32)
    query_pre = qkv[:, :own_features]
    key_pre = qkv[:, own_features : 2 * own_features]
    squares = jnp.stack([jnp.sum(query_pre * query_pre, -1), jnp.sum(key_pre * key_pre, -1)])
    cosine, sine_part = rotation(jnp.arange(row_len, dtype=jnp.int32), head_size)
    tables = jnp.concatenate([cosine, cosine], 1), jnp.concatenate([-sine_part, sine_part], 1)
    inverse = lax.rsqrt(total_seq(squares) / feature_count + eps)
    inverses = [inverse[at].reshape(row_count, row_len, 1) for at in range(2)]
    norm_gains = gain_query[None, :], gain_key[None, :]
    qkv_rows = qkv.reshape(row_count, row_len, 3 * own_features)
    *kept, mixed_low, log_total = attend(
        qkv_rows, inverses, tables, norm_gains, ids_all, head_size, scale
    )
    mixed_low = mixed_low.reshape(all_count, own_features)
    mixed_all = lax.all_gather(mixed_low, "seq", axis=1, tiled=True)
    attn_out = jnp.dot(mixed_all, wo_full, preferred_element_type=jnp.float32)
    attn_inv_all = inverse_rms(attn_out)
    hidden_all = tokens_all.astype(jnp.float32) + attn_out * attn_inv_all * gain_attn
    hidden_low = hidden_all.astype(low)
    attn_inv = own_piece(attn_inv_all)
    attn_unit = own_piece(attn_out) * attn_inv
    hidden_state = tokens.reshape(tok_count, model_width).astype(jnp.float32) + attn_unit * gain_attn

    gate_up = jnp.dot(hidden_low, w_hidden, preferred_element_type=jnp.float32)
    gate, up_proj = gate_up[:, :own_hidden], gate_up[:, own_hidden:]
    sigma = jax.nn.sigmoid(gate)
    active = gate * sigma
    inner_low = (active * up_proj).astype(low)
    branch_part = jnp.dot(inner_low, w_back, preferred_element_type=jnp.float32).astype(low)
    w_hidden_turned, branch_part = stored_turned(w_hidden, branch_part)
    w_back_turned, branch_part = stored_turned(w_back, branch_part)
    branch = (
        scatter_seq(branch_part.reshape(row_count, row_len, model_width))
        .astype(jnp.float32)
        .reshape(tok_count, model_width)
    )
    branch_inv = inverse_rms(branch)
    branch_unit = branch * branch_inv
    result = (
        (hidden_state + branch_unit * gain_ffn)
        .astype(low)
        .reshape(row_count, piece_len, model_width)
    )

    grad_out = cotangent.reshape(tok_count, model_width).astype(jnp.float32)
    ffn_gain_term = jnp.sum(grad_out * branch_unit, 0)
    d_branch = norm_back(grad_out * gain_ffn, branch_unit, branch_inv).astype(low)
    d_branch_all = gather_seq(d_branch.reshape(row_count, piece_len, model_width)).reshape(all_count, model_width)
    d_inner = jnp.dot(d_branch_all, w_back_turned, preferred_element_type=jnp.float32)
    d_gate = (d_inner * up_proj * sigma * (1.0 + gate * (1.0 - sigma))).astype(low)
    d_up = (d_inner * active).astype(low)
    d_gate_up = jnp.concatenate([d_gate, d_up], 1)
    d_hidden_part = jnp.dot(d_gate_up, w_hidden_turned, preferred_element_type=jnp.float32).astype(low)
    d_hidden_sum = scatter_seq(d_hidden_part.reshape(row_count, row_len, model_width))
    hidden_part = jnp.einsum("nd,nf->df", hidden_low, d_gate_up, preferred_element_type=jnp.float32).astype(low)
    down_part = jnp.einsum("nf,nd->fd", inner_low, d_branch_all, preferred_element_type=jnp.float32).astype(low)
    down_grad = sum_dp(*shares_for(down_part))
    hidden_own = sum_dp(*shares_for(hidden_part)).astype(low)
    d_hidden = grad_out + d_hidden_sum.astype(jnp.float32).reshape(tok_count, model_width)

    attn_gain_term = jnp.sum(d_hidden * attn_unit, 0)
    d_attn = norm_back(d_hidden * gain_attn, attn_unit, attn_inv).astype(low)
    d_mixed = jnp.einsum("nd,fd->nf", d_attn, wo_full, preferred_element_type=jnp.float32).astype(low)

    def own_columns_of_all(tensor):
        split = tensor.reshape(row_count, piece_len, seq_count, -1).transpose(2, 0, 1, 3)
        width = split.shape[-1]
        split = lax.all_to_all(split.reshape(seq_count, tok_count, width), "seq", split_axis=0, concat_axis=0)
        split = split.reshape(seq_count, row_count, piece_len, width).transpose(1, 0, 2, 3)
        return split.reshape(row_count, row_len, width)

    d_mixed = own_columns_of_all(d_mixed)
    d_mixed, d_attn = lax.optimization_barrier((d_mixed, d_attn))
    d_attn_own = own_columns_of_all(d_attn).reshape(all_count, -1)
    out_part = jnp.einsum("nf,nd->fd", mixed_all, d_attn_own, preferred_element_type=jnp.float32).astype(low)
    out_own = sum_dp(*shares_for(out_part)).astype(low)
    gate_grad, up_grad = rows_home(hidden_own, dp_count, own_hidden // dp_count)

    dq_gained, dk_gained, d_value, dots, gain_terms = attend_back(
        qkv_rows, inverses, tables, norm_gains, ids_all, (*kept, log_total), d_mixed, head_size, scale
    )
    norm_terms = lax.dynamic_update_slice_in_dim(
        jnp.zeros((2, feature_count), jnp.float32), jnp.sum(gain_terms, 0), seq_at * own_features, 1
    )
    dots = dots[:, :2].transpose(1, 0, 2).reshape(-1, LANES)
    stat_rows = dots.shape[0]
    sums = total_seq(
        jnp.concatenate(
            [dots]
            + [part.reshape(-1, LANES) for part in (norm_terms, attn_gain_term, ffn_gain_term)]
        )
    )
    means = sums[:stat_rows].reshape(2, all_count) / feature_count

    def norm_back_wide(gained, pre, at):
        inv = inverse[at][:, None]
        gained = gained.reshape(all_count, own_features)
        return (inv * (gained - pre * inv * means[at][:, None])).astype(low)

    dq_pre = norm_back_wide(dq_gained, query_pre, 0)
    dk_pre = norm_back_wide(dk_gained, key_pre, 1)
    d_value = d_value.reshape(all_count, own_features)
    d_qkv = jnp.concatenate([dq_pre, dk_pre, d_value], 1)
    d_tokens_part = jnp.einsum("nf,df->nd", d_qkv, w_qkv, preferred_element_type=jnp.float32).astype(low)
    d_qkv, d_tokens_part = lax.optimization_barrier((d_qkv, d_tokens_part))
    d_tokens_sum = scatter_seq(d_tokens_part.reshape(row_count, row_len, model_width))
    d_tokens = d_hidden + d_tokens_sum.astype(jnp.float32).reshape(tok_count, model_width)
    qkv_part = jnp.einsum("nd,nf->df", tokens_all, d_qkv, preferred_element_type=jnp.float32).astype(low)
    qkv_own = sum_dp(*shares_for(qkv_part)).astype(low)
    attn_home = rows_home(jnp.concatenate([qkv_own, out_own], 1), 1, own_features)
    share = feature_count // (dp_count * seq_count)
    gains = lax.dynamic_index_in_dim(
        sums[stat_rows:].reshape(4, dp_count, seq_count, share), seq_at, 2, False
    )
    gains = share_dp(gains.transpose(1, 0, 2).reshape(dp_count, 4 * share)).reshape(4, share)
    return (
        result,
        d_tokens.reshape(row_count, piece_len, model_width),
        attn_home[0],
        attn_home[1],
        attn_home[2],
        attn_home[3],
        gate_grad,
        up_grad,
        down_grad,
        gains[0],
        gains[1],
        gains[2],
        gains[3],
    )


def shards(tokens, doc_ids, cotangent, w_query, *rest):
    if w_query.shape[1] // HEAD % lax.axis_size("seq"):
        return shards_by_slab(tokens, doc_ids, cotangent, w_query, *rest)
    return shards_by_feature(tokens, doc_ids, cotangent, w_query, *rest)


def solution(mesh):
    return jax.shard_map(
        shards,
        mesh=mesh,
        in_specs=(
            P("dp", "seq", None),
            P("dp", "seq"),
            P("dp", "seq", None),
            P("dp", None),
            P("dp", None),
            P("dp", None),
            P("dp", None),
            P("dp", None),
            P("dp", None),
            P("dp", None),
            P(),
            P(),
            P(),
            P(),
        ),
        out_specs=(
            P("dp", "seq", None),
            P("dp", "seq", None),
            P(("dp", "seq"), None),
            P(("dp", "seq"), None),
            P(("dp", "seq"), None),
            P(("dp", "seq"), None),
            P(("dp", "seq"), None),
            P(("dp", "seq"), None),
            P(("dp", "seq"), None),
            P(("dp", "seq")),
            P(("dp", "seq")),
            P(("dp", "seq")),
            P(("dp", "seq")),
        ),
        check_vma=False,
    )
```

```python
import functools

import jax
import jax.numpy as jnp
from jax import lax
from jax.experimental import pallas as pl
from jax.experimental.layout import Layout, with_layout_constraint
from jax.experimental.pallas import tpu as pltpu
from jax.sharding import PartitionSpec as P


HEAD = 128
SLABS = 4
LANES = 128


eps = 1e-06
theta = 500000.0


def rotation(positions, head_size):
    half_size = head_size // 2
    frequency = theta ** (-(2.0 * jnp.arange(half_size, dtype=jnp.float32)) / head_size)
    angles = positions.astype(jnp.float32)[:, None] * frequency[None, :]
    return (jnp.cos(angles), jnp.sin(angles))


def rotate(tensor, cosine, sine_part):
    half_size = tensor.shape[-1] // 2
    first_half = tensor[..., :half_size]
    second_half = tensor[..., half_size:]
    cos_wide = cosine[:, None, :]
    sin_wide = sine_part[:, None, :]
    return jnp.concatenate(
        [
            first_half * cos_wide - second_half * sin_wide,
            second_half * cos_wide + first_half * sin_wide,
        ],
        -1,
    )


def unrotate(tensor, cosine, sine_part):
    half_size = tensor.shape[-1] // 2
    first_half = tensor[..., :half_size]
    second_half = tensor[..., half_size:]
    cos_wide = cosine[:, None, :]
    sin_wide = sine_part[:, None, :]
    return jnp.concatenate(
        [
            first_half * cos_wide + second_half * sin_wide,
            second_half * cos_wide - first_half * sin_wide,
        ],
        -1,
    )


def inverse_rms(tensor):
    return lax.rsqrt(jnp.mean(tensor * tensor, -1, keepdims=True) + eps)


def norm_back(grad_unit, unit_vec, inverse):
    return inverse * (grad_unit - unit_vec * jnp.mean(grad_unit * unit_vec, -1, keepdims=True))


def visible(own_ids, key_ids, query_at, key_at):
    causal = key_at[None, :] <= query_at[:, None]
    same_doc = own_ids[:, :, None] == key_ids[:, None, :]
    return (causal[None] & same_doc)[:, None]


def masked_scores(query_low, pair_all, allowed, head_count, head_size):
    row_count = pair_all.shape[0]
    row_length = pair_all.shape[1]
    feature_count = head_count * head_size
    key_rows = pair_all[..., :feature_count].reshape(row_count, row_length, head_count, head_size)
    value_rows = pair_all[..., feature_count:].reshape(row_count, row_length, head_count, head_size)
    scores = jnp.einsum(
        "rche,rlhe->rhcl", query_low, key_rows, preferred_element_type=jnp.float32
    ) * head_size ** (-0.5)
    return (jnp.where(allowed, scores, -1e30), key_rows, value_rows)


def columns_of(matrix, parts, slab_count, index):
    lead = matrix.shape[0]
    width = matrix.shape[1] // (parts * slab_count)
    return matrix.reshape(lead, parts, slab_count, width)[:, :, index].reshape(lead, parts * width)


def entries_of(vector, parts, slab_count, index):
    width = vector.shape[0] // (parts * slab_count)
    return vector.reshape(parts, slab_count, width)[:, index].reshape(parts * width)


def shards_by_slab(
    tokens,
    doc_ids,
    cotangent,
    w_query,
    w_key,
    w_value,
    w_out,
    w_gate,
    w_up,
    w_down,
    g_query,
    g_key,
    g_attn,
    g_ffn,
):
    row_count, piece_len, model_width = tokens.shape
    head_size = HEAD
    feature_count = w_query.shape[1]
    head_count = feature_count // head_size
    tok_count = row_count * piece_len
    scale = head_size ** (-0.5)
    seq_count = lax.axis_size("seq")
    parts = lax.axis_size("dp") * seq_count
    slab_count = SLABS
    gather_all = (
        lax.all_gather(w_query, "dp", axis=0, tiled=True),
        lax.all_gather(w_key, "dp", axis=0, tiled=True),
        lax.all_gather(w_value, "dp", axis=0, tiled=True),
        lax.all_gather(w_out, "dp", axis=0, tiled=True),
        lax.all_gather(w_gate, "dp", axis=0, tiled=True),
        lax.all_gather(w_up, "dp", axis=0, tiled=True),
        lax.all_gather(w_down, "dp", axis=0, tiled=True),
    )
    wq_full, wk_full, wv_full, wo_full, wg_full, wu_full, wd_full = gather_all
    gain_query = g_query.astype(jnp.float32)
    gain_key = g_key.astype(jnp.float32)
    gain_attn = g_attn.astype(jnp.float32)
    gain_ffn = g_ffn.astype(jnp.float32)
    flat_tokens = tokens.reshape(tok_count, model_width)
    query_pre = jnp.dot(flat_tokens, wq_full, preferred_element_type=jnp.float32)
    key_pre = jnp.dot(flat_tokens, wk_full, preferred_element_type=jnp.float32)
    value_pre = jnp.dot(flat_tokens, wv_full, preferred_element_type=jnp.float32)
    query_inv = inverse_rms(query_pre)
    query_unit = query_pre * query_inv
    key_inv = inverse_rms(key_pre)
    key_unit = key_pre * key_inv
    first_row = lax.axis_index("seq") * piece_len
    positions = first_row + jnp.tile(jnp.arange(piece_len, dtype=jnp.int32), row_count)
    cosine, sine_part = rotation(positions, head_size)
    query_rot = rotate(
        (query_unit * gain_query).reshape(tok_count, head_count, head_size), cosine, sine_part
    )
    key_rot = rotate(
        (key_unit * gain_key).reshape(tok_count, head_count, head_size), cosine, sine_part
    )
    query_low = query_rot.astype(jnp.bfloat16).reshape(row_count, piece_len, head_count, head_size)
    key_low = key_rot.astype(jnp.bfloat16).reshape(row_count, piece_len, feature_count)
    value_low = value_pre.astype(jnp.bfloat16).reshape(row_count, piece_len, feature_count)
    pair_low = jnp.concatenate([key_low, value_low], -1)
    ids_low = doc_ids.astype(jnp.bfloat16)
    pair_all, ids_all = (
        lax.all_gather(pair_low, "seq", axis=1, tiled=True),
        lax.all_gather(ids_low, "seq", axis=1, tiled=True),
    )
    query_at = first_row + jnp.arange(piece_len, dtype=jnp.int32)
    allowed = visible(ids_low, ids_all, query_at, jnp.arange(pair_all.shape[1], dtype=jnp.int32))
    masked, _, value_rows = masked_scores(
        query_low, pair_all, allowed, head_count, head_size
    )
    row_max = jnp.max(masked, -1, keepdims=True)
    log_total = jnp.log(jnp.sum(jnp.exp(masked - row_max), -1, keepdims=True)) + row_max
    probs_low = jnp.exp(masked - log_total).astype(jnp.bfloat16)
    mixed = jnp.einsum("rhcl,rlhe->rche", probs_low, value_rows, preferred_element_type=jnp.float32)
    mixed_low = mixed.reshape(tok_count, feature_count).astype(jnp.bfloat16)
    attn_out = jnp.dot(mixed_low, wo_full, preferred_element_type=jnp.float32)
    attn_inv = inverse_rms(attn_out)
    attn_unit = attn_out * attn_inv
    hidden_state = flat_tokens.astype(jnp.float32) + attn_unit * gain_attn
    hidden_low = hidden_state.astype(jnp.bfloat16)
    gate = jnp.dot(hidden_low, wg_full, preferred_element_type=jnp.float32)
    up_proj = jnp.dot(hidden_low, wu_full, preferred_element_type=jnp.float32)
    sigma = jax.nn.sigmoid(gate)
    active = gate * sigma
    inner_low = (active * up_proj).astype(jnp.bfloat16)
    branch = jnp.dot(inner_low, wd_full, preferred_element_type=jnp.float32)
    branch_inv = inverse_rms(branch)
    branch_unit = branch * branch_inv
    result = (
        (hidden_state + branch_unit * gain_ffn)
        .astype(jnp.bfloat16)
        .reshape(row_count, piece_len, model_width)
    )
    wq_back, wk_back, wv_back, wo_back, wg_back, wu_back, wd_back = gather_all
    pair_back, ids_back = (pair_all, ids_all)
    grad_out = cotangent.reshape(tok_count, model_width).astype(jnp.float32)
    ffn_gain_term = jnp.sum(grad_out * branch_unit, 0)
    d_branch = norm_back(grad_out * gain_ffn, branch_unit, branch_inv).astype(jnp.bfloat16)
    d_inner = jnp.einsum("nd,fd->nf", d_branch, wd_back, preferred_element_type=jnp.float32)
    d_gate = (d_inner * up_proj * sigma * (1.0 + gate * (1.0 - sigma))).astype(jnp.bfloat16)
    d_up = (d_inner * active).astype(jnp.bfloat16)
    d_hidden = grad_out + jnp.einsum(
        "nf,df->nd", d_gate, wg_back, preferred_element_type=jnp.float32
    )
    d_hidden = d_hidden + jnp.einsum("nf,df->nd", d_up, wu_back, preferred_element_type=jnp.float32)
    mlp_shares = []
    for index in range(slab_count):
        hidden_part = columns_of(hidden_low, parts, slab_count, index)
        inner_part = columns_of(inner_low, parts, slab_count, index)
        gate_term = jnp.einsum("nd,nf->df", hidden_part, d_gate, preferred_element_type=jnp.float32)
        up_term = jnp.einsum("nd,nf->df", hidden_part, d_up, preferred_element_type=jnp.float32)
        down_term = jnp.einsum(
            "nf,nd->fd", inner_part, d_branch, preferred_element_type=jnp.float32
        )
        ffn_term = entries_of(ffn_gain_term, parts, slab_count, index)
        shares = (
            lax.psum_scatter(down_term, ("dp", "seq"), scatter_dimension=0, tiled=True),
            lax.psum_scatter(gate_term, ("dp", "seq"), scatter_dimension=0, tiled=True),
            lax.psum_scatter(up_term, ("dp", "seq"), scatter_dimension=0, tiled=True),
            lax.psum_scatter(ffn_term, ("dp", "seq"), scatter_dimension=0, tiled=True),
        )
        mlp_shares.append(shares)
    down_grad = jnp.concatenate([s[0] for s in mlp_shares], 0)
    gate_grad = jnp.concatenate([s[1] for s in mlp_shares], 0)
    up_grad = jnp.concatenate([s[2] for s in mlp_shares], 0)
    ffn_grad = jnp.concatenate([s[3] for s in mlp_shares], 0)
    attn_gain_term = jnp.sum(d_hidden * attn_unit, 0)
    d_attn = norm_back(d_hidden * gain_attn, attn_unit, attn_inv).astype(jnp.bfloat16)
    d_mixed = jnp.einsum("nd,fd->nf", d_attn, wo_back, preferred_element_type=jnp.float32).astype(
        jnp.bfloat16
    )
    d_mixed = d_mixed.reshape(row_count, piece_len, head_count, head_size)
    sub_len = piece_len // slab_count
    pair_width = pair_back.shape[-1]
    pair_view = pair_back.reshape(row_count, seq_count, slab_count, sub_len, pair_width)
    ids_view = ids_back.reshape(row_count, seq_count, slab_count, sub_len)

    def slab_scores(index):
        pair_part = pair_view[:, :, index].reshape(row_count, seq_count * sub_len, pair_width)
        ids_part = ids_view[:, :, index].reshape(row_count, seq_count * sub_len)
        key_at = (
            jnp.arange(seq_count, dtype=jnp.int32)[:, None] * piece_len
            + index * sub_len
            + jnp.arange(sub_len, dtype=jnp.int32)[None, :]
        ).reshape(seq_count * sub_len)
        allowed_part = visible(ids_low, ids_part, query_at, key_at)
        masked_part, key_part, value_part = masked_scores(
            query_low, pair_part, allowed_part, head_count, head_size
        )
        probs_part = jnp.exp(masked_part - log_total)
        d_probs_part = jnp.einsum(
            "rche,rlhe->rhcl", d_mixed, value_part, preferred_element_type=jnp.float32
        )
        return (probs_part, d_probs_part, key_part)

    row_dot = jnp.zeros((row_count, head_count, piece_len, 1), jnp.float32)
    for index in range(slab_count):
        probs_part, d_probs_part, key_part = slab_scores(index)
        row_dot = row_dot + jnp.sum(probs_part * d_probs_part, -1, keepdims=True)
    query_acc = jnp.zeros((row_count, piece_len, head_count, head_size), jnp.float32)
    pair_shares = []
    for index in range(slab_count):
        probs_part, d_probs_part, key_part = slab_scores(index)
        d_scores = (probs_part * (d_probs_part - row_dot)).astype(jnp.bfloat16)
        query_acc = query_acc + jnp.einsum(
            "rhcl,rlhe->rche", d_scores, key_part, preferred_element_type=jnp.float32
        )
        key_term = (
            jnp.einsum("rhcl,rche->rlhe", d_scores, query_low, preferred_element_type=jnp.float32)
            * scale
        )
        value_term = jnp.einsum(
            "rhcl,rche->rlhe",
            probs_part.astype(jnp.bfloat16),
            d_mixed,
            preferred_element_type=jnp.float32,
        )
        key_count = seq_count * sub_len
        pair_term = jnp.concatenate(
            [
                key_term.reshape(row_count, key_count, feature_count),
                value_term.reshape(row_count, key_count, feature_count),
            ],
            -1,
        )
        pair_shares.append(
            lax.psum_scatter(
                pair_term.astype(jnp.bfloat16), "seq", scatter_dimension=1, tiled=True
            ).astype(jnp.float32)
        )
    pair_grad = jnp.concatenate(pair_shares, 1)
    d_query = (query_acc * scale).astype(jnp.bfloat16)
    d_key = (
        pair_grad[..., :feature_count]
        .astype(jnp.bfloat16)
        .reshape(tok_count, head_count, head_size)
    )
    d_value = pair_grad[..., feature_count:].astype(jnp.bfloat16).reshape(tok_count, feature_count)
    dq_norm = unrotate(
        d_query.reshape(tok_count, head_count, head_size).astype(jnp.float32), cosine, sine_part
    ).reshape(tok_count, feature_count)
    dk_norm = unrotate(d_key.astype(jnp.float32), cosine, sine_part).reshape(
        tok_count, feature_count
    )
    query_gain_term = jnp.sum(dq_norm * query_unit, 0)
    key_gain_term = jnp.sum(dk_norm * key_unit, 0)
    dq_pre = norm_back(dq_norm * gain_query, query_unit, query_inv).astype(jnp.bfloat16)
    dk_pre = norm_back(dk_norm * gain_key, key_unit, key_inv).astype(jnp.bfloat16)
    d_tokens = d_hidden + jnp.einsum(
        "nf,df->nd", dq_pre, wq_back, preferred_element_type=jnp.float32
    )
    d_tokens = d_tokens + jnp.einsum(
        "nf,df->nd", dk_pre, wk_back, preferred_element_type=jnp.float32
    )
    d_tokens = d_tokens + jnp.einsum(
        "nf,df->nd", d_value, wv_back, preferred_element_type=jnp.float32
    )
    attn_shares = []
    for index in range(slab_count):
        token_part = columns_of(flat_tokens, parts, slab_count, index)
        mixed_part = columns_of(mixed_low, parts, slab_count, index)
        query_term = jnp.einsum("nd,nf->df", token_part, dq_pre, preferred_element_type=jnp.float32)
        key_wterm = jnp.einsum("nd,nf->df", token_part, dk_pre, preferred_element_type=jnp.float32)
        value_wterm = jnp.einsum(
            "nd,nf->df", token_part, d_value, preferred_element_type=jnp.float32
        )
        out_term = jnp.einsum("nf,nd->fd", mixed_part, d_attn, preferred_element_type=jnp.float32)
        gq_term = entries_of(query_gain_term, parts, slab_count, index)
        gk_term = entries_of(key_gain_term, parts, slab_count, index)
        ga_term = entries_of(attn_gain_term, parts, slab_count, index)
        shares = (
            lax.psum_scatter(query_term, ("dp", "seq"), scatter_dimension=0, tiled=True),
            lax.psum_scatter(key_wterm, ("dp", "seq"), scatter_dimension=0, tiled=True),
            lax.psum_scatter(value_wterm, ("dp", "seq"), scatter_dimension=0, tiled=True),
            lax.psum_scatter(out_term, ("dp", "seq"), scatter_dimension=0, tiled=True),
            lax.psum_scatter(gq_term, ("dp", "seq"), scatter_dimension=0, tiled=True),
            lax.psum_scatter(gk_term, ("dp", "seq"), scatter_dimension=0, tiled=True),
            lax.psum_scatter(ga_term, ("dp", "seq"), scatter_dimension=0, tiled=True),
        )
        attn_shares.append(shares)
    query_grad = jnp.concatenate([s[0] for s in attn_shares], 0)
    key_grad = jnp.concatenate([s[1] for s in attn_shares], 0)
    value_grad = jnp.concatenate([s[2] for s in attn_shares], 0)
    out_grad = jnp.concatenate([s[3] for s in attn_shares], 0)
    gq_grad = jnp.concatenate([s[4] for s in attn_shares], 0)
    gk_grad = jnp.concatenate([s[5] for s in attn_shares], 0)
    ga_grad = jnp.concatenate([s[6] for s in attn_shares], 0)
    tokens_grad = d_tokens.reshape(row_count, piece_len, model_width)
    return (
        result,
        tokens_grad,
        query_grad,
        key_grad,
        value_grad,
        out_grad,
        gate_grad,
        up_grad,
        down_grad,
        gq_grad,
        gk_grad,
        ga_grad,
        ffn_grad,
    )


def own_columns(matrix, groups, parts, index):
    width = matrix.shape[1] // (groups * parts)
    pieces = [
        lax.dynamic_slice_in_dim(matrix, (group * parts + index) * width, width, 1)
        for group in range(groups)
    ]
    return jnp.concatenate(pieces, 1) if groups > 1 else pieces[0]


def gather_seq(piece):
    return lax.all_gather(piece, "seq", axis=1, tiled=True)


def scatter_seq(partial):
    return lax.psum_scatter(partial, "seq", scatter_dimension=1, tiled=True)


def swap(value, axis, flip):
    return lax.ppermute(value, axis, [(at, at ^ flip) for at in range(lax.axis_size(axis))])


def place_kernel(spots_ref, *refs, count):
    in_refs, (out_ref, sems) = refs[:count], refs[-2:]
    copies = []
    for at, in_ref in enumerate(in_refs):
        rows, width = in_ref.shape
        row = pl.multiple_of(spots_ref[2 * at], LANES)
        column = pl.multiple_of(spots_ref[2 * at + 1], LANES)
        copies.append(
            pltpu.make_async_copy(
                in_ref, out_ref.at[pl.ds(row, rows), pl.ds(column, width)], sems.at[at]
            )
        )
    for copy in copies:
        copy.start()
    for copy in copies:
        copy.wait()


def placed(pieces, shape, whole=None):
    spots = jnp.stack([jnp.int32(at) for _, row, column in pieces for at in (row, column)])
    outside = pl.BlockSpec(memory_space=pl.ANY)
    given = [] if whole is None else [whole]
    return pl.pallas_call(
        functools.partial(place_kernel, count=len(pieces)),
        grid_spec=pltpu.PrefetchScalarGridSpec(
            num_scalar_prefetch=1,
            grid=(1,),
            in_specs=[
                pl.BlockSpec(piece.shape, lambda at, spots: (0, 0), pipeline_mode=pl.Buffered(1))
                for piece, _, _ in pieces
            ]
            + [outside] * len(given),
            out_specs=outside,
            scratch_shapes=[pltpu.SemaphoreType.DMA((len(pieces),))],
        ),
        out_shape=jax.ShapeDtypeStruct(shape, pieces[0][0].dtype),
        input_output_aliases={1 + len(pieces): 0} if given else {},
        name="place",
    )(spots, *[piece for piece, _, _ in pieces], *given)


def pieces_for(value, name, split_axis):
    count, index = lax.axis_size(name), lax.axis_index(name)
    width = value.shape[split_axis] // count
    return [
        lax.dynamic_slice_in_dim(value, (index ^ flip) * width, width, split_axis)
        for flip in range(count)
    ]


def swapped(pieces, name):
    return [swap(piece, name, flip) if flip else piece for flip, piece in enumerate(pieces)]


def exchanged(value, name, split_axis):
    return swapped(pieces_for(value, name, split_axis), name)


def pieces_dp(piece):
    half = piece.shape[0] // 2
    halves = piece[:half], piece[half:]
    first = [swap(part, "dp", 1) for part in halves]
    second = [swap(part, "dp", 2) for part in halves]
    far = swap(first[0], "dp", 2), swap(second[1], "dp", 1)
    index = lax.axis_index("dp")
    return [
        (part, (2 * (index ^ flip) + side) * half)
        for flip, parts in ((1, first), (2, second), (3, far))
        for side, part in enumerate(parts)
    ]


def gather_dp(piece):
    rows, width = piece.shape
    pieces = [(piece, lax.axis_index("dp") * rows), *pieces_dp(piece)]
    pieces = [(part, row, 0) for part, row in pieces]
    whole = placed(pieces[:5], (4 * rows, width))
    return placed(pieces[5:], (4 * rows, width), whole)


def sum_dp(sent, kept):
    got = swap(sent[0], "dp", 1), swap(sent[1], "dp", 2)
    wide = [(kept[at].astype(jnp.float32) + got[at].astype(jnp.float32)) for at in range(2)]
    onward = [side[1].astype(jnp.bfloat16) for side in wide]
    last = swap(onward[0], "dp", 2), swap(onward[1], "dp", 1)
    return jnp.concatenate(
        [wide[at][0] + last[at].astype(jnp.float32) for at in range(2)], 0
    )


def shares_for(partial):
    index = lax.axis_index("dp")
    width = partial.shape[0] // 4
    half = width // 2

    def part(flip, side):
        return lax.dynamic_slice_in_dim(partial, (index ^ flip) * width + side * half, half, 0)

    sent = [jnp.stack([part(1, 0), part(3, 0)]), jnp.stack([part(2, 1), part(3, 1)])]
    kept = [jnp.stack([part(0, 0), part(2, 0)]), jnp.stack([part(0, 1), part(1, 1)])]
    return sent, kept


def stored_turned(matrix, after):
    matrix, after = lax.optimization_barrier((matrix, after))
    return with_layout_constraint(matrix.T, Layout((0, 1))), after


def total_seq(value):
    shape = value.shape
    value = value.reshape(-1, LANES)
    flip = 1
    while flip < lax.axis_size("seq"):
        value = value + swap(value, "seq", flip)
        flip *= 2
    return value.reshape(shape)


def share_dp(rows):
    flip = lax.axis_size("dp") // 2
    while flip:
        halves = rows.reshape(2, rows.shape[0] // 2, rows.shape[1])
        side = lax.axis_index("dp") // flip % 2
        kept = lax.dynamic_index_in_dim(halves, side, 0, False)
        sent = lax.dynamic_index_in_dim(halves, 1 - side, 0, False)
        rows = kept + swap(sent, "dp", flip)
        flip //= 2
    return rows[0]


def settle_kernel(index_ref, *refs, groups, width, count):
    in_refs, out_refs = refs[:count], refs[count:]
    for flip, in_ref in enumerate(in_refs):
        source = index_ref[0] ^ flip
        for at, out_ref in enumerate(out_refs):
            for group in range(groups):
                column = (at * groups + group) * width
                place = pl.multiple_of((group * count + source) * width, width)
                out_ref[:, pl.ds(place, width)] = in_ref[:, column : column + width].astype(jnp.float32)


def rows_home(summed, groups, width):
    pieces = exchanged(summed, "seq", 0)
    count = len(pieces)
    rows, total = pieces[0].shape
    outs = total // (groups * width)
    step = min(16, rows)
    wide = count * groups * width
    return pl.pallas_call(
        functools.partial(settle_kernel, groups=groups, width=width, count=count),
        grid_spec=pltpu.PrefetchScalarGridSpec(
            num_scalar_prefetch=1,
            grid=(rows // step,),
            in_specs=[pl.BlockSpec((step, total), lambda r, index: (r, 0))] * count,
            out_specs=[pl.BlockSpec((step, wide), lambda r, index: (r, 0))] * outs,
        ),
        out_shape=[jax.ShapeDtypeStruct((rows, wide), jnp.float32)] * outs,
        name="settle",
    )(lax.axis_index("seq").reshape(1), *pieces)


QUERY_BLOCK = 256


def attention_masks(ids_col, ids_row, block, width, start):
    rows = start + lax.broadcasted_iota(jnp.int32, (block, width), 0)
    columns = lax.broadcasted_iota(jnp.int32, (block, width), 1)
    return (columns <= rows) & (ids_col[start : start + block] == ids_row[:, :width])


def attend_kernel(
    q_ref, k_ref, v_ref, qinv_ref, kinv_ref, cos_ref, sin_ref, gq_ref, gk_ref, col_ref, row_ref,
    qlow_ref, klow_ref, vlow_ref, mixed_ref, total_ref, *, scale
):
    low = jnp.bfloat16
    half = q_ref.shape[-1] // 2
    cosine, sine_part = cos_ref[...], sin_ref[...]

    def rotated(ref, inv_ref, gain_ref):
        value = ref[0] * inv_ref[0] * gain_ref[...]
        return (value * cosine + pltpu.roll(value, half, 1) * sine_part).astype(low)

    qlow_ref[0] = rotated(q_ref, qinv_ref, gq_ref)
    klow_ref[0] = rotated(k_ref, kinv_ref, gk_ref)
    vlow_ref[0] = v_ref[0].astype(low)
    length = q_ref.shape[1]
    block = min(QUERY_BLOCK, length)
    ids_col, ids_row = col_ref[0], row_ref[0]
    for start in range(0, length, block):
        width = start + block
        scores = lax.dot_general(
            qlow_ref[0, start:width], klow_ref[0, :width], (((1,), (1,)), ((), ())),
            preferred_element_type=jnp.float32,
        ) * scale
        allowed = attention_masks(ids_col, ids_row, block, width, start)
        masked = jnp.where(allowed, scores, -1e30)
        row_max = jnp.max(masked, -1, keepdims=True)
        log_total = jnp.log(jnp.sum(jnp.exp(masked - row_max), -1, keepdims=True)) + row_max
        total_ref[0, 0, start:width] = log_total
        probs = jnp.exp(masked - log_total).astype(low)
        mixed_ref[0, start:width] = jnp.dot(
            probs, vlow_ref[0, :width], preferred_element_type=jnp.float32
        ).astype(low)


def attend_back_kernel(
    q_ref, k_ref, qinv_ref, kinv_ref, cos_ref, sin_ref, gq_ref, gk_ref, col_ref, row_ref,
    qlow_ref, klow_ref, vlow_ref, total_ref, dmixed_ref,
    dq_ref, dk_ref, dv_ref, dots_ref, gains_ref, key_acc, value_acc, query_acc, *, scale
):
    low = jnp.bfloat16
    half = q_ref.shape[-1] // 2
    length = q_ref.shape[1]
    block = min(QUERY_BLOCK, length)
    ids_col, ids_row = col_ref[0], row_ref[0]
    turned = (((0,), (0,)), ((), ()))
    across = (((1,), (1,)), ((), ()))
    key_acc[...] = jnp.zeros_like(key_acc)
    value_acc[...] = jnp.zeros_like(value_acc)
    for start in range(0, length, block):
        width = start + block
        query = qlow_ref[0, start:width]
        d_mixed = dmixed_ref[0, start:width]
        keys = klow_ref[0, :width]
        scores = lax.dot_general(query, keys, across, preferred_element_type=jnp.float32) * scale
        allowed = attention_masks(ids_col, ids_row, block, width, start)
        probs = jnp.exp(jnp.where(allowed, scores, -1e30) - total_ref[0, 0, start:width])
        d_probs = lax.dot_general(
            d_mixed, vlow_ref[0, :width], across, preferred_element_type=jnp.float32
        )
        row_dot = jnp.sum(probs * d_probs, -1, keepdims=True)
        d_scores = (probs * (d_probs - row_dot)).astype(low)
        query_acc[start:width] = jnp.dot(d_scores, keys, preferred_element_type=jnp.float32)
        key_acc[:width] += lax.dot_general(d_scores, query, turned, preferred_element_type=jnp.float32)
        value_acc[:width] += lax.dot_general(
            probs.astype(low), d_mixed, turned, preferred_element_type=jnp.float32
        )
    dv_ref[0] = value_acc[...].astype(low)
    cosine, sine_part = cos_ref[...], sin_ref[...]

    def turned_back(acc, ref, inv_ref, gain_ref, out_ref, at):
        value = (acc[...] * scale).astype(low).astype(jnp.float32)
        value = value * cosine - pltpu.roll(value, half, 1) * sine_part
        unit = ref[0] * inv_ref[0]
        gains_ref[0, at : at + 1] = jnp.sum(value * unit, 0, keepdims=True)
        value = value * gain_ref[...]
        out_ref[0] = value
        return jnp.sum(value * unit, -1, keepdims=True)

    query_dot = turned_back(query_acc, q_ref, qinv_ref, gq_ref, dq_ref, 0)
    key_dot = turned_back(key_acc, k_ref, kinv_ref, gk_ref, dk_ref, 1)
    lane = lax.broadcasted_iota(jnp.int32, (length, LANES), 1)
    dots = jnp.where(lane == 0, query_dot, jnp.where(lane == 1, key_dot, 0.0)).T[:8]

    @pl.when(pl.program_id(1) == 0)
    def _():
        dots_ref[0] = dots

    @pl.when(pl.program_id(1) != 0)
    def _():
        dots_ref[0] += dots


def attention_specs(length, heads, head_size):
    wide = lambda at: pl.BlockSpec((1, length, head_size), lambda r, h, at=at: (r, 0, at * heads + h))
    thin = pl.BlockSpec((1, length, 1), lambda r, h: (r, 0, 0))
    table = pl.BlockSpec((length, head_size), lambda r, h: (0, 0))
    gain = pl.BlockSpec((1, head_size), lambda r, h: (0, h))
    flat = pl.BlockSpec((1, 1, length), lambda r, h: (r, 0, 0))
    total = pl.BlockSpec((1, 1, length, 1), lambda r, h: (r, h, 0, 0))
    return wide, thin, table, gain, flat, total


def attend(qkv, inverses, tables, gains, ids, head_size, scale):
    rows, length, width = qkv.shape
    heads = width // (3 * head_size)
    wide, thin, table, gain, flat, total = attention_specs(length, heads, head_size)
    narrow = jax.ShapeDtypeStruct((rows, length, heads * head_size), jnp.bfloat16)
    return pl.pallas_call(
        functools.partial(attend_kernel, scale=scale),
        grid=(rows, heads),
        in_specs=[wide(0), wide(1), wide(2), thin, thin, table, table, gain, gain, thin, flat],
        out_specs=[wide(0), wide(0), wide(0), wide(0), total],
        out_shape=[narrow] * 4 + [jax.ShapeDtypeStruct((rows, heads, length, 1), jnp.float32)],
        name="attend",
    )(qkv, qkv, qkv, *inverses, *tables, *gains, ids[:, :, None], ids[:, None, :])


def attend_back(qkv, inverses, tables, gains, ids, kept, d_mixed, head_size, scale):
    rows, length, width = qkv.shape
    heads = width // (3 * head_size)
    wide, thin, table, gain, flat, total = attention_specs(length, heads, head_size)
    shape = (rows, length, heads * head_size)
    return pl.pallas_call(
        functools.partial(attend_back_kernel, scale=scale),
        grid=(rows, heads),
        in_specs=[wide(0), wide(1), thin, thin, table, table, gain, gain, thin, flat]
        + [wide(0), wide(0), wide(0), total, wide(0)],
        out_specs=[
            wide(0),
            wide(0),
            wide(0),
            pl.BlockSpec((1, 8, length), lambda r, h: (r, 0, 0)),
            pl.BlockSpec((1, 2, head_size), lambda r, h: (r, 0, h)),
        ],
        out_shape=[
            jax.ShapeDtypeStruct(shape, jnp.float32),
            jax.ShapeDtypeStruct(shape, jnp.float32),
            jax.ShapeDtypeStruct(shape, jnp.bfloat16),
            jax.ShapeDtypeStruct((rows, 8, length), jnp.float32),
            jax.ShapeDtypeStruct((rows, 2, heads * head_size), jnp.float32),
        ],
        scratch_shapes=[pltpu.VMEM((length, head_size), jnp.float32)] * 3,
        name="attend_back",
    )(qkv, qkv, *inverses, *tables, *gains, ids[:, :, None], ids[:, None, :], *kept, d_mixed)


def shards_by_feature(
    tokens,
    doc_ids,
    cotangent,
    w_query,
    w_key,
    w_value,
    w_out,
    w_gate,
    w_up,
    w_down,
    g_query,
    g_key,
    g_attn,
    g_ffn,
):
    row_count, piece_len, model_width = tokens.shape
    head_size = HEAD
    feature_count = w_query.shape[1]
    scale = head_size ** (-0.5)
    seq_count = lax.axis_size("seq")
    dp_count = lax.axis_size("dp")
    seq_at = lax.axis_index("seq")
    row_len = piece_len * seq_count
    all_count = row_count * row_len
    tok_count = row_count * piece_len
    own_features = feature_count // seq_count
    own_hidden = w_gate.shape[1] // seq_count
    low = jnp.bfloat16

    def own_piece(tensor):
        view = tensor.reshape(row_count, row_len, -1)
        return lax.dynamic_slice_in_dim(view, seq_at * piece_len, piece_len, 1).reshape(tok_count, -1)

    w_qkv = gather_dp(jnp.concatenate([own_columns(w, 1, seq_count, seq_at) for w in (w_query, w_key, w_value)], 1))
    tokens_all = gather_seq(tokens).reshape(all_count, model_width)
    ids_all = total_seq(
        lax.dynamic_update_slice_in_dim(
            jnp.zeros((row_count, row_len), jnp.int32), doc_ids, seq_at * piece_len, 1
        )
    )
    core = seq_at % 2
    half = model_width // 2
    out_rows = w_out.shape[0]
    out_pieces = pieces_dp(lax.dynamic_slice_in_dim(w_out, core * half, half, 1))
    other_pieces = [(swap(piece, "seq", 1), row) for piece, row in out_pieces]
    wo_full = placed(
        [(w_out, lax.axis_index("dp") * out_rows, 0)]
        + [(piece, row, core * half) for piece, row in out_pieces]
        + [(piece, row, half - core * half) for piece, row in other_pieces],
        (feature_count, model_width),
    )
    w_hidden = gather_dp(jnp.concatenate([own_columns(w, dp_count, seq_count, seq_at) for w in (w_gate, w_up)], 1))
    w_back = gather_dp(
        lax.dynamic_slice_in_dim(
            w_down, seq_at * (own_hidden // dp_count), own_hidden // dp_count, 0
        ),
    )
    gain_query = lax.dynamic_slice_in_dim(g_query, seq_at * own_features, own_features).astype(jnp.float32)
    gain_key = lax.dynamic_slice_in_dim(g_key, seq_at * own_features, own_features).astype(jnp.float32)
    gain_attn = g_attn.astype(jnp.float32)
    gain_ffn = g_ffn.astype(jnp.float32)

    tokens_all, ids_all = lax.optimization_barrier((tokens_all, ids_all))
    qkv = jnp.dot(tokens_all, w_qkv, preferred_element_type=jnp.float32)
    query_pre = qkv[:, :own_features]
    key_pre = qkv[:, own_features : 2 * own_features]
    squares = jnp.stack([jnp.sum(query_pre * query_pre, -1), jnp.sum(key_pre * key_pre, -1)])
    cosine, sine_part = rotation(jnp.arange(row_len, dtype=jnp.int32), head_size)
    tables = jnp.concatenate([cosine, cosine], 1), jnp.concatenate([-sine_part, sine_part], 1)
    inverse = lax.rsqrt(total_seq(squares) / feature_count + eps)
    inverses = [inverse[at].reshape(row_count, row_len, 1) for at in range(2)]
    norm_gains = gain_query[None, :], gain_key[None, :]
    qkv_rows = qkv.reshape(row_count, row_len, 3 * own_features)
    *kept, mixed_low, log_total = attend(
        qkv_rows, inverses, tables, norm_gains, ids_all, head_size, scale
    )
    mixed_low = mixed_low.reshape(all_count, own_features)
    mixed_all = lax.all_gather(mixed_low, "seq", axis=1, tiled=True)
    attn_out = jnp.dot(mixed_all, wo_full, preferred_element_type=jnp.float32)
    attn_inv_all = inverse_rms(attn_out)
    hidden_all = tokens_all.astype(jnp.float32) + attn_out * attn_inv_all * gain_attn
    hidden_low = hidden_all.astype(low)
    attn_inv = own_piece(attn_inv_all)
    attn_unit = own_piece(attn_out) * attn_inv
    hidden_state = tokens.reshape(tok_count, model_width).astype(jnp.float32) + attn_unit * gain_attn

    gate_up = jnp.dot(hidden_low, w_hidden, preferred_element_type=jnp.float32)
    gate, up_proj = gate_up[:, :own_hidden], gate_up[:, own_hidden:]
    sigma = jax.nn.sigmoid(gate)
    active = gate * sigma
    inner_low = (active * up_proj).astype(low)
    branch_part = jnp.dot(inner_low, w_back, preferred_element_type=jnp.float32).astype(low)
    w_hidden_turned, branch_part = stored_turned(w_hidden, branch_part)
    w_back_turned, branch_part = stored_turned(w_back, branch_part)
    branch = (
        scatter_seq(branch_part.reshape(row_count, row_len, model_width))
        .astype(jnp.float32)
        .reshape(tok_count, model_width)
    )
    branch_inv = inverse_rms(branch)
    branch_unit = branch * branch_inv
    result = (
        (hidden_state + branch_unit * gain_ffn)
        .astype(low)
        .reshape(row_count, piece_len, model_width)
    )

    grad_out = cotangent.reshape(tok_count, model_width).astype(jnp.float32)
    ffn_gain_term = jnp.sum(grad_out * branch_unit, 0)
    d_branch = norm_back(grad_out * gain_ffn, branch_unit, branch_inv).astype(low)
    d_branch_all = gather_seq(d_branch.reshape(row_count, piece_len, model_width)).reshape(all_count, model_width)
    d_inner = jnp.dot(d_branch_all, w_back_turned, preferred_element_type=jnp.float32)
    d_gate = (d_inner * up_proj * sigma * (1.0 + gate * (1.0 - sigma))).astype(low)
    d_up = (d_inner * active).astype(low)
    d_gate_up = jnp.concatenate([d_gate, d_up], 1)
    d_hidden_part = jnp.dot(d_gate_up, w_hidden_turned, preferred_element_type=jnp.float32).astype(low)
    d_hidden_sum = scatter_seq(d_hidden_part.reshape(row_count, row_len, model_width))
    gate_part = jnp.einsum("nd,nf->df", hidden_low, d_gate, preferred_element_type=jnp.float32).astype(low)
    up_part = jnp.einsum("nd,nf->df", hidden_low, d_up, preferred_element_type=jnp.float32).astype(low)
    down_part = jnp.einsum("nf,nd->fd", inner_low, d_branch_all, preferred_element_type=jnp.float32).astype(low)
    down_grad = sum_dp(*shares_for(down_part))
    gate_own = sum_dp(*shares_for(gate_part)).astype(low)
    up_own = sum_dp(*shares_for(up_part)).astype(low)
    d_hidden = grad_out + d_hidden_sum.astype(jnp.float32).reshape(tok_count, model_width)

    attn_gain_term = jnp.sum(d_hidden * attn_unit, 0)
    d_attn = norm_back(d_hidden * gain_attn, attn_unit, attn_inv).astype(low)
    d_mixed = jnp.einsum("nd,fd->nf", d_attn, wo_full, preferred_element_type=jnp.float32).astype(low)

    def own_columns_of_all(tensor):
        split = tensor.reshape(row_count, piece_len, seq_count, -1).transpose(2, 0, 1, 3)
        width = split.shape[-1]
        split = lax.all_to_all(split.reshape(seq_count, tok_count, width), "seq", split_axis=0, concat_axis=0)
        split = split.reshape(seq_count, row_count, piece_len, width).transpose(1, 0, 2, 3)
        return split.reshape(row_count, row_len, width)

    d_mixed = own_columns_of_all(d_mixed)
    d_mixed, d_attn = lax.optimization_barrier((d_mixed, d_attn))
    d_attn_own = own_columns_of_all(d_attn).reshape(all_count, -1)
    out_part = jnp.einsum("nf,nd->fd", mixed_all, d_attn_own, preferred_element_type=jnp.float32).astype(low)
    out_own = sum_dp(*shares_for(out_part)).astype(low)
    (gate_grad,) = rows_home(gate_own, dp_count, own_hidden // dp_count)
    (up_grad,) = rows_home(up_own, dp_count, own_hidden // dp_count)

    dq_gained, dk_gained, d_value, dots, gain_terms = attend_back(
        qkv_rows, inverses, tables, norm_gains, ids_all, (*kept, log_total), d_mixed, head_size, scale
    )
    norm_terms = lax.dynamic_update_slice_in_dim(
        jnp.zeros((2, feature_count), jnp.float32), jnp.sum(gain_terms, 0), seq_at * own_features, 1
    )
    dots = dots[:, :2].transpose(1, 0, 2).reshape(-1, LANES)
    stat_rows = dots.shape[0]
    sums = total_seq(
        jnp.concatenate(
            [dots]
            + [part.reshape(-1, LANES) for part in (norm_terms, attn_gain_term, ffn_gain_term)]
        )
    )
    means = sums[:stat_rows].reshape(2, all_count) / feature_count

    def norm_back_wide(gained, pre, at):
        inv = inverse[at][:, None]
        gained = gained.reshape(all_count, own_features)
        return (inv * (gained - pre * inv * means[at][:, None])).astype(low)

    dq_pre = norm_back_wide(dq_gained, query_pre, 0)
    dk_pre = norm_back_wide(dk_gained, key_pre, 1)
    d_value = d_value.reshape(all_count, own_features)
    d_qkv = jnp.concatenate([dq_pre, dk_pre, d_value], 1)
    d_tokens_part = jnp.einsum("nf,df->nd", d_qkv, w_qkv, preferred_element_type=jnp.float32).astype(low)
    d_qkv, d_tokens_part = lax.optimization_barrier((d_qkv, d_tokens_part))
    d_tokens_sum = scatter_seq(d_tokens_part.reshape(row_count, row_len, model_width))
    d_tokens = d_hidden + d_tokens_sum.astype(jnp.float32).reshape(tok_count, model_width)
    qkv_part = jnp.einsum("nd,nf->df", tokens_all, d_qkv, preferred_element_type=jnp.float32).astype(low)
    qkv_own = sum_dp(*shares_for(qkv_part)).astype(low)
    attn_home = rows_home(jnp.concatenate([qkv_own, out_own], 1), 1, own_features)
    share = feature_count // (dp_count * seq_count)
    gains = lax.dynamic_index_in_dim(
        sums[stat_rows:].reshape(4, dp_count, seq_count, share), seq_at, 2, False
    )
    gains = share_dp(gains.transpose(1, 0, 2).reshape(dp_count, 4 * share)).reshape(4, share)
    return (
        result,
        d_tokens.reshape(row_count, piece_len, model_width),
        attn_home[0],
        attn_home[1],
        attn_home[2],
        attn_home[3],
        gate_grad,
        up_grad,
        down_grad,
        gains[0],
        gains[1],
        gains[2],
        gains[3],
    )


def shards(tokens, doc_ids, cotangent, w_query, *rest):
    if w_query.shape[1] // HEAD % lax.axis_size("seq"):
        return shards_by_slab(tokens, doc_ids, cotangent, w_query, *rest)
    return shards_by_feature(tokens, doc_ids, cotangent, w_query, *rest)


def solution(mesh):
    return jax.shard_map(
        shards,
        mesh=mesh,
        in_specs=(
            P("dp", "seq", None),
            P("dp", "seq"),
            P("dp", "seq", None),
            P("dp", None),
            P("dp", None),
            P("dp", None),
            P("dp", None),
            P("dp", None),
            P("dp", None),
            P("dp", None),
            P(),
            P(),
            P(),
            P(),
        ),
        out_specs=(
            P("dp", "seq", None),
            P("dp", "seq", None),
            P(("dp", "seq"), None),
            P(("dp", "seq"), None),
            P(("dp", "seq"), None),
            P(("dp", "seq"), None),
            P(("dp", "seq"), None),
            P(("dp", "seq"), None),
            P(("dp", "seq"), None),
            P(("dp", "seq")),
            P(("dp", "seq")),
            P(("dp", "seq")),
            P(("dp", "seq")),
        ),
        check_vma=False,
    )
```

```python
import functools

import jax
import jax.numpy as jnp
from jax import lax
from jax.experimental import pallas as pl
from jax.experimental.layout import Layout, with_layout_constraint
from jax.experimental.pallas import tpu as pltpu
from jax.sharding import PartitionSpec as P


HEAD = 128
SLABS = 4
LANES = 128


eps = 1e-06
theta = 500000.0


def rotation(positions, head_size):
    half_size = head_size // 2
    frequency = theta ** (-(2.0 * jnp.arange(half_size, dtype=jnp.float32)) / head_size)
    angles = positions.astype(jnp.float32)[:, None] * frequency[None, :]
    return (jnp.cos(angles), jnp.sin(angles))


def rotate(tensor, cosine, sine_part):
    half_size = tensor.shape[-1] // 2
    first_half = tensor[..., :half_size]
    second_half = tensor[..., half_size:]
    cos_wide = cosine[:, None, :]
    sin_wide = sine_part[:, None, :]
    return jnp.concatenate(
        [
            first_half * cos_wide - second_half * sin_wide,
            second_half * cos_wide + first_half * sin_wide,
        ],
        -1,
    )


def unrotate(tensor, cosine, sine_part):
    half_size = tensor.shape[-1] // 2
    first_half = tensor[..., :half_size]
    second_half = tensor[..., half_size:]
    cos_wide = cosine[:, None, :]
    sin_wide = sine_part[:, None, :]
    return jnp.concatenate(
        [
            first_half * cos_wide + second_half * sin_wide,
            second_half * cos_wide - first_half * sin_wide,
        ],
        -1,
    )


def inverse_rms(tensor):
    return lax.rsqrt(jnp.mean(tensor * tensor, -1, keepdims=True) + eps)


def norm_back(grad_unit, unit_vec, inverse):
    return inverse * (grad_unit - unit_vec * jnp.mean(grad_unit * unit_vec, -1, keepdims=True))


def visible(own_ids, key_ids, query_at, key_at):
    causal = key_at[None, :] <= query_at[:, None]
    same_doc = own_ids[:, :, None] == key_ids[:, None, :]
    return (causal[None] & same_doc)[:, None]


def masked_scores(query_low, pair_all, allowed, head_count, head_size):
    row_count = pair_all.shape[0]
    row_length = pair_all.shape[1]
    feature_count = head_count * head_size
    key_rows = pair_all[..., :feature_count].reshape(row_count, row_length, head_count, head_size)
    value_rows = pair_all[..., feature_count:].reshape(row_count, row_length, head_count, head_size)
    scores = jnp.einsum(
        "rche,rlhe->rhcl", query_low, key_rows, preferred_element_type=jnp.float32
    ) * head_size ** (-0.5)
    return (jnp.where(allowed, scores, -1e30), key_rows, value_rows)


def columns_of(matrix, parts, slab_count, index):
    lead = matrix.shape[0]
    width = matrix.shape[1] // (parts * slab_count)
    return matrix.reshape(lead, parts, slab_count, width)[:, :, index].reshape(lead, parts * width)


def entries_of(vector, parts, slab_count, index):
    width = vector.shape[0] // (parts * slab_count)
    return vector.reshape(parts, slab_count, width)[:, index].reshape(parts * width)


def shards_by_slab(
    tokens,
    doc_ids,
    cotangent,
    w_query,
    w_key,
    w_value,
    w_out,
    w_gate,
    w_up,
    w_down,
    g_query,
    g_key,
    g_attn,
    g_ffn,
):
    row_count, piece_len, model_width = tokens.shape
    head_size = HEAD
    feature_count = w_query.shape[1]
    head_count = feature_count // head_size
    tok_count = row_count * piece_len
    scale = head_size ** (-0.5)
    seq_count = lax.axis_size("seq")
    parts = lax.axis_size("dp") * seq_count
    slab_count = SLABS
    gather_all = (
        lax.all_gather(w_query, "dp", axis=0, tiled=True),
        lax.all_gather(w_key, "dp", axis=0, tiled=True),
        lax.all_gather(w_value, "dp", axis=0, tiled=True),
        lax.all_gather(w_out, "dp", axis=0, tiled=True),
        lax.all_gather(w_gate, "dp", axis=0, tiled=True),
        lax.all_gather(w_up, "dp", axis=0, tiled=True),
        lax.all_gather(w_down, "dp", axis=0, tiled=True),
    )
    wq_full, wk_full, wv_full, wo_full, wg_full, wu_full, wd_full = gather_all
    gain_query = g_query.astype(jnp.float32)
    gain_key = g_key.astype(jnp.float32)
    gain_attn = g_attn.astype(jnp.float32)
    gain_ffn = g_ffn.astype(jnp.float32)
    flat_tokens = tokens.reshape(tok_count, model_width)
    query_pre = jnp.dot(flat_tokens, wq_full, preferred_element_type=jnp.float32)
    key_pre = jnp.dot(flat_tokens, wk_full, preferred_element_type=jnp.float32)
    value_pre = jnp.dot(flat_tokens, wv_full, preferred_element_type=jnp.float32)
    query_inv = inverse_rms(query_pre)
    query_unit = query_pre * query_inv
    key_inv = inverse_rms(key_pre)
    key_unit = key_pre * key_inv
    first_row = lax.axis_index("seq") * piece_len
    positions = first_row + jnp.tile(jnp.arange(piece_len, dtype=jnp.int32), row_count)
    cosine, sine_part = rotation(positions, head_size)
    query_rot = rotate(
        (query_unit * gain_query).reshape(tok_count, head_count, head_size), cosine, sine_part
    )
    key_rot = rotate(
        (key_unit * gain_key).reshape(tok_count, head_count, head_size), cosine, sine_part
    )
    query_low = query_rot.astype(jnp.bfloat16).reshape(row_count, piece_len, head_count, head_size)
    key_low = key_rot.astype(jnp.bfloat16).reshape(row_count, piece_len, feature_count)
    value_low = value_pre.astype(jnp.bfloat16).reshape(row_count, piece_len, feature_count)
    pair_low = jnp.concatenate([key_low, value_low], -1)
    ids_low = doc_ids.astype(jnp.bfloat16)
    pair_all, ids_all = (
        lax.all_gather(pair_low, "seq", axis=1, tiled=True),
        lax.all_gather(ids_low, "seq", axis=1, tiled=True),
    )
    query_at = first_row + jnp.arange(piece_len, dtype=jnp.int32)
    allowed = visible(ids_low, ids_all, query_at, jnp.arange(pair_all.shape[1], dtype=jnp.int32))
    masked, _, value_rows = masked_scores(
        query_low, pair_all, allowed, head_count, head_size
    )
    row_max = jnp.max(masked, -1, keepdims=True)
    log_total = jnp.log(jnp.sum(jnp.exp(masked - row_max), -1, keepdims=True)) + row_max
    probs_low = jnp.exp(masked - log_total).astype(jnp.bfloat16)
    mixed = jnp.einsum("rhcl,rlhe->rche", probs_low, value_rows, preferred_element_type=jnp.float32)
    mixed_low = mixed.reshape(tok_count, feature_count).astype(jnp.bfloat16)
    attn_out = jnp.dot(mixed_low, wo_full, preferred_element_type=jnp.float32)
    attn_inv = inverse_rms(attn_out)
    attn_unit = attn_out * attn_inv
    hidden_state = flat_tokens.astype(jnp.float32) + attn_unit * gain_attn
    hidden_low = hidden_state.astype(jnp.bfloat16)
    gate = jnp.dot(hidden_low, wg_full, preferred_element_type=jnp.float32)
    up_proj = jnp.dot(hidden_low, wu_full, preferred_element_type=jnp.float32)
    sigma = jax.nn.sigmoid(gate)
    active = gate * sigma
    inner_low = (active * up_proj).astype(jnp.bfloat16)
    branch = jnp.dot(inner_low, wd_full, preferred_element_type=jnp.float32)
    branch_inv = inverse_rms(branch)
    branch_unit = branch * branch_inv
    result = (
        (hidden_state + branch_unit * gain_ffn)
        .astype(jnp.bfloat16)
        .reshape(row_count, piece_len, model_width)
    )
    wq_back, wk_back, wv_back, wo_back, wg_back, wu_back, wd_back = gather_all
    pair_back, ids_back = (pair_all, ids_all)
    grad_out = cotangent.reshape(tok_count, model_width).astype(jnp.float32)
    ffn_gain_term = jnp.sum(grad_out * branch_unit, 0)
    d_branch = norm_back(grad_out * gain_ffn, branch_unit, branch_inv).astype(jnp.bfloat16)
    d_inner = jnp.einsum("nd,fd->nf", d_branch, wd_back, preferred_element_type=jnp.float32)
    d_gate = (d_inner * up_proj * sigma * (1.0 + gate * (1.0 - sigma))).astype(jnp.bfloat16)
    d_up = (d_inner * active).astype(jnp.bfloat16)
    d_hidden = grad_out + jnp.einsum(
        "nf,df->nd", d_gate, wg_back, preferred_element_type=jnp.float32
    )
    d_hidden = d_hidden + jnp.einsum("nf,df->nd", d_up, wu_back, preferred_element_type=jnp.float32)
    mlp_shares = []
    for index in range(slab_count):
        hidden_part = columns_of(hidden_low, parts, slab_count, index)
        inner_part = columns_of(inner_low, parts, slab_count, index)
        gate_term = jnp.einsum("nd,nf->df", hidden_part, d_gate, preferred_element_type=jnp.float32)
        up_term = jnp.einsum("nd,nf->df", hidden_part, d_up, preferred_element_type=jnp.float32)
        down_term = jnp.einsum(
            "nf,nd->fd", inner_part, d_branch, preferred_element_type=jnp.float32
        )
        ffn_term = entries_of(ffn_gain_term, parts, slab_count, index)
        shares = (
            lax.psum_scatter(down_term, ("dp", "seq"), scatter_dimension=0, tiled=True),
            lax.psum_scatter(gate_term, ("dp", "seq"), scatter_dimension=0, tiled=True),
            lax.psum_scatter(up_term, ("dp", "seq"), scatter_dimension=0, tiled=True),
            lax.psum_scatter(ffn_term, ("dp", "seq"), scatter_dimension=0, tiled=True),
        )
        mlp_shares.append(shares)
    down_grad = jnp.concatenate([s[0] for s in mlp_shares], 0)
    gate_grad = jnp.concatenate([s[1] for s in mlp_shares], 0)
    up_grad = jnp.concatenate([s[2] for s in mlp_shares], 0)
    ffn_grad = jnp.concatenate([s[3] for s in mlp_shares], 0)
    attn_gain_term = jnp.sum(d_hidden * attn_unit, 0)
    d_attn = norm_back(d_hidden * gain_attn, attn_unit, attn_inv).astype(jnp.bfloat16)
    d_mixed = jnp.einsum("nd,fd->nf", d_attn, wo_back, preferred_element_type=jnp.float32).astype(
        jnp.bfloat16
    )
    d_mixed = d_mixed.reshape(row_count, piece_len, head_count, head_size)
    sub_len = piece_len // slab_count
    pair_width = pair_back.shape[-1]
    pair_view = pair_back.reshape(row_count, seq_count, slab_count, sub_len, pair_width)
    ids_view = ids_back.reshape(row_count, seq_count, slab_count, sub_len)

    def slab_scores(index):
        pair_part = pair_view[:, :, index].reshape(row_count, seq_count * sub_len, pair_width)
        ids_part = ids_view[:, :, index].reshape(row_count, seq_count * sub_len)
        key_at = (
            jnp.arange(seq_count, dtype=jnp.int32)[:, None] * piece_len
            + index * sub_len
            + jnp.arange(sub_len, dtype=jnp.int32)[None, :]
        ).reshape(seq_count * sub_len)
        allowed_part = visible(ids_low, ids_part, query_at, key_at)
        masked_part, key_part, value_part = masked_scores(
            query_low, pair_part, allowed_part, head_count, head_size
        )
        probs_part = jnp.exp(masked_part - log_total)
        d_probs_part = jnp.einsum(
            "rche,rlhe->rhcl", d_mixed, value_part, preferred_element_type=jnp.float32
        )
        return (probs_part, d_probs_part, key_part)

    row_dot = jnp.zeros((row_count, head_count, piece_len, 1), jnp.float32)
    for index in range(slab_count):
        probs_part, d_probs_part, key_part = slab_scores(index)
        row_dot = row_dot + jnp.sum(probs_part * d_probs_part, -1, keepdims=True)
    query_acc = jnp.zeros((row_count, piece_len, head_count, head_size), jnp.float32)
    pair_shares = []
    for index in range(slab_count):
        probs_part, d_probs_part, key_part = slab_scores(index)
        d_scores = (probs_part * (d_probs_part - row_dot)).astype(jnp.bfloat16)
        query_acc = query_acc + jnp.einsum(
            "rhcl,rlhe->rche", d_scores, key_part, preferred_element_type=jnp.float32
        )
        key_term = (
            jnp.einsum("rhcl,rche->rlhe", d_scores, query_low, preferred_element_type=jnp.float32)
            * scale
        )
        value_term = jnp.einsum(
            "rhcl,rche->rlhe",
            probs_part.astype(jnp.bfloat16),
            d_mixed,
            preferred_element_type=jnp.float32,
        )
        key_count = seq_count * sub_len
        pair_term = jnp.concatenate(
            [
                key_term.reshape(row_count, key_count, feature_count),
                value_term.reshape(row_count, key_count, feature_count),
            ],
            -1,
        )
        pair_shares.append(
            lax.psum_scatter(
                pair_term.astype(jnp.bfloat16), "seq", scatter_dimension=1, tiled=True
            ).astype(jnp.float32)
        )
    pair_grad = jnp.concatenate(pair_shares, 1)
    d_query = (query_acc * scale).astype(jnp.bfloat16)
    d_key = (
        pair_grad[..., :feature_count]
        .astype(jnp.bfloat16)
        .reshape(tok_count, head_count, head_size)
    )
    d_value = pair_grad[..., feature_count:].astype(jnp.bfloat16).reshape(tok_count, feature_count)
    dq_norm = unrotate(
        d_query.reshape(tok_count, head_count, head_size).astype(jnp.float32), cosine, sine_part
    ).reshape(tok_count, feature_count)
    dk_norm = unrotate(d_key.astype(jnp.float32), cosine, sine_part).reshape(
        tok_count, feature_count
    )
    query_gain_term = jnp.sum(dq_norm * query_unit, 0)
    key_gain_term = jnp.sum(dk_norm * key_unit, 0)
    dq_pre = norm_back(dq_norm * gain_query, query_unit, query_inv).astype(jnp.bfloat16)
    dk_pre = norm_back(dk_norm * gain_key, key_unit, key_inv).astype(jnp.bfloat16)
    d_tokens = d_hidden + jnp.einsum(
        "nf,df->nd", dq_pre, wq_back, preferred_element_type=jnp.float32
    )
    d_tokens = d_tokens + jnp.einsum(
        "nf,df->nd", dk_pre, wk_back, preferred_element_type=jnp.float32
    )
    d_tokens = d_tokens + jnp.einsum(
        "nf,df->nd", d_value, wv_back, preferred_element_type=jnp.float32
    )
    attn_shares = []
    for index in range(slab_count):
        token_part = columns_of(flat_tokens, parts, slab_count, index)
        mixed_part = columns_of(mixed_low, parts, slab_count, index)
        query_term = jnp.einsum("nd,nf->df", token_part, dq_pre, preferred_element_type=jnp.float32)
        key_wterm = jnp.einsum("nd,nf->df", token_part, dk_pre, preferred_element_type=jnp.float32)
        value_wterm = jnp.einsum(
            "nd,nf->df", token_part, d_value, preferred_element_type=jnp.float32
        )
        out_term = jnp.einsum("nf,nd->fd", mixed_part, d_attn, preferred_element_type=jnp.float32)
        gq_term = entries_of(query_gain_term, parts, slab_count, index)
        gk_term = entries_of(key_gain_term, parts, slab_count, index)
        ga_term = entries_of(attn_gain_term, parts, slab_count, index)
        shares = (
            lax.psum_scatter(query_term, ("dp", "seq"), scatter_dimension=0, tiled=True),
            lax.psum_scatter(key_wterm, ("dp", "seq"), scatter_dimension=0, tiled=True),
            lax.psum_scatter(value_wterm, ("dp", "seq"), scatter_dimension=0, tiled=True),
            lax.psum_scatter(out_term, ("dp", "seq"), scatter_dimension=0, tiled=True),
            lax.psum_scatter(gq_term, ("dp", "seq"), scatter_dimension=0, tiled=True),
            lax.psum_scatter(gk_term, ("dp", "seq"), scatter_dimension=0, tiled=True),
            lax.psum_scatter(ga_term, ("dp", "seq"), scatter_dimension=0, tiled=True),
        )
        attn_shares.append(shares)
    query_grad = jnp.concatenate([s[0] for s in attn_shares], 0)
    key_grad = jnp.concatenate([s[1] for s in attn_shares], 0)
    value_grad = jnp.concatenate([s[2] for s in attn_shares], 0)
    out_grad = jnp.concatenate([s[3] for s in attn_shares], 0)
    gq_grad = jnp.concatenate([s[4] for s in attn_shares], 0)
    gk_grad = jnp.concatenate([s[5] for s in attn_shares], 0)
    ga_grad = jnp.concatenate([s[6] for s in attn_shares], 0)
    tokens_grad = d_tokens.reshape(row_count, piece_len, model_width)
    return (
        result,
        tokens_grad,
        query_grad,
        key_grad,
        value_grad,
        out_grad,
        gate_grad,
        up_grad,
        down_grad,
        gq_grad,
        gk_grad,
        ga_grad,
        ffn_grad,
    )


def own_columns(matrix, groups, parts, index):
    width = matrix.shape[1] // (groups * parts)
    pieces = [
        lax.dynamic_slice_in_dim(matrix, (group * parts + index) * width, width, 1)
        for group in range(groups)
    ]
    return jnp.concatenate(pieces, 1) if groups > 1 else pieces[0]


def gather_seq(piece):
    return lax.all_gather(piece, "seq", axis=1, tiled=True)


def scatter_seq(partial):
    return lax.psum_scatter(partial, "seq", scatter_dimension=1, tiled=True)


def swap(value, axis, flip):
    return lax.ppermute(value, axis, [(at, at ^ flip) for at in range(lax.axis_size(axis))])


def place_kernel(spots_ref, *refs, count):
    in_refs, (out_ref, sems) = refs[:count], refs[-2:]
    copies = []
    for at, in_ref in enumerate(in_refs):
        rows, width = in_ref.shape
        row = pl.multiple_of(spots_ref[2 * at], LANES)
        column = pl.multiple_of(spots_ref[2 * at + 1], LANES)
        copies.append(
            pltpu.make_async_copy(
                in_ref, out_ref.at[pl.ds(row, rows), pl.ds(column, width)], sems.at[at]
            )
        )
    for copy in copies:
        copy.start()
    for copy in copies:
        copy.wait()


def placed(pieces, shape, whole=None):
    spots = jnp.stack([jnp.int32(at) for _, row, column in pieces for at in (row, column)])
    outside = pl.BlockSpec(memory_space=pl.ANY)
    given = [] if whole is None else [whole]
    return pl.pallas_call(
        functools.partial(place_kernel, count=len(pieces)),
        grid_spec=pltpu.PrefetchScalarGridSpec(
            num_scalar_prefetch=1,
            grid=(1,),
            in_specs=[
                pl.BlockSpec(piece.shape, lambda at, spots: (0, 0), pipeline_mode=pl.Buffered(1))
                for piece, _, _ in pieces
            ]
            + [outside] * len(given),
            out_specs=outside,
            scratch_shapes=[pltpu.SemaphoreType.DMA((len(pieces),))],
        ),
        out_shape=jax.ShapeDtypeStruct(shape, pieces[0][0].dtype),
        input_output_aliases={1 + len(pieces): 0} if given else {},
        name="place",
    )(spots, *[piece for piece, _, _ in pieces], *given)


def pieces_for(value, name, split_axis):
    count, index = lax.axis_size(name), lax.axis_index(name)
    width = value.shape[split_axis] // count
    return [
        lax.dynamic_slice_in_dim(value, (index ^ flip) * width, width, split_axis)
        for flip in range(count)
    ]


def swapped(pieces, name):
    return [swap(piece, name, flip) if flip else piece for flip, piece in enumerate(pieces)]


def exchanged(value, name, split_axis):
    return swapped(pieces_for(value, name, split_axis), name)


def pieces_dp(piece):
    half = piece.shape[0] // 2
    first, second = swap(piece, "dp", 1), swap(piece, "dp", 2)
    top, bottom = swap(first[:half], "dp", 2), swap(second[half:], "dp", 1)
    index = lax.axis_index("dp")
    width = piece.shape[0]
    far = (index ^ 3) * width
    return [
        (first, (index ^ 1) * width),
        (second, (index ^ 2) * width),
        (top, far),
        (bottom, far + half),
    ]


def gather_dp(piece):
    rows, width = piece.shape
    pieces = [(piece, lax.axis_index("dp") * rows), *pieces_dp(piece)]
    pieces = [(part, row, 0) for part, row in pieces]
    whole = placed(pieces[:3], (4 * rows, width))
    return placed(pieces[3:], (4 * rows, width), whole)


def sum_dp(sent, kept):
    got = swap(sent[0], "dp", 1), swap(sent[1], "dp", 2)
    wide = [(kept[at].astype(jnp.float32) + got[at].astype(jnp.float32)) for at in range(2)]
    onward = [side[1].astype(jnp.bfloat16) for side in wide]
    last = swap(onward[0], "dp", 2), swap(onward[1], "dp", 1)
    return jnp.concatenate(
        [wide[at][0] + last[at].astype(jnp.float32) for at in range(2)], 0
    )


def shares_for(partial):
    index = lax.axis_index("dp")
    width = partial.shape[0] // 4
    half = width // 2

    def part(flip, side):
        return lax.dynamic_slice_in_dim(partial, (index ^ flip) * width + side * half, half, 0)

    sent = [jnp.stack([part(1, 0), part(3, 0)]), jnp.stack([part(2, 1), part(3, 1)])]
    kept = [jnp.stack([part(0, 0), part(2, 0)]), jnp.stack([part(0, 1), part(1, 1)])]
    return sent, kept


def stored_turned(matrix, after):
    matrix, after = lax.optimization_barrier((matrix, after))
    return with_layout_constraint(matrix.T, Layout((0, 1))), after


def total_seq(value):
    shape = value.shape
    value = value.reshape(-1, LANES)
    flip = 1
    while flip < lax.axis_size("seq"):
        value = value + swap(value, "seq", flip)
        flip *= 2
    return value.reshape(shape)


def share_dp(rows):
    flip = lax.axis_size("dp") // 2
    while flip:
        halves = rows.reshape(2, rows.shape[0] // 2, rows.shape[1])
        side = lax.axis_index("dp") // flip % 2
        kept = lax.dynamic_index_in_dim(halves, side, 0, False)
        sent = lax.dynamic_index_in_dim(halves, 1 - side, 0, False)
        rows = kept + swap(sent, "dp", flip)
        flip //= 2
    return rows[0]


def settle_kernel(index_ref, *refs, groups, width, count):
    in_refs, out_refs = refs[:count], refs[count:]
    for flip, in_ref in enumerate(in_refs):
        source = index_ref[0] ^ flip
        for at, out_ref in enumerate(out_refs):
            for group in range(groups):
                column = (at * groups + group) * width
                place = pl.multiple_of((group * count + source) * width, width)
                out_ref[:, pl.ds(place, width)] = in_ref[:, column : column + width].astype(jnp.float32)


def rows_home(summed, groups, width):
    pieces = exchanged(summed, "seq", 0)
    count = len(pieces)
    rows, total = pieces[0].shape
    outs = total // (groups * width)
    step = min(16, rows)
    wide = count * groups * width
    return pl.pallas_call(
        functools.partial(settle_kernel, groups=groups, width=width, count=count),
        grid_spec=pltpu.PrefetchScalarGridSpec(
            num_scalar_prefetch=1,
            grid=(rows // step,),
            in_specs=[pl.BlockSpec((step, total), lambda r, index: (r, 0))] * count,
            out_specs=[pl.BlockSpec((step, wide), lambda r, index: (r, 0))] * outs,
        ),
        out_shape=[jax.ShapeDtypeStruct((rows, wide), jnp.float32)] * outs,
        name="settle",
    )(lax.axis_index("seq").reshape(1), *pieces)


QUERY_BLOCK = 256


def attention_masks(ids_col, ids_row, block, width, start):
    rows = start + lax.broadcasted_iota(jnp.int32, (block, width), 0)
    columns = lax.broadcasted_iota(jnp.int32, (block, width), 1)
    return (columns <= rows) & (ids_col[start : start + block] == ids_row[:, :width])


def attend_kernel(
    q_ref, k_ref, v_ref, qinv_ref, kinv_ref, cos_ref, sin_ref, gq_ref, gk_ref, col_ref, row_ref,
    qlow_ref, klow_ref, vlow_ref, mixed_ref, total_ref, *, scale
):
    low = jnp.bfloat16
    half = q_ref.shape[-1] // 2
    cosine, sine_part = cos_ref[...], sin_ref[...]

    def rotated(ref, inv_ref, gain_ref):
        value = ref[0] * inv_ref[0] * gain_ref[...]
        return (value * cosine + pltpu.roll(value, half, 1) * sine_part).astype(low)

    qlow_ref[0] = rotated(q_ref, qinv_ref, gq_ref)
    klow_ref[0] = rotated(k_ref, kinv_ref, gk_ref)
    vlow_ref[0] = v_ref[0].astype(low)
    length = q_ref.shape[1]
    block = min(QUERY_BLOCK, length)
    ids_col, ids_row = col_ref[0], row_ref[0]
    for start in range(0, length, block):
        width = start + block
        scores = lax.dot_general(
            qlow_ref[0, start:width], klow_ref[0, :width], (((1,), (1,)), ((), ())),
            preferred_element_type=jnp.float32,
        ) * scale
        allowed = attention_masks(ids_col, ids_row, block, width, start)
        masked = jnp.where(allowed, scores, -1e30)
        row_max = jnp.max(masked, -1, keepdims=True)
        log_total = jnp.log(jnp.sum(jnp.exp(masked - row_max), -1, keepdims=True)) + row_max
        total_ref[0, 0, start:width] = log_total
        probs = jnp.exp(masked - log_total).astype(low)
        mixed_ref[0, start:width] = jnp.dot(
            probs, vlow_ref[0, :width], preferred_element_type=jnp.float32
        ).astype(low)


def attend_back_kernel(
    q_ref, k_ref, qinv_ref, kinv_ref, cos_ref, sin_ref, gq_ref, gk_ref, col_ref, row_ref,
    qlow_ref, klow_ref, vlow_ref, total_ref, dmixed_ref,
    dq_ref, dk_ref, dv_ref, dots_ref, gains_ref, key_acc, value_acc, query_acc, *, scale
):
    low = jnp.bfloat16
    half = q_ref.shape[-1] // 2
    length = q_ref.shape[1]
    block = min(QUERY_BLOCK, length)
    ids_col, ids_row = col_ref[0], row_ref[0]
    turned = (((0,), (0,)), ((), ()))
    across = (((1,), (1,)), ((), ()))
    key_acc[...] = jnp.zeros_like(key_acc)
    value_acc[...] = jnp.zeros_like(value_acc)
    for start in range(0, length, block):
        width = start + block
        query = qlow_ref[0, start:width]
        d_mixed = dmixed_ref[0, start:width]
        keys = klow_ref[0, :width]
        scores = lax.dot_general(query, keys, across, preferred_element_type=jnp.float32) * scale
        allowed = attention_masks(ids_col, ids_row, block, width, start)
        probs = jnp.exp(jnp.where(allowed, scores, -1e30) - total_ref[0, 0, start:width])
        d_probs = lax.dot_general(
            d_mixed, vlow_ref[0, :width], across, preferred_element_type=jnp.float32
        )
        row_dot = jnp.sum(probs * d_probs, -1, keepdims=True)
        d_scores = (probs * (d_probs - row_dot)).astype(low)
        query_acc[start:width] = jnp.dot(d_scores, keys, preferred_element_type=jnp.float32)
        key_acc[:width] += lax.dot_general(d_scores, query, turned, preferred_element_type=jnp.float32)
        value_acc[:width] += lax.dot_general(
            probs.astype(low), d_mixed, turned, preferred_element_type=jnp.float32
        )
    dv_ref[0] = value_acc[...].astype(low)
    cosine, sine_part = cos_ref[...], sin_ref[...]

    def turned_back(acc, ref, inv_ref, gain_ref, out_ref, at):
        value = (acc[...] * scale).astype(low).astype(jnp.float32)
        value = value * cosine - pltpu.roll(value, half, 1) * sine_part
        unit = ref[0] * inv_ref[0]
        gains_ref[0, at : at + 1] = jnp.sum(value * unit, 0, keepdims=True)
        value = value * gain_ref[...]
        out_ref[0] = value
        return jnp.sum(value * unit, -1, keepdims=True)

    query_dot = turned_back(query_acc, q_ref, qinv_ref, gq_ref, dq_ref, 0)
    key_dot = turned_back(key_acc, k_ref, kinv_ref, gk_ref, dk_ref, 1)
    lane = lax.broadcasted_iota(jnp.int32, (length, LANES), 1)
    dots = jnp.where(lane == 0, query_dot, jnp.where(lane == 1, key_dot, 0.0)).T[:8]

    @pl.when(pl.program_id(1) == 0)
    def _():
        dots_ref[0] = dots

    @pl.when(pl.program_id(1) != 0)
    def _():
        dots_ref[0] += dots


def attention_specs(length, heads, head_size):
    wide = lambda at: pl.BlockSpec((1, length, head_size), lambda r, h, at=at: (r, 0, at * heads + h))
    thin = pl.BlockSpec((1, length, 1), lambda r, h: (r, 0, 0))
    table = pl.BlockSpec((length, head_size), lambda r, h: (0, 0))
    gain = pl.BlockSpec((1, head_size), lambda r, h: (0, h))
    flat = pl.BlockSpec((1, 1, length), lambda r, h: (r, 0, 0))
    total = pl.BlockSpec((1, 1, length, 1), lambda r, h: (r, h, 0, 0))
    return wide, thin, table, gain, flat, total


def attend(qkv, inverses, tables, gains, ids, head_size, scale):
    rows, length, width = qkv.shape
    heads = width // (3 * head_size)
    wide, thin, table, gain, flat, total = attention_specs(length, heads, head_size)
    narrow = jax.ShapeDtypeStruct((rows, length, heads * head_size), jnp.bfloat16)
    return pl.pallas_call(
        functools.partial(attend_kernel, scale=scale),
        grid=(rows, heads),
        in_specs=[wide(0), wide(1), wide(2), thin, thin, table, table, gain, gain, thin, flat],
        out_specs=[wide(0), wide(0), wide(0), wide(0), total],
        out_shape=[narrow] * 4 + [jax.ShapeDtypeStruct((rows, heads, length, 1), jnp.float32)],
        name="attend",
    )(qkv, qkv, qkv, *inverses, *tables, *gains, ids[:, :, None], ids[:, None, :])


def attend_back(qkv, inverses, tables, gains, ids, kept, d_mixed, head_size, scale):
    rows, length, width = qkv.shape
    heads = width // (3 * head_size)
    wide, thin, table, gain, flat, total = attention_specs(length, heads, head_size)
    shape = (rows, length, heads * head_size)
    return pl.pallas_call(
        functools.partial(attend_back_kernel, scale=scale),
        grid=(rows, heads),
        in_specs=[wide(0), wide(1), thin, thin, table, table, gain, gain, thin, flat]
        + [wide(0), wide(0), wide(0), total, wide(0)],
        out_specs=[
            wide(0),
            wide(0),
            wide(0),
            pl.BlockSpec((1, 8, length), lambda r, h: (r, 0, 0)),
            pl.BlockSpec((1, 2, head_size), lambda r, h: (r, 0, h)),
        ],
        out_shape=[
            jax.ShapeDtypeStruct(shape, jnp.float32),
            jax.ShapeDtypeStruct(shape, jnp.float32),
            jax.ShapeDtypeStruct(shape, jnp.bfloat16),
            jax.ShapeDtypeStruct((rows, 8, length), jnp.float32),
            jax.ShapeDtypeStruct((rows, 2, heads * head_size), jnp.float32),
        ],
        scratch_shapes=[pltpu.VMEM((length, head_size), jnp.float32)] * 3,
        name="attend_back",
    )(qkv, qkv, *inverses, *tables, *gains, ids[:, :, None], ids[:, None, :], *kept, d_mixed)


def shards_by_feature(
    tokens,
    doc_ids,
    cotangent,
    w_query,
    w_key,
    w_value,
    w_out,
    w_gate,
    w_up,
    w_down,
    g_query,
    g_key,
    g_attn,
    g_ffn,
):
    row_count, piece_len, model_width = tokens.shape
    head_size = HEAD
    feature_count = w_query.shape[1]
    scale = head_size ** (-0.5)
    seq_count = lax.axis_size("seq")
    dp_count = lax.axis_size("dp")
    seq_at = lax.axis_index("seq")
    row_len = piece_len * seq_count
    all_count = row_count * row_len
    tok_count = row_count * piece_len
    own_features = feature_count // seq_count
    own_hidden = w_gate.shape[1] // seq_count
    low = jnp.bfloat16

    def own_piece(tensor):
        view = tensor.reshape(row_count, row_len, -1)
        return lax.dynamic_slice_in_dim(view, seq_at * piece_len, piece_len, 1).reshape(tok_count, -1)

    w_qkv = gather_dp(jnp.concatenate([own_columns(w, 1, seq_count, seq_at) for w in (w_query, w_key, w_value)], 1))
    tokens_all = gather_seq(tokens).reshape(all_count, model_width)
    ids_all = total_seq(
        lax.dynamic_update_slice_in_dim(
            jnp.zeros((row_count, row_len), jnp.int32), doc_ids, seq_at * piece_len, 1
        )
    )
    core = seq_at % 2
    half = model_width // 2
    out_rows = w_out.shape[0]
    out_pieces = pieces_dp(lax.dynamic_slice_in_dim(w_out, core * half, half, 1))
    other_pieces = [(swap(piece, "seq", 1), row) for piece, row in out_pieces]
    wo_full = placed(
        [(w_out, lax.axis_index("dp") * out_rows, 0)]
        + [(piece, row, core * half) for piece, row in out_pieces]
        + [(piece, row, half - core * half) for piece, row in other_pieces],
        (feature_count, model_width),
    )
    w_hidden = gather_dp(jnp.concatenate([own_columns(w, dp_count, seq_count, seq_at) for w in (w_gate, w_up)], 1))
    w_back = gather_dp(
        lax.dynamic_slice_in_dim(
            w_down, seq_at * (own_hidden // dp_count), own_hidden // dp_count, 0
        ),
    )
    gain_query = lax.dynamic_slice_in_dim(g_query, seq_at * own_features, own_features).astype(jnp.float32)
    gain_key = lax.dynamic_slice_in_dim(g_key, seq_at * own_features, own_features).astype(jnp.float32)
    gain_attn = g_attn.astype(jnp.float32)
    gain_ffn = g_ffn.astype(jnp.float32)

    tokens_all, ids_all = lax.optimization_barrier((tokens_all, ids_all))
    qkv = jnp.dot(tokens_all, w_qkv, preferred_element_type=jnp.float32)
    query_pre = qkv[:, :own_features]
    key_pre = qkv[:, own_features : 2 * own_features]
    squares = jnp.stack([jnp.sum(query_pre * query_pre, -1), jnp.sum(key_pre * key_pre, -1)])
    cosine, sine_part = rotation(jnp.arange(row_len, dtype=jnp.int32), head_size)
    tables = jnp.concatenate([cosine, cosine], 1), jnp.concatenate([-sine_part, sine_part], 1)
    inverse = lax.rsqrt(total_seq(squares) / feature_count + eps)
    inverses = [inverse[at].reshape(row_count, row_len, 1) for at in range(2)]
    norm_gains = gain_query[None, :], gain_key[None, :]
    qkv_rows = qkv.reshape(row_count, row_len, 3 * own_features)
    *kept, mixed_low, log_total = attend(
        qkv_rows, inverses, tables, norm_gains, ids_all, head_size, scale
    )
    mixed_low = mixed_low.reshape(all_count, own_features)
    mixed_all = lax.all_gather(mixed_low, "seq", axis=1, tiled=True)
    attn_out = jnp.dot(mixed_all, wo_full, preferred_element_type=jnp.float32)
    attn_inv_all = inverse_rms(attn_out)
    hidden_all = tokens_all.astype(jnp.float32) + attn_out * attn_inv_all * gain_attn
    hidden_low = hidden_all.astype(low)
    attn_inv = own_piece(attn_inv_all)
    attn_unit = own_piece(attn_out) * attn_inv
    hidden_state = tokens.reshape(tok_count, model_width).astype(jnp.float32) + attn_unit * gain_attn

    gate_up = jnp.dot(hidden_low, w_hidden, preferred_element_type=jnp.float32)
    gate, up_proj = gate_up[:, :own_hidden], gate_up[:, own_hidden:]
    sigma = jax.nn.sigmoid(gate)
    active = gate * sigma
    inner_low = (active * up_proj).astype(low)
    branch_part = jnp.dot(inner_low, w_back, preferred_element_type=jnp.float32).astype(low)
    w_hidden_turned, branch_part = stored_turned(w_hidden, branch_part)
    w_back_turned, branch_part = stored_turned(w_back, branch_part)
    branch = (
        scatter_seq(branch_part.reshape(row_count, row_len, model_width))
        .astype(jnp.float32)
        .reshape(tok_count, model_width)
    )
    branch_inv = inverse_rms(branch)
    branch_unit = branch * branch_inv
    result = (
        (hidden_state + branch_unit * gain_ffn)
        .astype(low)
        .reshape(row_count, piece_len, model_width)
    )

    grad_out = cotangent.reshape(tok_count, model_width).astype(jnp.float32)
    ffn_gain_term = jnp.sum(grad_out * branch_unit, 0)
    d_branch = norm_back(grad_out * gain_ffn, branch_unit, branch_inv).astype(low)
    d_branch_all = gather_seq(d_branch.reshape(row_count, piece_len, model_width)).reshape(all_count, model_width)
    d_inner = jnp.dot(d_branch_all, w_back_turned, preferred_element_type=jnp.float32)
    d_gate = (d_inner * up_proj * sigma * (1.0 + gate * (1.0 - sigma))).astype(low)
    d_up = (d_inner * active).astype(low)
    d_gate_up = jnp.concatenate([d_gate, d_up], 1)
    d_hidden_part = jnp.dot(d_gate_up, w_hidden_turned, preferred_element_type=jnp.float32).astype(low)
    d_hidden_sum = scatter_seq(d_hidden_part.reshape(row_count, row_len, model_width))
    gate_part = jnp.einsum("nd,nf->df", hidden_low, d_gate, preferred_element_type=jnp.float32).astype(low)
    up_part = jnp.einsum("nd,nf->df", hidden_low, d_up, preferred_element_type=jnp.float32).astype(low)
    down_part = jnp.einsum("nf,nd->fd", inner_low, d_branch_all, preferred_element_type=jnp.float32).astype(low)
    down_grad = sum_dp(*shares_for(down_part))
    gate_own = sum_dp(*shares_for(gate_part)).astype(low)
    up_own = sum_dp(*shares_for(up_part)).astype(low)
    d_hidden = grad_out + d_hidden_sum.astype(jnp.float32).reshape(tok_count, model_width)

    attn_gain_term = jnp.sum(d_hidden * attn_unit, 0)
    d_attn = norm_back(d_hidden * gain_attn, attn_unit, attn_inv).astype(low)
    d_mixed = jnp.einsum("nd,fd->nf", d_attn, wo_full, preferred_element_type=jnp.float32).astype(low)

    def own_columns_of_all(tensor):
        split = tensor.reshape(row_count, piece_len, seq_count, -1).transpose(2, 0, 1, 3)
        width = split.shape[-1]
        split = lax.all_to_all(split.reshape(seq_count, tok_count, width), "seq", split_axis=0, concat_axis=0)
        split = split.reshape(seq_count, row_count, piece_len, width).transpose(1, 0, 2, 3)
        return split.reshape(row_count, row_len, width)

    d_mixed = own_columns_of_all(d_mixed)
    (gate_grad,) = rows_home(gate_own, dp_count, own_hidden // dp_count)
    (up_grad,) = rows_home(up_own, dp_count, own_hidden // dp_count)

    dq_gained, dk_gained, d_value, dots, gain_terms = attend_back(
        qkv_rows, inverses, tables, norm_gains, ids_all, (*kept, log_total), d_mixed, head_size, scale
    )
    norm_terms = lax.dynamic_update_slice_in_dim(
        jnp.zeros((2, feature_count), jnp.float32), jnp.sum(gain_terms, 0), seq_at * own_features, 1
    )
    dots = dots[:, :2].transpose(1, 0, 2).reshape(-1, LANES)
    stat_rows = dots.shape[0]
    sums = total_seq(
        jnp.concatenate(
            [dots]
            + [part.reshape(-1, LANES) for part in (norm_terms, attn_gain_term, ffn_gain_term)]
        )
    )
    means = sums[:stat_rows].reshape(2, all_count) / feature_count

    def norm_back_wide(gained, pre, at):
        inv = inverse[at][:, None]
        gained = gained.reshape(all_count, own_features)
        return (inv * (gained - pre * inv * means[at][:, None])).astype(low)

    dq_pre = norm_back_wide(dq_gained, query_pre, 0)
    dk_pre = norm_back_wide(dk_gained, key_pre, 1)
    d_value = d_value.reshape(all_count, own_features)
    d_qkv = jnp.concatenate([dq_pre, dk_pre, d_value], 1)
    d_tokens_part = jnp.einsum("nf,df->nd", d_qkv, w_qkv, preferred_element_type=jnp.float32).astype(low)
    d_qkv, d_tokens_part = lax.optimization_barrier((d_qkv, d_tokens_part))
    qkv_part = jnp.einsum("nd,nf->df", tokens_all, d_qkv, preferred_element_type=jnp.float32).astype(low)
    d_attn, qkv_part = lax.optimization_barrier((d_attn, qkv_part))
    d_attn_own = own_columns_of_all(d_attn).reshape(all_count, -1)
    out_part = jnp.einsum("nf,nd->fd", mixed_all, d_attn_own, preferred_element_type=jnp.float32).astype(low)
    out_own = sum_dp(*shares_for(out_part)).astype(low)
    d_tokens_sum = scatter_seq(d_tokens_part.reshape(row_count, row_len, model_width))
    d_tokens = d_hidden + d_tokens_sum.astype(jnp.float32).reshape(tok_count, model_width)
    qkv_own = sum_dp(*shares_for(qkv_part)).astype(low)
    attn_home = rows_home(jnp.concatenate([qkv_own, out_own], 1), 1, own_features)
    share = feature_count // (dp_count * seq_count)
    gains = lax.dynamic_index_in_dim(
        sums[stat_rows:].reshape(4, dp_count, seq_count, share), seq_at, 2, False
    )
    gains = share_dp(gains.transpose(1, 0, 2).reshape(dp_count, 4 * share)).reshape(4, share)
    return (
        result,
        d_tokens.reshape(row_count, piece_len, model_width),
        attn_home[0],
        attn_home[1],
        attn_home[2],
        attn_home[3],
        gate_grad,
        up_grad,
        down_grad,
        gains[0],
        gains[1],
        gains[2],
        gains[3],
    )


def shards(tokens, doc_ids, cotangent, w_query, *rest):
    if w_query.shape[1] // HEAD % lax.axis_size("seq"):
        return shards_by_slab(tokens, doc_ids, cotangent, w_query, *rest)
    return shards_by_feature(tokens, doc_ids, cotangent, w_query, *rest)


def solution(mesh):
    return jax.shard_map(
        shards,
        mesh=mesh,
        in_specs=(
            P("dp", "seq", None),
            P("dp", "seq"),
            P("dp", "seq", None),
            P("dp", None),
            P("dp", None),
            P("dp", None),
            P("dp", None),
            P("dp", None),
            P("dp", None),
            P("dp", None),
            P(),
            P(),
            P(),
            P(),
        ),
        out_specs=(
            P("dp", "seq", None),
            P("dp", "seq", None),
            P(("dp", "seq"), None),
            P(("dp", "seq"), None),
            P(("dp", "seq"), None),
            P(("dp", "seq"), None),
            P(("dp", "seq"), None),
            P(("dp", "seq"), None),
            P(("dp", "seq"), None),
            P(("dp", "seq")),
            P(("dp", "seq")),
            P(("dp", "seq")),
            P(("dp", "seq")),
        ),
        check_vma=False,
    )
```

```python
import functools

import jax
import jax.numpy as jnp
from jax import lax
from jax.experimental import pallas as pl
from jax.experimental.layout import Layout, with_layout_constraint
from jax.experimental.pallas import tpu as pltpu
from jax.sharding import PartitionSpec as P


HEAD = 128
SLABS = 4
LANES = 128


eps = 1e-06
theta = 500000.0


def rotation(positions, head_size):
    half_size = head_size // 2
    frequency = theta ** (-(2.0 * jnp.arange(half_size, dtype=jnp.float32)) / head_size)
    angles = positions.astype(jnp.float32)[:, None] * frequency[None, :]
    return (jnp.cos(angles), jnp.sin(angles))


def rotate(tensor, cosine, sine_part):
    half_size = tensor.shape[-1] // 2
    first_half = tensor[..., :half_size]
    second_half = tensor[..., half_size:]
    cos_wide = cosine[:, None, :]
    sin_wide = sine_part[:, None, :]
    return jnp.concatenate(
        [
            first_half * cos_wide - second_half * sin_wide,
            second_half * cos_wide + first_half * sin_wide,
        ],
        -1,
    )


def unrotate(tensor, cosine, sine_part):
    half_size = tensor.shape[-1] // 2
    first_half = tensor[..., :half_size]
    second_half = tensor[..., half_size:]
    cos_wide = cosine[:, None, :]
    sin_wide = sine_part[:, None, :]
    return jnp.concatenate(
        [
            first_half * cos_wide + second_half * sin_wide,
            second_half * cos_wide - first_half * sin_wide,
        ],
        -1,
    )


def inverse_rms(tensor):
    return lax.rsqrt(jnp.mean(tensor * tensor, -1, keepdims=True) + eps)


def norm_back(grad_unit, unit_vec, inverse):
    return inverse * (grad_unit - unit_vec * jnp.mean(grad_unit * unit_vec, -1, keepdims=True))


def visible(own_ids, key_ids, query_at, key_at):
    causal = key_at[None, :] <= query_at[:, None]
    same_doc = own_ids[:, :, None] == key_ids[:, None, :]
    return (causal[None] & same_doc)[:, None]


def masked_scores(query_low, pair_all, allowed, head_count, head_size):
    row_count = pair_all.shape[0]
    row_length = pair_all.shape[1]
    feature_count = head_count * head_size
    key_rows = pair_all[..., :feature_count].reshape(row_count, row_length, head_count, head_size)
    value_rows = pair_all[..., feature_count:].reshape(row_count, row_length, head_count, head_size)
    scores = jnp.einsum(
        "rche,rlhe->rhcl", query_low, key_rows, preferred_element_type=jnp.float32
    ) * head_size ** (-0.5)
    return (jnp.where(allowed, scores, -1e30), key_rows, value_rows)


def columns_of(matrix, parts, slab_count, index):
    lead = matrix.shape[0]
    width = matrix.shape[1] // (parts * slab_count)
    return matrix.reshape(lead, parts, slab_count, width)[:, :, index].reshape(lead, parts * width)


def entries_of(vector, parts, slab_count, index):
    width = vector.shape[0] // (parts * slab_count)
    return vector.reshape(parts, slab_count, width)[:, index].reshape(parts * width)


def shards_by_slab(
    tokens,
    doc_ids,
    cotangent,
    w_query,
    w_key,
    w_value,
    w_out,
    w_gate,
    w_up,
    w_down,
    g_query,
    g_key,
    g_attn,
    g_ffn,
):
    row_count, piece_len, model_width = tokens.shape
    head_size = HEAD
    feature_count = w_query.shape[1]
    head_count = feature_count // head_size
    tok_count = row_count * piece_len
    scale = head_size ** (-0.5)
    seq_count = lax.axis_size("seq")
    parts = lax.axis_size("dp") * seq_count
    slab_count = SLABS
    gather_all = (
        lax.all_gather(w_query, "dp", axis=0, tiled=True),
        lax.all_gather(w_key, "dp", axis=0, tiled=True),
        lax.all_gather(w_value, "dp", axis=0, tiled=True),
        lax.all_gather(w_out, "dp", axis=0, tiled=True),
        lax.all_gather(w_gate, "dp", axis=0, tiled=True),
        lax.all_gather(w_up, "dp", axis=0, tiled=True),
        lax.all_gather(w_down, "dp", axis=0, tiled=True),
    )
    wq_full, wk_full, wv_full, wo_full, wg_full, wu_full, wd_full = gather_all
    gain_query = g_query.astype(jnp.float32)
    gain_key = g_key.astype(jnp.float32)
    gain_attn = g_attn.astype(jnp.float32)
    gain_ffn = g_ffn.astype(jnp.float32)
    flat_tokens = tokens.reshape(tok_count, model_width)
    query_pre = jnp.dot(flat_tokens, wq_full, preferred_element_type=jnp.float32)
    key_pre = jnp.dot(flat_tokens, wk_full, preferred_element_type=jnp.float32)
    value_pre = jnp.dot(flat_tokens, wv_full, preferred_element_type=jnp.float32)
    query_inv = inverse_rms(query_pre)
    query_unit = query_pre * query_inv
    key_inv = inverse_rms(key_pre)
    key_unit = key_pre * key_inv
    first_row = lax.axis_index("seq") * piece_len
    positions = first_row + jnp.tile(jnp.arange(piece_len, dtype=jnp.int32), row_count)
    cosine, sine_part = rotation(positions, head_size)
    query_rot = rotate(
        (query_unit * gain_query).reshape(tok_count, head_count, head_size), cosine, sine_part
    )
    key_rot = rotate(
        (key_unit * gain_key).reshape(tok_count, head_count, head_size), cosine, sine_part
    )
    query_low = query_rot.astype(jnp.bfloat16).reshape(row_count, piece_len, head_count, head_size)
    key_low = key_rot.astype(jnp.bfloat16).reshape(row_count, piece_len, feature_count)
    value_low = value_pre.astype(jnp.bfloat16).reshape(row_count, piece_len, feature_count)
    pair_low = jnp.concatenate([key_low, value_low], -1)
    ids_low = doc_ids.astype(jnp.bfloat16)
    pair_all, ids_all = (
        lax.all_gather(pair_low, "seq", axis=1, tiled=True),
        lax.all_gather(ids_low, "seq", axis=1, tiled=True),
    )
    query_at = first_row + jnp.arange(piece_len, dtype=jnp.int32)
    allowed = visible(ids_low, ids_all, query_at, jnp.arange(pair_all.shape[1], dtype=jnp.int32))
    masked, _, value_rows = masked_scores(
        query_low, pair_all, allowed, head_count, head_size
    )
    row_max = jnp.max(masked, -1, keepdims=True)
    log_total = jnp.log(jnp.sum(jnp.exp(masked - row_max), -1, keepdims=True)) + row_max
    probs_low = jnp.exp(masked - log_total).astype(jnp.bfloat16)
    mixed = jnp.einsum("rhcl,rlhe->rche", probs_low, value_rows, preferred_element_type=jnp.float32)
    mixed_low = mixed.reshape(tok_count, feature_count).astype(jnp.bfloat16)
    attn_out = jnp.dot(mixed_low, wo_full, preferred_element_type=jnp.float32)
    attn_inv = inverse_rms(attn_out)
    attn_unit = attn_out * attn_inv
    hidden_state = flat_tokens.astype(jnp.float32) + attn_unit * gain_attn
    hidden_low = hidden_state.astype(jnp.bfloat16)
    gate = jnp.dot(hidden_low, wg_full, preferred_element_type=jnp.float32)
    up_proj = jnp.dot(hidden_low, wu_full, preferred_element_type=jnp.float32)
    sigma = jax.nn.sigmoid(gate)
    active = gate * sigma
    inner_low = (active * up_proj).astype(jnp.bfloat16)
    branch = jnp.dot(inner_low, wd_full, preferred_element_type=jnp.float32)
    branch_inv = inverse_rms(branch)
    branch_unit = branch * branch_inv
    result = (
        (hidden_state + branch_unit * gain_ffn)
        .astype(jnp.bfloat16)
        .reshape(row_count, piece_len, model_width)
    )
    wq_back, wk_back, wv_back, wo_back, wg_back, wu_back, wd_back = gather_all
    pair_back, ids_back = (pair_all, ids_all)
    grad_out = cotangent.reshape(tok_count, model_width).astype(jnp.float32)
    ffn_gain_term = jnp.sum(grad_out * branch_unit, 0)
    d_branch = norm_back(grad_out * gain_ffn, branch_unit, branch_inv).astype(jnp.bfloat16)
    d_inner = jnp.einsum("nd,fd->nf", d_branch, wd_back, preferred_element_type=jnp.float32)
    d_gate = (d_inner * up_proj * sigma * (1.0 + gate * (1.0 - sigma))).astype(jnp.bfloat16)
    d_up = (d_inner * active).astype(jnp.bfloat16)
    d_hidden = grad_out + jnp.einsum(
        "nf,df->nd", d_gate, wg_back, preferred_element_type=jnp.float32
    )
    d_hidden = d_hidden + jnp.einsum("nf,df->nd", d_up, wu_back, preferred_element_type=jnp.float32)
    mlp_shares = []
    for index in range(slab_count):
        hidden_part = columns_of(hidden_low, parts, slab_count, index)
        inner_part = columns_of(inner_low, parts, slab_count, index)
        gate_term = jnp.einsum("nd,nf->df", hidden_part, d_gate, preferred_element_type=jnp.float32)
        up_term = jnp.einsum("nd,nf->df", hidden_part, d_up, preferred_element_type=jnp.float32)
        down_term = jnp.einsum(
            "nf,nd->fd", inner_part, d_branch, preferred_element_type=jnp.float32
        )
        ffn_term = entries_of(ffn_gain_term, parts, slab_count, index)
        shares = (
            lax.psum_scatter(down_term, ("dp", "seq"), scatter_dimension=0, tiled=True),
            lax.psum_scatter(gate_term, ("dp", "seq"), scatter_dimension=0, tiled=True),
            lax.psum_scatter(up_term, ("dp", "seq"), scatter_dimension=0, tiled=True),
            lax.psum_scatter(ffn_term, ("dp", "seq"), scatter_dimension=0, tiled=True),
        )
        mlp_shares.append(shares)
    down_grad = jnp.concatenate([s[0] for s in mlp_shares], 0)
    gate_grad = jnp.concatenate([s[1] for s in mlp_shares], 0)
    up_grad = jnp.concatenate([s[2] for s in mlp_shares], 0)
    ffn_grad = jnp.concatenate([s[3] for s in mlp_shares], 0)
    attn_gain_term = jnp.sum(d_hidden * attn_unit, 0)
    d_attn = norm_back(d_hidden * gain_attn, attn_unit, attn_inv).astype(jnp.bfloat16)
    d_mixed = jnp.einsum("nd,fd->nf", d_attn, wo_back, preferred_element_type=jnp.float32).astype(
        jnp.bfloat16
    )
    d_mixed = d_mixed.reshape(row_count, piece_len, head_count, head_size)
    sub_len = piece_len // slab_count
    pair_width = pair_back.shape[-1]
    pair_view = pair_back.reshape(row_count, seq_count, slab_count, sub_len, pair_width)
    ids_view = ids_back.reshape(row_count, seq_count, slab_count, sub_len)

    def slab_scores(index):
        pair_part = pair_view[:, :, index].reshape(row_count, seq_count * sub_len, pair_width)
        ids_part = ids_view[:, :, index].reshape(row_count, seq_count * sub_len)
        key_at = (
            jnp.arange(seq_count, dtype=jnp.int32)[:, None] * piece_len
            + index * sub_len
            + jnp.arange(sub_len, dtype=jnp.int32)[None, :]
        ).reshape(seq_count * sub_len)
        allowed_part = visible(ids_low, ids_part, query_at, key_at)
        masked_part, key_part, value_part = masked_scores(
            query_low, pair_part, allowed_part, head_count, head_size
        )
        probs_part = jnp.exp(masked_part - log_total)
        d_probs_part = jnp.einsum(
            "rche,rlhe->rhcl", d_mixed, value_part, preferred_element_type=jnp.float32
        )
        return (probs_part, d_probs_part, key_part)

    row_dot = jnp.zeros((row_count, head_count, piece_len, 1), jnp.float32)
    for index in range(slab_count):
        probs_part, d_probs_part, key_part = slab_scores(index)
        row_dot = row_dot + jnp.sum(probs_part * d_probs_part, -1, keepdims=True)
    query_acc = jnp.zeros((row_count, piece_len, head_count, head_size), jnp.float32)
    pair_shares = []
    for index in range(slab_count):
        probs_part, d_probs_part, key_part = slab_scores(index)
        d_scores = (probs_part * (d_probs_part - row_dot)).astype(jnp.bfloat16)
        query_acc = query_acc + jnp.einsum(
            "rhcl,rlhe->rche", d_scores, key_part, preferred_element_type=jnp.float32
        )
        key_term = (
            jnp.einsum("rhcl,rche->rlhe", d_scores, query_low, preferred_element_type=jnp.float32)
            * scale
        )
        value_term = jnp.einsum(
            "rhcl,rche->rlhe",
            probs_part.astype(jnp.bfloat16),
            d_mixed,
            preferred_element_type=jnp.float32,
        )
        key_count = seq_count * sub_len
        pair_term = jnp.concatenate(
            [
                key_term.reshape(row_count, key_count, feature_count),
                value_term.reshape(row_count, key_count, feature_count),
            ],
            -1,
        )
        pair_shares.append(
            lax.psum_scatter(
                pair_term.astype(jnp.bfloat16), "seq", scatter_dimension=1, tiled=True
            ).astype(jnp.float32)
        )
    pair_grad = jnp.concatenate(pair_shares, 1)
    d_query = (query_acc * scale).astype(jnp.bfloat16)
    d_key = (
        pair_grad[..., :feature_count]
        .astype(jnp.bfloat16)
        .reshape(tok_count, head_count, head_size)
    )
    d_value = pair_grad[..., feature_count:].astype(jnp.bfloat16).reshape(tok_count, feature_count)
    dq_norm = unrotate(
        d_query.reshape(tok_count, head_count, head_size).astype(jnp.float32), cosine, sine_part
    ).reshape(tok_count, feature_count)
    dk_norm = unrotate(d_key.astype(jnp.float32), cosine, sine_part).reshape(
        tok_count, feature_count
    )
    query_gain_term = jnp.sum(dq_norm * query_unit, 0)
    key_gain_term = jnp.sum(dk_norm * key_unit, 0)
    dq_pre = norm_back(dq_norm * gain_query, query_unit, query_inv).astype(jnp.bfloat16)
    dk_pre = norm_back(dk_norm * gain_key, key_unit, key_inv).astype(jnp.bfloat16)
    d_tokens = d_hidden + jnp.einsum(
        "nf,df->nd", dq_pre, wq_back, preferred_element_type=jnp.float32
    )
    d_tokens = d_tokens + jnp.einsum(
        "nf,df->nd", dk_pre, wk_back, preferred_element_type=jnp.float32
    )
    d_tokens = d_tokens + jnp.einsum(
        "nf,df->nd", d_value, wv_back, preferred_element_type=jnp.float32
    )
    attn_shares = []
    for index in range(slab_count):
        token_part = columns_of(flat_tokens, parts, slab_count, index)
        mixed_part = columns_of(mixed_low, parts, slab_count, index)
        query_term = jnp.einsum("nd,nf->df", token_part, dq_pre, preferred_element_type=jnp.float32)
        key_wterm = jnp.einsum("nd,nf->df", token_part, dk_pre, preferred_element_type=jnp.float32)
        value_wterm = jnp.einsum(
            "nd,nf->df", token_part, d_value, preferred_element_type=jnp.float32
        )
        out_term = jnp.einsum("nf,nd->fd", mixed_part, d_attn, preferred_element_type=jnp.float32)
        gq_term = entries_of(query_gain_term, parts, slab_count, index)
        gk_term = entries_of(key_gain_term, parts, slab_count, index)
        ga_term = entries_of(attn_gain_term, parts, slab_count, index)
        shares = (
            lax.psum_scatter(query_term, ("dp", "seq"), scatter_dimension=0, tiled=True),
            lax.psum_scatter(key_wterm, ("dp", "seq"), scatter_dimension=0, tiled=True),
            lax.psum_scatter(value_wterm, ("dp", "seq"), scatter_dimension=0, tiled=True),
            lax.psum_scatter(out_term, ("dp", "seq"), scatter_dimension=0, tiled=True),
            lax.psum_scatter(gq_term, ("dp", "seq"), scatter_dimension=0, tiled=True),
            lax.psum_scatter(gk_term, ("dp", "seq"), scatter_dimension=0, tiled=True),
            lax.psum_scatter(ga_term, ("dp", "seq"), scatter_dimension=0, tiled=True),
        )
        attn_shares.append(shares)
    query_grad = jnp.concatenate([s[0] for s in attn_shares], 0)
    key_grad = jnp.concatenate([s[1] for s in attn_shares], 0)
    value_grad = jnp.concatenate([s[2] for s in attn_shares], 0)
    out_grad = jnp.concatenate([s[3] for s in attn_shares], 0)
    gq_grad = jnp.concatenate([s[4] for s in attn_shares], 0)
    gk_grad = jnp.concatenate([s[5] for s in attn_shares], 0)
    ga_grad = jnp.concatenate([s[6] for s in attn_shares], 0)
    tokens_grad = d_tokens.reshape(row_count, piece_len, model_width)
    return (
        result,
        tokens_grad,
        query_grad,
        key_grad,
        value_grad,
        out_grad,
        gate_grad,
        up_grad,
        down_grad,
        gq_grad,
        gk_grad,
        ga_grad,
        ffn_grad,
    )


def own_columns(matrix, groups, parts, index):
    width = matrix.shape[1] // (groups * parts)
    pieces = [
        lax.dynamic_slice_in_dim(matrix, (group * parts + index) * width, width, 1)
        for group in range(groups)
    ]
    return jnp.concatenate(pieces, 1) if groups > 1 else pieces[0]


def gather_seq(piece):
    return lax.all_gather(piece, "seq", axis=1, tiled=True)


def scatter_seq(partial):
    return lax.psum_scatter(partial, "seq", scatter_dimension=1, tiled=True)


def swap(value, axis, flip):
    return lax.ppermute(value, axis, [(at, at ^ flip) for at in range(lax.axis_size(axis))])


def place_kernel(spots_ref, *refs, count):
    in_refs, (out_ref, sems) = refs[:count], refs[-2:]
    copies = []
    for at, in_ref in enumerate(in_refs):
        rows, width = in_ref.shape
        row = pl.multiple_of(spots_ref[2 * at], LANES)
        column = pl.multiple_of(spots_ref[2 * at + 1], LANES)
        copies.append(
            pltpu.make_async_copy(
                in_ref, out_ref.at[pl.ds(row, rows), pl.ds(column, width)], sems.at[at]
            )
        )
    for copy in copies:
        copy.start()
    for copy in copies:
        copy.wait()


def placed(pieces, shape, whole=None):
    spots = jnp.stack([jnp.int32(at) for _, row, column in pieces for at in (row, column)])
    outside = pl.BlockSpec(memory_space=pl.ANY)
    given = [] if whole is None else [whole]
    return pl.pallas_call(
        functools.partial(place_kernel, count=len(pieces)),
        grid_spec=pltpu.PrefetchScalarGridSpec(
            num_scalar_prefetch=1,
            grid=(1,),
            in_specs=[
                pl.BlockSpec(piece.shape, lambda at, spots: (0, 0), pipeline_mode=pl.Buffered(1))
                for piece, _, _ in pieces
            ]
            + [outside] * len(given),
            out_specs=outside,
            scratch_shapes=[pltpu.SemaphoreType.DMA((len(pieces),))],
        ),
        out_shape=jax.ShapeDtypeStruct(shape, pieces[0][0].dtype),
        input_output_aliases={1 + len(pieces): 0} if given else {},
        name="place",
    )(spots, *[piece for piece, _, _ in pieces], *given)


def pieces_for(value, name, split_axis):
    count, index = lax.axis_size(name), lax.axis_index(name)
    width = value.shape[split_axis] // count
    return [
        lax.dynamic_slice_in_dim(value, (index ^ flip) * width, width, split_axis)
        for flip in range(count)
    ]


def swapped(pieces, name):
    return [swap(piece, name, flip) if flip else piece for flip, piece in enumerate(pieces)]


def exchanged(value, name, split_axis):
    return swapped(pieces_for(value, name, split_axis), name)


def pieces_dp(piece):
    half = piece.shape[0] // 2
    first, second = swap(piece, "dp", 1), swap(piece, "dp", 2)
    top, bottom = swap(first[:half], "dp", 2), swap(second[half:], "dp", 1)
    index = lax.axis_index("dp")
    width = piece.shape[0]
    far = (index ^ 3) * width
    return [
        (first, (index ^ 1) * width),
        (second, (index ^ 2) * width),
        (top, far),
        (bottom, far + half),
    ]


def gather_dp(piece):
    rows, width = piece.shape
    pieces = [(piece, lax.axis_index("dp") * rows), *pieces_dp(piece)]
    pieces = [(part, row, 0) for part, row in pieces]
    whole = placed(pieces[:3], (4 * rows, width))
    return placed(pieces[3:], (4 * rows, width), whole)


def sum_dp(sent, kept):
    got = swap(sent[0], "dp", 1), swap(sent[1], "dp", 2)
    wide = [(kept[at].astype(jnp.float32) + got[at].astype(jnp.float32)) for at in range(2)]
    onward = [side[1].astype(jnp.bfloat16) for side in wide]
    last = swap(onward[0], "dp", 2), swap(onward[1], "dp", 1)
    return jnp.concatenate(
        [wide[at][0] + last[at].astype(jnp.float32) for at in range(2)], 0
    )


def shares_for(partial):
    index = lax.axis_index("dp")
    width = partial.shape[0] // 4
    half = width // 2

    def part(flip, side):
        return lax.dynamic_slice_in_dim(partial, (index ^ flip) * width + side * half, half, 0)

    sent = [jnp.stack([part(1, 0), part(3, 0)]), jnp.stack([part(2, 1), part(3, 1)])]
    kept = [jnp.stack([part(0, 0), part(2, 0)]), jnp.stack([part(0, 1), part(1, 1)])]
    return sent, kept


def stored_turned(matrix, after):
    matrix, after = lax.optimization_barrier((matrix, after))
    return with_layout_constraint(matrix.T, Layout((0, 1))), after


def total_seq(value):
    shape = value.shape
    value = value.reshape(-1, LANES)
    flip = 1
    while flip < lax.axis_size("seq"):
        value = value + swap(value, "seq", flip)
        flip *= 2
    return value.reshape(shape)


def share_dp(rows):
    flip = lax.axis_size("dp") // 2
    while flip:
        halves = rows.reshape(2, rows.shape[0] // 2, rows.shape[1])
        side = lax.axis_index("dp") // flip % 2
        kept = lax.dynamic_index_in_dim(halves, side, 0, False)
        sent = lax.dynamic_index_in_dim(halves, 1 - side, 0, False)
        rows = kept + swap(sent, "dp", flip)
        flip //= 2
    return rows[0]


def settle_kernel(index_ref, *refs, groups, width, count):
    in_refs, out_refs = refs[:count], refs[count:]
    for flip, in_ref in enumerate(in_refs):
        source = index_ref[0] ^ flip
        for at, out_ref in enumerate(out_refs):
            for group in range(groups):
                column = (at * groups + group) * width
                place = pl.multiple_of((group * count + source) * width, width)
                out_ref[:, pl.ds(place, width)] = in_ref[:, column : column + width].astype(jnp.float32)


def rows_home(summed, groups, width):
    pieces = exchanged(summed, "seq", 0)
    count = len(pieces)
    rows, total = pieces[0].shape
    outs = total // (groups * width)
    step = min(16, rows)
    wide = count * groups * width
    return pl.pallas_call(
        functools.partial(settle_kernel, groups=groups, width=width, count=count),
        grid_spec=pltpu.PrefetchScalarGridSpec(
            num_scalar_prefetch=1,
            grid=(rows // step,),
            in_specs=[pl.BlockSpec((step, total), lambda r, index: (r, 0))] * count,
            out_specs=[pl.BlockSpec((step, wide), lambda r, index: (r, 0))] * outs,
        ),
        out_shape=[jax.ShapeDtypeStruct((rows, wide), jnp.float32)] * outs,
        name="settle",
    )(lax.axis_index("seq").reshape(1), *pieces)


QUERY_BLOCK = 256


def attention_masks(ids_col, ids_row, block, width, start):
    rows = start + lax.broadcasted_iota(jnp.int32, (block, width), 0)
    columns = lax.broadcasted_iota(jnp.int32, (block, width), 1)
    return (columns <= rows) & (ids_col[start : start + block] == ids_row[:, :width])


def attend_kernel(
    q_ref, k_ref, v_ref, qinv_ref, kinv_ref, cos_ref, sin_ref, gq_ref, gk_ref, col_ref, row_ref,
    qlow_ref, klow_ref, vlow_ref, mixed_ref, total_ref, *, scale
):
    low = jnp.bfloat16
    half = q_ref.shape[-1] // 2
    cosine, sine_part = cos_ref[...], sin_ref[...]

    def rotated(ref, inv_ref, gain_ref):
        value = ref[0] * inv_ref[0] * gain_ref[...]
        return (value * cosine + pltpu.roll(value, half, 1) * sine_part).astype(low)

    qlow_ref[0] = rotated(q_ref, qinv_ref, gq_ref)
    klow_ref[0] = rotated(k_ref, kinv_ref, gk_ref)
    vlow_ref[0] = v_ref[0].astype(low)
    length = q_ref.shape[1]
    block = min(QUERY_BLOCK, length)
    ids_col, ids_row = col_ref[0], row_ref[0]
    for start in range(0, length, block):
        width = start + block
        scores = lax.dot_general(
            qlow_ref[0, start:width], klow_ref[0, :width], (((1,), (1,)), ((), ())),
            preferred_element_type=jnp.float32,
        ) * scale
        allowed = attention_masks(ids_col, ids_row, block, width, start)
        masked = jnp.where(allowed, scores, -1e30)
        row_max = jnp.max(masked, -1, keepdims=True)
        log_total = jnp.log(jnp.sum(jnp.exp(masked - row_max), -1, keepdims=True)) + row_max
        total_ref[0, 0, start:width] = log_total
        probs = jnp.exp(masked - log_total).astype(low)
        mixed_ref[0, start:width] = jnp.dot(
            probs, vlow_ref[0, :width], preferred_element_type=jnp.float32
        ).astype(low)


def attend_back_kernel(
    q_ref, k_ref, qinv_ref, kinv_ref, cos_ref, sin_ref, gq_ref, gk_ref, col_ref, row_ref,
    qlow_ref, klow_ref, vlow_ref, total_ref, dmixed_ref,
    dq_ref, dk_ref, dv_ref, dots_ref, gains_ref, key_acc, value_acc, query_acc, *, scale
):
    low = jnp.bfloat16
    half = q_ref.shape[-1] // 2
    length = q_ref.shape[1]
    block = min(QUERY_BLOCK, length)
    ids_col, ids_row = col_ref[0], row_ref[0]
    turned = (((0,), (0,)), ((), ()))
    across = (((1,), (1,)), ((), ()))
    key_acc[...] = jnp.zeros_like(key_acc)
    value_acc[...] = jnp.zeros_like(value_acc)
    for start in range(0, length, block):
        width = start + block
        query = qlow_ref[0, start:width]
        d_mixed = dmixed_ref[0, start:width]
        keys = klow_ref[0, :width]
        scores = lax.dot_general(query, keys, across, preferred_element_type=jnp.float32) * scale
        allowed = attention_masks(ids_col, ids_row, block, width, start)
        probs = jnp.exp(jnp.where(allowed, scores, -1e30) - total_ref[0, 0, start:width])
        d_probs = lax.dot_general(
            d_mixed, vlow_ref[0, :width], across, preferred_element_type=jnp.float32
        )
        row_dot = jnp.sum(probs * d_probs, -1, keepdims=True)
        d_scores = (probs * (d_probs - row_dot)).astype(low)
        query_acc[start:width] = jnp.dot(d_scores, keys, preferred_element_type=jnp.float32)
        key_acc[:width] += lax.dot_general(d_scores, query, turned, preferred_element_type=jnp.float32)
        value_acc[:width] += lax.dot_general(
            probs.astype(low), d_mixed, turned, preferred_element_type=jnp.float32
        )
    dv_ref[0] = value_acc[...].astype(low)
    cosine, sine_part = cos_ref[...], sin_ref[...]

    def turned_back(acc, ref, inv_ref, gain_ref, out_ref, at):
        value = (acc[...] * scale).astype(low).astype(jnp.float32)
        value = value * cosine - pltpu.roll(value, half, 1) * sine_part
        unit = ref[0] * inv_ref[0]
        gains_ref[0, at : at + 1] = jnp.sum(value * unit, 0, keepdims=True)
        value = value * gain_ref[...]
        out_ref[0] = value
        return jnp.sum(value * unit, -1, keepdims=True)

    query_dot = turned_back(query_acc, q_ref, qinv_ref, gq_ref, dq_ref, 0)
    key_dot = turned_back(key_acc, k_ref, kinv_ref, gk_ref, dk_ref, 1)
    lane = lax.broadcasted_iota(jnp.int32, (length, LANES), 1)
    dots = jnp.where(lane == 0, query_dot, jnp.where(lane == 1, key_dot, 0.0)).T[:8]

    @pl.when(pl.program_id(1) == 0)
    def _():
        dots_ref[0] = dots

    @pl.when(pl.program_id(1) != 0)
    def _():
        dots_ref[0] += dots


def attention_specs(length, heads, head_size):
    wide = lambda at: pl.BlockSpec((1, length, head_size), lambda r, h, at=at: (r, 0, at * heads + h))
    thin = pl.BlockSpec((1, length, 1), lambda r, h: (r, 0, 0))
    table = pl.BlockSpec((length, head_size), lambda r, h: (0, 0))
    gain = pl.BlockSpec((1, head_size), lambda r, h: (0, h))
    flat = pl.BlockSpec((1, 1, length), lambda r, h: (r, 0, 0))
    total = pl.BlockSpec((1, 1, length, 1), lambda r, h: (r, h, 0, 0))
    return wide, thin, table, gain, flat, total


def attend(qkv, inverses, tables, gains, ids, head_size, scale):
    rows, length, width = qkv.shape
    heads = width // (3 * head_size)
    wide, thin, table, gain, flat, total = attention_specs(length, heads, head_size)
    narrow = jax.ShapeDtypeStruct((rows, length, heads * head_size), jnp.bfloat16)
    return pl.pallas_call(
        functools.partial(attend_kernel, scale=scale),
        grid=(rows, heads),
        in_specs=[wide(0), wide(1), wide(2), thin, thin, table, table, gain, gain, thin, flat],
        out_specs=[wide(0), wide(0), wide(0), wide(0), total],
        out_shape=[narrow] * 4 + [jax.ShapeDtypeStruct((rows, heads, length, 1), jnp.float32)],
        name="attend",
    )(qkv, qkv, qkv, *inverses, *tables, *gains, ids[:, :, None], ids[:, None, :])


def attend_back(qkv, inverses, tables, gains, ids, kept, d_mixed, head_size, scale):
    rows, length, width = qkv.shape
    heads = width // (3 * head_size)
    wide, thin, table, gain, flat, total = attention_specs(length, heads, head_size)
    shape = (rows, length, heads * head_size)
    return pl.pallas_call(
        functools.partial(attend_back_kernel, scale=scale),
        grid=(rows, heads),
        in_specs=[wide(0), wide(1), thin, thin, table, table, gain, gain, thin, flat]
        + [wide(0), wide(0), wide(0), total, wide(0)],
        out_specs=[
            wide(0),
            wide(0),
            wide(0),
            pl.BlockSpec((1, 8, length), lambda r, h: (r, 0, 0)),
            pl.BlockSpec((1, 2, head_size), lambda r, h: (r, 0, h)),
        ],
        out_shape=[
            jax.ShapeDtypeStruct(shape, jnp.float32),
            jax.ShapeDtypeStruct(shape, jnp.float32),
            jax.ShapeDtypeStruct(shape, jnp.bfloat16),
            jax.ShapeDtypeStruct((rows, 8, length), jnp.float32),
            jax.ShapeDtypeStruct((rows, 2, heads * head_size), jnp.float32),
        ],
        scratch_shapes=[pltpu.VMEM((length, head_size), jnp.float32)] * 3,
        name="attend_back",
    )(qkv, qkv, *inverses, *tables, *gains, ids[:, :, None], ids[:, None, :], *kept, d_mixed)


def shards_by_feature(
    tokens,
    doc_ids,
    cotangent,
    w_query,
    w_key,
    w_value,
    w_out,
    w_gate,
    w_up,
    w_down,
    g_query,
    g_key,
    g_attn,
    g_ffn,
):
    row_count, piece_len, model_width = tokens.shape
    head_size = HEAD
    feature_count = w_query.shape[1]
    scale = head_size ** (-0.5)
    seq_count = lax.axis_size("seq")
    dp_count = lax.axis_size("dp")
    seq_at = lax.axis_index("seq")
    row_len = piece_len * seq_count
    all_count = row_count * row_len
    tok_count = row_count * piece_len
    own_features = feature_count // seq_count
    own_hidden = w_gate.shape[1] // seq_count
    low = jnp.bfloat16

    def own_piece(tensor):
        view = tensor.reshape(row_count, row_len, -1)
        return lax.dynamic_slice_in_dim(view, seq_at * piece_len, piece_len, 1).reshape(tok_count, -1)

    w_qkv = gather_dp(jnp.concatenate([own_columns(w, 1, seq_count, seq_at) for w in (w_query, w_key, w_value)], 1))
    tokens_all = gather_seq(tokens).reshape(all_count, model_width)
    ids_all = total_seq(
        lax.dynamic_update_slice_in_dim(
            jnp.zeros((row_count, row_len), jnp.int32), doc_ids, seq_at * piece_len, 1
        )
    )
    core = seq_at % 2
    half = model_width // 2
    out_rows = w_out.shape[0]
    out_pieces = pieces_dp(lax.dynamic_slice_in_dim(w_out, core * half, half, 1))
    other_pieces = [(swap(piece, "seq", 1), row) for piece, row in out_pieces]
    wo_full = placed(
        [(w_out, lax.axis_index("dp") * out_rows, 0)]
        + [(piece, row, core * half) for piece, row in out_pieces]
        + [(piece, row, half - core * half) for piece, row in other_pieces],
        (feature_count, model_width),
    )
    w_hidden = gather_dp(jnp.concatenate([own_columns(w, dp_count, seq_count, seq_at) for w in (w_gate, w_up)], 1))
    w_back = gather_dp(
        lax.dynamic_slice_in_dim(
            w_down, seq_at * (own_hidden // dp_count), own_hidden // dp_count, 0
        ),
    )
    gain_query = lax.dynamic_slice_in_dim(g_query, seq_at * own_features, own_features).astype(jnp.float32)
    gain_key = lax.dynamic_slice_in_dim(g_key, seq_at * own_features, own_features).astype(jnp.float32)
    gain_attn = g_attn.astype(jnp.float32)
    gain_ffn = g_ffn.astype(jnp.float32)

    tokens_all, ids_all = lax.optimization_barrier((tokens_all, ids_all))
    qkv = jnp.dot(tokens_all, w_qkv, preferred_element_type=jnp.float32)
    query_pre = qkv[:, :own_features]
    key_pre = qkv[:, own_features : 2 * own_features]
    squares = jnp.stack([jnp.sum(query_pre * query_pre, -1), jnp.sum(key_pre * key_pre, -1)])
    cosine, sine_part = rotation(jnp.arange(row_len, dtype=jnp.int32), head_size)
    tables = jnp.concatenate([cosine, cosine], 1), jnp.concatenate([-sine_part, sine_part], 1)
    inverse = lax.rsqrt(total_seq(squares) / feature_count + eps)
    inverses = [inverse[at].reshape(row_count, row_len, 1) for at in range(2)]
    norm_gains = gain_query[None, :], gain_key[None, :]
    qkv_rows = qkv.reshape(row_count, row_len, 3 * own_features)
    *kept, mixed_low, log_total = attend(
        qkv_rows, inverses, tables, norm_gains, ids_all, head_size, scale
    )
    mixed_low = mixed_low.reshape(all_count, own_features)
    mixed_all = lax.all_gather(mixed_low, "seq", axis=1, tiled=True)
    attn_out = jnp.dot(mixed_all, wo_full, preferred_element_type=jnp.float32)
    attn_inv_all = inverse_rms(attn_out)
    hidden_all = tokens_all.astype(jnp.float32) + attn_out * attn_inv_all * gain_attn
    hidden_low = hidden_all.astype(low)
    attn_inv = own_piece(attn_inv_all)
    attn_unit = own_piece(attn_out) * attn_inv
    hidden_state = tokens.reshape(tok_count, model_width).astype(jnp.float32) + attn_unit * gain_attn

    gate_up = jnp.dot(hidden_low, w_hidden, preferred_element_type=jnp.float32)
    gate, up_proj = gate_up[:, :own_hidden], gate_up[:, own_hidden:]
    sigma = jax.nn.sigmoid(gate)
    active = gate * sigma
    inner_low = (active * up_proj).astype(low)
    branch_part = jnp.dot(inner_low, w_back, preferred_element_type=jnp.float32).astype(low)
    w_hidden_turned, branch_part = stored_turned(w_hidden, branch_part)
    w_back_turned, branch_part = stored_turned(w_back, branch_part)
    branch = (
        scatter_seq(branch_part.reshape(row_count, row_len, model_width))
        .astype(jnp.float32)
        .reshape(tok_count, model_width)
    )
    branch_inv = inverse_rms(branch)
    branch_unit = branch * branch_inv
    result = (
        (hidden_state + branch_unit * gain_ffn)
        .astype(low)
        .reshape(row_count, piece_len, model_width)
    )

    grad_out = cotangent.reshape(tok_count, model_width).astype(jnp.float32)
    ffn_gain_term = jnp.sum(grad_out * branch_unit, 0)
    d_branch = norm_back(grad_out * gain_ffn, branch_unit, branch_inv).astype(low)
    d_branch_all = gather_seq(d_branch.reshape(row_count, piece_len, model_width)).reshape(all_count, model_width)
    d_inner = jnp.dot(d_branch_all, w_back_turned, preferred_element_type=jnp.float32)
    d_gate = (d_inner * up_proj * sigma * (1.0 + gate * (1.0 - sigma))).astype(low)
    d_up = (d_inner * active).astype(low)
    d_gate_up = jnp.concatenate([d_gate, d_up], 1)
    d_hidden_part = jnp.dot(d_gate_up, w_hidden_turned, preferred_element_type=jnp.float32).astype(low)
    d_hidden_sum = scatter_seq(d_hidden_part.reshape(row_count, row_len, model_width))
    gate_part = jnp.einsum("nd,nf->df", hidden_low, d_gate, preferred_element_type=jnp.float32).astype(low)
    up_part = jnp.einsum("nd,nf->df", hidden_low, d_up, preferred_element_type=jnp.float32).astype(low)
    down_part = jnp.einsum("nf,nd->fd", inner_low, d_branch_all, preferred_element_type=jnp.float32).astype(low)
    down_grad = sum_dp(*shares_for(down_part))
    gate_own = sum_dp(*shares_for(gate_part)).astype(low)
    up_own = sum_dp(*shares_for(up_part)).astype(low)
    d_hidden = grad_out + d_hidden_sum.astype(jnp.float32).reshape(tok_count, model_width)

    attn_gain_term = jnp.sum(d_hidden * attn_unit, 0)
    d_attn = norm_back(d_hidden * gain_attn, attn_unit, attn_inv).astype(low)
    d_mixed = jnp.einsum("nd,fd->nf", d_attn, wo_full, preferred_element_type=jnp.float32).astype(low)

    def own_columns_of_all(tensor):
        split = tensor.reshape(row_count, piece_len, seq_count, -1).transpose(2, 0, 1, 3)
        width = split.shape[-1]
        split = lax.all_to_all(split.reshape(seq_count, tok_count, width), "seq", split_axis=0, concat_axis=0)
        split = split.reshape(seq_count, row_count, piece_len, width).transpose(1, 0, 2, 3)
        return split.reshape(row_count, row_len, width)

    d_mixed = own_columns_of_all(d_mixed)
    (gate_grad,) = rows_home(gate_own, dp_count, own_hidden // dp_count)
    (up_grad,) = rows_home(up_own, dp_count, own_hidden // dp_count)

    dq_gained, dk_gained, d_value, dots, gain_terms = attend_back(
        qkv_rows, inverses, tables, norm_gains, ids_all, (*kept, log_total), d_mixed, head_size, scale
    )
    norm_terms = lax.dynamic_update_slice_in_dim(
        jnp.zeros((2, feature_count), jnp.float32), jnp.sum(gain_terms, 0), seq_at * own_features, 1
    )
    dots = dots[:, :2].transpose(1, 0, 2).reshape(-1, LANES)
    stat_rows = dots.shape[0]
    sums = total_seq(
        jnp.concatenate(
            [dots]
            + [part.reshape(-1, LANES) for part in (norm_terms, attn_gain_term, ffn_gain_term)]
        )
    )
    means = sums[:stat_rows].reshape(2, all_count) / feature_count

    def norm_back_wide(gained, pre, at):
        inv = inverse[at][:, None]
        gained = gained.reshape(all_count, own_features)
        return (inv * (gained - pre * inv * means[at][:, None])).astype(low)

    dq_pre = norm_back_wide(dq_gained, query_pre, 0)
    dk_pre = norm_back_wide(dk_gained, key_pre, 1)
    d_value = d_value.reshape(all_count, own_features)
    d_qkv = jnp.concatenate([dq_pre, dk_pre, d_value], 1)
    qkv_part = jnp.einsum("nd,nf->df", tokens_all, d_qkv, preferred_element_type=jnp.float32).astype(low)
    d_qkv, qkv_part = lax.optimization_barrier((d_qkv, qkv_part))
    d_tokens_part = jnp.einsum("nf,df->nd", d_qkv, w_qkv, preferred_element_type=jnp.float32).astype(low)
    d_attn, d_tokens_part = lax.optimization_barrier((d_attn, d_tokens_part))
    d_tokens_sum = scatter_seq(d_tokens_part.reshape(row_count, row_len, model_width))
    d_tokens = d_hidden + d_tokens_sum.astype(jnp.float32).reshape(tok_count, model_width)
    qkv_own = sum_dp(*shares_for(qkv_part)).astype(low)
    query_grad, key_grad, value_grad = rows_home(qkv_own, 1, own_features)
    d_attn_own = own_columns_of_all(d_attn).reshape(all_count, -1)
    out_part = jnp.einsum("nf,nd->fd", mixed_all, d_attn_own, preferred_element_type=jnp.float32).astype(low)
    out_own = sum_dp(*shares_for(out_part)).astype(low)
    (out_grad,) = rows_home(out_own, 1, own_features)
    share = feature_count // (dp_count * seq_count)
    gains = lax.dynamic_index_in_dim(
        sums[stat_rows:].reshape(4, dp_count, seq_count, share), seq_at, 2, False
    )
    gains = share_dp(gains.transpose(1, 0, 2).reshape(dp_count, 4 * share)).reshape(4, share)
    return (
        result,
        d_tokens.reshape(row_count, piece_len, model_width),
        query_grad,
        key_grad,
        value_grad,
        out_grad,
        gate_grad,
        up_grad,
        down_grad,
        gains[0],
        gains[1],
        gains[2],
        gains[3],
    )


def shards(tokens, doc_ids, cotangent, w_query, *rest):
    if w_query.shape[1] // HEAD % lax.axis_size("seq"):
        return shards_by_slab(tokens, doc_ids, cotangent, w_query, *rest)
    return shards_by_feature(tokens, doc_ids, cotangent, w_query, *rest)


def solution(mesh):
    return jax.shard_map(
        shards,
        mesh=mesh,
        in_specs=(
            P("dp", "seq", None),
            P("dp", "seq"),
            P("dp", "seq", None),
            P("dp", None),
            P("dp", None),
            P("dp", None),
            P("dp", None),
            P("dp", None),
            P("dp", None),
            P("dp", None),
            P(),
            P(),
            P(),
            P(),
        ),
        out_specs=(
            P("dp", "seq", None),
            P("dp", "seq", None),
            P(("dp", "seq"), None),
            P(("dp", "seq"), None),
            P(("dp", "seq"), None),
            P(("dp", "seq"), None),
            P(("dp", "seq"), None),
            P(("dp", "seq"), None),
            P(("dp", "seq"), None),
            P(("dp", "seq")),
            P(("dp", "seq")),
            P(("dp", "seq")),
            P(("dp", "seq")),
        ),
        check_vma=False,
    )
```

```python
import functools

import jax
import jax.numpy as jnp
from jax import lax
from jax.experimental import pallas as pl
from jax.experimental.layout import Layout, with_layout_constraint
from jax.experimental.pallas import tpu as pltpu
from jax.sharding import PartitionSpec as P


HEAD = 128
SLABS = 4
LANES = 128
MEBI = 1 << 20


eps = 1e-06
theta = 500000.0


def rotation(positions, head_size):
    half_size = head_size // 2
    frequency = theta ** (-(2.0 * jnp.arange(half_size, dtype=jnp.float32)) / head_size)
    angles = positions.astype(jnp.float32)[:, None] * frequency[None, :]
    return (jnp.cos(angles), jnp.sin(angles))


def rotate(tensor, cosine, sine_part):
    half_size = tensor.shape[-1] // 2
    first_half = tensor[..., :half_size]
    second_half = tensor[..., half_size:]
    cos_wide = cosine[:, None, :]
    sin_wide = sine_part[:, None, :]
    return jnp.concatenate(
        [
            first_half * cos_wide - second_half * sin_wide,
            second_half * cos_wide + first_half * sin_wide,
        ],
        -1,
    )


def unrotate(tensor, cosine, sine_part):
    half_size = tensor.shape[-1] // 2
    first_half = tensor[..., :half_size]
    second_half = tensor[..., half_size:]
    cos_wide = cosine[:, None, :]
    sin_wide = sine_part[:, None, :]
    return jnp.concatenate(
        [
            first_half * cos_wide + second_half * sin_wide,
            second_half * cos_wide - first_half * sin_wide,
        ],
        -1,
    )


def inverse_rms(tensor):
    return lax.rsqrt(jnp.mean(tensor * tensor, -1, keepdims=True) + eps)


def norm_back(grad_unit, unit_vec, inverse):
    return inverse * (grad_unit - unit_vec * jnp.mean(grad_unit * unit_vec, -1, keepdims=True))


def visible(own_ids, key_ids, query_at, key_at):
    causal = key_at[None, :] <= query_at[:, None]
    same_doc = own_ids[:, :, None] == key_ids[:, None, :]
    return (causal[None] & same_doc)[:, None]


def masked_scores(query_low, pair_all, allowed, head_count, head_size):
    row_count = pair_all.shape[0]
    row_length = pair_all.shape[1]
    feature_count = head_count * head_size
    key_rows = pair_all[..., :feature_count].reshape(row_count, row_length, head_count, head_size)
    value_rows = pair_all[..., feature_count:].reshape(row_count, row_length, head_count, head_size)
    scores = jnp.einsum(
        "rche,rlhe->rhcl", query_low, key_rows, preferred_element_type=jnp.float32
    ) * head_size ** (-0.5)
    return (jnp.where(allowed, scores, -1e30), key_rows, value_rows)


def columns_of(matrix, parts, slab_count, index):
    lead = matrix.shape[0]
    width = matrix.shape[1] // (parts * slab_count)
    return matrix.reshape(lead, parts, slab_count, width)[:, :, index].reshape(lead, parts * width)


def entries_of(vector, parts, slab_count, index):
    width = vector.shape[0] // (parts * slab_count)
    return vector.reshape(parts, slab_count, width)[:, index].reshape(parts * width)


def shards_by_slab(
    tokens,
    doc_ids,
    cotangent,
    w_query,
    w_key,
    w_value,
    w_out,
    w_gate,
    w_up,
    w_down,
    g_query,
    g_key,
    g_attn,
    g_ffn,
):
    row_count, piece_len, model_width = tokens.shape
    head_size = HEAD
    feature_count = w_query.shape[1]
    head_count = feature_count // head_size
    tok_count = row_count * piece_len
    scale = head_size ** (-0.5)
    seq_count = lax.axis_size("seq")
    parts = lax.axis_size("dp") * seq_count
    slab_count = SLABS
    gather_all = (
        lax.all_gather(w_query, "dp", axis=0, tiled=True),
        lax.all_gather(w_key, "dp", axis=0, tiled=True),
        lax.all_gather(w_value, "dp", axis=0, tiled=True),
        lax.all_gather(w_out, "dp", axis=0, tiled=True),
        lax.all_gather(w_gate, "dp", axis=0, tiled=True),
        lax.all_gather(w_up, "dp", axis=0, tiled=True),
        lax.all_gather(w_down, "dp", axis=0, tiled=True),
    )
    wq_full, wk_full, wv_full, wo_full, wg_full, wu_full, wd_full = gather_all
    gain_query = g_query.astype(jnp.float32)
    gain_key = g_key.astype(jnp.float32)
    gain_attn = g_attn.astype(jnp.float32)
    gain_ffn = g_ffn.astype(jnp.float32)
    flat_tokens = tokens.reshape(tok_count, model_width)
    query_pre = jnp.dot(flat_tokens, wq_full, preferred_element_type=jnp.float32)
    key_pre = jnp.dot(flat_tokens, wk_full, preferred_element_type=jnp.float32)
    value_pre = jnp.dot(flat_tokens, wv_full, preferred_element_type=jnp.float32)
    query_inv = inverse_rms(query_pre)
    query_unit = query_pre * query_inv
    key_inv = inverse_rms(key_pre)
    key_unit = key_pre * key_inv
    first_row = lax.axis_index("seq") * piece_len
    positions = first_row + jnp.tile(jnp.arange(piece_len, dtype=jnp.int32), row_count)
    cosine, sine_part = rotation(positions, head_size)
    query_rot = rotate(
        (query_unit * gain_query).reshape(tok_count, head_count, head_size), cosine, sine_part
    )
    key_rot = rotate(
        (key_unit * gain_key).reshape(tok_count, head_count, head_size), cosine, sine_part
    )
    query_low = query_rot.astype(jnp.bfloat16).reshape(row_count, piece_len, head_count, head_size)
    key_low = key_rot.astype(jnp.bfloat16).reshape(row_count, piece_len, feature_count)
    value_low = value_pre.astype(jnp.bfloat16).reshape(row_count, piece_len, feature_count)
    pair_low = jnp.concatenate([key_low, value_low], -1)
    ids_low = doc_ids.astype(jnp.bfloat16)
    pair_all, ids_all = (
        lax.all_gather(pair_low, "seq", axis=1, tiled=True),
        lax.all_gather(ids_low, "seq", axis=1, tiled=True),
    )
    query_at = first_row + jnp.arange(piece_len, dtype=jnp.int32)
    allowed = visible(ids_low, ids_all, query_at, jnp.arange(pair_all.shape[1], dtype=jnp.int32))
    masked, _, value_rows = masked_scores(
        query_low, pair_all, allowed, head_count, head_size
    )
    row_max = jnp.max(masked, -1, keepdims=True)
    log_total = jnp.log(jnp.sum(jnp.exp(masked - row_max), -1, keepdims=True)) + row_max
    probs_low = jnp.exp(masked - log_total).astype(jnp.bfloat16)
    mixed = jnp.einsum("rhcl,rlhe->rche", probs_low, value_rows, preferred_element_type=jnp.float32)
    mixed_low = mixed.reshape(tok_count, feature_count).astype(jnp.bfloat16)
    attn_out = jnp.dot(mixed_low, wo_full, preferred_element_type=jnp.float32)
    attn_inv = inverse_rms(attn_out)
    attn_unit = attn_out * attn_inv
    hidden_state = flat_tokens.astype(jnp.float32) + attn_unit * gain_attn
    hidden_low = hidden_state.astype(jnp.bfloat16)
    gate = jnp.dot(hidden_low, wg_full, preferred_element_type=jnp.float32)
    up_proj = jnp.dot(hidden_low, wu_full, preferred_element_type=jnp.float32)
    sigma = jax.nn.sigmoid(gate)
    active = gate * sigma
    inner_low = (active * up_proj).astype(jnp.bfloat16)
    branch = jnp.dot(inner_low, wd_full, preferred_element_type=jnp.float32)
    branch_inv = inverse_rms(branch)
    branch_unit = branch * branch_inv
    result = (
        (hidden_state + branch_unit * gain_ffn)
        .astype(jnp.bfloat16)
        .reshape(row_count, piece_len, model_width)
    )
    wq_back, wk_back, wv_back, wo_back, wg_back, wu_back, wd_back = gather_all
    pair_back, ids_back = (pair_all, ids_all)
    grad_out = cotangent.reshape(tok_count, model_width).astype(jnp.float32)
    ffn_gain_term = jnp.sum(grad_out * branch_unit, 0)
    d_branch = norm_back(grad_out * gain_ffn, branch_unit, branch_inv).astype(jnp.bfloat16)
    d_inner = jnp.einsum("nd,fd->nf", d_branch, wd_back, preferred_element_type=jnp.float32)
    d_gate = (d_inner * up_proj * sigma * (1.0 + gate * (1.0 - sigma))).astype(jnp.bfloat16)
    d_up = (d_inner * active).astype(jnp.bfloat16)
    d_hidden = grad_out + jnp.einsum(
        "nf,df->nd", d_gate, wg_back, preferred_element_type=jnp.float32
    )
    d_hidden = d_hidden + jnp.einsum("nf,df->nd", d_up, wu_back, preferred_element_type=jnp.float32)
    mlp_shares = []
    for index in range(slab_count):
        hidden_part = columns_of(hidden_low, parts, slab_count, index)
        inner_part = columns_of(inner_low, parts, slab_count, index)
        gate_term = jnp.einsum("nd,nf->df", hidden_part, d_gate, preferred_element_type=jnp.float32)
        up_term = jnp.einsum("nd,nf->df", hidden_part, d_up, preferred_element_type=jnp.float32)
        down_term = jnp.einsum(
            "nf,nd->fd", inner_part, d_branch, preferred_element_type=jnp.float32
        )
        ffn_term = entries_of(ffn_gain_term, parts, slab_count, index)
        shares = (
            lax.psum_scatter(down_term, ("dp", "seq"), scatter_dimension=0, tiled=True),
            lax.psum_scatter(gate_term, ("dp", "seq"), scatter_dimension=0, tiled=True),
            lax.psum_scatter(up_term, ("dp", "seq"), scatter_dimension=0, tiled=True),
            lax.psum_scatter(ffn_term, ("dp", "seq"), scatter_dimension=0, tiled=True),
        )
        mlp_shares.append(shares)
    down_grad = jnp.concatenate([s[0] for s in mlp_shares], 0)
    gate_grad = jnp.concatenate([s[1] for s in mlp_shares], 0)
    up_grad = jnp.concatenate([s[2] for s in mlp_shares], 0)
    ffn_grad = jnp.concatenate([s[3] for s in mlp_shares], 0)
    attn_gain_term = jnp.sum(d_hidden * attn_unit, 0)
    d_attn = norm_back(d_hidden * gain_attn, attn_unit, attn_inv).astype(jnp.bfloat16)
    d_mixed = jnp.einsum("nd,fd->nf", d_attn, wo_back, preferred_element_type=jnp.float32).astype(
        jnp.bfloat16
    )
    d_mixed = d_mixed.reshape(row_count, piece_len, head_count, head_size)
    sub_len = piece_len // slab_count
    pair_width = pair_back.shape[-1]
    pair_view = pair_back.reshape(row_count, seq_count, slab_count, sub_len, pair_width)
    ids_view = ids_back.reshape(row_count, seq_count, slab_count, sub_len)

    def slab_scores(index):
        pair_part = pair_view[:, :, index].reshape(row_count, seq_count * sub_len, pair_width)
        ids_part = ids_view[:, :, index].reshape(row_count, seq_count * sub_len)
        key_at = (
            jnp.arange(seq_count, dtype=jnp.int32)[:, None] * piece_len
            + index * sub_len
            + jnp.arange(sub_len, dtype=jnp.int32)[None, :]
        ).reshape(seq_count * sub_len)
        allowed_part = visible(ids_low, ids_part, query_at, key_at)
        masked_part, key_part, value_part = masked_scores(
            query_low, pair_part, allowed_part, head_count, head_size
        )
        probs_part = jnp.exp(masked_part - log_total)
        d_probs_part = jnp.einsum(
            "rche,rlhe->rhcl", d_mixed, value_part, preferred_element_type=jnp.float32
        )
        return (probs_part, d_probs_part, key_part)

    row_dot = jnp.zeros((row_count, head_count, piece_len, 1), jnp.float32)
    for index in range(slab_count):
        probs_part, d_probs_part, key_part = slab_scores(index)
        row_dot = row_dot + jnp.sum(probs_part * d_probs_part, -1, keepdims=True)
    query_acc = jnp.zeros((row_count, piece_len, head_count, head_size), jnp.float32)
    pair_shares = []
    for index in range(slab_count):
        probs_part, d_probs_part, key_part = slab_scores(index)
        d_scores = (probs_part * (d_probs_part - row_dot)).astype(jnp.bfloat16)
        query_acc = query_acc + jnp.einsum(
            "rhcl,rlhe->rche", d_scores, key_part, preferred_element_type=jnp.float32
        )
        key_term = (
            jnp.einsum("rhcl,rche->rlhe", d_scores, query_low, preferred_element_type=jnp.float32)
            * scale
        )
        value_term = jnp.einsum(
            "rhcl,rche->rlhe",
            probs_part.astype(jnp.bfloat16),
            d_mixed,
            preferred_element_type=jnp.float32,
        )
        key_count = seq_count * sub_len
        pair_term = jnp.concatenate(
            [
                key_term.reshape(row_count, key_count, feature_count),
                value_term.reshape(row_count, key_count, feature_count),
            ],
            -1,
        )
        pair_shares.append(
            lax.psum_scatter(
                pair_term.astype(jnp.bfloat16), "seq", scatter_dimension=1, tiled=True
            ).astype(jnp.float32)
        )
    pair_grad = jnp.concatenate(pair_shares, 1)
    d_query = (query_acc * scale).astype(jnp.bfloat16)
    d_key = (
        pair_grad[..., :feature_count]
        .astype(jnp.bfloat16)
        .reshape(tok_count, head_count, head_size)
    )
    d_value = pair_grad[..., feature_count:].astype(jnp.bfloat16).reshape(tok_count, feature_count)
    dq_norm = unrotate(
        d_query.reshape(tok_count, head_count, head_size).astype(jnp.float32), cosine, sine_part
    ).reshape(tok_count, feature_count)
    dk_norm = unrotate(d_key.astype(jnp.float32), cosine, sine_part).reshape(
        tok_count, feature_count
    )
    query_gain_term = jnp.sum(dq_norm * query_unit, 0)
    key_gain_term = jnp.sum(dk_norm * key_unit, 0)
    dq_pre = norm_back(dq_norm * gain_query, query_unit, query_inv).astype(jnp.bfloat16)
    dk_pre = norm_back(dk_norm * gain_key, key_unit, key_inv).astype(jnp.bfloat16)
    d_tokens = d_hidden + jnp.einsum(
        "nf,df->nd", dq_pre, wq_back, preferred_element_type=jnp.float32
    )
    d_tokens = d_tokens + jnp.einsum(
        "nf,df->nd", dk_pre, wk_back, preferred_element_type=jnp.float32
    )
    d_tokens = d_tokens + jnp.einsum(
        "nf,df->nd", d_value, wv_back, preferred_element_type=jnp.float32
    )
    attn_shares = []
    for index in range(slab_count):
        token_part = columns_of(flat_tokens, parts, slab_count, index)
        mixed_part = columns_of(mixed_low, parts, slab_count, index)
        query_term = jnp.einsum("nd,nf->df", token_part, dq_pre, preferred_element_type=jnp.float32)
        key_wterm = jnp.einsum("nd,nf->df", token_part, dk_pre, preferred_element_type=jnp.float32)
        value_wterm = jnp.einsum(
            "nd,nf->df", token_part, d_value, preferred_element_type=jnp.float32
        )
        out_term = jnp.einsum("nf,nd->fd", mixed_part, d_attn, preferred_element_type=jnp.float32)
        gq_term = entries_of(query_gain_term, parts, slab_count, index)
        gk_term = entries_of(key_gain_term, parts, slab_count, index)
        ga_term = entries_of(attn_gain_term, parts, slab_count, index)
        shares = (
            lax.psum_scatter(query_term, ("dp", "seq"), scatter_dimension=0, tiled=True),
            lax.psum_scatter(key_wterm, ("dp", "seq"), scatter_dimension=0, tiled=True),
            lax.psum_scatter(value_wterm, ("dp", "seq"), scatter_dimension=0, tiled=True),
            lax.psum_scatter(out_term, ("dp", "seq"), scatter_dimension=0, tiled=True),
            lax.psum_scatter(gq_term, ("dp", "seq"), scatter_dimension=0, tiled=True),
            lax.psum_scatter(gk_term, ("dp", "seq"), scatter_dimension=0, tiled=True),
            lax.psum_scatter(ga_term, ("dp", "seq"), scatter_dimension=0, tiled=True),
        )
        attn_shares.append(shares)
    query_grad = jnp.concatenate([s[0] for s in attn_shares], 0)
    key_grad = jnp.concatenate([s[1] for s in attn_shares], 0)
    value_grad = jnp.concatenate([s[2] for s in attn_shares], 0)
    out_grad = jnp.concatenate([s[3] for s in attn_shares], 0)
    gq_grad = jnp.concatenate([s[4] for s in attn_shares], 0)
    gk_grad = jnp.concatenate([s[5] for s in attn_shares], 0)
    ga_grad = jnp.concatenate([s[6] for s in attn_shares], 0)
    tokens_grad = d_tokens.reshape(row_count, piece_len, model_width)
    return (
        result,
        tokens_grad,
        query_grad,
        key_grad,
        value_grad,
        out_grad,
        gate_grad,
        up_grad,
        down_grad,
        gq_grad,
        gk_grad,
        ga_grad,
        ffn_grad,
    )


def own_columns(matrix, groups, parts, index):
    width = matrix.shape[1] // (groups * parts)
    pieces = [
        lax.dynamic_slice_in_dim(matrix, (group * parts + index) * width, width, 1)
        for group in range(groups)
    ]
    return jnp.concatenate(pieces, 1) if groups > 1 else pieces[0]


def gather_seq(piece):
    return lax.all_gather(piece, "seq", axis=1, tiled=True)


def scatter_seq(partial):
    return lax.psum_scatter(partial, "seq", scatter_dimension=1, tiled=True)


def swap(value, axis, flip):
    return lax.ppermute(value, axis, [(at, at ^ flip) for at in range(lax.axis_size(axis))])


def place_kernel(spots_ref, *refs, count):
    in_refs, (out_ref, sems) = refs[:count], refs[-2:]
    copies = []
    for at, in_ref in enumerate(in_refs):
        rows, width = in_ref.shape
        row = pl.multiple_of(spots_ref[2 * at], LANES)
        column = pl.multiple_of(spots_ref[2 * at + 1], LANES)
        copies.append(
            pltpu.make_async_copy(
                in_ref, out_ref.at[pl.ds(row, rows), pl.ds(column, width)], sems.at[at]
            )
        )
    for copy in copies:
        copy.start()
    for copy in copies:
        copy.wait()


def placed(pieces, shape, whole=None):
    spots = jnp.stack([jnp.int32(at) for _, row, column in pieces for at in (row, column)])
    outside = pl.BlockSpec(memory_space=pl.ANY)
    given = [] if whole is None else [whole]
    return pl.pallas_call(
        functools.partial(place_kernel, count=len(pieces)),
        grid_spec=pltpu.PrefetchScalarGridSpec(
            num_scalar_prefetch=1,
            grid=(1,),
            in_specs=[
                pl.BlockSpec(piece.shape, lambda at, spots: (0, 0), pipeline_mode=pl.Buffered(1))
                for piece, _, _ in pieces
            ]
            + [outside] * len(given),
            out_specs=outside,
            scratch_shapes=[pltpu.SemaphoreType.DMA((len(pieces),))],
        ),
        out_shape=jax.ShapeDtypeStruct(shape, pieces[0][0].dtype),
        input_output_aliases={1 + len(pieces): 0} if given else {},
        compiler_params=pltpu.CompilerParams(
            vmem_limit_bytes=MEBI
            + sum(piece.size * piece.dtype.itemsize for piece, _, _ in pieces)
        ),
        name="place",
    )(spots, *[piece for piece, _, _ in pieces], *given)


def pieces_for(value, name, split_axis):
    count, index = lax.axis_size(name), lax.axis_index(name)
    width = value.shape[split_axis] // count
    return [
        lax.dynamic_slice_in_dim(value, (index ^ flip) * width, width, split_axis)
        for flip in range(count)
    ]


def swapped(pieces, name):
    return [swap(piece, name, flip) if flip else piece for flip, piece in enumerate(pieces)]


def exchanged(value, name, split_axis):
    return swapped(pieces_for(value, name, split_axis), name)


def pieces_dp(piece):
    half = piece.shape[0] // 2
    first, second = swap(piece, "dp", 1), swap(piece, "dp", 2)
    top, bottom = swap(first[:half], "dp", 2), swap(second[half:], "dp", 1)
    index = lax.axis_index("dp")
    width = piece.shape[0]
    far = (index ^ 3) * width
    return [
        (first, (index ^ 1) * width),
        (second, (index ^ 2) * width),
        (top, far),
        (bottom, far + half),
    ]


def gather_dp(piece):
    rows, width = piece.shape
    pieces = [(piece, lax.axis_index("dp") * rows), *pieces_dp(piece)]
    pieces = [(part, row, 0) for part, row in pieces]
    whole = placed(pieces[:3], (4 * rows, width))
    return placed(pieces[3:], (4 * rows, width), whole)


def sum_dp(sent, kept):
    got = swap(sent[0], "dp", 1), swap(sent[1], "dp", 2)
    wide = [(kept[at].astype(jnp.float32) + got[at].astype(jnp.float32)) for at in range(2)]
    onward = [side[1].astype(jnp.bfloat16) for side in wide]
    last = swap(onward[0], "dp", 2), swap(onward[1], "dp", 1)
    return jnp.concatenate(
        [wide[at][0] + last[at].astype(jnp.float32) for at in range(2)], 0
    )


def shares_for(partial):
    index = lax.axis_index("dp")
    width = partial.shape[0] // 4
    half = width // 2

    def part(flip, side):
        return lax.dynamic_slice_in_dim(partial, (index ^ flip) * width + side * half, half, 0)

    sent = [jnp.stack([part(1, 0), part(3, 0)]), jnp.stack([part(2, 1), part(3, 1)])]
    kept = [jnp.stack([part(0, 0), part(2, 0)]), jnp.stack([part(0, 1), part(1, 1)])]
    return sent, kept


def stored_turned(matrix, after):
    matrix, after = lax.optimization_barrier((matrix, after))
    return with_layout_constraint(matrix.T, Layout((0, 1))), after


def total_seq(value):
    shape = value.shape
    value = value.reshape(-1, LANES)
    flip = 1
    while flip < lax.axis_size("seq"):
        value = value + swap(value, "seq", flip)
        flip *= 2
    return value.reshape(shape)


def share_dp(rows):
    flip = lax.axis_size("dp") // 2
    while flip:
        halves = rows.reshape(2, rows.shape[0] // 2, rows.shape[1])
        side = lax.axis_index("dp") // flip % 2
        kept = lax.dynamic_index_in_dim(halves, side, 0, False)
        sent = lax.dynamic_index_in_dim(halves, 1 - side, 0, False)
        rows = kept + swap(sent, "dp", flip)
        flip //= 2
    return rows[0]


def settle_kernel(index_ref, *refs, groups, width, count):
    in_refs, out_refs = refs[:count], refs[count:]
    for flip, in_ref in enumerate(in_refs):
        source = index_ref[0] ^ flip
        for at, out_ref in enumerate(out_refs):
            for group in range(groups):
                column = (at * groups + group) * width
                place = pl.multiple_of((group * count + source) * width, width)
                out_ref[:, pl.ds(place, width)] = in_ref[:, column : column + width].astype(jnp.float32)


def rows_home(summed, groups, width):
    pieces = exchanged(summed, "seq", 0)
    count = len(pieces)
    rows, total = pieces[0].shape
    outs = total // (groups * width)
    step = min(16, rows)
    wide = count * groups * width
    return pl.pallas_call(
        functools.partial(settle_kernel, groups=groups, width=width, count=count),
        grid_spec=pltpu.PrefetchScalarGridSpec(
            num_scalar_prefetch=1,
            grid=(rows // step,),
            in_specs=[pl.BlockSpec((step, total), lambda r, index: (r, 0))] * count,
            out_specs=[pl.BlockSpec((step, wide), lambda r, index: (r, 0))] * outs,
        ),
        out_shape=[jax.ShapeDtypeStruct((rows, wide), jnp.float32)] * outs,
        compiler_params=pltpu.CompilerParams(vmem_limit_bytes=8 * MEBI),
        name="settle",
    )(lax.axis_index("seq").reshape(1), *pieces)


QUERY_BLOCK = 256


def attention_masks(ids_col, ids_row, block, width, start):
    rows = start + lax.broadcasted_iota(jnp.int32, (block, width), 0)
    columns = lax.broadcasted_iota(jnp.int32, (block, width), 1)
    return (columns <= rows) & (ids_col[start : start + block] == ids_row[:, :width])


def attend_kernel(
    q_ref, k_ref, v_ref, qinv_ref, kinv_ref, cos_ref, sin_ref, gq_ref, gk_ref, col_ref, row_ref,
    qlow_ref, klow_ref, vlow_ref, mixed_ref, total_ref, *, scale
):
    low = jnp.bfloat16
    half = q_ref.shape[-1] // 2
    cosine, sine_part = cos_ref[...], sin_ref[...]

    def rotated(ref, inv_ref, gain_ref):
        value = ref[0] * inv_ref[0] * gain_ref[...]
        return (value * cosine + pltpu.roll(value, half, 1) * sine_part).astype(low)

    qlow_ref[0] = rotated(q_ref, qinv_ref, gq_ref)
    klow_ref[0] = rotated(k_ref, kinv_ref, gk_ref)
    vlow_ref[0] = v_ref[0].astype(low)
    length = q_ref.shape[1]
    block = min(QUERY_BLOCK, length)
    ids_col, ids_row = col_ref[0], row_ref[0]
    for start in range(0, length, block):
        width = start + block
        scores = lax.dot_general(
            qlow_ref[0, start:width], klow_ref[0, :width], (((1,), (1,)), ((), ())),
            preferred_element_type=jnp.float32,
        ) * scale
        allowed = attention_masks(ids_col, ids_row, block, width, start)
        masked = jnp.where(allowed, scores, -1e30)
        row_max = jnp.max(masked, -1, keepdims=True)
        log_total = jnp.log(jnp.sum(jnp.exp(masked - row_max), -1, keepdims=True)) + row_max
        total_ref[0, 0, start:width] = log_total
        probs = jnp.exp(masked - log_total).astype(low)
        mixed_ref[0, start:width] = jnp.dot(
            probs, vlow_ref[0, :width], preferred_element_type=jnp.float32
        ).astype(low)


def attend_back_kernel(
    q_ref, k_ref, qinv_ref, kinv_ref, cos_ref, sin_ref, gq_ref, gk_ref, col_ref, row_ref,
    qlow_ref, klow_ref, vlow_ref, total_ref, dmixed_ref,
    dq_ref, dk_ref, dv_ref, dots_ref, gains_ref, key_acc, value_acc, query_acc, *, scale
):
    low = jnp.bfloat16
    half = q_ref.shape[-1] // 2
    length = q_ref.shape[1]
    block = min(QUERY_BLOCK, length)
    ids_col, ids_row = col_ref[0], row_ref[0]
    turned = (((0,), (0,)), ((), ()))
    across = (((1,), (1,)), ((), ()))
    key_acc[...] = jnp.zeros_like(key_acc)
    value_acc[...] = jnp.zeros_like(value_acc)
    for start in range(0, length, block):
        width = start + block
        query = qlow_ref[0, start:width]
        d_mixed = dmixed_ref[0, start:width]
        keys = klow_ref[0, :width]
        scores = lax.dot_general(query, keys, across, preferred_element_type=jnp.float32) * scale
        allowed = attention_masks(ids_col, ids_row, block, width, start)
        probs = jnp.exp(jnp.where(allowed, scores, -1e30) - total_ref[0, 0, start:width])
        d_probs = lax.dot_general(
            d_mixed, vlow_ref[0, :width], across, preferred_element_type=jnp.float32
        )
        row_dot = jnp.sum(probs * d_probs, -1, keepdims=True)
        d_scores = (probs * (d_probs - row_dot)).astype(low)
        query_acc[start:width] = jnp.dot(d_scores, keys, preferred_element_type=jnp.float32)
        key_acc[:width] += lax.dot_general(d_scores, query, turned, preferred_element_type=jnp.float32)
        value_acc[:width] += lax.dot_general(
            probs.astype(low), d_mixed, turned, preferred_element_type=jnp.float32
        )
    dv_ref[0] = value_acc[...].astype(low)
    cosine, sine_part = cos_ref[...], sin_ref[...]

    def turned_back(acc, ref, inv_ref, gain_ref, out_ref, at):
        value = (acc[...] * scale).astype(low).astype(jnp.float32)
        value = value * cosine - pltpu.roll(value, half, 1) * sine_part
        unit = ref[0] * inv_ref[0]
        gains_ref[0, at : at + 1] = jnp.sum(value * unit, 0, keepdims=True)
        value = value * gain_ref[...]
        out_ref[0] = value
        return jnp.sum(value * unit, -1, keepdims=True)

    query_dot = turned_back(query_acc, q_ref, qinv_ref, gq_ref, dq_ref, 0)
    key_dot = turned_back(key_acc, k_ref, kinv_ref, gk_ref, dk_ref, 1)
    lane = lax.broadcasted_iota(jnp.int32, (length, LANES), 1)
    dots = jnp.where(lane == 0, query_dot, jnp.where(lane == 1, key_dot, 0.0)).T[:8]

    @pl.when(pl.program_id(1) == 0)
    def _():
        dots_ref[0] = dots

    @pl.when(pl.program_id(1) != 0)
    def _():
        dots_ref[0] += dots


def attention_specs(length, heads, head_size):
    wide = lambda at: pl.BlockSpec((1, length, head_size), lambda r, h, at=at: (r, 0, at * heads + h))
    thin = pl.BlockSpec((1, length, 1), lambda r, h: (r, 0, 0))
    table = pl.BlockSpec((length, head_size), lambda r, h: (0, 0))
    gain = pl.BlockSpec((1, head_size), lambda r, h: (0, h))
    flat = pl.BlockSpec((1, 1, length), lambda r, h: (r, 0, 0))
    total = pl.BlockSpec((1, 1, length, 1), lambda r, h: (r, h, 0, 0))
    return wide, thin, table, gain, flat, total


def attend(qkv, inverses, tables, gains, ids, head_size, scale):
    rows, length, width = qkv.shape
    heads = width // (3 * head_size)
    wide, thin, table, gain, flat, total = attention_specs(length, heads, head_size)
    narrow = jax.ShapeDtypeStruct((rows, length, heads * head_size), jnp.bfloat16)
    return pl.pallas_call(
        functools.partial(attend_kernel, scale=scale),
        grid=(rows, heads),
        in_specs=[wide(0), wide(1), wide(2), thin, thin, table, table, gain, gain, thin, flat],
        out_specs=[wide(0), wide(0), wide(0), wide(0), total],
        out_shape=[narrow] * 4 + [jax.ShapeDtypeStruct((rows, heads, length, 1), jnp.float32)],
        name="attend",
    )(qkv, qkv, qkv, *inverses, *tables, *gains, ids[:, :, None], ids[:, None, :])


def attend_back(qkv, inverses, tables, gains, ids, kept, d_mixed, head_size, scale):
    rows, length, width = qkv.shape
    heads = width // (3 * head_size)
    wide, thin, table, gain, flat, total = attention_specs(length, heads, head_size)
    shape = (rows, length, heads * head_size)
    return pl.pallas_call(
        functools.partial(attend_back_kernel, scale=scale),
        grid=(rows, heads),
        in_specs=[wide(0), wide(1), thin, thin, table, table, gain, gain, thin, flat]
        + [wide(0), wide(0), wide(0), total, wide(0)],
        out_specs=[
            wide(0),
            wide(0),
            wide(0),
            pl.BlockSpec((1, 8, length), lambda r, h: (r, 0, 0)),
            pl.BlockSpec((1, 2, head_size), lambda r, h: (r, 0, h)),
        ],
        out_shape=[
            jax.ShapeDtypeStruct(shape, jnp.float32),
            jax.ShapeDtypeStruct(shape, jnp.float32),
            jax.ShapeDtypeStruct(shape, jnp.bfloat16),
            jax.ShapeDtypeStruct((rows, 8, length), jnp.float32),
            jax.ShapeDtypeStruct((rows, 2, heads * head_size), jnp.float32),
        ],
        scratch_shapes=[pltpu.VMEM((length, head_size), jnp.float32)] * 3,
        name="attend_back",
    )(qkv, qkv, *inverses, *tables, *gains, ids[:, :, None], ids[:, None, :], *kept, d_mixed)


def shards_by_feature(
    tokens,
    doc_ids,
    cotangent,
    w_query,
    w_key,
    w_value,
    w_out,
    w_gate,
    w_up,
    w_down,
    g_query,
    g_key,
    g_attn,
    g_ffn,
):
    row_count, piece_len, model_width = tokens.shape
    head_size = HEAD
    feature_count = w_query.shape[1]
    scale = head_size ** (-0.5)
    seq_count = lax.axis_size("seq")
    dp_count = lax.axis_size("dp")
    seq_at = lax.axis_index("seq")
    row_len = piece_len * seq_count
    all_count = row_count * row_len
    tok_count = row_count * piece_len
    own_features = feature_count // seq_count
    own_hidden = w_gate.shape[1] // seq_count
    low = jnp.bfloat16

    def own_piece(tensor):
        view = tensor.reshape(row_count, row_len, -1)
        return lax.dynamic_slice_in_dim(view, seq_at * piece_len, piece_len, 1).reshape(tok_count, -1)

    w_qkv = gather_dp(jnp.concatenate([own_columns(w, 1, seq_count, seq_at) for w in (w_query, w_key, w_value)], 1))
    tokens_all = gather_seq(tokens).reshape(all_count, model_width)
    ids_all = total_seq(
        lax.dynamic_update_slice_in_dim(
            jnp.zeros((row_count, row_len), jnp.int32), doc_ids, seq_at * piece_len, 1
        )
    )
    core = seq_at % 2
    half = model_width // 2
    out_rows = w_out.shape[0]
    out_pieces = pieces_dp(lax.dynamic_slice_in_dim(w_out, core * half, half, 1))
    other_pieces = [(swap(piece, "seq", 1), row) for piece, row in out_pieces]
    wo_full = placed(
        [(w_out, lax.axis_index("dp") * out_rows, 0)]
        + [(piece, row, core * half) for piece, row in out_pieces]
        + [(piece, row, half - core * half) for piece, row in other_pieces],
        (feature_count, model_width),
    )
    w_hidden = gather_dp(jnp.concatenate([own_columns(w, dp_count, seq_count, seq_at) for w in (w_gate, w_up)], 1))
    w_back = gather_dp(
        lax.dynamic_slice_in_dim(
            w_down, seq_at * (own_hidden // dp_count), own_hidden // dp_count, 0
        ),
    )
    gain_query = lax.dynamic_slice_in_dim(g_query, seq_at * own_features, own_features).astype(jnp.float32)
    gain_key = lax.dynamic_slice_in_dim(g_key, seq_at * own_features, own_features).astype(jnp.float32)
    gain_attn = g_attn.astype(jnp.float32)
    gain_ffn = g_ffn.astype(jnp.float32)

    tokens_all, ids_all = lax.optimization_barrier((tokens_all, ids_all))
    qkv = jnp.dot(tokens_all, w_qkv, preferred_element_type=jnp.float32)
    query_pre = qkv[:, :own_features]
    key_pre = qkv[:, own_features : 2 * own_features]
    squares = jnp.stack([jnp.sum(query_pre * query_pre, -1), jnp.sum(key_pre * key_pre, -1)])
    cosine, sine_part = rotation(jnp.arange(row_len, dtype=jnp.int32), head_size)
    tables = jnp.concatenate([cosine, cosine], 1), jnp.concatenate([-sine_part, sine_part], 1)
    inverse = lax.rsqrt(total_seq(squares) / feature_count + eps)
    inverses = [inverse[at].reshape(row_count, row_len, 1) for at in range(2)]
    norm_gains = gain_query[None, :], gain_key[None, :]
    qkv_rows = qkv.reshape(row_count, row_len, 3 * own_features)
    *kept, mixed_low, log_total = attend(
        qkv_rows, inverses, tables, norm_gains, ids_all, head_size, scale
    )
    mixed_low = mixed_low.reshape(all_count, own_features)
    mixed_all = lax.all_gather(mixed_low, "seq", axis=1, tiled=True)
    attn_out = jnp.dot(mixed_all, wo_full, preferred_element_type=jnp.float32)
    attn_inv_all = inverse_rms(attn_out)
    hidden_all = tokens_all.astype(jnp.float32) + attn_out * attn_inv_all * gain_attn
    hidden_low = hidden_all.astype(low)
    attn_inv = own_piece(attn_inv_all)
    attn_unit = own_piece(attn_out) * attn_inv
    hidden_state = tokens.reshape(tok_count, model_width).astype(jnp.float32) + attn_unit * gain_attn

    gate_up = jnp.dot(hidden_low, w_hidden, preferred_element_type=jnp.float32)
    gate, up_proj = gate_up[:, :own_hidden], gate_up[:, own_hidden:]
    sigma = jax.nn.sigmoid(gate)
    active = gate * sigma
    inner_low = (active * up_proj).astype(low)
    branch_part = jnp.dot(inner_low, w_back, preferred_element_type=jnp.float32).astype(low)
    w_hidden_turned, branch_part = stored_turned(w_hidden, branch_part)
    w_back_turned, branch_part = stored_turned(w_back, branch_part)
    branch = (
        scatter_seq(branch_part.reshape(row_count, row_len, model_width))
        .astype(jnp.float32)
        .reshape(tok_count, model_width)
    )
    branch_inv = inverse_rms(branch)
    branch_unit = branch * branch_inv
    result = (
        (hidden_state + branch_unit * gain_ffn)
        .astype(low)
        .reshape(row_count, piece_len, model_width)
    )

    grad_out = cotangent.reshape(tok_count, model_width).astype(jnp.float32)
    ffn_gain_term = jnp.sum(grad_out * branch_unit, 0)
    d_branch = norm_back(grad_out * gain_ffn, branch_unit, branch_inv).astype(low)
    d_branch_all = gather_seq(d_branch.reshape(row_count, piece_len, model_width)).reshape(all_count, model_width)
    d_inner = jnp.dot(d_branch_all, w_back_turned, preferred_element_type=jnp.float32)
    d_gate = (d_inner * up_proj * sigma * (1.0 + gate * (1.0 - sigma))).astype(low)
    d_up = (d_inner * active).astype(low)
    d_gate_up = jnp.concatenate([d_gate, d_up], 1)
    d_hidden_part = jnp.dot(d_gate_up, w_hidden_turned, preferred_element_type=jnp.float32).astype(low)
    d_hidden_sum = scatter_seq(d_hidden_part.reshape(row_count, row_len, model_width))
    gate_part = jnp.einsum("nd,nf->df", hidden_low, d_gate, preferred_element_type=jnp.float32).astype(low)
    up_part = jnp.einsum("nd,nf->df", hidden_low, d_up, preferred_element_type=jnp.float32).astype(low)
    down_part = jnp.einsum("nf,nd->fd", inner_low, d_branch_all, preferred_element_type=jnp.float32).astype(low)
    down_grad = sum_dp(*shares_for(down_part))
    gate_own = sum_dp(*shares_for(gate_part)).astype(low)
    up_own = sum_dp(*shares_for(up_part)).astype(low)
    d_hidden = grad_out + d_hidden_sum.astype(jnp.float32).reshape(tok_count, model_width)

    attn_gain_term = jnp.sum(d_hidden * attn_unit, 0)
    d_attn = norm_back(d_hidden * gain_attn, attn_unit, attn_inv).astype(low)
    d_mixed = jnp.einsum("nd,fd->nf", d_attn, wo_full, preferred_element_type=jnp.float32).astype(low)

    def own_columns_of_all(tensor):
        split = tensor.reshape(row_count, piece_len, seq_count, -1).transpose(2, 0, 1, 3)
        width = split.shape[-1]
        split = lax.all_to_all(split.reshape(seq_count, tok_count, width), "seq", split_axis=0, concat_axis=0)
        split = split.reshape(seq_count, row_count, piece_len, width).transpose(1, 0, 2, 3)
        return split.reshape(row_count, row_len, width)

    d_mixed = own_columns_of_all(d_mixed)
    (gate_grad,) = rows_home(gate_own, dp_count, own_hidden // dp_count)
    (up_grad,) = rows_home(up_own, dp_count, own_hidden // dp_count)

    dq_gained, dk_gained, d_value, dots, gain_terms = attend_back(
        qkv_rows, inverses, tables, norm_gains, ids_all, (*kept, log_total), d_mixed, head_size, scale
    )
    norm_terms = lax.dynamic_update_slice_in_dim(
        jnp.zeros((2, feature_count), jnp.float32), jnp.sum(gain_terms, 0), seq_at * own_features, 1
    )
    dots = dots[:, :2].transpose(1, 0, 2).reshape(-1, LANES)
    stat_rows = dots.shape[0]
    sums = total_seq(
        jnp.concatenate(
            [dots]
            + [part.reshape(-1, LANES) for part in (norm_terms, attn_gain_term, ffn_gain_term)]
        )
    )
    means = sums[:stat_rows].reshape(2, all_count) / feature_count

    def norm_back_wide(gained, pre, at):
        inv = inverse[at][:, None]
        gained = gained.reshape(all_count, own_features)
        return (inv * (gained - pre * inv * means[at][:, None])).astype(low)

    dq_pre = norm_back_wide(dq_gained, query_pre, 0)
    dk_pre = norm_back_wide(dk_gained, key_pre, 1)
    d_value = d_value.reshape(all_count, own_features)
    d_qkv = jnp.concatenate([dq_pre, dk_pre, d_value], 1)
    qkv_part = jnp.einsum("nd,nf->df", tokens_all, d_qkv, preferred_element_type=jnp.float32).astype(low)
    d_qkv, qkv_part = lax.optimization_barrier((d_qkv, qkv_part))
    d_tokens_part = jnp.einsum("nf,df->nd", d_qkv, w_qkv, preferred_element_type=jnp.float32).astype(low)
    d_attn, d_tokens_part = lax.optimization_barrier((d_attn, d_tokens_part))
    d_tokens_sum = scatter_seq(d_tokens_part.reshape(row_count, row_len, model_width))
    d_tokens = d_hidden + d_tokens_sum.astype(jnp.float32).reshape(tok_count, model_width)
    qkv_own = sum_dp(*shares_for(qkv_part)).astype(low)
    query_grad, key_grad, value_grad = rows_home(qkv_own, 1, own_features)
    d_attn_own = own_columns_of_all(d_attn).reshape(all_count, -1)
    out_part = jnp.einsum("nf,nd->fd", mixed_all, d_attn_own, preferred_element_type=jnp.float32).astype(low)
    out_own = sum_dp(*shares_for(out_part)).astype(low)
    (out_grad,) = rows_home(out_own, 1, own_features)
    share = feature_count // (dp_count * seq_count)
    gains = lax.dynamic_index_in_dim(
        sums[stat_rows:].reshape(4, dp_count, seq_count, share), seq_at, 2, False
    )
    gains = share_dp(gains.transpose(1, 0, 2).reshape(dp_count, 4 * share)).reshape(4, share)
    return (
        result,
        d_tokens.reshape(row_count, piece_len, model_width),
        query_grad,
        key_grad,
        value_grad,
        out_grad,
        gate_grad,
        up_grad,
        down_grad,
        gains[0],
        gains[1],
        gains[2],
        gains[3],
    )


def shards(tokens, doc_ids, cotangent, w_query, *rest):
    if w_query.shape[1] // HEAD % lax.axis_size("seq"):
        return shards_by_slab(tokens, doc_ids, cotangent, w_query, *rest)
    return shards_by_feature(tokens, doc_ids, cotangent, w_query, *rest)


def solution(mesh):
    return jax.shard_map(
        shards,
        mesh=mesh,
        in_specs=(
            P("dp", "seq", None),
            P("dp", "seq"),
            P("dp", "seq", None),
            P("dp", None),
            P("dp", None),
            P("dp", None),
            P("dp", None),
            P("dp", None),
            P("dp", None),
            P("dp", None),
            P(),
            P(),
            P(),
            P(),
        ),
        out_specs=(
            P("dp", "seq", None),
            P("dp", "seq", None),
            P(("dp", "seq"), None),
            P(("dp", "seq"), None),
            P(("dp", "seq"), None),
            P(("dp", "seq"), None),
            P(("dp", "seq"), None),
            P(("dp", "seq"), None),
            P(("dp", "seq"), None),
            P(("dp", "seq")),
            P(("dp", "seq")),
            P(("dp", "seq")),
            P(("dp", "seq")),
        ),
        check_vma=False,
    )
```

```python
import functools

import jax
import jax.numpy as jnp
from jax import lax
from jax.experimental import pallas as pl
from jax.experimental.layout import Layout, with_layout_constraint
from jax.experimental.pallas import tpu as pltpu
from jax.sharding import PartitionSpec as P


HEAD = 128
SLABS = 4
LANES = 128
MEBI = 1 << 20


eps = 1e-06
theta = 500000.0


def rotation(positions, head_size):
    half_size = head_size // 2
    frequency = theta ** (-(2.0 * jnp.arange(half_size, dtype=jnp.float32)) / head_size)
    angles = positions.astype(jnp.float32)[:, None] * frequency[None, :]
    return (jnp.cos(angles), jnp.sin(angles))


def rotate(tensor, cosine, sine_part):
    half_size = tensor.shape[-1] // 2
    first_half = tensor[..., :half_size]
    second_half = tensor[..., half_size:]
    cos_wide = cosine[:, None, :]
    sin_wide = sine_part[:, None, :]
    return jnp.concatenate(
        [
            first_half * cos_wide - second_half * sin_wide,
            second_half * cos_wide + first_half * sin_wide,
        ],
        -1,
    )


def unrotate(tensor, cosine, sine_part):
    half_size = tensor.shape[-1] // 2
    first_half = tensor[..., :half_size]
    second_half = tensor[..., half_size:]
    cos_wide = cosine[:, None, :]
    sin_wide = sine_part[:, None, :]
    return jnp.concatenate(
        [
            first_half * cos_wide + second_half * sin_wide,
            second_half * cos_wide - first_half * sin_wide,
        ],
        -1,
    )


def inverse_rms(tensor):
    return lax.rsqrt(jnp.mean(tensor * tensor, -1, keepdims=True) + eps)


def norm_back(grad_unit, unit_vec, inverse):
    return inverse * (grad_unit - unit_vec * jnp.mean(grad_unit * unit_vec, -1, keepdims=True))


def visible(own_ids, key_ids, query_at, key_at):
    causal = key_at[None, :] <= query_at[:, None]
    same_doc = own_ids[:, :, None] == key_ids[:, None, :]
    return (causal[None] & same_doc)[:, None]


def masked_scores(query_low, pair_all, allowed, head_count, head_size):
    row_count = pair_all.shape[0]
    row_length = pair_all.shape[1]
    feature_count = head_count * head_size
    key_rows = pair_all[..., :feature_count].reshape(row_count, row_length, head_count, head_size)
    value_rows = pair_all[..., feature_count:].reshape(row_count, row_length, head_count, head_size)
    scores = jnp.einsum(
        "rche,rlhe->rhcl", query_low, key_rows, preferred_element_type=jnp.float32
    ) * head_size ** (-0.5)
    return (jnp.where(allowed, scores, -1e30), key_rows, value_rows)


def columns_of(matrix, parts, slab_count, index):
    lead = matrix.shape[0]
    width = matrix.shape[1] // (parts * slab_count)
    return matrix.reshape(lead, parts, slab_count, width)[:, :, index].reshape(lead, parts * width)


def entries_of(vector, parts, slab_count, index):
    width = vector.shape[0] // (parts * slab_count)
    return vector.reshape(parts, slab_count, width)[:, index].reshape(parts * width)


def shards_by_slab(
    tokens,
    doc_ids,
    cotangent,
    w_query,
    w_key,
    w_value,
    w_out,
    w_gate,
    w_up,
    w_down,
    g_query,
    g_key,
    g_attn,
    g_ffn,
):
    row_count, piece_len, model_width = tokens.shape
    head_size = HEAD
    feature_count = w_query.shape[1]
    head_count = feature_count // head_size
    tok_count = row_count * piece_len
    scale = head_size ** (-0.5)
    seq_count = lax.axis_size("seq")
    parts = lax.axis_size("dp") * seq_count
    slab_count = SLABS
    gather_all = (
        lax.all_gather(w_query, "dp", axis=0, tiled=True),
        lax.all_gather(w_key, "dp", axis=0, tiled=True),
        lax.all_gather(w_value, "dp", axis=0, tiled=True),
        lax.all_gather(w_out, "dp", axis=0, tiled=True),
        lax.all_gather(w_gate, "dp", axis=0, tiled=True),
        lax.all_gather(w_up, "dp", axis=0, tiled=True),
        lax.all_gather(w_down, "dp", axis=0, tiled=True),
    )
    wq_full, wk_full, wv_full, wo_full, wg_full, wu_full, wd_full = gather_all
    gain_query = g_query.astype(jnp.float32)
    gain_key = g_key.astype(jnp.float32)
    gain_attn = g_attn.astype(jnp.float32)
    gain_ffn = g_ffn.astype(jnp.float32)
    flat_tokens = tokens.reshape(tok_count, model_width)
    query_pre = jnp.dot(flat_tokens, wq_full, preferred_element_type=jnp.float32)
    key_pre = jnp.dot(flat_tokens, wk_full, preferred_element_type=jnp.float32)
    value_pre = jnp.dot(flat_tokens, wv_full, preferred_element_type=jnp.float32)
    query_inv = inverse_rms(query_pre)
    query_unit = query_pre * query_inv
    key_inv = inverse_rms(key_pre)
    key_unit = key_pre * key_inv
    first_row = lax.axis_index("seq") * piece_len
    positions = first_row + jnp.tile(jnp.arange(piece_len, dtype=jnp.int32), row_count)
    cosine, sine_part = rotation(positions, head_size)
    query_rot = rotate(
        (query_unit * gain_query).reshape(tok_count, head_count, head_size), cosine, sine_part
    )
    key_rot = rotate(
        (key_unit * gain_key).reshape(tok_count, head_count, head_size), cosine, sine_part
    )
    query_low = query_rot.astype(jnp.bfloat16).reshape(row_count, piece_len, head_count, head_size)
    key_low = key_rot.astype(jnp.bfloat16).reshape(row_count, piece_len, feature_count)
    value_low = value_pre.astype(jnp.bfloat16).reshape(row_count, piece_len, feature_count)
    pair_low = jnp.concatenate([key_low, value_low], -1)
    ids_low = doc_ids.astype(jnp.bfloat16)
    pair_all, ids_all = (
        lax.all_gather(pair_low, "seq", axis=1, tiled=True),
        lax.all_gather(ids_low, "seq", axis=1, tiled=True),
    )
    query_at = first_row + jnp.arange(piece_len, dtype=jnp.int32)
    allowed = visible(ids_low, ids_all, query_at, jnp.arange(pair_all.shape[1], dtype=jnp.int32))
    masked, _, value_rows = masked_scores(
        query_low, pair_all, allowed, head_count, head_size
    )
    row_max = jnp.max(masked, -1, keepdims=True)
    log_total = jnp.log(jnp.sum(jnp.exp(masked - row_max), -1, keepdims=True)) + row_max
    probs_low = jnp.exp(masked - log_total).astype(jnp.bfloat16)
    mixed = jnp.einsum("rhcl,rlhe->rche", probs_low, value_rows, preferred_element_type=jnp.float32)
    mixed_low = mixed.reshape(tok_count, feature_count).astype(jnp.bfloat16)
    attn_out = jnp.dot(mixed_low, wo_full, preferred_element_type=jnp.float32)
    attn_inv = inverse_rms(attn_out)
    attn_unit = attn_out * attn_inv
    hidden_state = flat_tokens.astype(jnp.float32) + attn_unit * gain_attn
    hidden_low = hidden_state.astype(jnp.bfloat16)
    gate = jnp.dot(hidden_low, wg_full, preferred_element_type=jnp.float32)
    up_proj = jnp.dot(hidden_low, wu_full, preferred_element_type=jnp.float32)
    sigma = jax.nn.sigmoid(gate)
    active = gate * sigma
    inner_low = (active * up_proj).astype(jnp.bfloat16)
    branch = jnp.dot(inner_low, wd_full, preferred_element_type=jnp.float32)
    branch_inv = inverse_rms(branch)
    branch_unit = branch * branch_inv
    result = (
        (hidden_state + branch_unit * gain_ffn)
        .astype(jnp.bfloat16)
        .reshape(row_count, piece_len, model_width)
    )
    wq_back, wk_back, wv_back, wo_back, wg_back, wu_back, wd_back = gather_all
    pair_back, ids_back = (pair_all, ids_all)
    grad_out = cotangent.reshape(tok_count, model_width).astype(jnp.float32)
    ffn_gain_term = jnp.sum(grad_out * branch_unit, 0)
    d_branch = norm_back(grad_out * gain_ffn, branch_unit, branch_inv).astype(jnp.bfloat16)
    d_inner = jnp.einsum("nd,fd->nf", d_branch, wd_back, preferred_element_type=jnp.float32)
    d_gate = (d_inner * up_proj * sigma * (1.0 + gate * (1.0 - sigma))).astype(jnp.bfloat16)
    d_up = (d_inner * active).astype(jnp.bfloat16)
    d_hidden = grad_out + jnp.einsum(
        "nf,df->nd", d_gate, wg_back, preferred_element_type=jnp.float32
    )
    d_hidden = d_hidden + jnp.einsum("nf,df->nd", d_up, wu_back, preferred_element_type=jnp.float32)
    mlp_shares = []
    for index in range(slab_count):
        hidden_part = columns_of(hidden_low, parts, slab_count, index)
        inner_part = columns_of(inner_low, parts, slab_count, index)
        gate_term = jnp.einsum("nd,nf->df", hidden_part, d_gate, preferred_element_type=jnp.float32)
        up_term = jnp.einsum("nd,nf->df", hidden_part, d_up, preferred_element_type=jnp.float32)
        down_term = jnp.einsum(
            "nf,nd->fd", inner_part, d_branch, preferred_element_type=jnp.float32
        )
        ffn_term = entries_of(ffn_gain_term, parts, slab_count, index)
        shares = (
            lax.psum_scatter(down_term, ("dp", "seq"), scatter_dimension=0, tiled=True),
            lax.psum_scatter(gate_term, ("dp", "seq"), scatter_dimension=0, tiled=True),
            lax.psum_scatter(up_term, ("dp", "seq"), scatter_dimension=0, tiled=True),
            lax.psum_scatter(ffn_term, ("dp", "seq"), scatter_dimension=0, tiled=True),
        )
        mlp_shares.append(shares)
    down_grad = jnp.concatenate([s[0] for s in mlp_shares], 0)
    gate_grad = jnp.concatenate([s[1] for s in mlp_shares], 0)
    up_grad = jnp.concatenate([s[2] for s in mlp_shares], 0)
    ffn_grad = jnp.concatenate([s[3] for s in mlp_shares], 0)
    attn_gain_term = jnp.sum(d_hidden * attn_unit, 0)
    d_attn = norm_back(d_hidden * gain_attn, attn_unit, attn_inv).astype(jnp.bfloat16)
    d_mixed = jnp.einsum("nd,fd->nf", d_attn, wo_back, preferred_element_type=jnp.float32).astype(
        jnp.bfloat16
    )
    d_mixed = d_mixed.reshape(row_count, piece_len, head_count, head_size)
    sub_len = piece_len // slab_count
    pair_width = pair_back.shape[-1]
    pair_view = pair_back.reshape(row_count, seq_count, slab_count, sub_len, pair_width)
    ids_view = ids_back.reshape(row_count, seq_count, slab_count, sub_len)

    def slab_scores(index):
        pair_part = pair_view[:, :, index].reshape(row_count, seq_count * sub_len, pair_width)
        ids_part = ids_view[:, :, index].reshape(row_count, seq_count * sub_len)
        key_at = (
            jnp.arange(seq_count, dtype=jnp.int32)[:, None] * piece_len
            + index * sub_len
            + jnp.arange(sub_len, dtype=jnp.int32)[None, :]
        ).reshape(seq_count * sub_len)
        allowed_part = visible(ids_low, ids_part, query_at, key_at)
        masked_part, key_part, value_part = masked_scores(
            query_low, pair_part, allowed_part, head_count, head_size
        )
        probs_part = jnp.exp(masked_part - log_total)
        d_probs_part = jnp.einsum(
            "rche,rlhe->rhcl", d_mixed, value_part, preferred_element_type=jnp.float32
        )
        return (probs_part, d_probs_part, key_part)

    row_dot = jnp.zeros((row_count, head_count, piece_len, 1), jnp.float32)
    for index in range(slab_count):
        probs_part, d_probs_part, key_part = slab_scores(index)
        row_dot = row_dot + jnp.sum(probs_part * d_probs_part, -1, keepdims=True)
    query_acc = jnp.zeros((row_count, piece_len, head_count, head_size), jnp.float32)
    pair_shares = []
    for index in range(slab_count):
        probs_part, d_probs_part, key_part = slab_scores(index)
        d_scores = (probs_part * (d_probs_part - row_dot)).astype(jnp.bfloat16)
        query_acc = query_acc + jnp.einsum(
            "rhcl,rlhe->rche", d_scores, key_part, preferred_element_type=jnp.float32
        )
        key_term = (
            jnp.einsum("rhcl,rche->rlhe", d_scores, query_low, preferred_element_type=jnp.float32)
            * scale
        )
        value_term = jnp.einsum(
            "rhcl,rche->rlhe",
            probs_part.astype(jnp.bfloat16),
            d_mixed,
            preferred_element_type=jnp.float32,
        )
        key_count = seq_count * sub_len
        pair_term = jnp.concatenate(
            [
                key_term.reshape(row_count, key_count, feature_count),
                value_term.reshape(row_count, key_count, feature_count),
            ],
            -1,
        )
        pair_shares.append(
            lax.psum_scatter(
                pair_term.astype(jnp.bfloat16), "seq", scatter_dimension=1, tiled=True
            ).astype(jnp.float32)
        )
    pair_grad = jnp.concatenate(pair_shares, 1)
    d_query = (query_acc * scale).astype(jnp.bfloat16)
    d_key = (
        pair_grad[..., :feature_count]
        .astype(jnp.bfloat16)
        .reshape(tok_count, head_count, head_size)
    )
    d_value = pair_grad[..., feature_count:].astype(jnp.bfloat16).reshape(tok_count, feature_count)
    dq_norm = unrotate(
        d_query.reshape(tok_count, head_count, head_size).astype(jnp.float32), cosine, sine_part
    ).reshape(tok_count, feature_count)
    dk_norm = unrotate(d_key.astype(jnp.float32), cosine, sine_part).reshape(
        tok_count, feature_count
    )
    query_gain_term = jnp.sum(dq_norm * query_unit, 0)
    key_gain_term = jnp.sum(dk_norm * key_unit, 0)
    dq_pre = norm_back(dq_norm * gain_query, query_unit, query_inv).astype(jnp.bfloat16)
    dk_pre = norm_back(dk_norm * gain_key, key_unit, key_inv).astype(jnp.bfloat16)
    d_tokens = d_hidden + jnp.einsum(
        "nf,df->nd", dq_pre, wq_back, preferred_element_type=jnp.float32
    )
    d_tokens = d_tokens + jnp.einsum(
        "nf,df->nd", dk_pre, wk_back, preferred_element_type=jnp.float32
    )
    d_tokens = d_tokens + jnp.einsum(
        "nf,df->nd", d_value, wv_back, preferred_element_type=jnp.float32
    )
    attn_shares = []
    for index in range(slab_count):
        token_part = columns_of(flat_tokens, parts, slab_count, index)
        mixed_part = columns_of(mixed_low, parts, slab_count, index)
        query_term = jnp.einsum("nd,nf->df", token_part, dq_pre, preferred_element_type=jnp.float32)
        key_wterm = jnp.einsum("nd,nf->df", token_part, dk_pre, preferred_element_type=jnp.float32)
        value_wterm = jnp.einsum(
            "nd,nf->df", token_part, d_value, preferred_element_type=jnp.float32
        )
        out_term = jnp.einsum("nf,nd->fd", mixed_part, d_attn, preferred_element_type=jnp.float32)
        gq_term = entries_of(query_gain_term, parts, slab_count, index)
        gk_term = entries_of(key_gain_term, parts, slab_count, index)
        ga_term = entries_of(attn_gain_term, parts, slab_count, index)
        shares = (
            lax.psum_scatter(query_term, ("dp", "seq"), scatter_dimension=0, tiled=True),
            lax.psum_scatter(key_wterm, ("dp", "seq"), scatter_dimension=0, tiled=True),
            lax.psum_scatter(value_wterm, ("dp", "seq"), scatter_dimension=0, tiled=True),
            lax.psum_scatter(out_term, ("dp", "seq"), scatter_dimension=0, tiled=True),
            lax.psum_scatter(gq_term, ("dp", "seq"), scatter_dimension=0, tiled=True),
            lax.psum_scatter(gk_term, ("dp", "seq"), scatter_dimension=0, tiled=True),
            lax.psum_scatter(ga_term, ("dp", "seq"), scatter_dimension=0, tiled=True),
        )
        attn_shares.append(shares)
    query_grad = jnp.concatenate([s[0] for s in attn_shares], 0)
    key_grad = jnp.concatenate([s[1] for s in attn_shares], 0)
    value_grad = jnp.concatenate([s[2] for s in attn_shares], 0)
    out_grad = jnp.concatenate([s[3] for s in attn_shares], 0)
    gq_grad = jnp.concatenate([s[4] for s in attn_shares], 0)
    gk_grad = jnp.concatenate([s[5] for s in attn_shares], 0)
    ga_grad = jnp.concatenate([s[6] for s in attn_shares], 0)
    tokens_grad = d_tokens.reshape(row_count, piece_len, model_width)
    return (
        result,
        tokens_grad,
        query_grad,
        key_grad,
        value_grad,
        out_grad,
        gate_grad,
        up_grad,
        down_grad,
        gq_grad,
        gk_grad,
        ga_grad,
        ffn_grad,
    )


def own_columns(matrix, groups, parts, index):
    width = matrix.shape[1] // (groups * parts)
    pieces = [
        lax.dynamic_slice_in_dim(matrix, (group * parts + index) * width, width, 1)
        for group in range(groups)
    ]
    return jnp.concatenate(pieces, 1) if groups > 1 else pieces[0]


def gather_seq(piece):
    return lax.all_gather(piece, "seq", axis=1, tiled=True)


def scatter_seq(partial):
    return lax.psum_scatter(partial, "seq", scatter_dimension=1, tiled=True)


def swap(value, axis, flip):
    return lax.ppermute(value, axis, [(at, at ^ flip) for at in range(lax.axis_size(axis))])


def place_kernel(spots_ref, *refs, count):
    in_refs, (out_ref, sems) = refs[:count], refs[-2:]
    copies = []
    for at, in_ref in enumerate(in_refs):
        rows, width = in_ref.shape
        row = pl.multiple_of(spots_ref[2 * at], LANES)
        column = pl.multiple_of(spots_ref[2 * at + 1], LANES)
        copies.append(
            pltpu.make_async_copy(
                in_ref, out_ref.at[pl.ds(row, rows), pl.ds(column, width)], sems.at[at]
            )
        )
    for copy in copies:
        copy.start()
    for copy in copies:
        copy.wait()


def placed(pieces, shape, whole=None):
    spots = jnp.stack([jnp.int32(at) for _, row, column in pieces for at in (row, column)])
    outside = pl.BlockSpec(memory_space=pl.ANY)
    given = [] if whole is None else [whole]
    return pl.pallas_call(
        functools.partial(place_kernel, count=len(pieces)),
        grid_spec=pltpu.PrefetchScalarGridSpec(
            num_scalar_prefetch=1,
            grid=(1,),
            in_specs=[
                pl.BlockSpec(piece.shape, lambda at, spots: (0, 0), pipeline_mode=pl.Buffered(1))
                for piece, _, _ in pieces
            ]
            + [outside] * len(given),
            out_specs=outside,
            scratch_shapes=[pltpu.SemaphoreType.DMA((len(pieces),))],
        ),
        out_shape=jax.ShapeDtypeStruct(shape, pieces[0][0].dtype),
        input_output_aliases={1 + len(pieces): 0} if given else {},
        compiler_params=pltpu.CompilerParams(
            vmem_limit_bytes=MEBI
            + sum(piece.size * piece.dtype.itemsize for piece, _, _ in pieces)
        ),
        name="place",
    )(spots, *[piece for piece, _, _ in pieces], *given)


def pieces_for(value, name, split_axis):
    count, index = lax.axis_size(name), lax.axis_index(name)
    width = value.shape[split_axis] // count
    return [
        lax.dynamic_slice_in_dim(value, (index ^ flip) * width, width, split_axis)
        for flip in range(count)
    ]


def swapped(pieces, name):
    return [swap(piece, name, flip) if flip else piece for flip, piece in enumerate(pieces)]


def exchanged(value, name, split_axis):
    return swapped(pieces_for(value, name, split_axis), name)


def pieces_dp(piece):
    half = piece.shape[0] // 2
    first, second = swap(piece, "dp", 1), swap(piece, "dp", 2)
    top, bottom = swap(first[:half], "dp", 2), swap(second[half:], "dp", 1)
    index = lax.axis_index("dp")
    width = piece.shape[0]
    far = (index ^ 3) * width
    return [
        (first, (index ^ 1) * width),
        (second, (index ^ 2) * width),
        (top, far),
        (bottom, far + half),
    ]


def gather_dp(piece):
    rows, width = piece.shape
    pieces = [(piece, lax.axis_index("dp") * rows), *pieces_dp(piece)]
    pieces = [(part, row, 0) for part, row in pieces]
    whole = placed(pieces[:3], (4 * rows, width))
    return placed(pieces[3:], (4 * rows, width), whole)


def sum_dp(sent, kept):
    got = swap(sent[0], "dp", 1), swap(sent[1], "dp", 2)
    wide = [(kept[at].astype(jnp.float32) + got[at].astype(jnp.float32)) for at in range(2)]
    onward = [side[1].astype(jnp.bfloat16) for side in wide]
    last = swap(onward[0], "dp", 2), swap(onward[1], "dp", 1)
    return jnp.concatenate(
        [wide[at][0] + last[at].astype(jnp.float32) for at in range(2)], 0
    )


def shares_for(partial):
    index = lax.axis_index("dp")
    width = partial.shape[0] // 4
    half = width // 2

    def part(flip, side):
        return lax.dynamic_slice_in_dim(partial, (index ^ flip) * width + side * half, half, 0)

    sent = [jnp.stack([part(1, 0), part(3, 0)]), jnp.stack([part(2, 1), part(3, 1)])]
    kept = [jnp.stack([part(0, 0), part(2, 0)]), jnp.stack([part(0, 1), part(1, 1)])]
    return sent, kept


def stored_turned(matrix, after):
    matrix, after = lax.optimization_barrier((matrix, after))
    return with_layout_constraint(matrix.T, Layout((0, 1))), after


def total_seq(value):
    shape = value.shape
    value = value.reshape(-1, LANES)
    flip = 1
    while flip < lax.axis_size("seq"):
        value = value + swap(value, "seq", flip)
        flip *= 2
    return value.reshape(shape)


def share_dp(rows):
    flip = lax.axis_size("dp") // 2
    while flip:
        halves = rows.reshape(2, rows.shape[0] // 2, rows.shape[1])
        side = lax.axis_index("dp") // flip % 2
        kept = lax.dynamic_index_in_dim(halves, side, 0, False)
        sent = lax.dynamic_index_in_dim(halves, 1 - side, 0, False)
        rows = kept + swap(sent, "dp", flip)
        flip //= 2
    return rows[0]


def settle_kernel(index_ref, *refs, groups, width, count):
    in_refs, out_refs = refs[:count], refs[count:]
    for flip, in_ref in enumerate(in_refs):
        source = index_ref[0] ^ flip
        for at, out_ref in enumerate(out_refs):
            for group in range(groups):
                column = (at * groups + group) * width
                place = pl.multiple_of((group * count + source) * width, width)
                out_ref[:, pl.ds(place, width)] = in_ref[:, column : column + width].astype(jnp.float32)


def rows_home(summed, groups, width):
    pieces = exchanged(summed, "seq", 0)
    count = len(pieces)
    rows, total = pieces[0].shape
    outs = total // (groups * width)
    step = min(16, rows)
    wide = count * groups * width
    return pl.pallas_call(
        functools.partial(settle_kernel, groups=groups, width=width, count=count),
        grid_spec=pltpu.PrefetchScalarGridSpec(
            num_scalar_prefetch=1,
            grid=(rows // step,),
            in_specs=[pl.BlockSpec((step, total), lambda r, index: (r, 0))] * count,
            out_specs=[pl.BlockSpec((step, wide), lambda r, index: (r, 0))] * outs,
        ),
        out_shape=[jax.ShapeDtypeStruct((rows, wide), jnp.float32)] * outs,
        compiler_params=pltpu.CompilerParams(vmem_limit_bytes=8 * MEBI),
        name="settle",
    )(lax.axis_index("seq").reshape(1), *pieces)


QUERY_BLOCK = 256


def attention_masks(ids_col, ids_row, block, width, start):
    rows = start + lax.broadcasted_iota(jnp.int32, (block, width), 0)
    columns = lax.broadcasted_iota(jnp.int32, (block, width), 1)
    return (columns <= rows) & (ids_col[start : start + block] == ids_row[:, :width])


def attend_kernel(
    q_ref, k_ref, v_ref, qinv_ref, kinv_ref, cos_ref, sin_ref, gq_ref, gk_ref, col_ref, row_ref,
    qlow_ref, klow_ref, vlow_ref, mixed_ref, total_ref, *, scale
):
    low = jnp.bfloat16
    half = q_ref.shape[-1] // 2
    cosine, sine_part = cos_ref[...], sin_ref[...]

    def rotated(ref, inv_ref, gain_ref):
        value = ref[0] * inv_ref[0] * gain_ref[...]
        return (value * cosine + pltpu.roll(value, half, 1) * sine_part).astype(low)

    qlow_ref[0] = rotated(q_ref, qinv_ref, gq_ref)
    klow_ref[0] = rotated(k_ref, kinv_ref, gk_ref)
    vlow_ref[0] = v_ref[0].astype(low)
    length = q_ref.shape[1]
    block = min(QUERY_BLOCK, length)
    ids_col, ids_row = col_ref[0], row_ref[0]
    for start in range(0, length, block):
        width = start + block
        scores = lax.dot_general(
            qlow_ref[0, start:width], klow_ref[0, :width], (((1,), (1,)), ((), ())),
            preferred_element_type=jnp.float32,
        ) * scale
        allowed = attention_masks(ids_col, ids_row, block, width, start)
        masked = jnp.where(allowed, scores, -1e30)
        row_max = jnp.max(masked, -1, keepdims=True)
        log_total = jnp.log(jnp.sum(jnp.exp(masked - row_max), -1, keepdims=True)) + row_max
        total_ref[0, 0, start:width] = log_total
        probs = jnp.exp(masked - log_total).astype(low)
        mixed_ref[0, start:width] = jnp.dot(
            probs, vlow_ref[0, :width], preferred_element_type=jnp.float32
        ).astype(low)


def attend_back_kernel(
    q_ref, k_ref, qinv_ref, kinv_ref, cos_ref, sin_ref, gq_ref, gk_ref, col_ref, row_ref,
    qlow_ref, klow_ref, vlow_ref, total_ref, dmixed_ref,
    dq_ref, dk_ref, dv_ref, dots_ref, gains_ref, key_acc, value_acc, query_acc, *, scale
):
    low = jnp.bfloat16
    half = q_ref.shape[-1] // 2
    length = q_ref.shape[1]
    block = min(QUERY_BLOCK, length)
    ids_col, ids_row = col_ref[0], row_ref[0]
    turned = (((0,), (0,)), ((), ()))
    across = (((1,), (1,)), ((), ()))
    key_acc[...] = jnp.zeros_like(key_acc)
    value_acc[...] = jnp.zeros_like(value_acc)
    for start in range(0, length, block):
        width = start + block
        query = qlow_ref[0, start:width]
        d_mixed = dmixed_ref[0, start:width]
        keys = klow_ref[0, :width]
        scores = lax.dot_general(query, keys, across, preferred_element_type=jnp.float32) * scale
        allowed = attention_masks(ids_col, ids_row, block, width, start)
        probs = jnp.exp(jnp.where(allowed, scores, -1e30) - total_ref[0, 0, start:width])
        d_probs = lax.dot_general(
            d_mixed, vlow_ref[0, :width], across, preferred_element_type=jnp.float32
        )
        row_dot = jnp.sum(probs * d_probs, -1, keepdims=True)
        d_scores = (probs * (d_probs - row_dot)).astype(low)
        query_acc[start:width] = jnp.dot(d_scores, keys, preferred_element_type=jnp.float32)
        key_acc[:width] += lax.dot_general(d_scores, query, turned, preferred_element_type=jnp.float32)
        value_acc[:width] += lax.dot_general(
            probs.astype(low), d_mixed, turned, preferred_element_type=jnp.float32
        )
    dv_ref[0] = value_acc[...].astype(low)
    cosine, sine_part = cos_ref[...], sin_ref[...]

    def turned_back(acc, ref, inv_ref, gain_ref, out_ref, at):
        value = (acc[...] * scale).astype(low).astype(jnp.float32)
        value = value * cosine - pltpu.roll(value, half, 1) * sine_part
        unit = ref[0] * inv_ref[0]
        gains_ref[0, at : at + 1] = jnp.sum(value * unit, 0, keepdims=True)
        value = value * gain_ref[...]
        out_ref[0] = value
        return jnp.sum(value * unit, -1, keepdims=True)

    query_dot = turned_back(query_acc, q_ref, qinv_ref, gq_ref, dq_ref, 0)
    key_dot = turned_back(key_acc, k_ref, kinv_ref, gk_ref, dk_ref, 1)
    lane = lax.broadcasted_iota(jnp.int32, (length, LANES), 1)
    dots = jnp.where(lane == 0, query_dot, jnp.where(lane == 1, key_dot, 0.0)).T[:8]

    @pl.when(pl.program_id(1) == 0)
    def _():
        dots_ref[0] = dots

    @pl.when(pl.program_id(1) != 0)
    def _():
        dots_ref[0] += dots


def attention_specs(length, heads, head_size):
    wide = lambda at: pl.BlockSpec((1, length, head_size), lambda r, h, at=at: (r, 0, at * heads + h))
    thin = pl.BlockSpec((1, length, 1), lambda r, h: (r, 0, 0))
    table = pl.BlockSpec((length, head_size), lambda r, h: (0, 0))
    gain = pl.BlockSpec((1, head_size), lambda r, h: (0, h))
    flat = pl.BlockSpec((1, 1, length), lambda r, h: (r, 0, 0))
    total = pl.BlockSpec((1, 1, length, 1), lambda r, h: (r, h, 0, 0))
    return wide, thin, table, gain, flat, total


def attend(qkv, inverses, tables, gains, ids, head_size, scale):
    rows, length, width = qkv.shape
    heads = width // (3 * head_size)
    wide, thin, table, gain, flat, total = attention_specs(length, heads, head_size)
    narrow = jax.ShapeDtypeStruct((rows, length, heads * head_size), jnp.bfloat16)
    return pl.pallas_call(
        functools.partial(attend_kernel, scale=scale),
        grid=(rows, heads),
        in_specs=[wide(0), wide(1), wide(2), thin, thin, table, table, gain, gain, thin, flat],
        out_specs=[wide(0), wide(0), wide(0), wide(0), total],
        out_shape=[narrow] * 4 + [jax.ShapeDtypeStruct((rows, heads, length, 1), jnp.float32)],
        name="attend",
    )(qkv, qkv, qkv, *inverses, *tables, *gains, ids[:, :, None], ids[:, None, :])


def attend_back(qkv, inverses, tables, gains, ids, kept, d_mixed, head_size, scale):
    rows, length, width = qkv.shape
    heads = width // (3 * head_size)
    wide, thin, table, gain, flat, total = attention_specs(length, heads, head_size)
    shape = (rows, length, heads * head_size)
    return pl.pallas_call(
        functools.partial(attend_back_kernel, scale=scale),
        grid=(rows, heads),
        in_specs=[wide(0), wide(1), thin, thin, table, table, gain, gain, thin, flat]
        + [wide(0), wide(0), wide(0), total, wide(0)],
        out_specs=[
            wide(0),
            wide(0),
            wide(0),
            pl.BlockSpec((1, 8, length), lambda r, h: (r, 0, 0)),
            pl.BlockSpec((1, 2, head_size), lambda r, h: (r, 0, h)),
        ],
        out_shape=[
            jax.ShapeDtypeStruct(shape, jnp.float32),
            jax.ShapeDtypeStruct(shape, jnp.float32),
            jax.ShapeDtypeStruct(shape, jnp.bfloat16),
            jax.ShapeDtypeStruct((rows, 8, length), jnp.float32),
            jax.ShapeDtypeStruct((rows, 2, heads * head_size), jnp.float32),
        ],
        scratch_shapes=[pltpu.VMEM((length, head_size), jnp.float32)] * 3,
        name="attend_back",
    )(qkv, qkv, *inverses, *tables, *gains, ids[:, :, None], ids[:, None, :], *kept, d_mixed)


def shards_by_feature(
    tokens,
    doc_ids,
    cotangent,
    w_query,
    w_key,
    w_value,
    w_out,
    w_gate,
    w_up,
    w_down,
    g_query,
    g_key,
    g_attn,
    g_ffn,
):
    row_count, piece_len, model_width = tokens.shape
    head_size = HEAD
    feature_count = w_query.shape[1]
    scale = head_size ** (-0.5)
    seq_count = lax.axis_size("seq")
    dp_count = lax.axis_size("dp")
    seq_at = lax.axis_index("seq")
    row_len = piece_len * seq_count
    all_count = row_count * row_len
    tok_count = row_count * piece_len
    own_features = feature_count // seq_count
    own_hidden = w_gate.shape[1] // seq_count
    low = jnp.bfloat16

    def own_piece(tensor):
        view = tensor.reshape(row_count, row_len, -1)
        return lax.dynamic_slice_in_dim(view, seq_at * piece_len, piece_len, 1).reshape(tok_count, -1)

    w_qkv = gather_dp(jnp.concatenate([own_columns(w, 1, seq_count, seq_at) for w in (w_query, w_key, w_value)], 1))
    tokens_all = gather_seq(tokens).reshape(all_count, model_width)
    ids_all = total_seq(
        lax.dynamic_update_slice_in_dim(
            jnp.zeros((row_count, row_len), jnp.int32), doc_ids, seq_at * piece_len, 1
        )
    )
    core = seq_at % 2
    half = model_width // 2
    out_rows = w_out.shape[0]
    out_pieces = pieces_dp(lax.dynamic_slice_in_dim(w_out, core * half, half, 1))
    other_pieces = [(swap(piece, "seq", 1), row) for piece, row in out_pieces]
    wo_full = placed(
        [(w_out, lax.axis_index("dp") * out_rows, 0)]
        + [(piece, row, core * half) for piece, row in out_pieces]
        + [(piece, row, half - core * half) for piece, row in other_pieces],
        (feature_count, model_width),
    )
    w_hidden = gather_dp(jnp.concatenate([own_columns(w, dp_count, seq_count, seq_at) for w in (w_gate, w_up)], 1))
    w_back = gather_dp(
        lax.dynamic_slice_in_dim(
            w_down, seq_at * (own_hidden // dp_count), own_hidden // dp_count, 0
        ),
    )
    gain_query = lax.dynamic_slice_in_dim(g_query, seq_at * own_features, own_features).astype(jnp.float32)
    gain_key = lax.dynamic_slice_in_dim(g_key, seq_at * own_features, own_features).astype(jnp.float32)
    gain_attn = g_attn.astype(jnp.float32)
    gain_ffn = g_ffn.astype(jnp.float32)

    tokens_all, ids_all = lax.optimization_barrier((tokens_all, ids_all))
    qkv = jnp.dot(tokens_all, w_qkv, preferred_element_type=jnp.float32)
    query_pre = qkv[:, :own_features]
    key_pre = qkv[:, own_features : 2 * own_features]
    squares = jnp.stack([jnp.sum(query_pre * query_pre, -1), jnp.sum(key_pre * key_pre, -1)])
    cosine, sine_part = rotation(jnp.arange(row_len, dtype=jnp.int32), head_size)
    tables = jnp.concatenate([cosine, cosine], 1), jnp.concatenate([-sine_part, sine_part], 1)
    inverse = lax.rsqrt(total_seq(squares) / feature_count + eps)
    inverses = [inverse[at].reshape(row_count, row_len, 1) for at in range(2)]
    norm_gains = gain_query[None, :], gain_key[None, :]
    qkv_rows = qkv.reshape(row_count, row_len, 3 * own_features)
    *kept, mixed_low, log_total = attend(
        qkv_rows, inverses, tables, norm_gains, ids_all, head_size, scale
    )
    mixed_low = mixed_low.reshape(all_count, own_features)
    mixed_all = lax.all_gather(mixed_low, "seq", axis=1, tiled=True)
    attn_out = jnp.dot(mixed_all, wo_full, preferred_element_type=jnp.float32)
    attn_inv_all = inverse_rms(attn_out)
    hidden_all = tokens_all.astype(jnp.float32) + attn_out * attn_inv_all * gain_attn
    hidden_low = hidden_all.astype(low)
    hidden_low, attn_inv, attn_own = lax.optimization_barrier(
        (hidden_low, own_piece(attn_inv_all), own_piece(attn_out))
    )
    attn_unit = attn_own * attn_inv
    hidden_state = tokens.reshape(tok_count, model_width).astype(jnp.float32) + attn_unit * gain_attn

    gate_up = jnp.dot(hidden_low, w_hidden, preferred_element_type=jnp.float32)
    gate, up_proj = gate_up[:, :own_hidden], gate_up[:, own_hidden:]
    sigma = jax.nn.sigmoid(gate)
    active = gate * sigma
    inner_low = (active * up_proj).astype(low)
    branch_part = jnp.dot(inner_low, w_back, preferred_element_type=jnp.float32).astype(low)
    w_hidden_turned, branch_part = stored_turned(w_hidden, branch_part)
    w_back_turned, branch_part = stored_turned(w_back, branch_part)
    branch = (
        scatter_seq(branch_part.reshape(row_count, row_len, model_width))
        .astype(jnp.float32)
        .reshape(tok_count, model_width)
    )
    branch_inv = inverse_rms(branch)
    branch_unit = branch * branch_inv
    result = (
        (hidden_state + branch_unit * gain_ffn)
        .astype(low)
        .reshape(row_count, piece_len, model_width)
    )

    grad_out = cotangent.reshape(tok_count, model_width).astype(jnp.float32)
    ffn_gain_term = jnp.sum(grad_out * branch_unit, 0)
    d_branch = norm_back(grad_out * gain_ffn, branch_unit, branch_inv).astype(low)
    d_branch_all = gather_seq(d_branch.reshape(row_count, piece_len, model_width)).reshape(all_count, model_width)
    d_inner = jnp.dot(d_branch_all, w_back_turned, preferred_element_type=jnp.float32)
    d_gate = (d_inner * up_proj * sigma * (1.0 + gate * (1.0 - sigma))).astype(low)
    d_up = (d_inner * active).astype(low)
    d_gate_up = jnp.concatenate([d_gate, d_up], 1)
    d_hidden_part = jnp.dot(d_gate_up, w_hidden_turned, preferred_element_type=jnp.float32).astype(low)
    d_hidden_sum = scatter_seq(d_hidden_part.reshape(row_count, row_len, model_width))
    gate_part = jnp.einsum("nd,nf->df", hidden_low, d_gate, preferred_element_type=jnp.float32).astype(low)
    up_part = jnp.einsum("nd,nf->df", hidden_low, d_up, preferred_element_type=jnp.float32).astype(low)
    down_part = jnp.einsum("nf,nd->fd", inner_low, d_branch_all, preferred_element_type=jnp.float32).astype(low)
    down_grad = sum_dp(*shares_for(down_part))
    gate_own = sum_dp(*shares_for(gate_part)).astype(low)
    up_own = sum_dp(*shares_for(up_part)).astype(low)
    d_hidden = grad_out + d_hidden_sum.astype(jnp.float32).reshape(tok_count, model_width)

    attn_gain_term = jnp.sum(d_hidden * attn_unit, 0)
    d_attn = norm_back(d_hidden * gain_attn, attn_unit, attn_inv).astype(low)
    d_mixed = jnp.einsum("nd,fd->nf", d_attn, wo_full, preferred_element_type=jnp.float32).astype(low)

    def own_columns_of_all(tensor):
        split = tensor.reshape(row_count, piece_len, seq_count, -1).transpose(2, 0, 1, 3)
        width = split.shape[-1]
        split = lax.all_to_all(split.reshape(seq_count, tok_count, width), "seq", split_axis=0, concat_axis=0)
        split = split.reshape(seq_count, row_count, piece_len, width).transpose(1, 0, 2, 3)
        return split.reshape(row_count, row_len, width)

    d_mixed = own_columns_of_all(d_mixed)
    (gate_grad,) = rows_home(gate_own, dp_count, own_hidden // dp_count)
    (up_grad,) = rows_home(up_own, dp_count, own_hidden // dp_count)

    dq_gained, dk_gained, d_value, dots, gain_terms = attend_back(
        qkv_rows, inverses, tables, norm_gains, ids_all, (*kept, log_total), d_mixed, head_size, scale
    )
    norm_terms = lax.dynamic_update_slice_in_dim(
        jnp.zeros((2, feature_count), jnp.float32), jnp.sum(gain_terms, 0), seq_at * own_features, 1
    )
    dots = dots[:, :2].transpose(1, 0, 2).reshape(-1, LANES)
    stat_rows = dots.shape[0]
    sums = total_seq(
        jnp.concatenate(
            [dots]
            + [part.reshape(-1, LANES) for part in (norm_terms, attn_gain_term, ffn_gain_term)]
        )
    )
    means = sums[:stat_rows].reshape(2, all_count) / feature_count

    def norm_back_wide(gained, pre, at):
        inv = inverse[at][:, None]
        gained = gained.reshape(all_count, own_features)
        return (inv * (gained - pre * inv * means[at][:, None])).astype(low)

    dq_pre = norm_back_wide(dq_gained, query_pre, 0)
    dk_pre = norm_back_wide(dk_gained, key_pre, 1)
    d_value = d_value.reshape(all_count, own_features)
    d_qkv = jnp.concatenate([dq_pre, dk_pre, d_value], 1)
    qkv_part = jnp.einsum("nd,nf->df", tokens_all, d_qkv, preferred_element_type=jnp.float32).astype(low)
    d_qkv, qkv_part = lax.optimization_barrier((d_qkv, qkv_part))
    d_tokens_part = jnp.einsum("nf,df->nd", d_qkv, w_qkv, preferred_element_type=jnp.float32).astype(low)
    d_tokens_sum = scatter_seq(d_tokens_part.reshape(row_count, row_len, model_width))
    d_tokens = d_hidden + d_tokens_sum.astype(jnp.float32).reshape(tok_count, model_width)
    qkv_own = sum_dp(*shares_for(qkv_part)).astype(low)
    query_grad, key_grad, value_grad = rows_home(qkv_own, 1, own_features)
    d_attn_own = own_columns_of_all(d_attn).reshape(all_count, -1)
    out_part = jnp.einsum("nf,nd->fd", mixed_all, d_attn_own, preferred_element_type=jnp.float32).astype(low)
    out_own = sum_dp(*shares_for(out_part)).astype(low)
    (out_grad,) = rows_home(out_own, 1, own_features)
    share = feature_count // (dp_count * seq_count)
    gains = lax.dynamic_index_in_dim(
        sums[stat_rows:].reshape(4, dp_count, seq_count, share), seq_at, 2, False
    )
    gains = share_dp(gains.transpose(1, 0, 2).reshape(dp_count, 4 * share)).reshape(4, share)
    return (
        result,
        d_tokens.reshape(row_count, piece_len, model_width),
        query_grad,
        key_grad,
        value_grad,
        out_grad,
        gate_grad,
        up_grad,
        down_grad,
        gains[0],
        gains[1],
        gains[2],
        gains[3],
    )


def shards(tokens, doc_ids, cotangent, w_query, *rest):
    if w_query.shape[1] // HEAD % lax.axis_size("seq"):
        return shards_by_slab(tokens, doc_ids, cotangent, w_query, *rest)
    return shards_by_feature(tokens, doc_ids, cotangent, w_query, *rest)


def solution(mesh):
    return jax.shard_map(
        shards,
        mesh=mesh,
        in_specs=(
            P("dp", "seq", None),
            P("dp", "seq"),
            P("dp", "seq", None),
            P("dp", None),
            P("dp", None),
            P("dp", None),
            P("dp", None),
            P("dp", None),
            P("dp", None),
            P("dp", None),
            P(),
            P(),
            P(),
            P(),
        ),
        out_specs=(
            P("dp", "seq", None),
            P("dp", "seq", None),
            P(("dp", "seq"), None),
            P(("dp", "seq"), None),
            P(("dp", "seq"), None),
            P(("dp", "seq"), None),
            P(("dp", "seq"), None),
            P(("dp", "seq"), None),
            P(("dp", "seq"), None),
            P(("dp", "seq")),
            P(("dp", "seq")),
            P(("dp", "seq")),
            P(("dp", "seq")),
        ),
        check_vma=False,
    )
```
